32 devices in a mesh: dp: 4 (over z), expert: 8 (over y, x, core).
Axes of the slice: x: 2, y: 2, z: 4, core: 2. Of those that a mesh axis runs over, the one named last changes fastest.
Arguments:
- tokens: bfloat16 [2, 2048, 1536], P(None, ('dp', 'expert')), may hold values from -6 to 6
- segments: int32 [2, 32, 64], P(None, ('dp', 'expert')), may hold values from 0 to 1, never falling along the last dimension, each value on 1 to 56 neighbouring positions
- routes: int32 [2, 2048, 8], P(None, ('dp', 'expert')), may hold values from 0 to 23, all different within a row; in each aligned block of 64 rows (0 to 63, 64 to 127, ..., all dimensions but the last counted through in order) at most 32 rows name the same one
- cotangent: bfloat16 [2, 2048, 1536], P(None, ('dp', 'expert')), may hold values from -6 to 6
- gain_attn: bfloat16 [1536], P(('dp', 'expert')), may hold values from 0.5 to 1.5
- attn_in: bfloat16 [1536, 2560], P(('dp', 'expert')), may hold values from -0.15625 to 0.15625
- attn_out: bfloat16 [1536, 1536], P(('dp', 'expert')), may hold values from -1.25 to 1.25
- gain_ffn: bfloat16 [1536], P(('dp', 'expert')), may hold values from 0.5 to 1.5
- router: bfloat16 [1536, 24], P(('dp', 'expert')), may hold values from -0.078125 to 0.078125
- expert_in: bfloat16 [24, 1536, 1024], P('expert', 'dp'), may hold values from -0.15625 to 0.15625
- expert_out: bfloat16 [24, 512, 1536], P('expert', 'dp'), may hold values from -1 to 1
Outputs:
- output: bfloat16 [2, 2048, 1536], P(None, ('dp', 'expert'))
- grad_tokens: float32 [2, 2048, 1536], P(None, ('dp', 'expert'))
- grad_gain_attn: float32 [1536], P(('dp', 'expert'))
- grad_attn_in: float32 [1536, 2560], P(('dp', 'expert'))
- grad_attn_out: float32 [1536, 1536], P(('dp', 'expert'))
- grad_gain_ffn: float32 [1536], P(('dp', 'expert'))
- grad_router: float32 [1536, 24], P(('dp', 'expert'))
- grad_expert_in: float32 [24, 1536, 1024], P('expert', 'dp')
- grad_expert_out: float32 [24, 512, 1536], P('expert', 'dp')
The draws below stay inside these ranges and needn't reach their ends.
Inputs may be any that keep to these rules, and one draw needn't show every extreme that they name: `routes`: in each aligned block of 64 rows (one pack), no expert is named by more than 32 pairs, a bound that some block reaches; a row names 8 different experts. `segments`: each pack holds 2 whole sequences numbered in order, each of 1 to 56 tokens.
All inputs are finite; a program needn't handle non-finite values.
Results may differ from the reference program's by a relative error of at most 0.014.
The reference program's roundings to bfloat16 on the way count: a program that leaves them out, or rounds other values in their place, can miss the bound.
Values may be sent and summed in bfloat16 or wider, within the bound.
A program may use at most 192 MiB of HBM per device.

```python
import math
import jax
import jax.numpy as jnp
import numpy as np
from jax import lax

D = 1536
HEADS = 24
KV_HEADS = 8
HEAD = 64
FF = 512
TOP_K = 8
MICRO = 2
SEQS = 2
TOK_DEV = 64
LONGEST = 56
EXPERTS = 24
CAP = 32
PACKS = 32
ROWS = 2048
QKV = 2560


def shard_levels(key, extent, cuts, smallest, largest):
    def one(axis_at, shards_of):
        draws = jax.random.uniform(jax.random.fold_in(jax.random.fold_in(key, 6), axis_at), (shards_of,), jnp.float32, smallest / len(cuts), largest / len(cuts))
        return jnp.repeat(jnp.exp(draws), extent[axis_at] // shards_of).reshape((-1,) + (1,) * (len(extent) - axis_at - 1))

    loudness = one(*cuts[0])
    for cut in cuts[1:]:
        loudness = loudness * one(*cut)
    return loudness


def profile(number_of, total, limit, slope):
    loads = [(1 << 20) // math.isqrt(rank ** slope) + 1 for rank in range(2, number_of + 1)]
    surplus, counts = total - limit - (number_of - 1), [1] * (number_of - 1)
    while surplus > 0:
        movable = [i for i in range(number_of - 1) if counts[i] < limit]
        whole, left = sum([loads[i] for i in movable]), surplus
        for i in movable:
            more = min(limit - counts[i], max(1, left * loads[i] // whole), surplus)
            counts[i] = counts[i] + more
            surplus = surplus - more
    return np.array([limit] + counts)


def ragged_sizes(stream_key, number_of, total, most, skew):
    if number_of == 2:
        one = jax.random.randint(stream_key, (), max(1, total - most), min(most, total - 1) + 1)
        return jnp.stack([one, total - one])
    sizes = jnp.asarray(profile(number_of, total, most, skew), jnp.int32)
    pairs = (number_of - 1) // 2
    giver, sink = sizes[1:1 + 2 * pairs:2], sizes[2:2 + 2 * pairs:2]
    margin = jnp.minimum(giver - 1, most - sink)
    passed = jax.random.randint(jax.random.fold_in(stream_key, 1), (pairs,), 0, 1 << 20) % (margin + 1)
    sizes = sizes.at[1:1 + 2 * pairs:2].set(giver - passed).at[2:2 + 2 * pairs:2].set(sink + passed)
    return sizes[jax.random.permutation(jax.random.fold_in(stream_key, 2), number_of)]


def shared_out(key, own, number, rows, number_of, top, bound, lean):
    sequence = jax.random.permutation(key, number_of)
    crowded, usual = shares(number_of, rows * top, bound, lean, True), shares(number_of, rows * top, bound, lean, False)
    places = jnp.arange(number_of)

    def named(tallies, turn):
        used = int((tallies > 0).sum())
        fixed = max(1, used // 4)
        moved = fixed + (places - fixed + turn * (used - fixed)) % max(1, number_of - fixed)
        return jnp.zeros((number_of,), jnp.int32).at[sequence[jnp.where(places < fixed, places, moved)]].set(jnp.asarray(tallies, jnp.int32))

    tallies = jnp.where(number % 4 == 0, named(crowded, number // 4), named(usual, number - number // 4 - 1))
    mixed = jax.random.permutation(jax.random.fold_in(own, 3), number_of)
    giver, taker = mixed[0:number_of // 2 * 2:2], mixed[1:number_of // 2 * 2:2]
    slack = jnp.minimum(tallies[giver] - 1, bound - tallies[taker]) // 2
    slack = jnp.where((giver == sequence[0]) | (taker == sequence[0]) | (tallies[taker] == 0), 0, jnp.maximum(slack, 0))
    moved = jax.random.randint(jax.random.fold_in(own, 4), (number_of // 2,), 0, 1 << 20) % (slack + 1)
    tallies = tallies.at[giver].add(-moved).at[taker].add(moved)
    members = jnp.searchsorted(jnp.cumsum(tallies), jnp.arange(rows * top), side="right").astype(jnp.int32)
    grid = members.reshape(top, rows).T
    grid = grid[jax.random.permutation(jax.random.fold_in(own, 1), rows)]
    turn = jax.random.randint(jax.random.fold_in(own, 2), (rows, 1), 0, top)
    return jnp.take_along_axis(grid, (jnp.arange(top)[None, :] + turn) % top, axis=1)


def shares(amount, total, most, skew, full):
    loads = [(1 << 20) // math.isqrt(rank ** skew) + 1 for rank in range(1, amount + 1)]
    largest = most if full else min(most, max(-(-total // amount), total * loads[0] // sum(loads)))
    least = 1 if total - largest >= amount - 1 else 0
    given, rest = [largest] + [least] * (amount - 1), total - largest - least * (amount - 1)
    while rest > 0:
        movable = [i for i in range(1, amount) if given[i] < largest] or [i for i in range(1, amount) if given[i] < most]
        mass, budget = sum([loads[i] for i in movable]), rest
        for i in movable:
            extra = min(most - given[i], max(1, budget * loads[i] // mass), rest)
            given[i] = given[i] + extra
            rest = rest - extra
    return np.array(given)


def gaussian(rng, extent, scale, most, split=(), kind=jnp.bfloat16):
    factor_of = shard_levels(rng, extent, split, -0.22, 0.18) if split else 1.0
    drawn = jax.random.normal(rng, extent, jnp.float32) * scale * factor_of
    return jnp.minimum(jnp.maximum(drawn, -most), most).astype(kind)


def setup_inputs(seed: int = 0) -> dict:
    keys = jax.random.split(jax.random.key(seed), 12)
    tokens = gaussian(keys[0], (MICRO, ROWS, D), 1.0, 6.0, ((1, 32),))
    segments = jax.vmap(lambda own: jnp.searchsorted(jnp.cumsum(ragged_sizes(own, SEQS, TOK_DEV, LONGEST, 0)), jnp.arange(TOK_DEV), side="right"))(jax.random.split(keys[1], MICRO * PACKS)).reshape((MICRO, PACKS, TOK_DEV)).astype(jnp.int32)
    routes_keys = jax.random.split(jax.random.fold_in(keys[2], 1), MICRO * ROWS // TOK_DEV)
    routes_turns = jax.random.permutation(jax.random.fold_in(keys[2], 3), MICRO * ROWS // TOK_DEV)
    routes = jax.vmap(lambda own, number: shared_out(jax.random.fold_in(keys[2], 2), own, number, TOK_DEV, EXPERTS, TOP_K, CAP, 1))(routes_keys, routes_turns).reshape((MICRO, ROWS, TOP_K))
    cotangent = gaussian(keys[3], (MICRO, ROWS, D), 1.0, 6.0, ((1, 32),))
    gain_attn = jnp.clip(1.0 + 0.1 * jax.random.normal(keys[4], (D,), jnp.float32), 0.5, 1.5).astype(jnp.bfloat16)
    attn_in = gaussian(keys[5], (D, QKV), D ** -0.5, 0.15625, ((0, 32),))
    attn_out = gaussian(keys[6], (HEADS * HEAD, D), (D // 64) ** -0.5, 1.25, ((0, 32),))
    gain_ffn = jnp.clip(1.0 + 0.1 * jax.random.normal(keys[7], (D,), jnp.float32), 0.5, 1.5).astype(jnp.bfloat16)
    router = gaussian(keys[8], (D, EXPERTS), (4 * D) ** -0.5, 0.078125, ((0, 32),))
    expert_in = gaussian(keys[9], (EXPERTS, D, 2 * FF), D ** -0.5, 0.15625, ((0, 8), (1, 4)))
    expert_out = gaussian(keys[10], (EXPERTS, FF, D), (FF // 16) ** -0.5, 1.0, ((0, 8), (1, 4)))
    return dict(tokens=tokens, segments=segments, routes=routes, cotangent=cotangent, gain_attn=gain_attn, attn_in=attn_in, attn_out=attn_out, gain_ffn=gain_ffn, router=router, expert_in=expert_in, expert_out=expert_out)


norm_eps = 1e-06
rope_base = 10000.0
neg_large = -1e+30
highest = lax.Precision.HIGHEST

@jax.custom_vjp
def low(v):
    return lax.optimization_barrier(v.astype(jnp.bfloat16)).astype(jnp.float32)

@jax.custom_vjp
def low_back(v):
    return v

def low_keep(v):
    return (low(v), None)

def low_pass(kept, grad):
    return (grad,)

def back_keep(v):
    return (v, None)

def back_low(kept, grad):
    return (low(grad),)
low.defvjp(low_keep, low_pass)
low_back.defvjp(back_keep, back_low)

def rope_tables(segment, half_width):
    row_count = segment.shape[0]
    places = jnp.arange(row_count, dtype=jnp.int32)
    same_seq = segment[:, None] == segment[None, :]
    seq_start = lax.optimization_barrier(jnp.min(jnp.where(same_seq, places[None, :], row_count), axis=1))
    offset = (places - seq_start).astype(jnp.float32)
    frequencies = rope_base ** (-jnp.arange(half_width, dtype=jnp.float32) / half_width)
    angles = offset[:, None] * frequencies[None, :]
    causal = same_seq & (places[None, :] <= places[:, None])
    return (jnp.cos(angles), jnp.sin(angles), causal)

def rotate(operand, cosine, sine_table):
    half_width = operand.shape[-1] // 2
    front_part = operand[..., :half_width]
    back_part = operand[..., half_width:]
    return jnp.concatenate([front_part * cosine - back_part * sine_table, back_part * cosine + front_part * sine_table], axis=-1)

def slot_targets(route_now, expert_count, capacity):
    flat_ids = route_now.reshape(-1).astype(jnp.int32)
    onehot = (flat_ids[:, None] == jnp.arange(expert_count, dtype=jnp.int32)[None, :]).astype(jnp.int32)
    earlier = jnp.cumsum(onehot, axis=0) - onehot
    slot_index = lax.optimization_barrier(jnp.sum(earlier * onehot, axis=1))
    return (flat_ids * capacity + slot_index).astype(jnp.int32)

def layer_block(params, item):
    inputs, segment, route_now = item
    gain_attn, qkv_weight, out_weight, gain_ffn, router_weight, expert_up, expert_down = params
    row_count = inputs.shape[0]
    groups = HEADS // KV_HEADS
    q_width = HEADS * HEAD
    k_width = KV_HEADS * HEAD
    score_scale = HEAD ** (-0.5)
    inv_first = lax.rsqrt(lax.optimization_barrier(jnp.mean(inputs * inputs, axis=1, keepdims=True)) + norm_eps)
    normed_first = low(inputs * inv_first * gain_attn)
    qkv_full = low_back(jnp.dot(normed_first, qkv_weight, precision=highest))
    cosine, sine_table, causal = rope_tables(segment, HEAD // 2)
    queries = low(rotate(qkv_full[:, :q_width].reshape(row_count, KV_HEADS, groups, HEAD), cosine[:, None, None, :], sine_table[:, None, None, :]))
    key_rot = low(rotate(qkv_full[:, q_width:q_width + k_width].reshape(row_count, KV_HEADS, HEAD), cosine[:, None, :], sine_table[:, None, :]))
    values = low(qkv_full[:, q_width + k_width:].reshape(row_count, KV_HEADS, HEAD))
    scores = jnp.einsum('tkgh,skh->kgts', queries, key_rot, precision=highest) * score_scale
    scores = low_back(jnp.where(causal[None, None], scores, neg_large))
    soft_probs = jax.nn.softmax(scores, axis=-1)
    attn_mixed = jnp.einsum('kgts,skh->tkgh', low(soft_probs), values, precision=highest)
    attn_mixed = low_back(low(attn_mixed.reshape(row_count, q_width)))
    middle = inputs + low_back(jnp.dot(attn_mixed, out_weight, precision=highest))
    inv_second = lax.rsqrt(lax.optimization_barrier(jnp.mean(middle * middle, axis=1, keepdims=True)) + norm_eps)
    normed_second = low(middle * inv_second * gain_ffn)
    expert_count = router_weight.shape[1]
    capacity = CAP
    logits = low_back(jnp.dot(normed_second, router_weight, precision=highest))
    chosen = (route_now[:, :, None] == jnp.arange(expert_count, dtype=jnp.int32)[None, None, :]).astype(jnp.float32)
    picked_logits = lax.optimization_barrier(jnp.sum(chosen * logits[:, None, :], axis=-1))
    gate_values = jax.nn.softmax(picked_logits, axis=-1)
    targets = slot_targets(route_now, expert_count, capacity)
    source_rows = low_back(jnp.repeat(normed_second, TOP_K, axis=0))
    dispatched = jnp.zeros((expert_count * capacity, D), jnp.float32).at[targets].set(source_rows)
    dispatched = dispatched.reshape(expert_count, capacity, D)
    gate_up = low_back(jnp.einsum('ecd,edf->ecf', dispatched, expert_up, precision=highest))
    hidden = low(jax.nn.silu(gate_up[..., :FF]) * gate_up[..., FF:])
    expert_result = low_back(low(jnp.einsum('ecf,efd->ecd', hidden, expert_down, precision=highest)))
    picked = expert_result.reshape(expert_count * capacity, D)[targets].reshape(row_count, TOP_K, D)
    return middle + jnp.einsum('tk,tkd->td', gate_values, picked, precision=highest)

def reference(tokens, segments, routes, cotangent, gain_attn, attn_in, attn_out, gain_ffn, router, expert_in, expert_out):
    block_count = MICRO * PACKS
    token_blocks = tokens.astype(jnp.float32).reshape(block_count, TOK_DEV, D)
    seg_blocks = segments.reshape(block_count, TOK_DEV).astype(jnp.int32)
    route_blocks = routes.reshape(block_count, TOK_DEV, TOP_K).astype(jnp.int32)
    weight_list = tuple((weight_arr.astype(jnp.float32) for weight_arr in (gain_attn, attn_in, attn_out, gain_ffn, router, expert_in, expert_out)))

    def forward(token_arr, *params):
        return lax.map(lambda item: jax.checkpoint(layer_block)(params, item), (token_arr, seg_blocks, route_blocks))
    result, pullback = jax.vjp(forward, token_blocks, *weight_list)
    grads = pullback(cotangent.astype(jnp.float32).reshape(block_count, TOK_DEV, D))
    return (result.reshape(MICRO, ROWS, D).astype(jnp.bfloat16), grads[0].reshape(MICRO, ROWS, D), grads[1], grads[2], grads[3], grads[4], grads[5], grads[6], grads[7])
```

```python
import functools

import jax
import jax.numpy as jnp
from jax import lax
from jax.experimental import pallas as pl
from jax.experimental.pallas import tpu as pltpu
from jax.sharding import PartitionSpec as P

MESH = pl.DeviceIdType.MESH

D = 1536
HEADS = 24
KV_HEADS = 8
HEAD = 64
FF = 512
TOP_K = 8


norm_eps = 1e-06
rope_base = 10000.0
neg_large = -1e30
highest = lax.Precision.HIGHEST


def rope_tables(segment, half_width):
    row_count = segment.shape[0]
    places = jnp.arange(row_count, dtype=jnp.int32)
    same_seq = segment[:, None] == segment[None, :]
    seq_start = jnp.min(jnp.where(same_seq, places[None, :], row_count), axis=1)
    offset = (places - seq_start).astype(jnp.float32)
    frequencies = rope_base ** (-jnp.arange(half_width, dtype=jnp.float32) / half_width)
    angles = offset[:, None] * frequencies[None, :]
    causal = same_seq & (places[None, :] <= places[:, None])
    return (jnp.cos(angles), jnp.sin(angles), causal)


def rotate(operand, cosine, sine_table):
    half_width = operand.shape[-1] // 2
    front_part = operand[..., :half_width]
    back_part = operand[..., half_width:]
    return jnp.concatenate(
        [
            front_part * cosine - back_part * sine_table,
            back_part * cosine + front_part * sine_table,
        ],
        axis=-1,
    )


def unrotate(gradient, cosine, sine_table):
    half_width = gradient.shape[-1] // 2
    front_part = gradient[..., :half_width]
    back_part = gradient[..., half_width:]
    return jnp.concatenate(
        [
            front_part * cosine + back_part * sine_table,
            back_part * cosine - front_part * sine_table,
        ],
        axis=-1,
    )


def slot_targets(route_now, expert_count, capacity):
    flat_ids = route_now.reshape(-1)
    onehot = (flat_ids[:, None] == jnp.arange(expert_count, dtype=jnp.int32)[None, :]).astype(
        jnp.int32
    )
    earlier = jnp.cumsum(onehot, axis=0) - onehot
    slot_index = jnp.sum(earlier * onehot, axis=1)
    return flat_ids * capacity + slot_index


def dense_fetch(gain_attn, attn_in, attn_out, gain_ffn, router):
    return (
        lax.all_gather(gain_attn, ("dp", "expert"), axis=0, tiled=True),
        lax.all_gather(attn_in, ("dp", "expert"), axis=0, tiled=True),
        lax.all_gather(attn_out, ("dp", "expert"), axis=0, tiled=True),
        lax.all_gather(gain_ffn, ("dp", "expert"), axis=0, tiled=True),
        lax.all_gather(router, ("dp", "expert"), axis=0, tiled=True),
    )


def expert_fetch(expert_in, expert_out):
    return (
        lax.all_gather(expert_in, "dp", axis=1, tiled=True),
        lax.all_gather(expert_out, "dp", axis=1, tiled=True),
    )


def dense_reduce(grad_set):
    return (
        lax.psum_scatter(grad_set[0], ("dp", "expert"), scatter_dimension=0, tiled=True),
        lax.psum_scatter(grad_set[1], ("dp", "expert"), scatter_dimension=0, tiled=True),
        lax.psum_scatter(grad_set[2], ("dp", "expert"), scatter_dimension=0, tiled=True),
        lax.psum_scatter(grad_set[3], ("dp", "expert"), scatter_dimension=0, tiled=True),
        lax.psum_scatter(grad_set[4], ("dp", "expert"), scatter_dimension=0, tiled=True),
    )


def expert_reduce(grad_set):
    return (
        lax.psum_scatter(grad_set[0], "dp", scatter_dimension=1, tiled=True),
        lax.psum_scatter(grad_set[1], "dp", scatter_dimension=1, tiled=True),
    )


def attention_scores(queries, key_rot, causal):
    score_scale = HEAD ** (-0.5)
    scores = (
        jnp.einsum("tkgh,skh->kgts", queries, key_rot, preferred_element_type=jnp.float32)
        * score_scale
    )
    return jnp.where(causal[None, None], scores, neg_large)


def forward_micro(tokens_now, segment, route_now, dense_set, expert_set, shapes):
    expert_count, capacity, group_count, local_experts = shapes
    gain_attn, qkv_weight, out_weight, gain_ffn, router_weight = dense_set
    expert_up, expert_down = expert_set
    row_count = tokens_now.shape[0]
    groups = HEADS // KV_HEADS
    q_width = HEADS * HEAD
    k_width = KV_HEADS * HEAD
    inputs = tokens_now.astype(jnp.float32)
    inv_first = lax.rsqrt(jnp.mean(inputs * inputs, axis=1, keepdims=True) + norm_eps)
    normed_first = (inputs * inv_first * gain_attn.astype(jnp.float32)).astype(jnp.bfloat16)
    qkv_full = jnp.dot(normed_first, qkv_weight, preferred_element_type=jnp.float32)
    cosine, sine_table, causal = rope_tables(segment, HEAD // 2)
    queries = rotate(
        qkv_full[:, :q_width].reshape(row_count, KV_HEADS, groups, HEAD),
        cosine[:, None, None, :],
        sine_table[:, None, None, :],
    ).astype(jnp.bfloat16)
    key_rot = rotate(
        qkv_full[:, q_width : q_width + k_width].reshape(row_count, KV_HEADS, HEAD),
        cosine[:, None, :],
        sine_table[:, None, :],
    ).astype(jnp.bfloat16)
    values = (
        qkv_full[:, q_width + k_width :].reshape(row_count, KV_HEADS, HEAD).astype(jnp.bfloat16)
    )
    scores = attention_scores(queries, key_rot, causal)
    score_peak = jnp.max(scores, axis=-1, keepdims=True)
    exp_scores = jnp.exp(scores - score_peak)
    exp_total = jnp.sum(exp_scores, axis=-1, keepdims=True)
    log_total = score_peak + jnp.log(exp_total)
    soft_probs = (exp_scores / exp_total).astype(jnp.bfloat16)
    attn_mixed = jnp.einsum(
        "kgts,skh->tkgh", soft_probs, values, preferred_element_type=jnp.float32
    )
    attn_mixed = attn_mixed.reshape(row_count, q_width).astype(jnp.bfloat16)
    middle = inputs + jnp.dot(attn_mixed, out_weight, preferred_element_type=jnp.float32)
    inv_second = lax.rsqrt(jnp.mean(middle * middle, axis=1, keepdims=True) + norm_eps)
    normed_second = (middle * inv_second * gain_ffn.astype(jnp.float32)).astype(jnp.bfloat16)
    logits = jnp.dot(normed_second, router_weight, preferred_element_type=jnp.float32)
    chosen = (
        route_now[:, :, None] == jnp.arange(expert_count, dtype=jnp.int32)[None, None, :]
    ).astype(jnp.float32)
    picked_logits = jnp.sum(chosen * logits[:, None, :], axis=-1)
    gate_values = jax.nn.softmax(picked_logits, axis=-1)
    targets = slot_targets(route_now, expert_count, capacity)
    source_rows = jnp.repeat(normed_second, TOP_K, axis=0)
    buffer = jnp.zeros((expert_count * capacity, D), jnp.bfloat16).at[targets].set(source_rows)
    send_rows = buffer.reshape(group_count, local_experts, capacity, D)
    received = lax.all_to_all(send_rows, "expert", split_axis=0, concat_axis=0, tiled=True)
    gate_up = jnp.einsum("secd,edf->secf", received, expert_up, preferred_element_type=jnp.float32)
    hidden = (jax.nn.silu(gate_up[..., :FF]) * gate_up[..., FF:]).astype(jnp.bfloat16)
    expert_result = jnp.einsum(
        "secf,efd->secd", hidden, expert_down, preferred_element_type=jnp.float32
    ).astype(jnp.bfloat16)
    returned = lax.all_to_all(expert_result, "expert", split_axis=0, concat_axis=0, tiled=True)
    picked = returned.reshape(expert_count * capacity, D)[targets].reshape(row_count, TOP_K, D)
    moe_sum = jnp.einsum(
        "tk,tkd->td", gate_values, picked, precision=highest, preferred_element_type=jnp.float32
    )
    result = (middle + moe_sum).astype(jnp.bfloat16)
    saved_state = (
        inputs,
        inv_first,
        normed_first,
        queries,
        key_rot,
        values,
        log_total,
        causal,
        cosine,
        sine_table,
        attn_mixed,
        middle,
        inv_second,
        normed_second,
        chosen,
        gate_values,
        targets,
        received,
        gate_up,
        hidden,
        picked,
    )
    return (result, saved_state)


def backward_micro(saved_state, cotan_now, dense_set, expert_set, shapes):
    expert_count, capacity, group_count, local_experts = shapes
    (
        inputs,
        inv_first,
        normed_first,
        queries,
        key_rot,
        values,
        log_total,
        causal,
        cosine,
        sine_table,
        attn_mixed,
        middle,
        inv_second,
        normed_second,
        chosen,
        gate_values,
        targets,
        received,
        gate_up,
        hidden,
        picked,
    ) = saved_state
    gain_attn, qkv_weight, out_weight, gain_ffn, router_weight = dense_set
    expert_up, expert_down = expert_set
    row_count = inputs.shape[0]
    groups = HEADS // KV_HEADS
    q_width = HEADS * HEAD
    k_width = KV_HEADS * HEAD
    score_scale = HEAD ** (-0.5)
    upstream = cotan_now.astype(jnp.float32)
    grad_gates = jnp.einsum(
        "td,tkd->tk", upstream, picked, precision=highest, preferred_element_type=jnp.float32
    )
    grad_picked = gate_values * (
        grad_gates - jnp.sum(gate_values * grad_gates, axis=-1, keepdims=True)
    )
    grad_logits = jnp.sum(chosen * grad_picked[:, :, None], axis=1).astype(jnp.bfloat16)
    grad_router = jnp.einsum(
        "td,te->de", normed_second, grad_logits, preferred_element_type=jnp.float32
    )
    grad_second = jnp.einsum(
        "te,de->td", grad_logits, router_weight, preferred_element_type=jnp.float32
    )
    grad_slots = (
        (gate_values[:, :, None] * upstream[:, None, :])
        .astype(jnp.bfloat16)
        .reshape(row_count * TOP_K, D)
    )
    grad_buffer = jnp.zeros((expert_count * capacity, D), jnp.bfloat16).at[targets].set(grad_slots)
    grad_buffer = grad_buffer.reshape(group_count, local_experts, capacity, D)
    grad_result = lax.all_to_all(grad_buffer, "expert", split_axis=0, concat_axis=0, tiled=True)
    grad_hidden = jnp.einsum(
        "secd,efd->secf", grad_result, expert_down, preferred_element_type=jnp.float32
    )
    grad_down = jnp.einsum(
        "secf,secd->efd", hidden, grad_result, preferred_element_type=jnp.float32
    )
    gate_part = gate_up[..., :FF]
    up_part = gate_up[..., FF:]
    gate_sigmoid = jax.nn.sigmoid(gate_part)
    grad_gate = grad_hidden * up_part * gate_sigmoid * (1.0 + gate_part * (1.0 - gate_sigmoid))
    grad_up_part = grad_hidden * (gate_part * gate_sigmoid)
    grad_gate_up = jnp.concatenate([grad_gate, grad_up_part], axis=-1).astype(jnp.bfloat16)
    grad_up = jnp.einsum(
        "secd,secf->edf", received, grad_gate_up, preferred_element_type=jnp.float32
    )
    grad_rows = jnp.einsum(
        "secf,edf->secd", grad_gate_up, expert_up, preferred_element_type=jnp.float32
    ).astype(jnp.bfloat16)
    grad_back = lax.all_to_all(grad_rows, "expert", split_axis=0, concat_axis=0, tiled=True)
    grad_choice = grad_back.reshape(expert_count * capacity, D)[targets].reshape(
        row_count, TOP_K, D
    )
    grad_second = grad_second + jnp.sum(grad_choice, axis=1, dtype=jnp.float32)
    unit_second = middle * inv_second
    pull_second = grad_second * gain_ffn.astype(jnp.float32)
    grad_gain_ffn = jnp.sum(grad_second * unit_second, axis=0)
    grad_middle = upstream + inv_second * (
        pull_second - unit_second * jnp.mean(pull_second * unit_second, axis=1, keepdims=True)
    )
    grad_branch = grad_middle.astype(jnp.bfloat16)
    grad_out_weight = jnp.einsum(
        "tc,td->cd", attn_mixed, grad_branch, preferred_element_type=jnp.float32
    )
    grad_mixed = jnp.einsum(
        "td,cd->tc", grad_branch, out_weight, preferred_element_type=jnp.float32
    )
    grad_mixed = grad_mixed.astype(jnp.bfloat16).reshape(row_count, KV_HEADS, groups, HEAD)
    scores = attention_scores(queries, key_rot, causal)
    soft_probs = jnp.exp(scores - log_total)
    grad_values = jnp.einsum(
        "kgts,tkgh->skh",
        soft_probs.astype(jnp.bfloat16),
        grad_mixed,
        preferred_element_type=jnp.float32,
    )
    grad_probs = jnp.einsum(
        "tkgh,skh->kgts", grad_mixed, values, preferred_element_type=jnp.float32
    )
    grad_scores = soft_probs * (
        grad_probs - jnp.sum(soft_probs * grad_probs, axis=-1, keepdims=True)
    )
    grad_scores = grad_scores.astype(jnp.bfloat16)
    grad_query = (
        jnp.einsum("kgts,skh->tkgh", grad_scores, key_rot, preferred_element_type=jnp.float32)
        * score_scale
    )
    grad_key = (
        jnp.einsum("kgts,tkgh->skh", grad_scores, queries, preferred_element_type=jnp.float32)
        * score_scale
    )
    grad_query = unrotate(grad_query, cosine[:, None, None, :], sine_table[:, None, None, :])
    grad_key = unrotate(grad_key, cosine[:, None, :], sine_table[:, None, :])
    grad_qkv = jnp.concatenate(
        [
            grad_query.reshape(row_count, q_width),
            grad_key.reshape(row_count, k_width),
            grad_values.reshape(row_count, k_width),
        ],
        axis=1,
    ).astype(jnp.bfloat16)
    grad_qkv_weight = jnp.einsum(
        "tc,tq->cq", normed_first, grad_qkv, preferred_element_type=jnp.float32
    )
    grad_first = jnp.einsum("tq,cq->tc", grad_qkv, qkv_weight, preferred_element_type=jnp.float32)
    unit_first = inputs * inv_first
    pull_first = grad_first * gain_attn.astype(jnp.float32)
    grad_gain_attn = jnp.sum(grad_first * unit_first, axis=0)
    grad_inputs = grad_middle + inv_first * (
        pull_first - unit_first * jnp.mean(pull_first * unit_first, axis=1, keepdims=True)
    )
    dense_grads = (grad_gain_attn, grad_qkv_weight, grad_out_weight, grad_gain_ffn, grad_router)
    expert_grads = (grad_up, grad_down)
    return (grad_inputs, dense_grads, expert_grads)


def add_pair(left_part, right_part):
    return left_part + right_part


def per_device(
    tokens,
    segments,
    routes,
    cotangent,
    gain_attn,
    attn_in,
    attn_out,
    gain_ffn,
    router,
    expert_in,
    expert_out,
):
    local_experts = expert_in.shape[0]
    group_count = lax.axis_size("expert")
    expert_count = local_experts * group_count
    micro_count = tokens.shape[0]
    row_count = tokens.shape[1]
    capacity = (row_count * TOP_K * 5 // (4 * expert_count) + 7) // 8 * 8
    shapes = (expert_count, capacity, group_count, local_experts)
    outputs = []
    grad_list = []
    dense_total = None
    expert_total = None
    for micro_index in range(micro_count):
        dense_set = dense_fetch(gain_attn, attn_in, attn_out, gain_ffn, router)
        expert_set = expert_fetch(expert_in, expert_out)
        result, saved_state = forward_micro(
            tokens[micro_index],
            segments[micro_index, 0],
            routes[micro_index],
            dense_set,
            expert_set,
            shapes,
        )
        dense_set = dense_fetch(gain_attn, attn_in, attn_out, gain_ffn, router)
        expert_set = expert_fetch(expert_in, expert_out)
        grad_inputs, dense_grads, expert_grads = backward_micro(
            saved_state, cotangent[micro_index], dense_set, expert_set, shapes
        )
        dense_grads = dense_reduce(dense_grads)
        expert_grads = expert_reduce(expert_grads)
        if dense_total is None:
            dense_total = dense_grads
            expert_total = expert_grads
        else:
            dense_total = jax.tree.map(add_pair, dense_total, dense_grads)
            expert_total = jax.tree.map(add_pair, expert_total, expert_grads)
        outputs.append(result)
        grad_list.append(grad_inputs)
    return (
        jnp.stack(outputs, axis=0),
        jnp.stack(grad_list, axis=0),
        dense_total[0],
        dense_total[1],
        dense_total[2],
        dense_total[3],
        dense_total[4],
        expert_total[0],
        expert_total[1],
    )


def gather_kernel(n, by_rows, in_ref, out_ref, local_sem, send_sem, recv_z, recv_x, recv_y, recv_d, recv_s):
    d = lax.axis_index("dp"); e = lax.axis_index("expert")
    c = lax.rem(e, 2); x = lax.rem(lax.div(e, 2), 2); y = lax.div(e, 4)
    sib = e + 1 - 2 * c
    ex = e + 2 - 4 * x
    ey = e + 4 - 8 * y
    exy = ex + 4 - 8 * y
    rows, cols = in_ref.shape
    F = (pl.ds(0, rows), pl.ds(0, cols))
    if by_rows:
        A = (pl.ds(0, rows // 2), F[1]); B = (pl.ds(rows // 2, rows - rows // 2), F[1])
    else:
        ca = (cols // 128 + 1) // 2 * 128
        A = (F[0], pl.ds(0, ca)); B = (F[0], pl.ds(ca, cols - ca))
    barrier = pltpu.get_barrier_semaphore()
    for dev in ((d, sib), (d, ex), (d, ey)):
        pl.semaphore_signal(barrier, inc=1, device_id=dev, device_id_type=MESH)
    @pl.when(d > 0)
    def _():
        pl.semaphore_signal(barrier, inc=1, device_id=(d - 1, e), device_id_type=MESH)
    @pl.when(d < n - 1)
    def _():
        pl.semaphore_signal(barrier, inc=1, device_id=(d + 1, e), device_id_type=MESH)
    pl.semaphore_wait(barrier, 3 + jnp.minimum(d, 1) + jnp.minimum(n - 1 - d, 1))

    def copy(zz, ee, rows, dev, slot, sem, own=None):
        dst = out_ref.at[zz * 8 + ee].at[rows]
        src = dst if own is None else own.at[rows]
        return pltpu.make_async_remote_copy(src, dst, send_sem.at[zz, slot], sem,
            device_id=dev, device_id_type=MESH)

    def column(zz, own=None):
        copy(zz, e, F, (d, ex), 2, recv_x.at[zz], own).start()
        copy(zz, e, F, (d, ey), 3, recv_y.at[zz], own).start()
        copy(zz, e, F, (d, sib), 4, recv_s.at[zz, 0], own).start()

    def down(zz, own=None):
        return copy(zz, e, F, (d - 1, e), 0, recv_z.at[zz], own)
    def up(zz, own=None):
        return copy(zz, e, F, (d + 1, e), 1, recv_z.at[zz], own)

    def plane(zz):
        copy(zz, ex, F, (d, ex), 2, recv_x.at[zz]).wait_recv()
        copy(zz, ex, A, (d, ey), 5, recv_d.at[zz, 0]).start()
        copy(zz, ex, F, (d, sib), 6, recv_s.at[zz, 1]).start()
        copy(zz, ey, F, (d, ey), 3, recv_y.at[zz]).wait_recv()
        copy(zz, ey, B, (d, ex), 7, recv_d.at[zz, 1]).start()
        copy(zz, ey, F, (d, sib), 8, recv_s.at[zz, 2]).start()

    def diag(zz):
        copy(zz, exy, A, (d, ey), 5, recv_d.at[zz, 0]).wait_recv()
        copy(zz, exy, A, (d, sib), 9, recv_s.at[zz, 3]).start()
        copy(zz, exy, B, (d, ex), 7, recv_d.at[zz, 1]).wait_recv()
        copy(zz, exy, B, (d, sib), 10, recv_s.at[zz, 4]).start()

    own_copy = pltpu.make_async_copy(in_ref, out_ref.at[d * 8 + e], local_sem)
    @pl.when(d > 0)
    def _(): down(d, in_ref).start()
    @pl.when(d < n - 1)
    def _(): up(d, in_ref).start()
    column(d, in_ref)
    own_copy.start()

    def each(k, fn):
        if k < 0 or k > n - 1: return
        if k == 0:
            fn(d, 0); return
        @pl.when(d - k >= 0)
        def _(): fn(d - k, -1)
        @pl.when(d + k <= n - 1)
        def _(): fn(d + k, 1)

    def first(zz, sign):
        if sign == -1:
            up(zz).wait_recv()
            @pl.when(d < n - 1)
            def _(): up(zz).start()
        else:
            down(zz).wait_recv()
            @pl.when(d > 0)
            def _(): down(zz).start()
        column(zz)

    for k in range(1, n + 2):
        each(k, first)
        each(k - 1, lambda zz, s: plane(zz))
        each(k - 2, lambda zz, s: diag(zz))

    own_copy.wait()
    es = sib; exs = sib + 2 - 4 * x; eys = sib + 4 - 8 * y; exys = exs + 4 - 8 * y
    for zz in range(n):
        copy(zz, es, F, (d, sib), 4, recv_s.at[zz, 0]).wait_recv()
        copy(zz, exs, F, (d, sib), 6, recv_s.at[zz, 1]).wait_recv()
        copy(zz, eys, F, (d, sib), 8, recv_s.at[zz, 2]).wait_recv()
        copy(zz, exys, A, (d, sib), 9, recv_s.at[zz, 3]).wait_recv()
        copy(zz, exys, B, (d, sib), 10, recv_s.at[zz, 4]).wait_recv()
        for slot, rows in ((2, F), (3, F), (4, F), (5, A), (6, F), (7, B), (8, F), (9, A), (10, B)):
            copy(zz, e, rows, (d, sib), slot, recv_s.at[zz, 0]).wait_send()
        @pl.when((d > 0) & (zz >= d))
        def _(): down(zz).wait_send()
        @pl.when((d < n - 1) & (zz <= d))
        def _(): up(zz).wait_send()

def all_gather(block, n, cid, by_rows, space=pl.ANY):
    R, C = block.shape
    D = pltpu.SemaphoreType.DMA
    return pl.pallas_call(
        functools.partial(gather_kernel, n, by_rows),
        out_shape=jax.ShapeDtypeStruct((n * 8, R, C), block.dtype),
        in_specs=[pl.BlockSpec(memory_space=space)],
        out_specs=pl.BlockSpec(memory_space=space),
        scratch_shapes=[D, D((n, 11)), D((n,)), D((n,)), D((n,)), D((n, 2)), D((n, 5))],
        compiler_params=pltpu.CompilerParams(collective_id=cid, has_side_effects=True, vmem_limit_bytes=60 << 20),
        name="gather_blocks",
    )(block)


def reduce_kernel(n, by_rows, in_ref, out_ref, acc, rc, rx1, ry1, ry2, rx2, rdn, rup,
                  loc_sem, ss_c, sr_c, ss_1, sr_x1, sr_y1, ss_2, sr_y2, sr_x2, ss_z, sr_dn, sr_up):
    d = lax.axis_index("dp"); e = lax.axis_index("expert")
    c = lax.rem(e, 2); x = lax.rem(lax.div(e, 2), 2); y = lax.div(e, 4)
    sib = (d, e + 1 - 2 * c); nx = (d, e + 2 - 4 * x); ny = (d, e + 4 - 8 * y)
    rows, cols = in_ref.shape[1:]
    if by_rows:
        ca = rows // 2
        A = (pl.ds(0, ca), pl.ds(0, cols)); B = (pl.ds(ca, rows - ca), pl.ds(0, cols))
        sa, sb = (ca, cols), (rows - ca, cols)
    else:
        ca = (cols // 128 + 1) // 2 * 128
        A = (pl.ds(0, rows), pl.ds(0, ca)); B = (pl.ds(0, rows), pl.ds(ca, cols - ca))
        sa, sb = (rows, ca), (rows, cols - ca)
    barrier = pltpu.get_barrier_semaphore()
    for dev in (sib, nx, ny):
        pl.semaphore_signal(barrier, inc=1, device_id=dev, device_id_type=MESH)
    @pl.when(d > 0)
    def _():
        pl.semaphore_signal(barrier, inc=1, device_id=(d - 1, e), device_id_type=MESH)
    @pl.when(d < n - 1)
    def _():
        pl.semaphore_signal(barrier, inc=1, device_id=(d + 1, e), device_id_type=MESH)
    pl.semaphore_wait(barrier, 3 + jnp.minimum(d, 1) + jnp.minimum(n - 1 - d, 1))

    low = d < n - d
    m = jnp.where(low, d, n - 1 - d)
    def target(i):
        t = jnp.where(i < n - 1 - m, n - 1 - i, jnp.where(i < n - 1, i - (n - 1 - m), m))
        return jnp.where(low, t, n - 1 - t)

    def rcopy(src, dst, ss, rs, dev):
        return pltpu.make_async_remote_copy(src, dst, ss, rs, device_id=dev, device_id_type=MESH)

    def add(dst, src, shape):
        step = 16
        @pl.loop(0, shape[0] // step)
        def _(r):
            w = pl.ds(pl.multiple_of(r * step, step), step)
            dst[w, :] = (dst[w, :].astype(jnp.float32) + src[w, :].astype(jnp.float32)).astype(jnp.bfloat16)

    def core_copy(zz, yy, xx):
        b = zz * 8 + yy * 4 + xx * 2
        return (rcopy(in_ref.at[b + 1 - c], rc.at[zz, yy, xx], ss_c.at[zz, yy, xx], sr_c.at[zz, yy, xx], sib),
                pltpu.make_async_copy(in_ref.at[b + c], acc.at[zz, yy, xx], loc_sem.at[zz, yy, xx]))
    def x1(zz, yy):
        return rcopy(acc.at[zz, yy, 1 - x].at[A], rx1.at[zz, yy], ss_1.at[zz, yy], sr_x1.at[zz, yy], nx)
    def y1(zz, xx):
        return rcopy(acc.at[zz, 1 - y, xx].at[B], ry1.at[zz, xx], ss_1.at[zz, 2 + xx], sr_y1.at[zz, xx], ny)
    def y2(zz):
        return rcopy(acc.at[zz, 1 - y, x].at[A], ry2.at[zz], ss_2.at[zz, 0], sr_y2.at[zz], ny)
    def x2(zz):
        return rcopy(acc.at[zz, y, 1 - x].at[B], rx2.at[zz], ss_2.at[zz, 1], sr_x2.at[zz], nx)
    def dn(zz):
        return rcopy(acc.at[zz, y, x], rdn.at[zz], ss_z.at[zz], sr_dn.at[zz], (d - 1, e))
    def up(zz):
        return rcopy(acc.at[zz, y, x], rup.at[zz], ss_z.at[zz], sr_up.at[zz], (d + 1, e))

    def s0(zz):
        for yy in range(2):
            for xx in range(2):
                r, l = core_copy(zz, yy, xx)
                r.start(); l.start()
    def s1(zz):
        for yy in range(2):
            for xx in range(2):
                r, l = core_copy(zz, yy, xx)
                l.wait(); r.wait_recv()
                add(acc.at[zz, yy, xx], rc.at[zz, yy, xx], (rows, cols))
        for k in range(2):
            x1(zz, k).start(); y1(zz, k).start()
    def s2(zz):
        for k in (1, 0):
            yy = jnp.where(k == 1, 1 - y, y); xx = jnp.where(k == 1, 1 - x, x)
            x1(zz, yy).wait_recv()
            add(acc.at[zz, yy, x].at[A], rx1.at[zz, yy], sa)
            if k == 1: y2(zz).start()
            y1(zz, xx).wait_recv()
            add(acc.at[zz, y, xx].at[B], ry1.at[zz, xx], sb)
            if k == 1: x2(zz).start()
    def s3(zz, last):
        y2(zz).wait_recv()
        add(acc.at[zz, y, x].at[A], ry2.at[zz], sa)
        x2(zz).wait_recv()
        add(acc.at[zz, y, x].at[B], rx2.at[zz], sb)
        if not last:
            @pl.when((zz < d) & (d < n - 1))
            def _():
                dn(zz).wait_recv()
                add(acc.at[zz, y, x], rdn.at[zz], (rows, cols))
            @pl.when(zz < d)
            def _(): dn(zz).start()
            @pl.when((zz > d) & (d > 0))
            def _():
                up(zz).wait_recv()
                add(acc.at[zz, y, x], rup.at[zz], (rows, cols))
            @pl.when(zz > d)
            def _(): up(zz).start()
        else:
            def store(w): out_ref[w, :] = acc[d, y, x, w, :].astype(jnp.float32)
            def more(w, src): out_ref[w, :] = out_ref[w, :] + src[d, w, :].astype(jnp.float32)
            def over(fn):
                @pl.loop(0, rows // 16)
                def _(r): fn(pl.ds(pl.multiple_of(r * 16, 16), 16))
            over(store)
            @pl.when(d < n - 1)
            def _():
                dn(d).wait_recv()
                over(lambda w: more(w, rdn))
            @pl.when(d > 0)
            def _():
                up(d).wait_recv()
                over(lambda w: more(w, rup))

    for i in range(n):
        s0(target(i))
    for i in range(n + 2):
        if i < n: s1(target(i))
        if 0 <= i - 1 < n: s2(target(i - 1))
        if 0 <= i - 2 < n: s3(target(i - 2), i - 2 == n - 1)
    for zz in range(n):
        for yy in range(2):
            for xx in range(2):
                core_copy(zz, yy, xx)[0].wait_send()
        for k in range(2):
            x1(zz, k).wait_send(); y1(zz, k).wait_send()
        y2(zz).wait_send(); x2(zz).wait_send()
        @pl.when(zz < d)
        def _(): dn(zz).wait_send()
        @pl.when(zz > d)
        def _(): up(zz).wait_send()

def reduce_scatter(parts, n, cid, by_rows):
    _, R, C = parts.shape
    D = pltpu.SemaphoreType.DMA
    V = lambda *s: pltpu.VMEM(s, parts.dtype)
    if by_rows:
        sa = sb = (R // 2, C)
    else:
        ca = (C // 128 + 1) // 2 * 128
        sa, sb = (R, ca), (R, C - ca)
    return pl.pallas_call(
        functools.partial(reduce_kernel, n, by_rows),
        out_shape=jax.ShapeDtypeStruct((R, C), jnp.float32),
        in_specs=[pl.BlockSpec(memory_space=pl.ANY)],
        out_specs=pl.BlockSpec(memory_space=pltpu.VMEM),
        scratch_shapes=[V(n, 2, 2, R, C), V(n, 2, 2, R, C), V(n, 2, *sa), V(n, 2, *sb), V(n, *sa), V(n, *sb), V(n, R, C), V(n, R, C),
                        D((n, 2, 2)), D((n, 2, 2)), D((n, 2, 2)), D((n, 4)), D((n, 2)), D((n, 2)), D((n, 2)), D((n,)), D((n,)), D((n,)), D((n,)), D((n,))],
        compiler_params=pltpu.CompilerParams(collective_id=cid, has_side_effects=True, vmem_limit_bytes=60 << 20),
        name="reduce_blocks",
    )(parts)


def moe_kernel(x_ref, cot_ref, up_ref, upt_ref, down_ref, downt_ref, pick_ref, place_ref,
               out_ref, gx_ref, gup_ref, gdown_ref, acc_up, acc_down):
    step = pl.program_id(0)
    f = down_ref.shape[0]
    x = x_ref[:, :, :D].reshape(-1, D)
    gate_cols = x_ref[:, :, D:].reshape(x.shape[0], -1)
    cot = cot_ref[...].reshape(-1, D)
    f32 = jnp.float32
    mix = jnp.dot(gate_cols, pick_ref[...], preferred_element_type=f32)
    gate_up = jnp.dot(x, up_ref[...], preferred_element_type=f32)
    back = jnp.dot(cot, downt_ref[...], preferred_element_type=f32)
    gate = gate_up[:, :f]
    up = gate_up[:, f:]
    sig = 1.0 / (1.0 + jnp.exp(-gate))
    act = gate * sig
    hidden = (act * up).astype(jnp.bfloat16).astype(f32)
    prod = hidden * back
    high = prod.astype(jnp.bfloat16)
    low = (prod - high.astype(f32)).astype(jnp.bfloat16)
    place = place_ref[...]
    sums = jnp.dot(high, place, preferred_element_type=f32) + jnp.dot(low, place, preferred_element_type=f32)
    mixed = (mix * hidden).astype(jnp.bfloat16)
    out_ref[...] = jnp.dot(mixed, down_ref[...], preferred_element_type=f32).astype(jnp.bfloat16).reshape(out_ref.shape)
    gh = mix * back
    g_gate = gh * up * sig * (1.0 + gate * (1.0 - sig))
    g_up = gh * act
    gg = jnp.concatenate([g_gate, g_up], axis=1).astype(jnp.bfloat16)
    gx = jnp.dot(gg, upt_ref[...], preferred_element_type=f32).astype(jnp.bfloat16)
    gx_ref[:, :, :D] = gx.reshape(x_ref.shape[0], x_ref.shape[1], D)
    gx_ref[:, :, D:] = sums.astype(jnp.bfloat16).reshape(x_ref.shape[0], x_ref.shape[1], -1)
    t_dims = (((0,), (0,)), ((), ()))
    d_up = lax.dot_general(gg, x, t_dims, preferred_element_type=f32)
    d_down = lax.dot_general(mixed, cot, t_dims, preferred_element_type=f32)

    @pl.when(step == 0)
    def _():
        acc_up[...] = d_up
        acc_down[...] = d_down

    @pl.when(step > 0)
    def _():
        acc_up[...] += d_up
        acc_down[...] += d_down

    @pl.when(step == pl.num_programs(0) - 1)
    def _():
        n = gup_ref.shape[0]
        w = D // n
        for q in range(n):
            gup_ref[q] = acc_up[:, q * w:(q + 1) * w].astype(jnp.bfloat16)
        gdown_ref[...] = acc_down[...]


def moe_call(x_all, cot_all, up, upt, down, downt, pick, place, n, group):
    blocks, rows, width = x_all.shape
    f = down.shape[0]
    once = dict(pipeline_mode=pl.Buffered(1))
    full = lambda a: pl.BlockSpec(a.shape, lambda i: (0,) * a.ndim, **once)
    return pl.pallas_call(
        moe_kernel,
        grid=(blocks // group,),
        out_shape=(
            jax.ShapeDtypeStruct((blocks, rows, D), jnp.bfloat16),
            jax.ShapeDtypeStruct((blocks, rows, width), jnp.bfloat16),
            jax.ShapeDtypeStruct((n, 2 * f, D // n), jnp.bfloat16),
            jax.ShapeDtypeStruct((f, D), jnp.float32),
        ),
        in_specs=[pl.BlockSpec((group, rows, width), lambda i: (i, 0, 0)),
                  pl.BlockSpec((group, rows, D), lambda i: (i, 0, 0)),
                  full(up), full(upt), full(down), full(downt), full(pick), full(place)],
        out_specs=[pl.BlockSpec((group, rows, D), lambda i: (i, 0, 0)),
                   pl.BlockSpec((group, rows, width), lambda i: (i, 0, 0)),
                   pl.BlockSpec((n, 2 * f, D // n), lambda i: (0, 0, 0), **once),
                   pl.BlockSpec((f, D), lambda i: (0, 0), **once)],
        scratch_shapes=[pltpu.VMEM((2 * f, D), jnp.float32), pltpu.VMEM((f, D), jnp.float32)],
        compiler_params=pltpu.CompilerParams(vmem_limit_bytes=60 << 20),
        cost_estimate=pl.CostEstimate(flops=2 * blocks * rows * D * f * 9, bytes_accessed=blocks * rows * D * 8, transcendentals=0),
        name="expert_layer",
    )(x_all, cot_all, up, upt, down, downt, pick, place)


def attention_forward(tokens, segment, gain, w_in, w_out):
    row_count = tokens.shape[0]
    groups = HEADS // KV_HEADS
    q_width = HEADS * HEAD
    k_width = KV_HEADS * HEAD
    inputs = tokens.astype(jnp.float32)
    inv_first = lax.rsqrt(jnp.mean(inputs * inputs, axis=1, keepdims=True) + norm_eps)
    normed_first = (inputs * inv_first * gain).astype(jnp.bfloat16)
    qkv_full = jnp.dot(normed_first, w_in, preferred_element_type=jnp.float32)
    cosine, sine_table, causal = rope_tables(segment, HEAD // 2)
    queries = rotate(
        qkv_full[:, :q_width].reshape(row_count, KV_HEADS, groups, HEAD),
        cosine[:, None, None, :],
        sine_table[:, None, None, :],
    ).astype(jnp.bfloat16)
    key_rot = rotate(
        qkv_full[:, q_width : q_width + k_width].reshape(row_count, KV_HEADS, HEAD),
        cosine[:, None, :],
        sine_table[:, None, :],
    ).astype(jnp.bfloat16)
    values = (
        qkv_full[:, q_width + k_width :].reshape(row_count, KV_HEADS, HEAD).astype(jnp.bfloat16)
    )
    scores = attention_scores(queries, key_rot, causal)
    probs = jax.nn.softmax(scores, axis=-1)
    attn_mixed = jnp.einsum(
        "kgts,skh->tkgh", probs.astype(jnp.bfloat16), values, preferred_element_type=jnp.float32
    )
    attn_mixed = attn_mixed.reshape(row_count, q_width).astype(jnp.bfloat16)
    middle = inputs + jnp.dot(attn_mixed, w_out, preferred_element_type=jnp.float32)
    return middle, (inputs, inv_first, normed_first, queries, key_rot, values, probs, cosine, sine_table, attn_mixed)


def attention_backward(saved, grad_middle, gain, w_in, w_out):
    inputs, inv_first, normed_first, queries, key_rot, values, probs, cosine, sine_table, attn_mixed = saved
    row_count = inputs.shape[0]
    groups = HEADS // KV_HEADS
    score_scale = HEAD ** (-0.5)
    f32 = jnp.float32
    grad_branch = grad_middle.astype(jnp.bfloat16)
    grad_out = jnp.einsum("tc,td->cd", attn_mixed, grad_branch, preferred_element_type=f32)
    grad_mixed = jnp.einsum("td,cd->tc", grad_branch, w_out, preferred_element_type=f32)
    grad_mixed = grad_mixed.astype(jnp.bfloat16).reshape(row_count, KV_HEADS, groups, HEAD)
    grad_values = jnp.einsum("kgts,tkgh->skh", probs.astype(jnp.bfloat16), grad_mixed, preferred_element_type=f32)
    grad_probs = jnp.einsum("tkgh,skh->kgts", grad_mixed, values, preferred_element_type=f32)
    grad_scores = (probs * (grad_probs - jnp.sum(probs * grad_probs, axis=-1, keepdims=True))).astype(jnp.bfloat16)
    grad_query = jnp.einsum("kgts,skh->tkgh", grad_scores, key_rot, preferred_element_type=f32) * score_scale
    grad_key = jnp.einsum("kgts,tkgh->skh", grad_scores, queries, preferred_element_type=f32) * score_scale
    grad_query = unrotate(grad_query, cosine[:, None, None, :], sine_table[:, None, None, :])
    grad_key = unrotate(grad_key, cosine[:, None, :], sine_table[:, None, :])
    grad_qkv = jnp.concatenate(
        [grad_query.reshape(row_count, -1), grad_key.reshape(row_count, -1), grad_values.reshape(row_count, -1)],
        axis=1,
    ).astype(jnp.bfloat16)
    grad_in = jnp.einsum("tc,tq->cq", normed_first, grad_qkv, preferred_element_type=f32)
    grad_first = jnp.einsum("tq,cq->tc", grad_qkv, w_in, preferred_element_type=f32)
    unit = inputs * inv_first
    pull = grad_first * gain
    grad_gain = jnp.sum(grad_first * unit, axis=0)
    grad_inputs = grad_middle + inv_first * (pull - unit * jnp.mean(pull * unit, axis=1, keepdims=True))
    return grad_inputs, grad_gain, grad_in, grad_out


def per_device_fast(n, tokens, segments, routes, cotangent, gain_attn, attn_in, attn_out, gain_ffn, router, expert_in, expert_out):
    f32, bf16 = jnp.float32, jnp.bfloat16
    micro, rows = tokens.shape[:2]
    total = micro * rows
    held = expert_in.shape[0]
    experts = held * 8
    f = FF // n
    shard = attn_in.shape[0]
    widths = (attn_in.shape[1], attn_out.shape[1], experts, 1, 1)
    used = sum(widths)
    wide = (used + 127) // 128 * 128
    x = tokens.reshape(total, D)
    cot = cotangent.reshape(total, D)

    dense = jnp.concatenate(
        [attn_in, attn_out, router, gain_attn[:, None], gain_ffn[:, None], jnp.zeros((shard, wide - used), bf16)], axis=1)
    dense = all_gather(dense, n, 0, False).reshape(-1, wide)
    w_in = dense[:, : widths[0]]
    w_out = dense[:, widths[0] : widths[0] + widths[1]]
    tail = dense[:, widths[0] + widths[1] :]
    w_router = tail[:, :experts]
    gain_first = tail[:, experts].astype(f32)[None, :]
    gain_second = tail[:, experts + 1].astype(f32)[None, :]
    cot_all = all_gather(cot, n, 1, True)

    ups = expert_in.reshape(held, D // n, 2, n, f).transpose(3, 1, 2, 0, 4).reshape(n, D // n, 2 * held * f)
    up = lax.all_to_all(ups, "dp", split_axis=0, concat_axis=0, tiled=True).reshape(D, 2 * held * f)
    down = expert_out.reshape(held * f, D)

    segment = (segments[:, 0, :] + 2 * rows * jnp.arange(micro, dtype=jnp.int32)[:, None]).reshape(total)
    middle, saved = attention_forward(x, segment, gain_first, w_in, w_out)
    inv_second = lax.rsqrt(jnp.mean(middle * middle, axis=1, keepdims=True) + norm_eps)
    normed_second = (middle * inv_second * gain_second).astype(bf16)
    logits = jnp.dot(normed_second, w_router, preferred_element_type=f32)
    route = routes.reshape(total, TOP_K)
    chosen = jnp.any(route[:, :, None] == jnp.arange(experts, dtype=jnp.int32)[None, None, :], axis=1)
    masked = jnp.where(chosen, logits, neg_large)
    raised = jnp.where(chosen, jnp.exp(masked - jnp.max(masked, axis=1, keepdims=True)), 0.0)
    gates = raised / jnp.sum(raised, axis=1, keepdims=True)

    high = gates.astype(bf16)
    low = (gates - high.astype(f32)).astype(bf16)
    x_all = all_gather(
        jnp.concatenate([normed_second, high, low, jnp.zeros((total, 128 - 2 * experts), bf16)], axis=1), n, 2, True)

    first = lax.axis_index("expert") * held
    lane = jnp.arange(128, dtype=jnp.int32)[:, None]
    owner = (first + jnp.arange(held * f, dtype=jnp.int32) // f)[None, :]
    pick = ((lane == owner) | (lane == owner + experts)).astype(bf16)
    place = (lane == owner).astype(bf16).T
    out_parts, grad_parts, grad_up, grad_down = moe_call(x_all, cot_all, up, up.T, down, down.T, pick, place, n, 2)

    moe_sum = reduce_scatter(out_parts, n, 3, True)
    result = (middle + moe_sum).astype(bf16)
    grad_sum = reduce_scatter(grad_parts, n, 4, True)
    grad_up = lax.all_to_all(grad_up, "dp", split_axis=0, concat_axis=0, tiled=True)
    grad_up = grad_up.reshape(n, 2, held, f, D // n).transpose(2, 4, 1, 0, 3).reshape(held, D // n, 2 * FF).astype(f32)

    upstream = cot.astype(f32)
    grad_gates = grad_sum[:, D : D + experts]
    grad_logits = (gates * (grad_gates - jnp.sum(gates * grad_gates, axis=1, keepdims=True))).astype(bf16)
    grad_router = jnp.einsum("td,te->de", normed_second, grad_logits, preferred_element_type=f32)
    grad_second = jnp.einsum("te,de->td", grad_logits, w_router, preferred_element_type=f32) + grad_sum[:, :D]
    unit = middle * inv_second
    pull = grad_second * gain_second
    grad_gain_ffn = jnp.sum(grad_second * unit, axis=0)
    grad_middle = upstream + inv_second * (pull - unit * jnp.mean(pull * unit, axis=1, keepdims=True))
    grad_inputs, grad_gain_attn, grad_in, grad_out = attention_backward(saved, grad_middle, gain_first, w_in, w_out)
    parts = jnp.concatenate(
        [grad_in, grad_out, grad_router, grad_gain_attn[:, None], grad_gain_ffn[:, None], jnp.zeros((D, wide - used), f32)],
        axis=1).astype(bf16)
    sums = reduce_scatter(parts.reshape(-1, shard, wide), n, 5, False)
    a, b = widths[0], widths[0] + widths[1]
    return (
        result.reshape(micro, rows, D),
        grad_inputs.reshape(micro, rows, D),
        sums[:, b + experts],
        sums[:, :a],
        sums[:, a:b],
        sums[:, b + experts + 1],
        sums[:, b : b + experts],
        grad_up,
        grad_down.reshape(held, f, D),
    )


def solution(mesh):
    placed = (
        P(None, ("dp", "expert"), None),
        P(None, ("dp", "expert"), None),
        P(None, ("dp", "expert"), None),
        P(None, ("dp", "expert"), None),
        P(("dp", "expert")),
        P(("dp", "expert"), None),
        P(("dp", "expert"), None),
        P(("dp", "expert")),
        P(("dp", "expert"), None),
        P("expert", "dp", None),
        P("expert", "dp", None),
    )
    fast = mesh.shape["expert"] == 8 and FF // mesh.shape["dp"] % 128 == 0
    body = functools.partial(per_device_fast, mesh.shape["dp"]) if fast else per_device
    return jax.shard_map(
        body,
        mesh=mesh,
        in_specs=placed,
        out_specs=(
            P(None, ("dp", "expert"), None),
            P(None, ("dp", "expert"), None),
            P(("dp", "expert")),
            P(("dp", "expert"), None),
            P(("dp", "expert"), None),
            P(("dp", "expert")),
            P(("dp", "expert"), None),
            P("expert", "dp", None),
            P("expert", "dp", None),
        ),
        check_vma=False,
    )
```

```python
import functools

import jax
import jax.numpy as jnp
from jax import lax
from jax.experimental import pallas as pl
from jax.experimental.pallas import tpu as pltpu
from jax.sharding import PartitionSpec as P

MESH = pl.DeviceIdType.MESH

D = 1536
HEADS = 24
KV_HEADS = 8
HEAD = 64
FF = 512
TOP_K = 8


norm_eps = 1e-06
rope_base = 10000.0
neg_large = -1e30
highest = lax.Precision.HIGHEST


def rope_tables(segment, half_width):
    row_count = segment.shape[0]
    places = jnp.arange(row_count, dtype=jnp.int32)
    same_seq = segment[:, None] == segment[None, :]
    seq_start = jnp.min(jnp.where(same_seq, places[None, :], row_count), axis=1)
    offset = (places - seq_start).astype(jnp.float32)
    frequencies = rope_base ** (-jnp.arange(half_width, dtype=jnp.float32) / half_width)
    angles = offset[:, None] * frequencies[None, :]
    causal = same_seq & (places[None, :] <= places[:, None])
    return (jnp.cos(angles), jnp.sin(angles), causal)


def rotate(operand, cosine, sine_table):
    half_width = operand.shape[-1] // 2
    front_part = operand[..., :half_width]
    back_part = operand[..., half_width:]
    return jnp.concatenate(
        [
            front_part * cosine - back_part * sine_table,
            back_part * cosine + front_part * sine_table,
        ],
        axis=-1,
    )


def unrotate(gradient, cosine, sine_table):
    half_width = gradient.shape[-1] // 2
    front_part = gradient[..., :half_width]
    back_part = gradient[..., half_width:]
    return jnp.concatenate(
        [
            front_part * cosine + back_part * sine_table,
            back_part * cosine - front_part * sine_table,
        ],
        axis=-1,
    )


def slot_targets(route_now, expert_count, capacity):
    flat_ids = route_now.reshape(-1)
    onehot = (flat_ids[:, None] == jnp.arange(expert_count, dtype=jnp.int32)[None, :]).astype(
        jnp.int32
    )
    earlier = jnp.cumsum(onehot, axis=0) - onehot
    slot_index = jnp.sum(earlier * onehot, axis=1)
    return flat_ids * capacity + slot_index


def dense_fetch(gain_attn, attn_in, attn_out, gain_ffn, router):
    return (
        lax.all_gather(gain_attn, ("dp", "expert"), axis=0, tiled=True),
        lax.all_gather(attn_in, ("dp", "expert"), axis=0, tiled=True),
        lax.all_gather(attn_out, ("dp", "expert"), axis=0, tiled=True),
        lax.all_gather(gain_ffn, ("dp", "expert"), axis=0, tiled=True),
        lax.all_gather(router, ("dp", "expert"), axis=0, tiled=True),
    )


def expert_fetch(expert_in, expert_out):
    return (
        lax.all_gather(expert_in, "dp", axis=1, tiled=True),
        lax.all_gather(expert_out, "dp", axis=1, tiled=True),
    )


def dense_reduce(grad_set):
    return (
        lax.psum_scatter(grad_set[0], ("dp", "expert"), scatter_dimension=0, tiled=True),
        lax.psum_scatter(grad_set[1], ("dp", "expert"), scatter_dimension=0, tiled=True),
        lax.psum_scatter(grad_set[2], ("dp", "expert"), scatter_dimension=0, tiled=True),
        lax.psum_scatter(grad_set[3], ("dp", "expert"), scatter_dimension=0, tiled=True),
        lax.psum_scatter(grad_set[4], ("dp", "expert"), scatter_dimension=0, tiled=True),
    )


def expert_reduce(grad_set):
    return (
        lax.psum_scatter(grad_set[0], "dp", scatter_dimension=1, tiled=True),
        lax.psum_scatter(grad_set[1], "dp", scatter_dimension=1, tiled=True),
    )


def attention_scores(queries, key_rot, causal):
    score_scale = HEAD ** (-0.5)
    scores = (
        jnp.einsum("tkgh,skh->kgts", queries, key_rot, preferred_element_type=jnp.float32)
        * score_scale
    )
    return jnp.where(causal[None, None], scores, neg_large)


def forward_micro(tokens_now, segment, route_now, dense_set, expert_set, shapes):
    expert_count, capacity, group_count, local_experts = shapes
    gain_attn, qkv_weight, out_weight, gain_ffn, router_weight = dense_set
    expert_up, expert_down = expert_set
    row_count = tokens_now.shape[0]
    groups = HEADS // KV_HEADS
    q_width = HEADS * HEAD
    k_width = KV_HEADS * HEAD
    inputs = tokens_now.astype(jnp.float32)
    inv_first = lax.rsqrt(jnp.mean(inputs * inputs, axis=1, keepdims=True) + norm_eps)
    normed_first = (inputs * inv_first * gain_attn.astype(jnp.float32)).astype(jnp.bfloat16)
    qkv_full = jnp.dot(normed_first, qkv_weight, preferred_element_type=jnp.float32)
    cosine, sine_table, causal = rope_tables(segment, HEAD // 2)
    queries = rotate(
        qkv_full[:, :q_width].reshape(row_count, KV_HEADS, groups, HEAD),
        cosine[:, None, None, :],
        sine_table[:, None, None, :],
    ).astype(jnp.bfloat16)
    key_rot = rotate(
        qkv_full[:, q_width : q_width + k_width].reshape(row_count, KV_HEADS, HEAD),
        cosine[:, None, :],
        sine_table[:, None, :],
    ).astype(jnp.bfloat16)
    values = (
        qkv_full[:, q_width + k_width :].reshape(row_count, KV_HEADS, HEAD).astype(jnp.bfloat16)
    )
    scores = attention_scores(queries, key_rot, causal)
    score_peak = jnp.max(scores, axis=-1, keepdims=True)
    exp_scores = jnp.exp(scores - score_peak)
    exp_total = jnp.sum(exp_scores, axis=-1, keepdims=True)
    log_total = score_peak + jnp.log(exp_total)
    soft_probs = (exp_scores / exp_total).astype(jnp.bfloat16)
    attn_mixed = jnp.einsum(
        "kgts,skh->tkgh", soft_probs, values, preferred_element_type=jnp.float32
    )
    attn_mixed = attn_mixed.reshape(row_count, q_width).astype(jnp.bfloat16)
    middle = inputs + jnp.dot(attn_mixed, out_weight, preferred_element_type=jnp.float32)
    inv_second = lax.rsqrt(jnp.mean(middle * middle, axis=1, keepdims=True) + norm_eps)
    normed_second = (middle * inv_second * gain_ffn.astype(jnp.float32)).astype(jnp.bfloat16)
    logits = jnp.dot(normed_second, router_weight, preferred_element_type=jnp.float32)
    chosen = (
        route_now[:, :, None] == jnp.arange(expert_count, dtype=jnp.int32)[None, None, :]
    ).astype(jnp.float32)
    picked_logits = jnp.sum(chosen * logits[:, None, :], axis=-1)
    gate_values = jax.nn.softmax(picked_logits, axis=-1)
    targets = slot_targets(route_now, expert_count, capacity)
    source_rows = jnp.repeat(normed_second, TOP_K, axis=0)
    buffer = jnp.zeros((expert_count * capacity, D), jnp.bfloat16).at[targets].set(source_rows)
    send_rows = buffer.reshape(group_count, local_experts, capacity, D)
    received = lax.all_to_all(send_rows, "expert", split_axis=0, concat_axis=0, tiled=True)
    gate_up = jnp.einsum("secd,edf->secf", received, expert_up, preferred_element_type=jnp.float32)
    hidden = (jax.nn.silu(gate_up[..., :FF]) * gate_up[..., FF:]).astype(jnp.bfloat16)
    expert_result = jnp.einsum(
        "secf,efd->secd", hidden, expert_down, preferred_element_type=jnp.float32
    ).astype(jnp.bfloat16)
    returned = lax.all_to_all(expert_result, "expert", split_axis=0, concat_axis=0, tiled=True)
    picked = returned.reshape(expert_count * capacity, D)[targets].reshape(row_count, TOP_K, D)
    moe_sum = jnp.einsum(
        "tk,tkd->td", gate_values, picked, precision=highest, preferred_element_type=jnp.float32
    )
    result = (middle + moe_sum).astype(jnp.bfloat16)
    saved_state = (
        inputs,
        inv_first,
        normed_first,
        queries,
        key_rot,
        values,
        log_total,
        causal,
        cosine,
        sine_table,
        attn_mixed,
        middle,
        inv_second,
        normed_second,
        chosen,
        gate_values,
        targets,
        received,
        gate_up,
        hidden,
        picked,
    )
    return (result, saved_state)


def backward_micro(saved_state, cotan_now, dense_set, expert_set, shapes):
    expert_count, capacity, group_count, local_experts = shapes
    (
        inputs,
        inv_first,
        normed_first,
        queries,
        key_rot,
        values,
        log_total,
        causal,
        cosine,
        sine_table,
        attn_mixed,
        middle,
        inv_second,
        normed_second,
        chosen,
        gate_values,
        targets,
        received,
        gate_up,
        hidden,
        picked,
    ) = saved_state
    gain_attn, qkv_weight, out_weight, gain_ffn, router_weight = dense_set
    expert_up, expert_down = expert_set
    row_count = inputs.shape[0]
    groups = HEADS // KV_HEADS
    q_width = HEADS * HEAD
    k_width = KV_HEADS * HEAD
    score_scale = HEAD ** (-0.5)
    upstream = cotan_now.astype(jnp.float32)
    grad_gates = jnp.einsum(
        "td,tkd->tk", upstream, picked, precision=highest, preferred_element_type=jnp.float32
    )
    grad_picked = gate_values * (
        grad_gates - jnp.sum(gate_values * grad_gates, axis=-1, keepdims=True)
    )
    grad_logits = jnp.sum(chosen * grad_picked[:, :, None], axis=1).astype(jnp.bfloat16)
    grad_router = jnp.einsum(
        "td,te->de", normed_second, grad_logits, preferred_element_type=jnp.float32
    )
    grad_second = jnp.einsum(
        "te,de->td", grad_logits, router_weight, preferred_element_type=jnp.float32
    )
    grad_slots = (
        (gate_values[:, :, None] * upstream[:, None, :])
        .astype(jnp.bfloat16)
        .reshape(row_count * TOP_K, D)
    )
    grad_buffer = jnp.zeros((expert_count * capacity, D), jnp.bfloat16).at[targets].set(grad_slots)
    grad_buffer = grad_buffer.reshape(group_count, local_experts, capacity, D)
    grad_result = lax.all_to_all(grad_buffer, "expert", split_axis=0, concat_axis=0, tiled=True)
    grad_hidden = jnp.einsum(
        "secd,efd->secf", grad_result, expert_down, preferred_element_type=jnp.float32
    )
    grad_down = jnp.einsum(
        "secf,secd->efd", hidden, grad_result, preferred_element_type=jnp.float32
    )
    gate_part = gate_up[..., :FF]
    up_part = gate_up[..., FF:]
    gate_sigmoid = jax.nn.sigmoid(gate_part)
    grad_gate = grad_hidden * up_part * gate_sigmoid * (1.0 + gate_part * (1.0 - gate_sigmoid))
    grad_up_part = grad_hidden * (gate_part * gate_sigmoid)
    grad_gate_up = jnp.concatenate([grad_gate, grad_up_part], axis=-1).astype(jnp.bfloat16)
    grad_up = jnp.einsum(
        "secd,secf->edf", received, grad_gate_up, preferred_element_type=jnp.float32
    )
    grad_rows = jnp.einsum(
        "secf,edf->secd", grad_gate_up, expert_up, preferred_element_type=jnp.float32
    ).astype(jnp.bfloat16)
    grad_back = lax.all_to_all(grad_rows, "expert", split_axis=0, concat_axis=0, tiled=True)
    grad_choice = grad_back.reshape(expert_count * capacity, D)[targets].reshape(
        row_count, TOP_K, D
    )
    grad_second = grad_second + jnp.sum(grad_choice, axis=1, dtype=jnp.float32)
    unit_second = middle * inv_second
    pull_second = grad_second * gain_ffn.astype(jnp.float32)
    grad_gain_ffn = jnp.sum(grad_second * unit_second, axis=0)
    grad_middle = upstream + inv_second * (
        pull_second - unit_second * jnp.mean(pull_second * unit_second, axis=1, keepdims=True)
    )
    grad_branch = grad_middle.astype(jnp.bfloat16)
    grad_out_weight = jnp.einsum(
        "tc,td->cd", attn_mixed, grad_branch, preferred_element_type=jnp.float32
    )
    grad_mixed = jnp.einsum(
        "td,cd->tc", grad_branch, out_weight, preferred_element_type=jnp.float32
    )
    grad_mixed = grad_mixed.astype(jnp.bfloat16).reshape(row_count, KV_HEADS, groups, HEAD)
    scores = attention_scores(queries, key_rot, causal)
    soft_probs = jnp.exp(scores - log_total)
    grad_values = jnp.einsum(
        "kgts,tkgh->skh",
        soft_probs.astype(jnp.bfloat16),
        grad_mixed,
        preferred_element_type=jnp.float32,
    )
    grad_probs = jnp.einsum(
        "tkgh,skh->kgts", grad_mixed, values, preferred_element_type=jnp.float32
    )
    grad_scores = soft_probs * (
        grad_probs - jnp.sum(soft_probs * grad_probs, axis=-1, keepdims=True)
    )
    grad_scores = grad_scores.astype(jnp.bfloat16)
    grad_query = (
        jnp.einsum("kgts,skh->tkgh", grad_scores, key_rot, preferred_element_type=jnp.float32)
        * score_scale
    )
    grad_key = (
        jnp.einsum("kgts,tkgh->skh", grad_scores, queries, preferred_element_type=jnp.float32)
        * score_scale
    )
    grad_query = unrotate(grad_query, cosine[:, None, None, :], sine_table[:, None, None, :])
    grad_key = unrotate(grad_key, cosine[:, None, :], sine_table[:, None, :])
    grad_qkv = jnp.concatenate(
        [
            grad_query.reshape(row_count, q_width),
            grad_key.reshape(row_count, k_width),
            grad_values.reshape(row_count, k_width),
        ],
        axis=1,
    ).astype(jnp.bfloat16)
    grad_qkv_weight = jnp.einsum(
        "tc,tq->cq", normed_first, grad_qkv, preferred_element_type=jnp.float32
    )
    grad_first = jnp.einsum("tq,cq->tc", grad_qkv, qkv_weight, preferred_element_type=jnp.float32)
    unit_first = inputs * inv_first
    pull_first = grad_first * gain_attn.astype(jnp.float32)
    grad_gain_attn = jnp.sum(grad_first * unit_first, axis=0)
    grad_inputs = grad_middle + inv_first * (
        pull_first - unit_first * jnp.mean(pull_first * unit_first, axis=1, keepdims=True)
    )
    dense_grads = (grad_gain_attn, grad_qkv_weight, grad_out_weight, grad_gain_ffn, grad_router)
    expert_grads = (grad_up, grad_down)
    return (grad_inputs, dense_grads, expert_grads)


def add_pair(left_part, right_part):
    return left_part + right_part


def per_device(
    tokens,
    segments,
    routes,
    cotangent,
    gain_attn,
    attn_in,
    attn_out,
    gain_ffn,
    router,
    expert_in,
    expert_out,
):
    local_experts = expert_in.shape[0]
    group_count = lax.axis_size("expert")
    expert_count = local_experts * group_count
    micro_count = tokens.shape[0]
    row_count = tokens.shape[1]
    capacity = (row_count * TOP_K * 5 // (4 * expert_count) + 7) // 8 * 8
    shapes = (expert_count, capacity, group_count, local_experts)
    outputs = []
    grad_list = []
    dense_total = None
    expert_total = None
    for micro_index in range(micro_count):
        dense_set = dense_fetch(gain_attn, attn_in, attn_out, gain_ffn, router)
        expert_set = expert_fetch(expert_in, expert_out)
        result, saved_state = forward_micro(
            tokens[micro_index],
            segments[micro_index, 0],
            routes[micro_index],
            dense_set,
            expert_set,
            shapes,
        )
        dense_set = dense_fetch(gain_attn, attn_in, attn_out, gain_ffn, router)
        expert_set = expert_fetch(expert_in, expert_out)
        grad_inputs, dense_grads, expert_grads = backward_micro(
            saved_state, cotangent[micro_index], dense_set, expert_set, shapes
        )
        dense_grads = dense_reduce(dense_grads)
        expert_grads = expert_reduce(expert_grads)
        if dense_total is None:
            dense_total = dense_grads
            expert_total = expert_grads
        else:
            dense_total = jax.tree.map(add_pair, dense_total, dense_grads)
            expert_total = jax.tree.map(add_pair, expert_total, expert_grads)
        outputs.append(result)
        grad_list.append(grad_inputs)
    return (
        jnp.stack(outputs, axis=0),
        jnp.stack(grad_list, axis=0),
        dense_total[0],
        dense_total[1],
        dense_total[2],
        dense_total[3],
        dense_total[4],
        expert_total[0],
        expert_total[1],
    )


def gather_kernel(n, by_rows, in_ref, out_ref, local_sem, send_sem, recv_z, recv_x, recv_y, recv_d, recv_s):
    d = lax.axis_index("dp"); e = lax.axis_index("expert")
    c = lax.rem(e, 2); x = lax.rem(lax.div(e, 2), 2); y = lax.div(e, 4)
    sib = e + 1 - 2 * c
    ex = e + 2 - 4 * x
    ey = e + 4 - 8 * y
    exy = ex + 4 - 8 * y
    rows, cols = in_ref.shape
    F = (pl.ds(0, rows), pl.ds(0, cols))
    if by_rows:
        A = (pl.ds(0, rows // 2), F[1]); B = (pl.ds(rows // 2, rows - rows // 2), F[1])
    else:
        ca = (cols // 128 + 1) // 2 * 128
        A = (F[0], pl.ds(0, ca)); B = (F[0], pl.ds(ca, cols - ca))
    barrier = pltpu.get_barrier_semaphore()
    for dev in ((d, sib), (d, ex), (d, ey)):
        pl.semaphore_signal(barrier, inc=1, device_id=dev, device_id_type=MESH)
    @pl.when(d > 0)
    def _():
        pl.semaphore_signal(barrier, inc=1, device_id=(d - 1, e), device_id_type=MESH)
    @pl.when(d < n - 1)
    def _():
        pl.semaphore_signal(barrier, inc=1, device_id=(d + 1, e), device_id_type=MESH)
    pl.semaphore_wait(barrier, 3 + jnp.minimum(d, 1) + jnp.minimum(n - 1 - d, 1))

    def copy(zz, ee, rows, dev, slot, sem, own=None):
        dst = out_ref.at[zz * 8 + ee].at[rows]
        src = dst if own is None else own.at[rows]
        return pltpu.make_async_remote_copy(src, dst, send_sem.at[zz, slot], sem,
            device_id=dev, device_id_type=MESH)

    def column(zz, own=None):
        copy(zz, e, F, (d, ex), 2, recv_x.at[zz], own).start()
        copy(zz, e, F, (d, ey), 3, recv_y.at[zz], own).start()
        copy(zz, e, F, (d, sib), 4, recv_s.at[zz, 0], own).start()

    def down(zz, own=None):
        return copy(zz, e, F, (d - 1, e), 0, recv_z.at[zz], own)
    def up(zz, own=None):
        return copy(zz, e, F, (d + 1, e), 1, recv_z.at[zz], own)

    def plane(zz):
        copy(zz, ex, F, (d, ex), 2, recv_x.at[zz]).wait_recv()
        copy(zz, ex, A, (d, ey), 5, recv_d.at[zz, 0]).start()
        copy(zz, ex, F, (d, sib), 6, recv_s.at[zz, 1]).start()
        copy(zz, ey, F, (d, ey), 3, recv_y.at[zz]).wait_recv()
        copy(zz, ey, B, (d, ex), 7, recv_d.at[zz, 1]).start()
        copy(zz, ey, F, (d, sib), 8, recv_s.at[zz, 2]).start()

    def diag(zz):
        copy(zz, exy, A, (d, ey), 5, recv_d.at[zz, 0]).wait_recv()
        copy(zz, exy, A, (d, sib), 9, recv_s.at[zz, 3]).start()
        copy(zz, exy, B, (d, ex), 7, recv_d.at[zz, 1]).wait_recv()
        copy(zz, exy, B, (d, sib), 10, recv_s.at[zz, 4]).start()

    own_copy = pltpu.make_async_copy(in_ref, out_ref.at[d * 8 + e], local_sem)
    @pl.when(d > 0)
    def _(): down(d, in_ref).start()
    @pl.when(d < n - 1)
    def _(): up(d, in_ref).start()
    column(d, in_ref)
    own_copy.start()

    def each(k, fn):
        if k < 0 or k > n - 1: return
        if k == 0:
            fn(d, 0); return
        @pl.when(d - k >= 0)
        def _(): fn(d - k, -1)
        @pl.when(d + k <= n - 1)
        def _(): fn(d + k, 1)

    def first(zz, sign):
        if sign == -1:
            up(zz).wait_recv()
            @pl.when(d < n - 1)
            def _(): up(zz).start()
        else:
            down(zz).wait_recv()
            @pl.when(d > 0)
            def _(): down(zz).start()
        column(zz)

    for k in range(1, n + 2):
        each(k, first)
        each(k - 1, lambda zz, s: plane(zz))
        each(k - 2, lambda zz, s: diag(zz))

    own_copy.wait()
    es = sib; exs = sib + 2 - 4 * x; eys = sib + 4 - 8 * y; exys = exs + 4 - 8 * y
    for zz in range(n):
        copy(zz, es, F, (d, sib), 4, recv_s.at[zz, 0]).wait_recv()
        copy(zz, exs, F, (d, sib), 6, recv_s.at[zz, 1]).wait_recv()
        copy(zz, eys, F, (d, sib), 8, recv_s.at[zz, 2]).wait_recv()
        copy(zz, exys, A, (d, sib), 9, recv_s.at[zz, 3]).wait_recv()
        copy(zz, exys, B, (d, sib), 10, recv_s.at[zz, 4]).wait_recv()
        for slot, rows in ((2, F), (3, F), (4, F), (5, A), (6, F), (7, B), (8, F), (9, A), (10, B)):
            copy(zz, e, rows, (d, sib), slot, recv_s.at[zz, 0]).wait_send()
        @pl.when((d > 0) & (zz >= d))
        def _(): down(zz).wait_send()
        @pl.when((d < n - 1) & (zz <= d))
        def _(): up(zz).wait_send()

def all_gather(block, n, cid, by_rows, space=pl.ANY):
    R, C = block.shape
    D = pltpu.SemaphoreType.DMA
    return pl.pallas_call(
        functools.partial(gather_kernel, n, by_rows),
        out_shape=jax.ShapeDtypeStruct((n * 8, R, C), block.dtype),
        in_specs=[pl.BlockSpec(memory_space=space)],
        out_specs=pl.BlockSpec(memory_space=space),
        scratch_shapes=[D, D((n, 11)), D((n,)), D((n,)), D((n,)), D((n, 2)), D((n, 5))],
        compiler_params=pltpu.CompilerParams(collective_id=cid, has_side_effects=True, vmem_limit_bytes=60 << 20),
        name="gather_blocks",
    )(block)


def reduce_kernel(n, by_rows, in_ref, out_ref, acc, rc, rx1, ry1, ry2, rx2, rdn, rup,
                  loc_sem, ss_c, sr_c, ss_1, sr_x1, sr_y1, ss_2, sr_y2, sr_x2, ss_z, sr_dn, sr_up):
    d = lax.axis_index("dp"); e = lax.axis_index("expert")
    c = lax.rem(e, 2); x = lax.rem(lax.div(e, 2), 2); y = lax.div(e, 4)
    sib = (d, e + 1 - 2 * c); nx = (d, e + 2 - 4 * x); ny = (d, e + 4 - 8 * y)
    rows, cols = in_ref.shape[1:]
    if by_rows:
        ca = rows // 2
        A = (pl.ds(0, ca), pl.ds(0, cols)); B = (pl.ds(ca, rows - ca), pl.ds(0, cols))
        sa, sb = (ca, cols), (rows - ca, cols)
    else:
        ca = (cols // 128 + 1) // 2 * 128
        A = (pl.ds(0, rows), pl.ds(0, ca)); B = (pl.ds(0, rows), pl.ds(ca, cols - ca))
        sa, sb = (rows, ca), (rows, cols - ca)
    barrier = pltpu.get_barrier_semaphore()
    for dev in (sib, nx, ny):
        pl.semaphore_signal(barrier, inc=1, device_id=dev, device_id_type=MESH)
    @pl.when(d > 0)
    def _():
        pl.semaphore_signal(barrier, inc=1, device_id=(d - 1, e), device_id_type=MESH)
    @pl.when(d < n - 1)
    def _():
        pl.semaphore_signal(barrier, inc=1, device_id=(d + 1, e), device_id_type=MESH)
    pl.semaphore_wait(barrier, 3 + jnp.minimum(d, 1) + jnp.minimum(n - 1 - d, 1))

    low = d < n - d
    m = jnp.where(low, d, n - 1 - d)
    def target(i):
        t = jnp.where(i < n - 1 - m, n - 1 - i, jnp.where(i < n - 1, i - (n - 1 - m), m))
        return jnp.where(low, t, n - 1 - t)

    def rcopy(src, dst, ss, rs, dev):
        return pltpu.make_async_remote_copy(src, dst, ss, rs, device_id=dev, device_id_type=MESH)

    def add(dst, src, shape):
        step = 16
        @pl.loop(0, shape[0] // step)
        def _(r):
            w = pl.ds(pl.multiple_of(r * step, step), step)
            dst[w, :] = (dst[w, :].astype(jnp.float32) + src[w, :].astype(jnp.float32)).astype(jnp.bfloat16)

    def core_copy(zz, yy, xx):
        b = zz * 8 + yy * 4 + xx * 2
        return (rcopy(in_ref.at[b + 1 - c], rc.at[zz, yy, xx], ss_c.at[zz, yy, xx], sr_c.at[zz, yy, xx], sib),
                pltpu.make_async_copy(in_ref.at[b + c], acc.at[zz, yy, xx], loc_sem.at[zz, yy, xx]))
    def x1(zz, yy):
        return rcopy(acc.at[zz, yy, 1 - x].at[A], rx1.at[zz, yy], ss_1.at[zz, yy], sr_x1.at[zz, yy], nx)
    def y1(zz, xx):
        return rcopy(acc.at[zz, 1 - y, xx].at[B], ry1.at[zz, xx], ss_1.at[zz, 2 + xx], sr_y1.at[zz, xx], ny)
    def y2(zz):
        return rcopy(acc.at[zz, 1 - y, x].at[A], ry2.at[zz], ss_2.at[zz, 0], sr_y2.at[zz], ny)
    def x2(zz):
        return rcopy(acc.at[zz, y, 1 - x].at[B], rx2.at[zz], ss_2.at[zz, 1], sr_x2.at[zz], nx)
    def dn(zz):
        return rcopy(acc.at[zz, y, x], rdn.at[zz], ss_z.at[zz], sr_dn.at[zz], (d - 1, e))
    def up(zz):
        return rcopy(acc.at[zz, y, x], rup.at[zz], ss_z.at[zz], sr_up.at[zz], (d + 1, e))

    def s0(zz):
        for yy in range(2):
            for xx in range(2):
                r, l = core_copy(zz, yy, xx)
                r.start(); l.start()
    def s1(zz):
        for yy in range(2):
            for xx in range(2):
                r, l = core_copy(zz, yy, xx)
                l.wait(); r.wait_recv()
                add(acc.at[zz, yy, xx], rc.at[zz, yy, xx], (rows, cols))
        for k in range(2):
            x1(zz, k).start(); y1(zz, k).start()
    def s2(zz):
        for k in (1, 0):
            yy = jnp.where(k == 1, 1 - y, y); xx = jnp.where(k == 1, 1 - x, x)
            x1(zz, yy).wait_recv()
            add(acc.at[zz, yy, x].at[A], rx1.at[zz, yy], sa)
            if k == 1: y2(zz).start()
            y1(zz, xx).wait_recv()
            add(acc.at[zz, y, xx].at[B], ry1.at[zz, xx], sb)
            if k == 1: x2(zz).start()
    def s3(zz, last):
        y2(zz).wait_recv()
        add(acc.at[zz, y, x].at[A], ry2.at[zz], sa)
        x2(zz).wait_recv()
        add(acc.at[zz, y, x].at[B], rx2.at[zz], sb)
        if not last:
            @pl.when((zz < d) & (d < n - 1))
            def _():
                dn(zz).wait_recv()
                add(acc.at[zz, y, x], rdn.at[zz], (rows, cols))
            @pl.when(zz < d)
            def _(): dn(zz).start()
            @pl.when((zz > d) & (d > 0))
            def _():
                up(zz).wait_recv()
                add(acc.at[zz, y, x], rup.at[zz], (rows, cols))
            @pl.when(zz > d)
            def _(): up(zz).start()
        else:
            def store(w): out_ref[w, :] = acc[d, y, x, w, :].astype(jnp.float32)
            def more(w, src): out_ref[w, :] = out_ref[w, :] + src[d, w, :].astype(jnp.float32)
            def over(fn):
                @pl.loop(0, rows // 16)
                def _(r): fn(pl.ds(pl.multiple_of(r * 16, 16), 16))
            over(store)
            @pl.when(d < n - 1)
            def _():
                dn(d).wait_recv()
                over(lambda w: more(w, rdn))
            @pl.when(d > 0)
            def _():
                up(d).wait_recv()
                over(lambda w: more(w, rup))

    for i in range(n):
        s0(target(i))
    for i in range(n + 2):
        if i < n: s1(target(i))
        if 0 <= i - 1 < n: s2(target(i - 1))
        if 0 <= i - 2 < n: s3(target(i - 2), i - 2 == n - 1)
    for zz in range(n):
        for yy in range(2):
            for xx in range(2):
                core_copy(zz, yy, xx)[0].wait_send()
        for k in range(2):
            x1(zz, k).wait_send(); y1(zz, k).wait_send()
        y2(zz).wait_send(); x2(zz).wait_send()
        @pl.when(zz < d)
        def _(): dn(zz).wait_send()
        @pl.when(zz > d)
        def _(): up(zz).wait_send()

def reduce_scatter(parts, n, cid, by_rows):
    _, R, C = parts.shape
    D = pltpu.SemaphoreType.DMA
    V = lambda *s: pltpu.VMEM(s, parts.dtype)
    if by_rows:
        sa = sb = (R // 2, C)
    else:
        ca = (C // 128 + 1) // 2 * 128
        sa, sb = (R, ca), (R, C - ca)
    return pl.pallas_call(
        functools.partial(reduce_kernel, n, by_rows),
        out_shape=jax.ShapeDtypeStruct((R, C), jnp.float32),
        in_specs=[pl.BlockSpec(memory_space=pl.ANY)],
        out_specs=pl.BlockSpec(memory_space=pltpu.VMEM),
        scratch_shapes=[V(n, 2, 2, R, C), V(n, 2, 2, R, C), V(n, 2, *sa), V(n, 2, *sb), V(n, *sa), V(n, *sb), V(n, R, C), V(n, R, C),
                        D((n, 2, 2)), D((n, 2, 2)), D((n, 2, 2)), D((n, 4)), D((n, 2)), D((n, 2)), D((n, 2)), D((n,)), D((n,)), D((n,)), D((n,)), D((n,))],
        compiler_params=pltpu.CompilerParams(collective_id=cid, has_side_effects=True, vmem_limit_bytes=60 << 20),
        name="reduce_blocks",
    )(parts)


NN = (((1,), (0,)), ((), ()))
NT = (((1,), (1,)), ((), ()))
TN = (((0,), (0,)), ((), ()))


def mm(a, b, dims=NN):
    return lax.dot_general(a, b, dims, preferred_element_type=jnp.float32)


class Place:
    def __init__(self, n):
        self.n = n
        d = self.d = lax.axis_index("dp")
        e = self.e = lax.axis_index("expert")
        c, x, y = lax.rem(e, 2), lax.rem(lax.div(e, 2), 2), lax.div(e, 4)
        self.sib = (d, e + 1 - 2 * c)
        self.nx = (d, e + 2 - 4 * x)
        self.ny = (d, e + 4 - 8 * y)
        self.below = (d - 1, e)
        self.above = (d + 1, e)
        self.has_below = d > 0
        self.has_above = d < n - 1

    def meet(self, everyone=False):
        barrier = pltpu.get_barrier_semaphore()
        d, n = self.d, self.n
        if everyone:
            others = n - 1 + 3

            @pl.loop(1, n)
            def _(k):
                pl.semaphore_signal(barrier, inc=1, device_id=(lax.rem(d + k, n), self.e), device_id_type=MESH)
        else:
            others = 3 + jnp.minimum(d, 1) + jnp.minimum(n - 1 - d, 1)

            @pl.when(self.has_below)
            def _():
                pl.semaphore_signal(barrier, inc=1, device_id=self.below, device_id_type=MESH)

            @pl.when(self.has_above)
            def _():
                pl.semaphore_signal(barrier, inc=1, device_id=self.above, device_id_type=MESH)

        for dev in (self.sib, self.nx, self.ny):
            pl.semaphore_signal(barrier, inc=1, device_id=dev, device_id_type=MESH)
        pl.semaphore_wait(barrier, others)

    def far(self, i):
        n, d = self.n, self.d
        low = d < n - d
        m = jnp.where(low, d, n - 1 - d)
        t = jnp.where(i < n - 1 - m, n - 1 - i, jnp.where(i < n - 1, i - (n - 1 - m), m))
        return jnp.where(low, t, n - 1 - t)

    def near(self, i):
        return self.far(self.n - 1 - i)


def send(src, dst, ss, rs, dev):
    return pltpu.make_async_remote_copy(src, dst, ss, rs, device_id=dev, device_id_type=MESH)


class Gather:
    def __init__(self, at, own, buf, send_sem, recv_z, recv_x, recv_y, recv_d):
        self.at, self.own, self.buf = at, own, buf
        self.ss, self.rz, self.rx, self.ry, self.rd = send_sem, recv_z, recv_x, recv_y, recv_d
        rows = own.shape[0]
        self.A, self.B = pl.ds(0, rows // 2), pl.ds(rows // 2, rows // 2)

    def source(self, zz, own):
        return self.own if own else self.buf.at[zz, 0]

    def down(self, zz, own=False):
        return send(self.source(zz, own), self.buf.at[zz, 0], self.ss.at[zz, 0], self.rz.at[zz], self.at.below)

    def up(self, zz, own=False):
        return send(self.source(zz, own), self.buf.at[zz, 0], self.ss.at[zz, 1], self.rz.at[zz], self.at.above)

    def to_x(self, zz, own=False):
        return send(self.source(zz, own), self.buf.at[zz, 1], self.ss.at[zz, 2], self.rx.at[zz], self.at.nx)

    def to_y(self, zz, own=False):
        return send(self.source(zz, own), self.buf.at[zz, 2], self.ss.at[zz, 3], self.ry.at[zz], self.at.ny)

    def turn_y(self, zz):
        return send(self.buf.at[zz, 1, self.A], self.buf.at[zz, 3, self.A], self.ss.at[zz, 4], self.rd.at[zz, 0], self.at.ny)

    def turn_x(self, zz):
        return send(self.buf.at[zz, 2, self.B], self.buf.at[zz, 3, self.B], self.ss.at[zz, 5], self.rd.at[zz, 1], self.at.nx)

    def begin(self):
        d = self.at.d

        @pl.when(self.at.has_below)
        def _():
            self.down(d, True).start()

        @pl.when(self.at.has_above)
        def _():
            self.up(d, True).start()

        self.to_x(d, True).start()
        self.to_y(d, True).start()

    def column(self, zz):
        d = self.at.d

        @pl.when(zz < d)
        def _():
            self.up(zz).wait_recv()

            @pl.when(self.at.has_above)
            def _():
                self.up(zz).start()

        @pl.when(zz > d)
        def _():
            self.down(zz).wait_recv()

            @pl.when(self.at.has_below)
            def _():
                self.down(zz).start()

        self.to_x(zz).start()
        self.to_y(zz).start()

    def plane(self, zz):
        self.to_x(zz).wait_recv()
        self.turn_y(zz).start()
        self.to_y(zz).wait_recv()
        self.turn_x(zz).start()

    def corner(self, zz):
        self.turn_y(zz).wait_recv()
        self.turn_x(zz).wait_recv()

    def finish(self):
        d = self.at.d

        @pl.loop(0, self.at.n)
        def _(zz):
            for copy in (self.to_x, self.to_y, self.turn_y, self.turn_x):
                copy(zz).wait_send()

            @pl.when((d > 0) & (zz >= d))
            def _():
                self.down(zz).wait_send()

            @pl.when(self.at.has_above & (zz <= d))
            def _():
                self.up(zz).wait_send()


def gather_sems(n):
    D_ = pltpu.SemaphoreType.DMA
    return [D_((n, 6)), D_((n,)), D_((n,)), D_((n,)), D_((n, 2))]


def add_rows(dst, src):
    rows = dst.shape[0]
    step = 16

    @pl.loop(0, rows // step)
    def _(r):
        w = pl.ds(pl.multiple_of(r * step, step), step)
        dst[w, :] = (dst[w, :].astype(jnp.float32) + src[w, :].astype(jnp.float32)).astype(dst.dtype)


class Reduce:
    def __init__(self, at, buf, total, r1, r2, rz, ss_1, sr_1, ss_2, sr_2, ss_z, sr_z):
        self.at, self.buf, self.total = at, buf, total
        self.r1, self.r2, self.rz = r1, r2, rz
        self.sems = (ss_1, sr_1, ss_2, sr_2, ss_z, sr_z)
        rows = total.shape[0]
        self.A, self.B = pl.ds(0, rows // 2), pl.ds(rows // 2, rows // 2)

    def first(self, zz, k):
        ss, sr = self.sems[0], self.sems[1]
        slot, part, dev = ((3, self.A, self.at.nx), (3, self.B, self.at.ny), (1, self.A, self.at.nx), (2, self.B, self.at.ny))[k]
        return send(self.buf.at[zz, slot, part], self.r1.at[zz, k], ss.at[zz, k], sr.at[zz, k], dev)

    def second(self, zz, k):
        ss, sr = self.sems[2], self.sems[3]
        slot, part, dev = ((2, self.A, self.at.ny), (1, self.B, self.at.nx))[k]
        return send(self.buf.at[zz, slot, part], self.r2.at[zz, k], ss.at[zz, k], sr.at[zz, k], dev)

    def down(self, zz):
        return send(self.buf.at[zz, 0], self.rz.at[zz], self.sems[4].at[zz], self.sems[5].at[zz], self.at.below)

    def up(self, zz):
        slot = jnp.where(zz == self.at.d + 1, self.at.n, zz)
        return send(self.buf.at[zz, 0], self.rz.at[slot], self.sems[4].at[zz], self.sems[5].at[slot], self.at.above)

    def arrive(self, slot):
        return send(self.buf.at[0, 0], self.rz.at[slot], self.sems[4].at[0], self.sems[5].at[slot], self.at.nx)

    def s1(self, zz):
        for k in range(4):
            self.first(zz, k).start()

    def s2(self, zz):
        self.first(zz, 0).wait_recv()
        add_rows(self.buf.at[zz, 2, self.A], self.r1.at[zz, 0])
        self.second(zz, 0).start()
        self.first(zz, 1).wait_recv()
        add_rows(self.buf.at[zz, 1, self.B], self.r1.at[zz, 1])
        self.second(zz, 1).start()
        self.first(zz, 2).wait_recv()
        add_rows(self.buf.at[zz, 0, self.A], self.r1.at[zz, 2])
        self.first(zz, 3).wait_recv()
        add_rows(self.buf.at[zz, 0, self.B], self.r1.at[zz, 3])

    def s3(self, zz):
        self.second(zz, 0).wait_recv()
        add_rows(self.buf.at[zz, 0, self.A], self.r2.at[zz, 0])
        self.second(zz, 1).wait_recv()
        add_rows(self.buf.at[zz, 0, self.B], self.r2.at[zz, 1])

    def line(self, zz):
        d = self.at.d

        @pl.when(((zz < d) & self.at.has_above) | ((zz > d) & self.at.has_below))
        def _():
            self.arrive(zz).wait_recv()
            add_rows(self.buf.at[zz, 0], self.rz.at[zz])

        @pl.when(zz < d)
        def _():
            self.down(zz).start()

        @pl.when(zz > d)
        def _():
            self.up(zz).start()

    def last(self):
        d, n, rows, step = self.at.d, self.at.n, self.total.shape[0], 16

        def over(fn):
            @pl.loop(0, rows // step)
            def _(r):
                fn(pl.ds(pl.multiple_of(r * step, step), step))

        def own(w):
            self.total[w, :] = self.buf[d, 0, w, :].astype(jnp.float32)

        def more(slot):
            def fn(w):
                self.total[w, :] += self.rz[slot, w, :].astype(jnp.float32)

            self.arrive(slot).wait_recv()
            over(fn)

        over(own)

        @pl.when(self.at.has_above)
        def _():
            more(d)

        @pl.when(self.at.has_below)
        def _():
            more(n)

    def finish(self):
        d = self.at.d

        @pl.loop(0, self.at.n)
        def _(zz):
            for k in range(4):
                self.first(zz, k).wait_send()
            for k in range(2):
                self.second(zz, k).wait_send()

            @pl.when(zz != d)
            def _():
                self.arrive(zz)
                send(self.buf.at[zz, 0], self.rz.at[zz], self.sems[4].at[zz], self.sems[5].at[zz], self.at.nx).wait_send()


def reduce_scratch(n, rows, cols):
    D_ = pltpu.SemaphoreType.DMA
    V = lambda *s: pltpu.VMEM(s, jnp.bfloat16)
    return [V(n, 4, rows // 2, cols), V(n, 2, rows // 2, cols), V(n + 1, rows, cols),
            D_((n, 4)), D_((n, 4)), D_((n, 2)), D_((n, 2)), D_((n,)), D_((n + 1,))]


def expert_kernel(n, x_ref, cot_ref, up_ref, down_ref, pick_ref, place_ref,
                  out_ref, gx_ref, gup_ref, gdown_ref,
                  xb, cb, gg, mixed, gb, wup, wdown, *rest):
    f32, bf16 = jnp.float32, jnp.bfloat16
    at = Place(n)
    d = at.d
    gather = Gather(at, x_ref, xb, *rest[:5])
    grads = Reduce(at, gb, gx_ref, *rest[5:14])
    outs = Reduce(at, gg, out_ref, *rest[14:23])
    load_sem, core_ss, core_sr, free, a2a_ss, a2a_sr = rest[23:]
    rows = x_ref.shape[0]
    f2 = up_ref.shape[1]
    f = f2 // 2
    held = f // 128
    loads = [
        pltpu.make_async_copy(x_ref, xb.at[d, 0], load_sem.at[0]),
        pltpu.make_async_copy(up_ref, wup.at[0], load_sem.at[1]),
        pltpu.make_async_copy(down_ref, wdown.at[0], load_sem.at[2]),
        pltpu.make_async_copy(cot_ref, cb, load_sem.at[3]),
    ]
    for load in loads:
        load.start()
    at.meet(True)
    gather.begin()
    swaps = [
        send(up_ref, wup.at[1], core_ss.at[0], core_sr.at[0], at.sib),
        send(down_ref, wdown.at[1], core_ss.at[1], core_sr.at[1], at.sib),
    ]
    for swap in swaps:
        swap.start()
    for load in loads:
        load.wait()
    for swap in swaps:
        swap.wait_recv()
    gather.plane(at.near(0))
    gather.column(at.near(1))

    def tokens(ref, zz, p, lo, width):
        return ref[zz, pl.ds(2 * p, 2), :, pl.ds(lo, width)].reshape(2 * rows, width)

    def half(zz, p):
        pair = pl.ds(2 * p, 2)
        x = tokens(xb, zz, p, 0, D)
        cot = tokens(cb, zz, p, 0, D)
        mix = mm(tokens(xb, zz, p, D, 128), pick_ref[...])
        sums = jnp.zeros((2 * rows, 128), f32)
        for h in range(2):
            gate_up = mm(x, wup[h])
            back = mm(cot, wdown[h], NT)
            for j in range(held):
                k = h * held + j
                gate = gate_up[:, j * 256 : j * 256 + 128]
                up = gate_up[:, j * 256 + 128 : j * 256 + 256]
                b = back[:, j * 128 : (j + 1) * 128]
                m = mix[:, k * 128 : (k + 1) * 128]
                sig = 1.0 / (1.0 + jnp.exp(-gate))
                act = gate * sig
                hidden = (act * up).astype(bf16).astype(f32)
                prod = hidden * b
                high = prod.astype(bf16)
                low = (prod - high.astype(f32)).astype(bf16)
                sel = place_ref[k * 128 : (k + 1) * 128, :]
                sums += mm(high, sel) + mm(low, sel)
                mixed[zz, pair, :, pl.ds(k * 128, 128)] = (m * hidden).astype(bf16).reshape(2, rows, 128)
                gh = m * b
                gg[zz, pair, :, pl.ds(k * 256, 128)] = (
                    (gh * up * sig * (1.0 + gate * (1.0 - sig))).astype(bf16).reshape(2, rows, 128))
                gg[zz, pair, :, pl.ds(k * 256 + 128, 128)] = (gh * act).astype(bf16).reshape(2, rows, 128)
        for q in range(D // 512):
            cols = pl.ds(q * 512, 512)
            part = mm(tokens(gg, zz, p, 0, f2), wup[0, cols, :], NT) + mm(tokens(gg, zz, p, f2, f2), wup[1, cols, :], NT)
            gb[zz, pair, :, cols] = part.astype(bf16).reshape(2, rows, 512)
        gb[zz, pair, :, pl.ds(D, 128)] = sums.astype(bf16).reshape(2, rows, 128)

    @pl.loop(0, n)
    def _(i):
        zz = at.near(i)
        half(zz, 0)

        @pl.when(i + 1 < n)
        def _():
            gather.plane(at.near(i + 1))

        @pl.when(i + 2 < n)
        def _():
            gather.column(at.near(i + 2))

        gather.corner(zz)
        half(zz, 1)
        grads.s1(zz)

        @pl.when(i >= 1)
        def _():
            grads.s2(at.near(i - 1))

        @pl.when(i >= 2)
        def _():
            grads.s3(at.near(i - 2))

    pl.semaphore_signal(free.at[0], inc=1, device_id=at.sib, device_id_type=MESH)

    def grad_up(h, more):
        @pl.loop(0, D // 256)
        def _(q):
            cols = pl.ds(pl.multiple_of(q * 256, 256), 256)
            xs = xb[:, :, :, cols].reshape(n * 4 * rows, 256)
            part = mm(xs, gg[:, :, :, pl.ds(h * f2, f2)].reshape(n * 4 * rows, f2), TN)
            if more:
                part += wup[h, cols, :].astype(f32)
            wup[h, cols, :] = part.astype(bf16)

    def grad_down(h):
        for q in range(D // 512):
            cols = pl.ds(q * 512, 512)
            part = mm(mixed[:, :, :, pl.ds(h * f, f)].reshape(n * 4 * rows, f), cb[:, :, :, cols].reshape(n * 4 * rows, 512), TN)
            if h == 0:
                gdown_ref[:, cols] = part + wdown[0, :, cols].astype(f32)
            else:
                wdown[1, :, cols] = part.astype(bf16)

    def output(zz):
        @pl.loop(0, 2)
        def _(p):
            for q in range(D // 512):
                cols = pl.ds(q * 512, 512)
                part = mm(tokens(mixed, zz, p, 0, f), wdown[0, :, cols]) + mm(tokens(mixed, zz, p, f, f), wdown[1, :, cols])
                gg[zz, pl.ds(2 * p, 2), :, cols] = part.astype(bf16).reshape(2, rows, 512)

    grad_up(1, False)
    pl.semaphore_wait(free.at[0], 1)
    up_swap = send(wup.at[1], wup.at[0], core_ss.at[2], core_sr.at[2], at.sib)
    for swap in swaps:
        swap.wait_send()
    up_swap.start()
    grads.s2(at.near(n - 1))
    grads.s3(at.near(n - 2))
    up_swap.wait_recv()
    grad_up(0, True)
    share = D // n
    own_share = pltpu.make_async_copy(wup.at[0, pl.ds(pl.multiple_of(d * share, share), share), :], gup_ref.at[d], load_sem.at[0])
    own_share.start()

    def exchange(k):
        to = lax.rem(d + k, n)
        return send(wup.at[0, pl.ds(pl.multiple_of(to * share, share), share), :], gup_ref.at[d], a2a_ss.at[k], a2a_sr.at[d], (to, at.e))

    for k in range(1, n):
        exchange(k).start()
    grads.s3(at.near(n - 1))
    for j in range(n + 3):
        if j < n - 1:
            grads.line(at.far(j))
        if j < n:
            output(at.far(j))
            outs.s1(at.far(j))
        if 0 <= j - 1 < n:
            outs.s2(at.far(j - 1))
        if 0 <= j - 2 < n:
            outs.s3(at.far(j - 2))
            if j - 2 < n - 1:
                outs.line(at.far(j - 2))
        if j == n - 1:
            pl.semaphore_signal(free.at[1], inc=1, device_id=at.sib, device_id_type=MESH)
            grad_down(1)
            pl.semaphore_wait(free.at[1], 1)
            down_swap = send(wdown.at[1], wdown.at[0], core_ss.at[3], core_sr.at[3], at.sib)
            down_swap.start()
        if j == n:
            down_swap.wait_recv()
            grad_down(0)
    grads.last()
    outs.last()
    own_share.wait()
    for k in range(1, n):
        exchange(k).wait_send()
        source = lax.rem(d + k, n)
        send(wup.at[0, pl.ds(0, share), :], gup_ref.at[source], a2a_ss.at[k], a2a_sr.at[source], (source, at.e)).wait_recv()
    up_swap.wait_send()
    down_swap.wait_send()
    gather.finish()
    grads.finish()
    outs.finish()


def expert_layer(x, cot_all, up, down, pick, place, n, cid):
    rows, wide = x.shape
    f2 = up.shape[1]
    f = f2 // 2
    bf16 = jnp.bfloat16
    V = lambda *s: pltpu.VMEM(s, bf16)
    D_ = pltpu.SemaphoreType.DMA
    any_, vm = pl.BlockSpec(memory_space=pl.ANY), pl.BlockSpec(memory_space=pltpu.VMEM)
    return pl.pallas_call(
        functools.partial(expert_kernel, n),
        out_shape=(
            jax.ShapeDtypeStruct((rows, D), jnp.float32),
            jax.ShapeDtypeStruct((rows, wide), jnp.float32),
            jax.ShapeDtypeStruct((n, D // n, f2), bf16),
            jax.ShapeDtypeStruct((f, D), jnp.float32),
        ),
        in_specs=[any_, any_, any_, any_, vm, vm],
        out_specs=[vm, vm, any_, vm],
        scratch_shapes=[V(n, 4, rows, wide), V(n, 4, rows, D), V(n, 4, rows, 2 * f2), V(n, 4, rows, 2 * f), V(n, 4, rows, wide),
                        V(2, D, f2), V(2, f, D)]
        + gather_sems(n) + reduce_scratch(n, rows, wide) + reduce_scratch(n, rows, D)
        + [D_((4,)), D_((4,)), D_((4,)), pltpu.SemaphoreType.REGULAR((2,)), D_((n,)), D_((n,))],
        compiler_params=pltpu.CompilerParams(collective_id=cid, has_side_effects=True, vmem_limit_bytes=63 << 20),
        name="expert_layer",
    )(x, cot_all, up, down, pick, place)


def column_kernel(n, own_ref, all_ref, load_sem, *sems):
    at = Place(n)
    gather = Gather(at, own_ref, all_ref, *sems)
    load = pltpu.make_async_copy(own_ref, all_ref.at[at.d, 0], load_sem)
    load.start()
    at.meet()
    gather.begin()
    gather.plane(at.near(0))
    for i in range(1, n + 1):
        if i < n:
            gather.column(at.near(i))
            gather.plane(at.near(i))
        gather.corner(at.near(i - 1))
    load.wait()
    gather.finish()


def gather_columns(block, n, cid):
    any_ = pl.BlockSpec(memory_space=pl.ANY)
    return pl.pallas_call(
        functools.partial(column_kernel, n),
        out_shape=jax.ShapeDtypeStruct((n, 4) + block.shape, block.dtype),
        in_specs=[any_],
        out_specs=any_,
        scratch_shapes=[pltpu.SemaphoreType.DMA] + gather_sems(n),
        compiler_params=pltpu.CompilerParams(collective_id=cid, has_side_effects=True),
        name="gather_columns",
    )(block)


def attention_forward(tokens, segment, gain, w_in, w_out):
    row_count = tokens.shape[0]
    groups = HEADS // KV_HEADS
    q_width = HEADS * HEAD
    k_width = KV_HEADS * HEAD
    inputs = tokens.astype(jnp.float32)
    inv_first = lax.rsqrt(jnp.mean(inputs * inputs, axis=1, keepdims=True) + norm_eps)
    normed_first = (inputs * inv_first * gain).astype(jnp.bfloat16)
    qkv_full = jnp.dot(normed_first, w_in, preferred_element_type=jnp.float32)
    cosine, sine_table, causal = rope_tables(segment, HEAD // 2)
    queries = rotate(
        qkv_full[:, :q_width].reshape(row_count, KV_HEADS, groups, HEAD),
        cosine[:, None, None, :],
        sine_table[:, None, None, :],
    ).astype(jnp.bfloat16)
    key_rot = rotate(
        qkv_full[:, q_width : q_width + k_width].reshape(row_count, KV_HEADS, HEAD),
        cosine[:, None, :],
        sine_table[:, None, :],
    ).astype(jnp.bfloat16)
    values = (
        qkv_full[:, q_width + k_width :].reshape(row_count, KV_HEADS, HEAD).astype(jnp.bfloat16)
    )
    scores = attention_scores(queries, key_rot, causal)
    probs = jax.nn.softmax(scores, axis=-1)
    attn_mixed = jnp.einsum(
        "kgts,skh->tkgh", probs.astype(jnp.bfloat16), values, preferred_element_type=jnp.float32
    )
    attn_mixed = attn_mixed.reshape(row_count, q_width).astype(jnp.bfloat16)
    middle = inputs + jnp.dot(attn_mixed, w_out, preferred_element_type=jnp.float32)
    return middle, (inputs, inv_first, normed_first, queries, key_rot, values, probs, cosine, sine_table, attn_mixed)


def attention_backward(saved, grad_middle, gain, w_in, w_out):
    inputs, inv_first, normed_first, queries, key_rot, values, probs, cosine, sine_table, attn_mixed = saved
    row_count = inputs.shape[0]
    groups = HEADS // KV_HEADS
    score_scale = HEAD ** (-0.5)
    f32 = jnp.float32
    grad_branch = grad_middle.astype(jnp.bfloat16)
    grad_out = jnp.einsum("tc,td->cd", attn_mixed, grad_branch, preferred_element_type=f32)
    grad_mixed = jnp.einsum("td,cd->tc", grad_branch, w_out, preferred_element_type=f32)
    grad_mixed = grad_mixed.astype(jnp.bfloat16).reshape(row_count, KV_HEADS, groups, HEAD)
    grad_values = jnp.einsum("kgts,tkgh->skh", probs.astype(jnp.bfloat16), grad_mixed, preferred_element_type=f32)
    grad_probs = jnp.einsum("tkgh,skh->kgts", grad_mixed, values, preferred_element_type=f32)
    grad_scores = (probs * (grad_probs - jnp.sum(probs * grad_probs, axis=-1, keepdims=True))).astype(jnp.bfloat16)
    grad_query = jnp.einsum("kgts,skh->tkgh", grad_scores, key_rot, preferred_element_type=f32) * score_scale
    grad_key = jnp.einsum("kgts,tkgh->skh", grad_scores, queries, preferred_element_type=f32) * score_scale
    grad_query = unrotate(grad_query, cosine[:, None, None, :], sine_table[:, None, None, :])
    grad_key = unrotate(grad_key, cosine[:, None, :], sine_table[:, None, :])
    grad_qkv = jnp.concatenate(
        [grad_query.reshape(row_count, -1), grad_key.reshape(row_count, -1), grad_values.reshape(row_count, -1)],
        axis=1,
    ).astype(jnp.bfloat16)
    grad_in = jnp.einsum("tc,tq->cq", normed_first, grad_qkv, preferred_element_type=f32)
    grad_first = jnp.einsum("tq,cq->tc", grad_qkv, w_in, preferred_element_type=f32)
    unit = inputs * inv_first
    pull = grad_first * gain
    grad_gain = jnp.sum(grad_first * unit, axis=0)
    grad_inputs = grad_middle + inv_first * (pull - unit * jnp.mean(pull * unit, axis=1, keepdims=True))
    return grad_inputs, grad_gain, grad_in, grad_out


def per_device_fast(n, tokens, segments, routes, cotangent, gain_attn, attn_in, attn_out, gain_ffn, router, expert_in, expert_out):
    f32, bf16 = jnp.float32, jnp.bfloat16
    micro, rows = tokens.shape[:2]
    total = micro * rows
    held = expert_in.shape[0]
    experts = held * 8
    f = FF // n
    shard = attn_in.shape[0]
    widths = (attn_in.shape[1], attn_out.shape[1], experts, 1, 1)
    used = sum(widths)
    wide = (used + 127) // 128 * 128
    x = tokens.reshape(total, D)
    cot = cotangent.reshape(total, D)

    dense = jnp.concatenate(
        [attn_in, attn_out, router, gain_attn[:, None], gain_ffn[:, None], jnp.zeros((shard, wide - used), bf16)], axis=1)
    dense = all_gather(dense, n, 0, False).reshape(-1, wide)
    w_in = dense[:, : widths[0]]
    w_out = dense[:, widths[0] : widths[0] + widths[1]]
    tail = dense[:, widths[0] + widths[1] :]
    w_router = tail[:, :experts]
    gain_first = tail[:, experts].astype(f32)[None, :]
    gain_second = tail[:, experts + 1].astype(f32)[None, :]
    cot_all = gather_columns(cot, n, 1)

    ups = expert_in.reshape(held, D // n, 2, n, f).transpose(3, 1, 0, 2, 4).reshape(n, D // n, 2 * held * f)
    up = lax.all_to_all(ups, "dp", split_axis=0, concat_axis=0, tiled=True).reshape(D, 2 * held * f)
    down = expert_out.reshape(held * f, D)

    segment = (segments[:, 0, :] + 2 * rows * jnp.arange(micro, dtype=jnp.int32)[:, None]).reshape(total)
    middle, saved = attention_forward(x, segment, gain_first, w_in, w_out)
    inv_second = lax.rsqrt(jnp.mean(middle * middle, axis=1, keepdims=True) + norm_eps)
    normed_second = (middle * inv_second * gain_second).astype(bf16)
    logits = jnp.dot(normed_second, w_router, preferred_element_type=f32)
    route = routes.reshape(total, TOP_K)
    chosen = jnp.any(route[:, :, None] == jnp.arange(experts, dtype=jnp.int32)[None, None, :], axis=1)
    masked = jnp.where(chosen, logits, neg_large)
    raised = jnp.where(chosen, jnp.exp(masked - jnp.max(masked, axis=1, keepdims=True)), 0.0)
    gates = raised / jnp.sum(raised, axis=1, keepdims=True)

    high = gates.astype(bf16)
    low = (gates - high.astype(f32)).astype(bf16)
    dispatched = jnp.concatenate([normed_second, high, low, jnp.zeros((total, 128 - 2 * experts), bf16)], axis=1)

    mine = lax.axis_index("expert")
    order = jnp.stack([mine, mine + 1 - 2 * lax.rem(mine, 2)])
    owner = (order[:, None] * held + jnp.arange(held, dtype=jnp.int32)[None, :]).reshape(-1)
    owner = jnp.repeat(owner, f)[None, :]
    lane = jnp.arange(128, dtype=jnp.int32)[:, None]
    pick = ((lane == owner) | (lane == owner + experts)).astype(bf16)
    place = (lane == owner).astype(bf16).T
    moe_sum, grad_sum, grad_up, grad_down = expert_layer(dispatched, cot_all, up, down, pick, place, n, 2)
    result = (middle + moe_sum).astype(bf16)
    grad_up = grad_up.reshape(n, D // n, held, 2, f).transpose(2, 1, 3, 0, 4).reshape(held, D // n, 2 * FF).astype(f32)

    upstream = cot.astype(f32)
    grad_gates = grad_sum[:, D : D + experts]
    grad_logits = (gates * (grad_gates - jnp.sum(gates * grad_gates, axis=1, keepdims=True))).astype(bf16)
    grad_router = jnp.einsum("td,te->de", normed_second, grad_logits, preferred_element_type=f32)
    grad_second = jnp.einsum("te,de->td", grad_logits, w_router, preferred_element_type=f32) + grad_sum[:, :D]
    unit = middle * inv_second
    pull = grad_second * gain_second
    grad_gain_ffn = jnp.sum(grad_second * unit, axis=0)
    grad_middle = upstream + inv_second * (pull - unit * jnp.mean(pull * unit, axis=1, keepdims=True))
    grad_inputs, grad_gain_attn, grad_in, grad_out = attention_backward(saved, grad_middle, gain_first, w_in, w_out)
    parts = jnp.concatenate(
        [grad_in, grad_out, grad_router, grad_gain_attn[:, None], grad_gain_ffn[:, None], jnp.zeros((D, wide - used), f32)],
        axis=1).astype(bf16)
    sums = reduce_scatter(parts.reshape(-1, shard, wide), n, 3, False)
    a, b = widths[0], widths[0] + widths[1]
    return (
        result.reshape(micro, rows, D),
        grad_inputs.reshape(micro, rows, D),
        sums[:, b + experts],
        sums[:, :a],
        sums[:, a:b],
        sums[:, b + experts + 1],
        sums[:, b : b + experts],
        grad_up,
        grad_down.reshape(held, f, D),
    )


def solution(mesh):
    placed = (
        P(None, ("dp", "expert"), None),
        P(None, ("dp", "expert"), None),
        P(None, ("dp", "expert"), None),
        P(None, ("dp", "expert"), None),
        P(("dp", "expert")),
        P(("dp", "expert"), None),
        P(("dp", "expert"), None),
        P(("dp", "expert")),
        P(("dp", "expert"), None),
        P("expert", "dp", None),
        P("expert", "dp", None),
    )
    fast = mesh.shape["expert"] == 8 and FF // mesh.shape["dp"] == 128
    body = functools.partial(per_device_fast, mesh.shape["dp"]) if fast else per_device
    return jax.shard_map(
        body,
        mesh=mesh,
        in_specs=placed,
        out_specs=(
            P(None, ("dp", "expert"), None),
            P(None, ("dp", "expert"), None),
            P(("dp", "expert")),
            P(("dp", "expert"), None),
            P(("dp", "expert"), None),
            P(("dp", "expert")),
            P(("dp", "expert"), None),
            P("expert", "dp", None),
            P("expert", "dp", None),
        ),
        check_vma=False,
    )
```

```python
import functools

import jax
import jax.numpy as jnp
from jax import lax
from jax.experimental import pallas as pl
from jax.experimental.pallas import tpu as pltpu
from jax.sharding import PartitionSpec as P

MESH = pl.DeviceIdType.MESH

D = 1536
HEADS = 24
KV_HEADS = 8
HEAD = 64
FF = 512
TOP_K = 8


norm_eps = 1e-06
rope_base = 10000.0
neg_large = -1e30
highest = lax.Precision.HIGHEST


def rope_tables(segment, half_width):
    row_count = segment.shape[0]
    places = jnp.arange(row_count, dtype=jnp.int32)
    same_seq = segment[:, None] == segment[None, :]
    seq_start = jnp.min(jnp.where(same_seq, places[None, :], row_count), axis=1)
    offset = (places - seq_start).astype(jnp.float32)
    frequencies = rope_base ** (-jnp.arange(half_width, dtype=jnp.float32) / half_width)
    angles = offset[:, None] * frequencies[None, :]
    causal = same_seq & (places[None, :] <= places[:, None])
    return (jnp.cos(angles), jnp.sin(angles), causal)


def rotate(operand, cosine, sine_table):
    half_width = operand.shape[-1] // 2
    front_part = operand[..., :half_width]
    back_part = operand[..., half_width:]
    return jnp.concatenate(
        [
            front_part * cosine - back_part * sine_table,
            back_part * cosine + front_part * sine_table,
        ],
        axis=-1,
    )


def unrotate(gradient, cosine, sine_table):
    half_width = gradient.shape[-1] // 2
    front_part = gradient[..., :half_width]
    back_part = gradient[..., half_width:]
    return jnp.concatenate(
        [
            front_part * cosine + back_part * sine_table,
            back_part * cosine - front_part * sine_table,
        ],
        axis=-1,
    )


def slot_targets(route_now, expert_count, capacity):
    flat_ids = route_now.reshape(-1)
    onehot = (flat_ids[:, None] == jnp.arange(expert_count, dtype=jnp.int32)[None, :]).astype(
        jnp.int32
    )
    earlier = jnp.cumsum(onehot, axis=0) - onehot
    slot_index = jnp.sum(earlier * onehot, axis=1)
    return flat_ids * capacity + slot_index


def dense_fetch(gain_attn, attn_in, attn_out, gain_ffn, router):
    return (
        lax.all_gather(gain_attn, ("dp", "expert"), axis=0, tiled=True),
        lax.all_gather(attn_in, ("dp", "expert"), axis=0, tiled=True),
        lax.all_gather(attn_out, ("dp", "expert"), axis=0, tiled=True),
        lax.all_gather(gain_ffn, ("dp", "expert"), axis=0, tiled=True),
        lax.all_gather(router, ("dp", "expert"), axis=0, tiled=True),
    )


def expert_fetch(expert_in, expert_out):
    return (
        lax.all_gather(expert_in, "dp", axis=1, tiled=True),
        lax.all_gather(expert_out, "dp", axis=1, tiled=True),
    )


def dense_reduce(grad_set):
    return (
        lax.psum_scatter(grad_set[0], ("dp", "expert"), scatter_dimension=0, tiled=True),
        lax.psum_scatter(grad_set[1], ("dp", "expert"), scatter_dimension=0, tiled=True),
        lax.psum_scatter(grad_set[2], ("dp", "expert"), scatter_dimension=0, tiled=True),
        lax.psum_scatter(grad_set[3], ("dp", "expert"), scatter_dimension=0, tiled=True),
        lax.psum_scatter(grad_set[4], ("dp", "expert"), scatter_dimension=0, tiled=True),
    )


def expert_reduce(grad_set):
    return (
        lax.psum_scatter(grad_set[0], "dp", scatter_dimension=1, tiled=True),
        lax.psum_scatter(grad_set[1], "dp", scatter_dimension=1, tiled=True),
    )


def attention_scores(queries, key_rot, causal):
    score_scale = HEAD ** (-0.5)
    scores = (
        jnp.einsum("tkgh,skh->kgts", queries, key_rot, preferred_element_type=jnp.float32)
        * score_scale
    )
    return jnp.where(causal[None, None], scores, neg_large)


def forward_micro(tokens_now, segment, route_now, dense_set, expert_set, shapes):
    expert_count, capacity, group_count, local_experts = shapes
    gain_attn, qkv_weight, out_weight, gain_ffn, router_weight = dense_set
    expert_up, expert_down = expert_set
    row_count = tokens_now.shape[0]
    groups = HEADS // KV_HEADS
    q_width = HEADS * HEAD
    k_width = KV_HEADS * HEAD
    inputs = tokens_now.astype(jnp.float32)
    inv_first = lax.rsqrt(jnp.mean(inputs * inputs, axis=1, keepdims=True) + norm_eps)
    normed_first = (inputs * inv_first * gain_attn.astype(jnp.float32)).astype(jnp.bfloat16)
    qkv_full = jnp.dot(normed_first, qkv_weight, preferred_element_type=jnp.float32)
    cosine, sine_table, causal = rope_tables(segment, HEAD // 2)
    queries = rotate(
        qkv_full[:, :q_width].reshape(row_count, KV_HEADS, groups, HEAD),
        cosine[:, None, None, :],
        sine_table[:, None, None, :],
    ).astype(jnp.bfloat16)
    key_rot = rotate(
        qkv_full[:, q_width : q_width + k_width].reshape(row_count, KV_HEADS, HEAD),
        cosine[:, None, :],
        sine_table[:, None, :],
    ).astype(jnp.bfloat16)
    values = (
        qkv_full[:, q_width + k_width :].reshape(row_count, KV_HEADS, HEAD).astype(jnp.bfloat16)
    )
    scores = attention_scores(queries, key_rot, causal)
    score_peak = jnp.max(scores, axis=-1, keepdims=True)
    exp_scores = jnp.exp(scores - score_peak)
    exp_total = jnp.sum(exp_scores, axis=-1, keepdims=True)
    log_total = score_peak + jnp.log(exp_total)
    soft_probs = (exp_scores / exp_total).astype(jnp.bfloat16)
    attn_mixed = jnp.einsum(
        "kgts,skh->tkgh", soft_probs, values, preferred_element_type=jnp.float32
    )
    attn_mixed = attn_mixed.reshape(row_count, q_width).astype(jnp.bfloat16)
    middle = inputs + jnp.dot(attn_mixed, out_weight, preferred_element_type=jnp.float32)
    inv_second = lax.rsqrt(jnp.mean(middle * middle, axis=1, keepdims=True) + norm_eps)
    normed_second = (middle * inv_second * gain_ffn.astype(jnp.float32)).astype(jnp.bfloat16)
    logits = jnp.dot(normed_second, router_weight, preferred_element_type=jnp.float32)
    chosen = (
        route_now[:, :, None] == jnp.arange(expert_count, dtype=jnp.int32)[None, None, :]
    ).astype(jnp.float32)
    picked_logits = jnp.sum(chosen * logits[:, None, :], axis=-1)
    gate_values = jax.nn.softmax(picked_logits, axis=-1)
    targets = slot_targets(route_now, expert_count, capacity)
    source_rows = jnp.repeat(normed_second, TOP_K, axis=0)
    buffer = jnp.zeros((expert_count * capacity, D), jnp.bfloat16).at[targets].set(source_rows)
    send_rows = buffer.reshape(group_count, local_experts, capacity, D)
    received = lax.all_to_all(send_rows, "expert", split_axis=0, concat_axis=0, tiled=True)
    gate_up = jnp.einsum("secd,edf->secf", received, expert_up, preferred_element_type=jnp.float32)
    hidden = (jax.nn.silu(gate_up[..., :FF]) * gate_up[..., FF:]).astype(jnp.bfloat16)
    expert_result = jnp.einsum(
        "secf,efd->secd", hidden, expert_down, preferred_element_type=jnp.float32
    ).astype(jnp.bfloat16)
    returned = lax.all_to_all(expert_result, "expert", split_axis=0, concat_axis=0, tiled=True)
    picked = returned.reshape(expert_count * capacity, D)[targets].reshape(row_count, TOP_K, D)
    moe_sum = jnp.einsum(
        "tk,tkd->td", gate_values, picked, precision=highest, preferred_element_type=jnp.float32
    )
    result = (middle + moe_sum).astype(jnp.bfloat16)
    saved_state = (
        inputs,
        inv_first,
        normed_first,
        queries,
        key_rot,
        values,
        log_total,
        causal,
        cosine,
        sine_table,
        attn_mixed,
        middle,
        inv_second,
        normed_second,
        chosen,
        gate_values,
        targets,
        received,
        gate_up,
        hidden,
        picked,
    )
    return (result, saved_state)


def backward_micro(saved_state, cotan_now, dense_set, expert_set, shapes):
    expert_count, capacity, group_count, local_experts = shapes
    (
        inputs,
        inv_first,
        normed_first,
        queries,
        key_rot,
        values,
        log_total,
        causal,
        cosine,
        sine_table,
        attn_mixed,
        middle,
        inv_second,
        normed_second,
        chosen,
        gate_values,
        targets,
        received,
        gate_up,
        hidden,
        picked,
    ) = saved_state
    gain_attn, qkv_weight, out_weight, gain_ffn, router_weight = dense_set
    expert_up, expert_down = expert_set
    row_count = inputs.shape[0]
    groups = HEADS // KV_HEADS
    q_width = HEADS * HEAD
    k_width = KV_HEADS * HEAD
    score_scale = HEAD ** (-0.5)
    upstream = cotan_now.astype(jnp.float32)
    grad_gates = jnp.einsum(
        "td,tkd->tk", upstream, picked, precision=highest, preferred_element_type=jnp.float32
    )
    grad_picked = gate_values * (
        grad_gates - jnp.sum(gate_values * grad_gates, axis=-1, keepdims=True)
    )
    grad_logits = jnp.sum(chosen * grad_picked[:, :, None], axis=1).astype(jnp.bfloat16)
    grad_router = jnp.einsum(
        "td,te->de", normed_second, grad_logits, preferred_element_type=jnp.float32
    )
    grad_second = jnp.einsum(
        "te,de->td", grad_logits, router_weight, preferred_element_type=jnp.float32
    )
    grad_slots = (
        (gate_values[:, :, None] * upstream[:, None, :])
        .astype(jnp.bfloat16)
        .reshape(row_count * TOP_K, D)
    )
    grad_buffer = jnp.zeros((expert_count * capacity, D), jnp.bfloat16).at[targets].set(grad_slots)
    grad_buffer = grad_buffer.reshape(group_count, local_experts, capacity, D)
    grad_result = lax.all_to_all(grad_buffer, "expert", split_axis=0, concat_axis=0, tiled=True)
    grad_hidden = jnp.einsum(
        "secd,efd->secf", grad_result, expert_down, preferred_element_type=jnp.float32
    )
    grad_down = jnp.einsum(
        "secf,secd->efd", hidden, grad_result, preferred_element_type=jnp.float32
    )
    gate_part = gate_up[..., :FF]
    up_part = gate_up[..., FF:]
    gate_sigmoid = jax.nn.sigmoid(gate_part)
    grad_gate = grad_hidden * up_part * gate_sigmoid * (1.0 + gate_part * (1.0 - gate_sigmoid))
    grad_up_part = grad_hidden * (gate_part * gate_sigmoid)
    grad_gate_up = jnp.concatenate([grad_gate, grad_up_part], axis=-1).astype(jnp.bfloat16)
    grad_up = jnp.einsum(
        "secd,secf->edf", received, grad_gate_up, preferred_element_type=jnp.float32
    )
    grad_rows = jnp.einsum(
        "secf,edf->secd", grad_gate_up, expert_up, preferred_element_type=jnp.float32
    ).astype(jnp.bfloat16)
    grad_back = lax.all_to_all(grad_rows, "expert", split_axis=0, concat_axis=0, tiled=True)
    grad_choice = grad_back.reshape(expert_count * capacity, D)[targets].reshape(
        row_count, TOP_K, D
    )
    grad_second = grad_second + jnp.sum(grad_choice, axis=1, dtype=jnp.float32)
    unit_second = middle * inv_second
    pull_second = grad_second * gain_ffn.astype(jnp.float32)
    grad_gain_ffn = jnp.sum(grad_second * unit_second, axis=0)
    grad_middle = upstream + inv_second * (
        pull_second - unit_second * jnp.mean(pull_second * unit_second, axis=1, keepdims=True)
    )
    grad_branch = grad_middle.astype(jnp.bfloat16)
    grad_out_weight = jnp.einsum(
        "tc,td->cd", attn_mixed, grad_branch, preferred_element_type=jnp.float32
    )
    grad_mixed = jnp.einsum(
        "td,cd->tc", grad_branch, out_weight, preferred_element_type=jnp.float32
    )
    grad_mixed = grad_mixed.astype(jnp.bfloat16).reshape(row_count, KV_HEADS, groups, HEAD)
    scores = attention_scores(queries, key_rot, causal)
    soft_probs = jnp.exp(scores - log_total)
    grad_values = jnp.einsum(
        "kgts,tkgh->skh",
        soft_probs.astype(jnp.bfloat16),
        grad_mixed,
        preferred_element_type=jnp.float32,
    )
    grad_probs = jnp.einsum(
        "tkgh,skh->kgts", grad_mixed, values, preferred_element_type=jnp.float32
    )
    grad_scores = soft_probs * (
        grad_probs - jnp.sum(soft_probs * grad_probs, axis=-1, keepdims=True)
    )
    grad_scores = grad_scores.astype(jnp.bfloat16)
    grad_query = (
        jnp.einsum("kgts,skh->tkgh", grad_scores, key_rot, preferred_element_type=jnp.float32)
        * score_scale
    )
    grad_key = (
        jnp.einsum("kgts,tkgh->skh", grad_scores, queries, preferred_element_type=jnp.float32)
        * score_scale
    )
    grad_query = unrotate(grad_query, cosine[:, None, None, :], sine_table[:, None, None, :])
    grad_key = unrotate(grad_key, cosine[:, None, :], sine_table[:, None, :])
    grad_qkv = jnp.concatenate(
        [
            grad_query.reshape(row_count, q_width),
            grad_key.reshape(row_count, k_width),
            grad_values.reshape(row_count, k_width),
        ],
        axis=1,
    ).astype(jnp.bfloat16)
    grad_qkv_weight = jnp.einsum(
        "tc,tq->cq", normed_first, grad_qkv, preferred_element_type=jnp.float32
    )
    grad_first = jnp.einsum("tq,cq->tc", grad_qkv, qkv_weight, preferred_element_type=jnp.float32)
    unit_first = inputs * inv_first
    pull_first = grad_first * gain_attn.astype(jnp.float32)
    grad_gain_attn = jnp.sum(grad_first * unit_first, axis=0)
    grad_inputs = grad_middle + inv_first * (
        pull_first - unit_first * jnp.mean(pull_first * unit_first, axis=1, keepdims=True)
    )
    dense_grads = (grad_gain_attn, grad_qkv_weight, grad_out_weight, grad_gain_ffn, grad_router)
    expert_grads = (grad_up, grad_down)
    return (grad_inputs, dense_grads, expert_grads)


def add_pair(left_part, right_part):
    return left_part + right_part


def per_device(
    tokens,
    segments,
    routes,
    cotangent,
    gain_attn,
    attn_in,
    attn_out,
    gain_ffn,
    router,
    expert_in,
    expert_out,
):
    local_experts = expert_in.shape[0]
    group_count = lax.axis_size("expert")
    expert_count = local_experts * group_count
    micro_count = tokens.shape[0]
    row_count = tokens.shape[1]
    capacity = (row_count * TOP_K * 5 // (4 * expert_count) + 7) // 8 * 8
    shapes = (expert_count, capacity, group_count, local_experts)
    outputs = []
    grad_list = []
    dense_total = None
    expert_total = None
    for micro_index in range(micro_count):
        dense_set = dense_fetch(gain_attn, attn_in, attn_out, gain_ffn, router)
        expert_set = expert_fetch(expert_in, expert_out)
        result, saved_state = forward_micro(
            tokens[micro_index],
            segments[micro_index, 0],
            routes[micro_index],
            dense_set,
            expert_set,
            shapes,
        )
        dense_set = dense_fetch(gain_attn, attn_in, attn_out, gain_ffn, router)
        expert_set = expert_fetch(expert_in, expert_out)
        grad_inputs, dense_grads, expert_grads = backward_micro(
            saved_state, cotangent[micro_index], dense_set, expert_set, shapes
        )
        dense_grads = dense_reduce(dense_grads)
        expert_grads = expert_reduce(expert_grads)
        if dense_total is None:
            dense_total = dense_grads
            expert_total = expert_grads
        else:
            dense_total = jax.tree.map(add_pair, dense_total, dense_grads)
            expert_total = jax.tree.map(add_pair, expert_total, expert_grads)
        outputs.append(result)
        grad_list.append(grad_inputs)
    return (
        jnp.stack(outputs, axis=0),
        jnp.stack(grad_list, axis=0),
        dense_total[0],
        dense_total[1],
        dense_total[2],
        dense_total[3],
        dense_total[4],
        expert_total[0],
        expert_total[1],
    )


NN = (((1,), (0,)), ((), ()))
NT = (((1,), (1,)), ((), ()))
TN = (((0,), (0,)), ((), ()))


def mm(a, b, dims=NN):
    return lax.dot_general(a, b, dims, preferred_element_type=jnp.float32)


class Place:
    def __init__(self, n):
        self.n = n
        d = self.d = lax.axis_index("dp")
        e = self.e = lax.axis_index("expert")
        c, x, y = lax.rem(e, 2), lax.rem(lax.div(e, 2), 2), lax.div(e, 4)
        self.sib = (d, e + 1 - 2 * c)
        self.nx = (d, e + 2 - 4 * x)
        self.ny = (d, e + 4 - 8 * y)
        self.diag = self.nx[1] + 4 - 8 * y
        self.c, self.x, self.y = c, x, y
        self.below = (d - 1, e)
        self.above = (d + 1, e)
        self.has_below = d > 0
        self.has_above = d < n - 1

    def meet(self, everyone=False):
        barrier = pltpu.get_barrier_semaphore()
        d, n = self.d, self.n
        if everyone:
            others = n - 1 + 3

            @pl.loop(1, n)
            def _(k):
                pl.semaphore_signal(barrier, inc=1, device_id=(lax.rem(d + k, n), self.e), device_id_type=MESH)
        else:
            others = 3 + jnp.minimum(d, 1) + jnp.minimum(n - 1 - d, 1)

            @pl.when(self.has_below)
            def _():
                pl.semaphore_signal(barrier, inc=1, device_id=self.below, device_id_type=MESH)

            @pl.when(self.has_above)
            def _():
                pl.semaphore_signal(barrier, inc=1, device_id=self.above, device_id_type=MESH)

        for dev in (self.sib, self.nx, self.ny):
            pl.semaphore_signal(barrier, inc=1, device_id=dev, device_id_type=MESH)
        pl.semaphore_wait(barrier, others)

    def far(self, i):
        n, d = self.n, self.d
        low = d < n - d
        m = jnp.where(low, d, n - 1 - d)
        t = jnp.where(i < n - 1 - m, n - 1 - i, jnp.where(i < n - 1, i - (n - 1 - m), m))
        return jnp.where(low, t, n - 1 - t)

    def near(self, i):
        return self.far(self.n - 1 - i)


def send(src, dst, ss, rs, dev):
    return pltpu.make_async_remote_copy(src, dst, ss, rs, device_id=dev, device_id_type=MESH)


class Gather:
    def __init__(self, at, own, buf, send_sem, recv_z, recv_x, recv_y, recv_d):
        self.at, self.own, self.buf = at, own, buf
        self.ss, self.rz, self.rx, self.ry, self.rd = send_sem, recv_z, recv_x, recv_y, recv_d
        rows = own.shape[0]
        self.A, self.B = pl.ds(0, rows // 2), pl.ds(rows // 2, rows // 2)

    def source(self, zz, own):
        return self.own if own else self.buf.at[zz, 0]

    def down(self, zz, own=False):
        return send(self.source(zz, own), self.buf.at[zz, 0], self.ss.at[zz, 0], self.rz.at[zz], self.at.below)

    def up(self, zz, own=False):
        return send(self.source(zz, own), self.buf.at[zz, 0], self.ss.at[zz, 1], self.rz.at[zz], self.at.above)

    def to_x(self, zz, own=False):
        return send(self.source(zz, own), self.buf.at[zz, 1], self.ss.at[zz, 2], self.rx.at[zz], self.at.nx)

    def to_y(self, zz, own=False):
        return send(self.source(zz, own), self.buf.at[zz, 2], self.ss.at[zz, 3], self.ry.at[zz], self.at.ny)

    def turn_y(self, zz):
        return send(self.buf.at[zz, 1, self.A], self.buf.at[zz, 3, self.A], self.ss.at[zz, 4], self.rd.at[zz, 0], self.at.ny)

    def turn_x(self, zz):
        return send(self.buf.at[zz, 2, self.B], self.buf.at[zz, 3, self.B], self.ss.at[zz, 5], self.rd.at[zz, 1], self.at.nx)

    def begin(self):
        self.begin_z()
        self.begin_xy()

    def begin_z(self):
        d = self.at.d

        @pl.when(self.at.has_below)
        def _():
            self.down(d, True).start()

        @pl.when(self.at.has_above)
        def _():
            self.up(d, True).start()

    def begin_xy(self):
        self.to_x(self.at.d, True).start()
        self.to_y(self.at.d, True).start()

    def column_z(self, zz):
        d = self.at.d

        @pl.when(zz < d)
        def _():
            self.up(zz).wait_recv()

            @pl.when(self.at.has_above)
            def _():
                self.up(zz).start()

        @pl.when(zz > d)
        def _():
            self.down(zz).wait_recv()

            @pl.when(self.at.has_below)
            def _():
                self.down(zz).start()

    def column_xy(self, zz):
        self.to_x(zz).start()
        self.to_y(zz).start()

    def column(self, zz):
        self.column_z(zz)
        self.column_xy(zz)

    def plane(self, zz):
        self.to_x(zz).wait_recv()
        self.turn_y(zz).start()
        self.to_y(zz).wait_recv()
        self.turn_x(zz).start()

    def corner(self, zz):
        self.turn_y(zz).wait_recv()
        self.turn_x(zz).wait_recv()

    def finish(self):
        d = self.at.d

        @pl.loop(0, self.at.n)
        def _(zz):
            for copy in (self.to_x, self.to_y, self.turn_y, self.turn_x):
                copy(zz).wait_send()

            @pl.when((d > 0) & (zz >= d))
            def _():
                self.down(zz).wait_send()

            @pl.when(self.at.has_above & (zz <= d))
            def _():
                self.up(zz).wait_send()


def gather_sems(n):
    D_ = pltpu.SemaphoreType.DMA
    return [D_((n, 6)), D_((n,)), D_((n,)), D_((n,)), D_((n, 2))]


def add_rows(dst, src):
    rows = dst.shape[0]
    step = 16

    @pl.loop(0, rows // step)
    def _(r):
        w = pl.ds(pl.multiple_of(r * step, step), step)
        dst[w, :] = (dst[w, :].astype(jnp.float32) + src[w, :].astype(jnp.float32)).astype(dst.dtype)


class Reduce:
    def __init__(self, at, buf, total, r1, r2, rz, ss_1, sr_1, ss_2, sr_2, ss_z, sr_z, start=None):
        self.start = start
        self.at, self.buf, self.total = at, buf, total
        self.r1, self.r2, self.rz = r1, r2, rz
        self.sems = (ss_1, sr_1, ss_2, sr_2, ss_z, sr_z)
        rows = total.shape[0]
        self.A, self.B = pl.ds(0, rows // 2), pl.ds(rows // 2, rows // 2)

    def first(self, zz, k):
        ss, sr = self.sems[0], self.sems[1]
        slot, part, dev = ((3, self.A, self.at.nx), (3, self.B, self.at.ny), (1, self.A, self.at.nx), (2, self.B, self.at.ny))[k]
        return send(self.buf.at[zz, slot, part], self.r1.at[zz, k], ss.at[zz, k], sr.at[zz, k], dev)

    def second(self, zz, k):
        ss, sr = self.sems[2], self.sems[3]
        slot, part, dev = ((2, self.A, self.at.ny), (1, self.B, self.at.nx))[k]
        return send(self.buf.at[zz, slot, part], self.r2.at[zz, k], ss.at[zz, k], sr.at[zz, k], dev)

    def down(self, zz):
        return send(self.buf.at[zz, 0], self.rz.at[zz], self.sems[4].at[zz], self.sems[5].at[zz], self.at.below)

    def up(self, zz):
        slot = jnp.where(zz == self.at.d + 1, self.at.n, zz)
        return send(self.buf.at[zz, 0], self.rz.at[slot], self.sems[4].at[zz], self.sems[5].at[slot], self.at.above)

    def arrive(self, slot):
        return send(self.buf.at[0, 0], self.rz.at[slot], self.sems[4].at[0], self.sems[5].at[slot], self.at.nx)

    def s1(self, zz):
        for k in range(4):
            self.first(zz, k).start()

    def s2(self, zz):
        self.first(zz, 0).wait_recv()
        add_rows(self.buf.at[zz, 2, self.A], self.r1.at[zz, 0])
        self.second(zz, 0).start()
        self.first(zz, 1).wait_recv()
        add_rows(self.buf.at[zz, 1, self.B], self.r1.at[zz, 1])
        self.second(zz, 1).start()
        self.first(zz, 2).wait_recv()
        add_rows(self.buf.at[zz, 0, self.A], self.r1.at[zz, 2])
        self.first(zz, 3).wait_recv()
        add_rows(self.buf.at[zz, 0, self.B], self.r1.at[zz, 3])

    def s3(self, zz):
        self.second(zz, 0).wait_recv()
        add_rows(self.buf.at[zz, 0, self.A], self.r2.at[zz, 0])
        self.second(zz, 1).wait_recv()
        add_rows(self.buf.at[zz, 0, self.B], self.r2.at[zz, 1])

    def line(self, zz):
        d = self.at.d

        @pl.when(((zz < d) & self.at.has_above) | ((zz > d) & self.at.has_below))
        def _():
            self.arrive(zz).wait_recv()
            add_rows(self.buf.at[zz, 0], self.rz.at[zz])

        @pl.when(zz < d)
        def _():
            self.down(zz).start()

        @pl.when(zz > d)
        def _():
            self.up(zz).start()

    def last(self):
        d, n, rows, step = self.at.d, self.at.n, self.total.shape[0], 16

        def over(fn):
            @pl.loop(0, rows // step)
            def _(r):
                fn(pl.ds(pl.multiple_of(r * step, step), step))

        def own(w):
            first = self.buf[d, 0, w, :].astype(jnp.float32)
            self.total[w, :] = first if self.start is None else first + self.start[w, :]

        def more(slot):
            def fn(w):
                self.total[w, :] += self.rz[slot, w, :].astype(jnp.float32)

            self.arrive(slot).wait_recv()
            over(fn)

        over(own)

        @pl.when(self.at.has_above)
        def _():
            more(d)

        @pl.when(self.at.has_below)
        def _():
            more(n)

    def finish(self):
        d = self.at.d

        @pl.loop(0, self.at.n)
        def _(zz):
            for k in range(4):
                self.first(zz, k).wait_send()
            for k in range(2):
                self.second(zz, k).wait_send()

            @pl.when(zz != d)
            def _():
                self.arrive(zz)
                send(self.buf.at[zz, 0], self.rz.at[zz], self.sems[4].at[zz], self.sems[5].at[zz], self.at.nx).wait_send()


def reduce_scratch(n, rows, cols):
    D_ = pltpu.SemaphoreType.DMA
    V = lambda *s: pltpu.VMEM(s, jnp.bfloat16)
    return [V(n, 4, rows // 2, cols), V(n, 2, rows // 2, cols), V(n + 1, rows, cols),
            D_((n, 4)), D_((n, 4)), D_((n, 2)), D_((n, 2)), D_((n,)), D_((n + 1,))]


def expert_kernel(n, x_ref, cot_ref, up_ref, down_ref, pick_ref, place_ref, mid_ref,
                  out_ref, gx_ref, gup_ref, gdown_ref,
                  xb, cb, gg, mixed, gb, wup, wdown, *rest):
    f32, bf16 = jnp.float32, jnp.bfloat16
    at = Place(n)
    d = at.d
    gather = Gather(at, x_ref, xb, *rest[:5])
    grads = Reduce(at, gb, gx_ref, *rest[5:14])
    outs = Reduce(at, gg, out_ref, *rest[14:23], start=mid_ref)
    load_sem, core_ss, core_sr, free = rest[23:]
    rows = x_ref.shape[0]
    f2 = up_ref.shape[1]
    f = f2 // 2
    held = f // 128
    loads = [
        pltpu.make_async_copy(x_ref, xb.at[d, 0], load_sem.at[0]),
        pltpu.make_async_copy(up_ref, wup.at[0], load_sem.at[1]),
        pltpu.make_async_copy(down_ref, wdown.at[0], load_sem.at[2]),
        pltpu.make_async_copy(cot_ref, cb, load_sem.at[3]),
    ]
    for load in loads:
        load.start()
    at.meet()
    gather.begin()
    swaps = [
        send(up_ref, wup.at[1], core_ss.at[0], core_sr.at[0], at.sib),
        send(down_ref, wdown.at[1], core_ss.at[1], core_sr.at[1], at.sib),
    ]
    for swap in swaps:
        swap.start()
    for load in loads:
        load.wait()
    for swap in swaps:
        swap.wait_recv()
    gather.plane(at.near(0))
    gather.column(at.near(1))

    def tokens(ref, zz, p, lo, width):
        return ref[zz, pl.ds(2 * p, 2), :, pl.ds(lo, width)].reshape(2 * rows, width)

    def half(zz, p):
        pair = pl.ds(2 * p, 2)
        x = tokens(xb, zz, p, 0, D)
        cot = tokens(cb, zz, p, 0, D)
        mix = mm(tokens(xb, zz, p, D, 128), pick_ref[...])
        sums = jnp.zeros((2 * rows, 128), f32)
        for h in range(2):
            gate_up = mm(x, wup[h])
            back = mm(cot, wdown[h], NT)
            for j in range(held):
                k = h * held + j
                gate = gate_up[:, j * 256 : j * 256 + 128]
                up = gate_up[:, j * 256 + 128 : j * 256 + 256]
                b = back[:, j * 128 : (j + 1) * 128]
                m = mix[:, k * 128 : (k + 1) * 128]
                sig = 1.0 / (1.0 + jnp.exp(-gate))
                act = gate * sig
                hidden = (act * up).astype(bf16).astype(f32)
                prod = hidden * b
                high = prod.astype(bf16)
                low = (prod - high.astype(f32)).astype(bf16)
                sel = place_ref[k * 128 : (k + 1) * 128, :]
                sums += mm(high, sel) + mm(low, sel)
                mixed[zz, pair, :, pl.ds(k * 128, 128)] = (m * hidden).astype(bf16).reshape(2, rows, 128)
                gh = m * b
                gg[zz, pair, :, pl.ds(k * 256, 128)] = (
                    (gh * up * sig * (1.0 + gate * (1.0 - sig))).astype(bf16).reshape(2, rows, 128))
                gg[zz, pair, :, pl.ds(k * 256 + 128, 128)] = (gh * act).astype(bf16).reshape(2, rows, 128)
        for q in range(D // 512):
            cols = pl.ds(q * 512, 512)
            part = mm(tokens(gg, zz, p, 0, f2), wup[0, cols, :], NT) + mm(tokens(gg, zz, p, f2, f2), wup[1, cols, :], NT)
            gb[zz, pair, :, cols] = part.astype(bf16).reshape(2, rows, 512)
        gb[zz, pair, :, pl.ds(D, 128)] = sums.astype(bf16).reshape(2, rows, 128)

    @pl.loop(0, n)
    def _(i):
        zz = at.near(i)
        half(zz, 0)

        @pl.when(i + 1 < n)
        def _():
            gather.plane(at.near(i + 1))

        @pl.when(i + 2 < n)
        def _():
            gather.column(at.near(i + 2))

        gather.corner(zz)
        half(zz, 1)
        grads.s1(zz)

        @pl.when(i >= 1)
        def _():
            grads.s2(at.near(i - 1))

        @pl.when(i >= 2)
        def _():
            grads.s3(at.near(i - 2))

    pl.semaphore_signal(free.at[0], inc=1, device_id=at.sib, device_id_type=MESH)

    def grad_up(h, more):
        @pl.loop(0, D // 256)
        def _(q):
            cols = pl.ds(pl.multiple_of(q * 256, 256), 256)
            xs = xb[:, :, :, cols].reshape(n * 4 * rows, 256)
            part = mm(xs, gg[:, :, :, pl.ds(h * f2, f2)].reshape(n * 4 * rows, f2), TN)
            if more:
                part += wup[h, cols, :].astype(f32)
            wup[h, cols, :] = part.astype(bf16)

    def grad_down(h):
        for q in range(D // 512):
            cols = pl.ds(q * 512, 512)
            part = mm(mixed[:, :, :, pl.ds(h * f, f)].reshape(n * 4 * rows, f), cb[:, :, :, cols].reshape(n * 4 * rows, 512), TN)
            if h == 0:
                gdown_ref[:, cols] = part + wdown[0, :, cols].astype(f32)
            else:
                wdown[1, :, cols] = part.astype(bf16)

    def output(zz):
        @pl.loop(0, 2)
        def _(p):
            for q in range(D // 512):
                cols = pl.ds(q * 512, 512)
                part = mm(tokens(mixed, zz, p, 0, f), wdown[0, :, cols]) + mm(tokens(mixed, zz, p, f, f), wdown[1, :, cols])
                gg[zz, pl.ds(2 * p, 2), :, cols] = part.astype(bf16).reshape(2, rows, 512)

    grad_up(1, False)
    pl.semaphore_wait(free.at[0], 1)
    up_swap = send(wup.at[1], wup.at[0], core_ss.at[2], core_sr.at[2], at.sib)
    for swap in swaps:
        swap.wait_send()
    up_swap.start()
    grads.s2(at.near(n - 1))
    grads.s3(at.near(n - 2))
    up_swap.wait_recv()
    grad_up(0, True)
    keep = pltpu.make_async_copy(wup.at[0], gup_ref, load_sem.at[0])
    keep.start()
    grads.s3(at.near(n - 1))
    for j in range(n + 3):
        if j < n - 1:
            grads.line(at.far(j))
        if j < n:
            output(at.far(j))
            outs.s1(at.far(j))
        if 0 <= j - 1 < n:
            outs.s2(at.far(j - 1))
        if 0 <= j - 2 < n:
            outs.s3(at.far(j - 2))
            if j - 2 < n - 1:
                outs.line(at.far(j - 2))
        if j == n - 1:
            pl.semaphore_signal(free.at[1], inc=1, device_id=at.sib, device_id_type=MESH)
            grad_down(1)
            pl.semaphore_wait(free.at[1], 1)
            down_swap = send(wdown.at[1], wdown.at[0], core_ss.at[3], core_sr.at[3], at.sib)
            down_swap.start()
        if j == n:
            down_swap.wait_recv()
            grad_down(0)
    grads.last()
    outs.last()
    keep.wait()
    up_swap.wait_send()
    down_swap.wait_send()
    gather.finish()
    grads.finish()
    outs.finish()


def expert_layer(x, cot_all, up, down, pick, place, middle, n, cid):
    rows, wide = x.shape
    f2 = up.shape[1]
    f = f2 // 2
    bf16 = jnp.bfloat16
    V = lambda *s: pltpu.VMEM(s, bf16)
    D_ = pltpu.SemaphoreType.DMA
    any_, vm = pl.BlockSpec(memory_space=pl.ANY), pl.BlockSpec(memory_space=pltpu.VMEM)
    return pl.pallas_call(
        functools.partial(expert_kernel, n),
        out_shape=(
            jax.ShapeDtypeStruct((rows, D), jnp.float32),
            jax.ShapeDtypeStruct((rows, wide), jnp.float32),
            jax.ShapeDtypeStruct((D, f2), bf16),
            jax.ShapeDtypeStruct((f, D), jnp.float32),
        ),
        in_specs=[any_, any_, any_, any_, vm, vm, vm],
        out_specs=[vm, vm, any_, vm],
        scratch_shapes=[V(n, 4, rows, wide), V(n, 4, rows, D), V(n, 4, rows, 2 * f2), V(n, 4, rows, 2 * f), V(n, 4, rows, wide),
                        V(2, D, f2), V(2, f, D)]
        + gather_sems(n) + reduce_scratch(n, rows, wide) + reduce_scratch(n, rows, D)
        + [D_((4,)), D_((4,)), D_((4,)), pltpu.SemaphoreType.REGULAR((2,))],
        compiler_params=pltpu.CompilerParams(collective_id=cid, has_side_effects=True, vmem_limit_bytes=63 << 20),
        name="expert_layer",
    )(x, cot_all, up, down, pick, place, middle)


class GatherAll:
    def __init__(self, at, own, buf, send_sem, recv_z, recv_x, recv_y, recv_d, recv_s):
        self.at, self.own, self.buf = at, own, buf
        self.ss, self.rz, self.rx, self.ry, self.rd, self.rs = send_sem, recv_z, recv_x, recv_y, recv_d, recv_s
        cols = own.shape[1]
        half = (cols // 128 + 1) // 2 * 128
        self.A, self.B, self.F = pl.ds(0, half), pl.ds(half, cols - half), pl.ds(0, cols)

    def move(self, zz, e, cols, slot, sem, dev, own=False):
        dst = self.buf.at[zz * 8 + e, :, cols]
        return send(self.own.at[:, cols] if own else dst, dst, self.ss.at[zz, slot], sem, dev)

    def down(self, zz, own=False):
        return self.move(zz, self.at.e, self.F, 0, self.rz.at[zz], self.at.below, own)

    def up(self, zz, own=False):
        return self.move(zz, self.at.e, self.F, 1, self.rz.at[zz], self.at.above, own)

    def spread(self, zz, own=False):
        at = self.at
        return (self.move(zz, at.e, self.F, 2, self.rx.at[zz], at.nx, own),
                self.move(zz, at.e, self.F, 3, self.ry.at[zz], at.ny, own),
                self.move(zz, at.e, self.F, 4, self.rs.at[zz, 0], at.sib, own))

    def from_x(self, zz):
        at = self.at
        ex = at.nx[1]
        return (self.move(zz, ex, self.F, 2, self.rx.at[zz], at.nx),
                self.move(zz, ex, self.A, 5, self.rd.at[zz, 0], at.ny),
                self.move(zz, ex, self.F, 6, self.rs.at[zz, 1], at.sib))

    def from_y(self, zz):
        at = self.at
        ey = at.ny[1]
        return (self.move(zz, ey, self.F, 3, self.ry.at[zz], at.ny),
                self.move(zz, ey, self.B, 7, self.rd.at[zz, 1], at.nx),
                self.move(zz, ey, self.F, 8, self.rs.at[zz, 2], at.sib))

    def turned(self, zz):
        at = self.at
        return (self.move(zz, at.diag, self.A, 5, self.rd.at[zz, 0], at.ny),
                self.move(zz, at.diag, self.A, 9, self.rs.at[zz, 3], at.sib),
                self.move(zz, at.diag, self.B, 7, self.rd.at[zz, 1], at.nx),
                self.move(zz, at.diag, self.B, 10, self.rs.at[zz, 4], at.sib))

    def begin(self):
        d = self.at.d

        @pl.when(self.at.has_below)
        def _():
            self.down(d, True).start()

        @pl.when(self.at.has_above)
        def _():
            self.up(d, True).start()

        for copy in self.spread(d, True):
            copy.start()

    def column(self, zz):
        d = self.at.d

        @pl.when(zz < d)
        def _():
            self.up(zz).wait_recv()

            @pl.when(self.at.has_above)
            def _():
                self.up(zz).start()

        @pl.when(zz > d)
        def _():
            self.down(zz).wait_recv()

            @pl.when(self.at.has_below)
            def _():
                self.down(zz).start()

        for copy in self.spread(zz):
            copy.start()

    def plane(self, zz):
        for arrive, turn, share in (self.from_x(zz), self.from_y(zz)):
            arrive.wait_recv()
            turn.start()
            share.start()

    def corner(self, zz):
        a, share_a, b, share_b = self.turned(zz)
        a.wait_recv()
        share_a.start()
        b.wait_recv()
        share_b.start()

    def siblings(self):
        at = self.at
        es = at.sib[1]
        exs, eys, exys = es + at.nx[1] - at.e, es + at.ny[1] - at.e, es + at.diag - at.e

        @pl.loop(0, at.n)
        def _(zz):
            for e, cols, k in ((es, self.F, 0), (exs, self.F, 1), (eys, self.F, 2), (exys, self.A, 3), (exys, self.B, 4)):
                self.move(zz, e, cols, 4, self.rs.at[zz, k], at.sib).wait_recv()

    def finish(self):
        d = self.at.d

        @pl.loop(0, self.at.n)
        def _(zz):
            for group in (self.spread(zz), self.from_x(zz)[1:], self.from_y(zz)[1:], self.turned(zz)[1::2]):
                for copy in group:
                    copy.wait_send()

            @pl.when((d > 0) & (zz >= d))
            def _():
                self.down(zz).wait_send()

            @pl.when(self.at.has_above & (zz <= d))
            def _():
                self.up(zz).wait_send()


def lane_tile(rows):
    return lax.broadcasted_iota(jnp.int32, (rows, 128), 1)


def swap_halves(tile):
    front = lax.rem(lane_tile(tile.shape[0]), HEAD) < HEAD // 2
    return jnp.where(front, pltpu.roll(tile, 128 - HEAD // 2, 1), pltpu.roll(tile, HEAD // 2, 1))


def inverse_rms(v):
    return lax.rsqrt(jnp.mean(v * v, axis=1, keepdims=True) + norm_eps)


def forward_kernel(n, experts, tok_ref, cot_ref, dense_ref, ein_ref, cos_ref, sin_ref, allowed_ref, chosen_ref,
                   w_all, cot_all, up_all, disp_ref, mid_ref, gates_ref, gain_ref, nf_ref, q_ref, k_ref, v_ref, p_ref, mixed_ref,
                   wv, *rest):
    f32, bf16 = jnp.float32, jnp.bfloat16
    at = Place(n)
    d = at.d
    dense = GatherAll(at, dense_ref, wv, *rest[:6])
    cot = Gather(at, cot_ref, cot_all, *rest[6:11])
    load_sem, part_sem, a2a_ss, a2a_sr = rest[11:]
    q_width, k_width = HEADS * HEAD, KV_HEADS * HEAD
    groups = HEADS // KV_HEADS
    held, share = ein_ref.shape[:2]
    f = FF // n
    loads = [
        pltpu.make_async_copy(dense_ref, wv.at[d * 8 + at.e], load_sem.at[0]),
        pltpu.make_async_copy(cot_ref, cot_all.at[d, 0], load_sem.at[1]),
    ]
    for load in loads:
        load.start()

    def piece(j, to):
        src = ein_ref.at[j // 2, :, pl.ds(pl.multiple_of((j % 2) * FF + to * f, 128), f)]
        dst = up_all.at[pl.ds(pl.multiple_of(d * share, share), share), pl.ds(j * f, f)]
        return src, dst

    own_pieces = [pltpu.make_async_copy(*piece(j, d), part_sem.at[j]) for j in range(2 * held)]

    def exchange(k, j):
        to = lax.rem(d + k, n)
        src, dst = piece(j, to)
        return send(src, dst, a2a_ss.at[k, j], a2a_sr.at[d, j], (to, at.e))

    at.meet(True)
    dense.begin()
    for i in range(1, n):
        dense.column(at.near(i))
        if i == n - 1:
            cot.begin_z()
        dense.plane(at.near(i - 1))
        if i >= 2:
            dense.corner(at.near(i - 2))
    cot.begin_xy()
    dense.plane(at.near(n - 1))
    if n > 1:
        dense.corner(at.near(n - 2))
        cot.column_z(at.near(1))
    dense.corner(at.near(n - 1))
    for i in range(2, n):
        cot.column_z(at.near(i))
    for piece_copy in own_pieces:
        piece_copy.start()
    for k in range(1, n):
        for j in range(2 * held):
            exchange(k, j).start()
    for load in loads:
        load.wait()
    dense.siblings()
    keep = pltpu.make_async_copy(wv, w_all, load_sem.at[0])
    keep.start()

    def weight(lo, width):
        return wv[:, :, lo : lo + width].reshape(D, width)

    tail_at = q_width + 2 * k_width + D
    turned = jnp.transpose(weight(tail_at, 128).astype(f32))
    gain_ref[0:1, :] = turned[experts : experts + 1, :]
    gain_ref[1:2, :] = turned[experts + 1 : experts + 2, :]
    x = tok_ref[...].astype(f32)
    nf_ref[...] = (x * inverse_rms(x) * gain_ref[0:1, :]).astype(bf16)
    cos, sin = cos_ref[...], sin_ref[...]
    for q in range((q_width + 2 * k_width) // 512):
        lo = q * 512
        part = mm(nf_ref[...], weight(lo, 512))
        for t in range(4):
            tile = part[:, t * 128 : (t + 1) * 128]
            col = lo + t * 128
            if col < q_width + k_width:
                tile = tile * cos + swap_halves(tile) * sin
            ref, base = (q_ref, 0) if col < q_width else (k_ref, q_width) if col < q_width + k_width else (v_ref, q_width + k_width)
            ref[:, col - base : col - base + 128] = tile.astype(bf16)
    cot.plane(at.near(0))
    if n > 1:
        cot.column_xy(at.near(1))
    allowed = jnp.concatenate([allowed_ref[...]] * groups, axis=0) > 0
    for g in range(KV_HEADS):
        qs = jnp.concatenate([q_ref[:, (g * groups + j) * HEAD : (g * groups + j + 1) * HEAD] for j in range(groups)], axis=0)
        ks, vs = k_ref[:, g * HEAD : (g + 1) * HEAD], v_ref[:, g * HEAD : (g + 1) * HEAD]
        scores = jnp.where(allowed, mm(qs, ks, NT) * HEAD ** (-0.5), neg_large)
        raised = jnp.exp(scores - jnp.max(scores, axis=1, keepdims=True))
        probs = raised / jnp.sum(raised, axis=1, keepdims=True)
        p_ref[g] = probs
        out = mm(probs.astype(bf16), vs).astype(bf16)
        rows = out.shape[0] // groups
        for j in range(groups):
            mixed_ref[:, (g * groups + j) * HEAD : (g * groups + j + 1) * HEAD] = out[j * rows : (j + 1) * rows]
    for q in range(D // 512):
        lo = q * 512
        mid_ref[:, lo : lo + 512] = tok_ref[:, lo : lo + 512].astype(f32) + mm(mixed_ref[...], weight(q_width + 2 * k_width + lo, 512))
    mid = mid_ref[...]
    disp_ref[:, :D] = (mid * inverse_rms(mid) * gain_ref[1:2, :]).astype(bf16)
    logits = mm(disp_ref[:, :D], weight(tail_at, 128))
    chosen = chosen_ref[...]
    masked = jnp.where(chosen > 0, logits, neg_large)
    raised = jnp.where(chosen > 0, jnp.exp(masked - jnp.max(masked, axis=1, keepdims=True)), 0.0)
    gates = raised / jnp.sum(raised, axis=1, keepdims=True)
    gates_ref[...] = gates
    high = gates.astype(bf16).astype(f32)
    low = (gates - high).astype(bf16).astype(f32)
    disp_ref[:, D:] = (high + pltpu.roll(low, experts, 1)).astype(bf16)

    for i in range(1, n):
        cot.plane(at.near(i))
        if i + 1 < n:
            cot.column_xy(at.near(i + 1))
        cot.corner(at.near(i - 1))
    cot.corner(at.near(n - 1))
    for piece_copy in own_pieces:
        piece_copy.wait()
    for k in range(1, n):
        source = lax.rem(d + k, n)
        for j in range(2 * held):
            exchange(k, j).wait_send()
            src, _ = piece(j, d)
            dst = up_all.at[pl.ds(pl.multiple_of(source * share, share), share), pl.ds(j * f, f)]
            send(src, dst, a2a_ss.at[k, j], a2a_sr.at[source, j], (source, at.e)).wait_recv()
    keep.wait()
    dense.finish()
    cot.finish()


def forward_layer(tok, cot, dense, ein, cos, sin, allowed, chosen, n, experts, cid):
    f32, bf16 = jnp.float32, jnp.bfloat16
    rows = tok.shape[0]
    shard, wide = dense.shape
    held, share = ein.shape[:2]
    q_width, k_width = HEADS * HEAD, KV_HEADS * HEAD
    groups = HEADS // KV_HEADS
    D_ = pltpu.SemaphoreType.DMA
    any_, vm = pl.BlockSpec(memory_space=pl.ANY), pl.BlockSpec(memory_space=pltpu.VMEM)
    S = jax.ShapeDtypeStruct
    return pl.pallas_call(
        functools.partial(forward_kernel, n, experts),
        out_shape=(
            S((n * 8, shard, wide), bf16), S((n, 4, rows, D), bf16), S((D, 2 * held * (FF // n)), bf16),
            S((rows, D + 128), bf16), S((rows, D), f32), S((rows, 128), f32), S((8, D), f32), S((rows, D), bf16),
            S((rows, q_width), bf16), S((rows, k_width), bf16), S((rows, k_width), bf16),
            S((KV_HEADS, groups * rows, rows), f32), S((rows, q_width), bf16),
        ),
        in_specs=[vm, any_, any_, any_, vm, vm, vm, vm],
        out_specs=[any_] * 3 + [vm] * 10,
        scratch_shapes=[pltpu.VMEM((n * 8, shard, wide), bf16)]
        + [D_((n, 11)), D_((n,)), D_((n,)), D_((n,)), D_((n, 2)), D_((n, 5))] + gather_sems(n)
        + [D_((2,)), D_((2 * held,)), D_((n, 2 * held)), D_((n, 2 * held))],
        compiler_params=pltpu.CompilerParams(collective_id=cid, has_side_effects=True, vmem_limit_bytes=60 << 20),
        name="forward_layer",
    )(tok, cot, dense, ein, cos, sin, allowed, chosen)


def backward_kernel(n, experts, gs_ref, tok_ref, cot_ref, mid_ref, gates_ref, gain_ref, nf_ref, disp_ref, q_ref, k_ref, v_ref, p_ref,
                    mixed_ref, cos_ref, sin_ref, w_ref, gup_ref,
                    gtok_ref, gout_ref, gin_ref, gtail_ref, gup_out,
                    wv, pout, pin, tot_out, tot_in, arrived, pair, gq, gl, sums, gb, gm, flat, *rest):
    f32, bf16 = jnp.float32, jnp.bfloat16
    at = Place(n)
    d, c = at.d, at.c
    outs = Reduce(at, pout, tot_out, *rest[:9])
    ins = Reduce(at, pin, tot_in, *rest[9:18])
    load_sem, pair_ss, pair_sr, a2a_ss, a2a_sr, end_ss, end_sr = rest[18:]
    q_width, k_width = HEADS * HEAD, KV_HEADS * HEAD
    groups = HEADS // KV_HEADS
    qkv_width = q_width + 2 * k_width
    tail_at = qkv_width + D
    rows = tok_ref.shape[0]
    shard = w_ref.shape[1]
    share = D // n
    f = FF // n
    loads = []
    for i, (lo, width) in enumerate(((tail_at, 128), (qkv_width, D), (0, qkv_width))):
        loads.append(pltpu.make_async_copy(w_ref.at[:, :, pl.ds(lo, width)], wv.at[:, :, pl.ds(lo, width)], load_sem.at[i]))
    for load in loads:
        load.start()
    own_share = pltpu.make_async_copy(gup_ref.at[pl.ds(pl.multiple_of(d * share, share), share), :], arrived.at[d], load_sem.at[3])
    own_share.start()

    def exchange(k):
        to = lax.rem(d + k, n)
        return send(gup_ref.at[pl.ds(pl.multiple_of(to * share, share), share), :], arrived.at[d], a2a_ss.at[k], a2a_sr.at[d], (to, at.e))

    swaps = [send(src, pair.at[i], pair_ss.at[i], pair_sr.at[i], at.sib)
             for i, src in enumerate((mixed_ref, nf_ref, disp_ref.at[:, pl.ds(0, D)], gb))]
    swap_q = send(gq.at[0], gq.at[1], pair_ss.at[4], pair_sr.at[4], at.sib)
    swap_l = send(gl.at[0], gl.at[1], pair_ss.at[5], pair_sr.at[5], at.sib)
    swap_s = send(sums.at[0], sums.at[1], pair_ss.at[6], pair_sr.at[6], at.sib)
    at.meet(True)
    for i in range(3):
        swaps[i].start()

    def weight(lo, width):
        return wv[:, :, lo : lo + width].reshape(D, width)

    loads[0].wait()
    mid = mid_ref[...]
    inv_second = inverse_rms(mid)
    unit = mid * inv_second
    gates, gg = gates_ref[...], gs_ref[:, D:]
    gl[0] = (gates * (gg - jnp.sum(gates * gg, axis=1, keepdims=True))).astype(bf16)
    swap_l.start()
    grad_second = mm(gl[0], weight(tail_at, 128), NT) + gs_ref[:, :D]
    pull = grad_second * gain_ref[1:2, :]
    sums[0, 1:2, :] = jnp.sum(grad_second * unit, axis=0, keepdims=True)
    grad_middle = cot_ref[...].astype(f32) + inv_second * (pull - unit * jnp.mean(pull * unit, axis=1, keepdims=True))
    gtok_ref[...] = grad_middle
    gb[...] = grad_middle.astype(bf16)
    swaps[3].start()
    loads[1].wait()
    for q in range(q_width // 512):
        gm[:, q * 512 : (q + 1) * 512] = mm(gb[...], wv[:, :, qkv_width : qkv_width + D].reshape(D, D)[q * 512 : (q + 1) * 512], NT).astype(bf16)

    def both(own, other, cols):
        return jnp.concatenate([own[:, cols], other[:, cols]], axis=0)

    def store(buf, zz, lo, value):
        blocks = value.astype(bf16).reshape(4, 2 * shard, value.shape[1])
        for a in range(4):
            slot = 2 * lax.rem(a // 2 + at.y, 2) + lax.rem(a % 2 + at.x, 2)
            buf[zz, slot, :, lo : lo + value.shape[1]] = blocks[a]

    def row_cols(zz):
        return pl.ds(pl.multiple_of(zz * share, 128), share)

    half_out, half_in = D // 2, qkv_width // 2
    swaps[0].wait_recv()
    swaps[3].wait_recv()

    @pl.loop(0, n)
    def _(j):
        zz = at.far(j)
        branch = both(gb, pair.at[3], pl.ds(pl.multiple_of(c * half_out, 128), half_out))
        store(pout, zz, 0, mm(both(mixed_ref, pair.at[0], row_cols(zz)), branch, TN))
        outs.s1(zz)

    for k in range(1, n):
        exchange(k).start()
    scale = HEAD ** (-0.5)
    for g in range(KV_HEADS):
        heads = [slice((g * groups + j) * HEAD, (g * groups + j + 1) * HEAD) for j in range(groups)]
        kv = slice(g * HEAD, (g + 1) * HEAD)
        qs = jnp.concatenate([q_ref[:, h] for h in heads], axis=0)
        ms = jnp.concatenate([gm[:, h] for h in heads], axis=0)
        ks, vs = k_ref[:, kv], v_ref[:, kv]
        probs = p_ref[g]
        grad_values = mm(probs.astype(bf16), ms, TN)
        grad_probs = mm(ms, vs, NT)
        grad_scores = (probs * (grad_probs - jnp.sum(probs * grad_probs, axis=1, keepdims=True))).astype(bf16)
        grad_query = mm(grad_scores, ks) * scale
        for j, h in enumerate(heads):
            flat[:, h] = grad_query[j * rows : (j + 1) * rows]
        flat[:, q_width + kv.start : q_width + kv.stop] = mm(grad_scores, qs, TN) * scale
        flat[:, q_width + k_width + kv.start : q_width + k_width + kv.stop] = grad_values
    cos, sin = cos_ref[...], sin_ref[...]
    for t in range(qkv_width // 128):
        tile = flat[:, t * 128 : (t + 1) * 128]
        if t * 128 < q_width + k_width:
            tile = tile * cos - swap_halves(tile) * sin
        gq[0, :, t * 128 : (t + 1) * 128] = tile.astype(bf16)
    swap_q.start()
    loads[2].wait()
    x = tok_ref[...].astype(f32)
    inv_first = inverse_rms(x)
    unit = x * inv_first
    grad_first = jnp.concatenate(
        [mm(gq[0], wv[8 * i : 8 * (i + 1), :, :qkv_width].reshape(8 * shard, qkv_width), NT) for i in range(n)], axis=1)
    pull = grad_first * gain_ref[0:1, :]
    sums[0, 0:1, :] = jnp.sum(grad_first * unit, axis=0, keepdims=True)
    sums[0, 2:, :] = jnp.zeros((6, D), f32)
    swap_s.start()
    gtok_ref[...] += inv_first * (pull - unit * jnp.mean(pull * unit, axis=1, keepdims=True))
    for i in (1, 2):
        swaps[i].wait_recv()
    swap_l.wait_recv()
    swap_q.wait_recv()
    swap_s.wait_recv()
    gains = sums[0] + sums[1]
    high = gains.astype(bf16)
    low = (gains - high.astype(f32)).astype(bf16)
    swap_s.wait_send()
    sums[0] = high.astype(f32)
    sums[1] = low.astype(f32)
    line = lax.rem(lax.broadcasted_iota(jnp.int32, (16, 128), 0), 8)
    where = (((line == 0) & (lane_tile(16) == experts)) | ((line == 1) & (lane_tile(16) == experts + 1))).astype(bf16)

    @pl.loop(0, n)
    def _(j):
        zz = at.far(j)
        cols = row_cols(zz)
        normed = both(nf_ref, pair.at[1], cols)
        for q in range(2):
            part = pl.ds(pl.multiple_of(c * half_in + q * (half_in // 2), 128), half_in // 2)
            grad = jnp.concatenate([gq[0, :, part], gq[1, :, part]], axis=0)
            store(pin, zz, q * (half_in // 2), mm(normed, grad, TN))
        tail = mm(both(disp_ref, pair.at[2], cols), jnp.concatenate([gl[0], gl[1]], axis=0), TN)
        rows_now = jnp.concatenate([sums[0, :, cols], sums[1, :, cols]], axis=0).astype(bf16)
        store(pin, zz, half_in, tail + mm(rows_now, where, TN))
        ins.s1(zz)

        outs.s2(zz)

    for j in range(n + 1):
        if j < n:
            outs.s3(at.far(j))
            if j < n - 1:
                outs.line(at.far(j))
            ins.s2(at.far(j))
        if j >= 1:
            ins.s3(at.far(j - 1))
            if j - 1 < n - 1:
                ins.line(at.far(j - 1))
    outs.last()
    mine, theirs = pl.ds(pl.multiple_of(c * shard, 8), shard), pl.ds(pl.multiple_of((1 - c) * shard, 8), shard)
    cols_out, cols_in = pl.ds(pl.multiple_of(c * half_out, 128), half_out), pl.ds(pl.multiple_of(c * half_in, 128), half_in)
    end_out = send(tot_out.at[theirs, :], gout_ref.at[:, cols_out], end_ss.at[0], end_sr.at[0], at.sib)
    end_out.start()
    gout_ref[:, cols_out] = tot_out[mine, :]
    ins.last()
    end_in = send(tot_in.at[theirs, pl.ds(0, half_in)], gin_ref.at[:, cols_in], end_ss.at[1], end_sr.at[1], at.sib)
    end_in.start()
    gin_ref[:, cols_in] = tot_in[mine, :half_in]
    gtail_ref[...] = tot_in[mine, half_in:]
    own_share.wait()
    for k in range(1, n):
        exchange(k).wait_send()
        source = lax.rem(d + k, n)
        send(gup_ref.at[pl.ds(0, share), :], arrived.at[source], a2a_ss.at[k], a2a_sr.at[source], (source, at.e)).wait_recv()

    @pl.loop(0, share // 32)
    def _(r):
        w = pl.ds(pl.multiple_of(r * 32, 32), 32)
        for q in range(n):
            for j in range(arrived.shape[2] // f):
                lo = (j % 2) * FF + q * f
                gup_out[j // 2, w, lo : lo + f] = arrived[q, w, j * f : (j + 1) * f].astype(f32)

    end_out.wait()
    end_in.wait()
    for swap in swaps + [swap_q, swap_l]:
        swap.wait_send()
    outs.finish()
    ins.finish()


def backward_layer(gs, tok, cot, mid, gates, gain, nf, disp, q, k, v, p, mixed, cos, sin, w_all, gup, held, n, experts, cid):
    f32, bf16 = jnp.float32, jnp.bfloat16
    rows = tok.shape[0]
    shard, wide = w_all.shape[1:]
    qkv_width = (HEADS + 2 * KV_HEADS) * HEAD
    share = D // n
    D_ = pltpu.SemaphoreType.DMA
    V = lambda *s: pltpu.VMEM(s, bf16)
    W = lambda *s: pltpu.VMEM(s, f32)
    any_, vm = pl.BlockSpec(memory_space=pl.ANY), pl.BlockSpec(memory_space=pltpu.VMEM)
    S = jax.ShapeDtypeStruct
    width_out, width_in = D // 2, qkv_width // 2 + 128
    return pl.pallas_call(
        functools.partial(backward_kernel, n, experts),
        out_shape=(S((rows, D), f32), S((shard, D), f32), S((shard, qkv_width), f32), S((shard, 128), f32), S((held, share, 2 * FF), f32)),
        in_specs=[vm] * 15 + [any_, any_],
        out_specs=[vm] * 5,
        scratch_shapes=[V(n * 8, shard, wide), V(n, 4, 2 * shard, width_out), V(n, 4, 2 * shard, width_in),
                        W(2 * shard, width_out), W(2 * shard, width_in), V(n, share, gup.shape[1]),
                        V(4, rows, D), V(2, rows, qkv_width), V(2, rows, 128), W(2, 8, D), V(rows, D), V(rows, D), W(rows, qkv_width)]
        + reduce_scratch(n, 2 * shard, width_out) + reduce_scratch(n, 2 * shard, width_in)
        + [D_((4,)), D_((7,)), D_((7,)), D_((n,)), D_((n,)), D_((2,)), D_((2,))],
        compiler_params=pltpu.CompilerParams(collective_id=cid, has_side_effects=True, vmem_limit_bytes=62 << 20),
        name="backward_layer",
    )(gs, tok, cot, mid, gates, gain, nf, disp, q, k, v, p, mixed, cos, sin, w_all, gup)


def per_device_fast(n, tokens, segments, routes, cotangent, gain_attn, attn_in, attn_out, gain_ffn, router, expert_in, expert_out):
    f32, bf16 = jnp.float32, jnp.bfloat16
    micro, rows = tokens.shape[:2]
    total = micro * rows
    held = expert_in.shape[0]
    experts = held * 8
    f = FF // n
    shard = attn_in.shape[0]
    x = tokens.reshape(total, D)
    cot = cotangent.reshape(total, D)
    tail = jnp.concatenate([router, gain_attn[:, None], gain_ffn[:, None], jnp.zeros((shard, 126 - experts), bf16)], axis=1)
    dense = jnp.concatenate([attn_in, attn_out, tail], axis=1)

    segment = (segments[:, 0, :] + 2 * rows * jnp.arange(micro, dtype=jnp.int32)[:, None]).reshape(total)
    cosine, sine_table, causal = rope_tables(segment, HEAD // 2)
    cos = jnp.tile(cosine, (1, 128 * 2 // HEAD))
    sin = jnp.tile(jnp.concatenate([-sine_table, sine_table], axis=1), (1, 128 // HEAD))
    route = routes.reshape(total, TOP_K)
    chosen = jnp.any(route[:, :, None] == jnp.arange(128, dtype=jnp.int32)[None, None, :], axis=1).astype(f32)
    w_all, cot_all, up, disp, middle, gates, gain, nf, q, k, v, p, mixed = forward_layer(
        x, cot, dense, expert_in, cos, sin, causal.astype(f32), chosen, n, experts, 0)

    mine = lax.axis_index("expert")
    order = jnp.stack([mine, mine + 1 - 2 * lax.rem(mine, 2)])
    owner = (order[:, None] * held + jnp.arange(held, dtype=jnp.int32)[None, :]).reshape(-1)
    owner = jnp.repeat(owner, f)[None, :]
    lane = jnp.arange(128, dtype=jnp.int32)[:, None]
    pick = ((lane == owner) | (lane == owner + experts)).astype(bf16)
    place = (lane == owner).astype(bf16).T
    out, grad_sum, grad_up, grad_down = expert_layer(
        disp, cot_all, up, expert_out.reshape(held * f, D), pick, place, middle, n, 1)
    grad_tokens, grad_out, grad_in, grad_tail, grad_up = backward_layer(
        grad_sum, x, cot, middle, gates, gain, nf, disp, q, k, v, p, mixed, cos, sin, w_all, grad_up, held, n, experts, 2)
    return (
        out.astype(bf16).reshape(micro, rows, D),
        grad_tokens.reshape(micro, rows, D),
        grad_tail[:, experts],
        grad_in,
        grad_out,
        grad_tail[:, experts + 1],
        grad_tail[:, :experts],
        grad_up,
        grad_down.reshape(held, f, D),
    )


def solution(mesh):
    placed = (
        P(None, ("dp", "expert"), None),
        P(None, ("dp", "expert"), None),
        P(None, ("dp", "expert"), None),
        P(None, ("dp", "expert"), None),
        P(("dp", "expert")),
        P(("dp", "expert"), None),
        P(("dp", "expert"), None),
        P(("dp", "expert")),
        P(("dp", "expert"), None),
        P("expert", "dp", None),
        P("expert", "dp", None),
    )
    fast = mesh.shape["expert"] == 8 and FF // mesh.shape["dp"] == 128
    body = functools.partial(per_device_fast, mesh.shape["dp"]) if fast else per_device
    return jax.shard_map(
        body,
        mesh=mesh,
        in_specs=placed,
        out_specs=(
            P(None, ("dp", "expert"), None),
            P(None, ("dp", "expert"), None),
            P(("dp", "expert")),
            P(("dp", "expert"), None),
            P(("dp", "expert"), None),
            P(("dp", "expert")),
            P(("dp", "expert"), None),
            P("expert", "dp", None),
            P("expert", "dp", None),
        ),
        check_vma=False,
    )
```

```python
import functools

import jax
import jax.numpy as jnp
from jax import lax
from jax.experimental import pallas as pl
from jax.experimental.pallas import tpu as pltpu
from jax.sharding import PartitionSpec as P

MESH = pl.DeviceIdType.MESH

D = 1536
HEADS = 24
KV_HEADS = 8
HEAD = 64
FF = 512
TOP_K = 8


norm_eps = 1e-06
rope_base = 10000.0
neg_large = -1e30
highest = lax.Precision.HIGHEST


def rope_tables(segment, half_width):
    row_count = segment.shape[0]
    places = jnp.arange(row_count, dtype=jnp.int32)
    same_seq = segment[:, None] == segment[None, :]
    seq_start = jnp.min(jnp.where(same_seq, places[None, :], row_count), axis=1)
    offset = (places - seq_start).astype(jnp.float32)
    frequencies = rope_base ** (-jnp.arange(half_width, dtype=jnp.float32) / half_width)
    angles = offset[:, None] * frequencies[None, :]
    causal = same_seq & (places[None, :] <= places[:, None])
    return (jnp.cos(angles), jnp.sin(angles), causal)


def rotate(operand, cosine, sine_table):
    half_width = operand.shape[-1] // 2
    front_part = operand[..., :half_width]
    back_part = operand[..., half_width:]
    return jnp.concatenate(
        [
            front_part * cosine - back_part * sine_table,
            back_part * cosine + front_part * sine_table,
        ],
        axis=-1,
    )


def unrotate(gradient, cosine, sine_table):
    half_width = gradient.shape[-1] // 2
    front_part = gradient[..., :half_width]
    back_part = gradient[..., half_width:]
    return jnp.concatenate(
        [
            front_part * cosine + back_part * sine_table,
            back_part * cosine - front_part * sine_table,
        ],
        axis=-1,
    )


def slot_targets(route_now, expert_count, capacity):
    flat_ids = route_now.reshape(-1)
    onehot = (flat_ids[:, None] == jnp.arange(expert_count, dtype=jnp.int32)[None, :]).astype(
        jnp.int32
    )
    earlier = jnp.cumsum(onehot, axis=0) - onehot
    slot_index = jnp.sum(earlier * onehot, axis=1)
    return flat_ids * capacity + slot_index


def dense_fetch(gain_attn, attn_in, attn_out, gain_ffn, router):
    return (
        lax.all_gather(gain_attn, ("dp", "expert"), axis=0, tiled=True),
        lax.all_gather(attn_in, ("dp", "expert"), axis=0, tiled=True),
        lax.all_gather(attn_out, ("dp", "expert"), axis=0, tiled=True),
        lax.all_gather(gain_ffn, ("dp", "expert"), axis=0, tiled=True),
        lax.all_gather(router, ("dp", "expert"), axis=0, tiled=True),
    )


def expert_fetch(expert_in, expert_out):
    return (
        lax.all_gather(expert_in, "dp", axis=1, tiled=True),
        lax.all_gather(expert_out, "dp", axis=1, tiled=True),
    )


def dense_reduce(grad_set):
    return (
        lax.psum_scatter(grad_set[0], ("dp", "expert"), scatter_dimension=0, tiled=True),
        lax.psum_scatter(grad_set[1], ("dp", "expert"), scatter_dimension=0, tiled=True),
        lax.psum_scatter(grad_set[2], ("dp", "expert"), scatter_dimension=0, tiled=True),
        lax.psum_scatter(grad_set[3], ("dp", "expert"), scatter_dimension=0, tiled=True),
        lax.psum_scatter(grad_set[4], ("dp", "expert"), scatter_dimension=0, tiled=True),
    )


def expert_reduce(grad_set):
    return (
        lax.psum_scatter(grad_set[0], "dp", scatter_dimension=1, tiled=True),
        lax.psum_scatter(grad_set[1], "dp", scatter_dimension=1, tiled=True),
    )


def attention_scores(queries, key_rot, causal):
    score_scale = HEAD ** (-0.5)
    scores = (
        jnp.einsum("tkgh,skh->kgts", queries, key_rot, preferred_element_type=jnp.float32)
        * score_scale
    )
    return jnp.where(causal[None, None], scores, neg_large)


def forward_micro(tokens_now, segment, route_now, dense_set, expert_set, shapes):
    expert_count, capacity, group_count, local_experts = shapes
    gain_attn, qkv_weight, out_weight, gain_ffn, router_weight = dense_set
    expert_up, expert_down = expert_set
    row_count = tokens_now.shape[0]
    groups = HEADS // KV_HEADS
    q_width = HEADS * HEAD
    k_width = KV_HEADS * HEAD
    inputs = tokens_now.astype(jnp.float32)
    inv_first = lax.rsqrt(jnp.mean(inputs * inputs, axis=1, keepdims=True) + norm_eps)
    normed_first = (inputs * inv_first * gain_attn.astype(jnp.float32)).astype(jnp.bfloat16)
    qkv_full = jnp.dot(normed_first, qkv_weight, preferred_element_type=jnp.float32)
    cosine, sine_table, causal = rope_tables(segment, HEAD // 2)
    queries = rotate(
        qkv_full[:, :q_width].reshape(row_count, KV_HEADS, groups, HEAD),
        cosine[:, None, None, :],
        sine_table[:, None, None, :],
    ).astype(jnp.bfloat16)
    key_rot = rotate(
        qkv_full[:, q_width : q_width + k_width].reshape(row_count, KV_HEADS, HEAD),
        cosine[:, None, :],
        sine_table[:, None, :],
    ).astype(jnp.bfloat16)
    values = (
        qkv_full[:, q_width + k_width :].reshape(row_count, KV_HEADS, HEAD).astype(jnp.bfloat16)
    )
    scores = attention_scores(queries, key_rot, causal)
    score_peak = jnp.max(scores, axis=-1, keepdims=True)
    exp_scores = jnp.exp(scores - score_peak)
    exp_total = jnp.sum(exp_scores, axis=-1, keepdims=True)
    log_total = score_peak + jnp.log(exp_total)
    soft_probs = (exp_scores / exp_total).astype(jnp.bfloat16)
    attn_mixed = jnp.einsum(
        "kgts,skh->tkgh", soft_probs, values, preferred_element_type=jnp.float32
    )
    attn_mixed = attn_mixed.reshape(row_count, q_width).astype(jnp.bfloat16)
    middle = inputs + jnp.dot(attn_mixed, out_weight, preferred_element_type=jnp.float32)
    inv_second = lax.rsqrt(jnp.mean(middle * middle, axis=1, keepdims=True) + norm_eps)
    normed_second = (middle * inv_second * gain_ffn.astype(jnp.float32)).astype(jnp.bfloat16)
    logits = jnp.dot(normed_second, router_weight, preferred_element_type=jnp.float32)
    chosen = (
        route_now[:, :, None] == jnp.arange(expert_count, dtype=jnp.int32)[None, None, :]
    ).astype(jnp.float32)
    picked_logits = jnp.sum(chosen * logits[:, None, :], axis=-1)
    gate_values = jax.nn.softmax(picked_logits, axis=-1)
    targets = slot_targets(route_now, expert_count, capacity)
    source_rows = jnp.repeat(normed_second, TOP_K, axis=0)
    buffer = jnp.zeros((expert_count * capacity, D), jnp.bfloat16).at[targets].set(source_rows)
    send_rows = buffer.reshape(group_count, local_experts, capacity, D)
    received = lax.all_to_all(send_rows, "expert", split_axis=0, concat_axis=0, tiled=True)
    gate_up = jnp.einsum("secd,edf->secf", received, expert_up, preferred_element_type=jnp.float32)
    hidden = (jax.nn.silu(gate_up[..., :FF]) * gate_up[..., FF:]).astype(jnp.bfloat16)
    expert_result = jnp.einsum(
        "secf,efd->secd", hidden, expert_down, preferred_element_type=jnp.float32
    ).astype(jnp.bfloat16)
    returned = lax.all_to_all(expert_result, "expert", split_axis=0, concat_axis=0, tiled=True)
    picked = returned.reshape(expert_count * capacity, D)[targets].reshape(row_count, TOP_K, D)
    moe_sum = jnp.einsum(
        "tk,tkd->td", gate_values, picked, precision=highest, preferred_element_type=jnp.float32
    )
    result = (middle + moe_sum).astype(jnp.bfloat16)
    saved_state = (
        inputs,
        inv_first,
        normed_first,
        queries,
        key_rot,
        values,
        log_total,
        causal,
        cosine,
        sine_table,
        attn_mixed,
        middle,
        inv_second,
        normed_second,
        chosen,
        gate_values,
        targets,
        received,
        gate_up,
        hidden,
        picked,
    )
    return (result, saved_state)


def backward_micro(saved_state, cotan_now, dense_set, expert_set, shapes):
    expert_count, capacity, group_count, local_experts = shapes
    (
        inputs,
        inv_first,
        normed_first,
        queries,
        key_rot,
        values,
        log_total,
        causal,
        cosine,
        sine_table,
        attn_mixed,
        middle,
        inv_second,
        normed_second,
        chosen,
        gate_values,
        targets,
        received,
        gate_up,
        hidden,
        picked,
    ) = saved_state
    gain_attn, qkv_weight, out_weight, gain_ffn, router_weight = dense_set
    expert_up, expert_down = expert_set
    row_count = inputs.shape[0]
    groups = HEADS // KV_HEADS
    q_width = HEADS * HEAD
    k_width = KV_HEADS * HEAD
    score_scale = HEAD ** (-0.5)
    upstream = cotan_now.astype(jnp.float32)
    grad_gates = jnp.einsum(
        "td,tkd->tk", upstream, picked, precision=highest, preferred_element_type=jnp.float32
    )
    grad_picked = gate_values * (
        grad_gates - jnp.sum(gate_values * grad_gates, axis=-1, keepdims=True)
    )
    grad_logits = jnp.sum(chosen * grad_picked[:, :, None], axis=1).astype(jnp.bfloat16)
    grad_router = jnp.einsum(
        "td,te->de", normed_second, grad_logits, preferred_element_type=jnp.float32
    )
    grad_second = jnp.einsum(
        "te,de->td", grad_logits, router_weight, preferred_element_type=jnp.float32
    )
    grad_slots = (
        (gate_values[:, :, None] * upstream[:, None, :])
        .astype(jnp.bfloat16)
        .reshape(row_count * TOP_K, D)
    )
    grad_buffer = jnp.zeros((expert_count * capacity, D), jnp.bfloat16).at[targets].set(grad_slots)
    grad_buffer = grad_buffer.reshape(group_count, local_experts, capacity, D)
    grad_result = lax.all_to_all(grad_buffer, "expert", split_axis=0, concat_axis=0, tiled=True)
    grad_hidden = jnp.einsum(
        "secd,efd->secf", grad_result, expert_down, preferred_element_type=jnp.float32
    )
    grad_down = jnp.einsum(
        "secf,secd->efd", hidden, grad_result, preferred_element_type=jnp.float32
    )
    gate_part = gate_up[..., :FF]
    up_part = gate_up[..., FF:]
    gate_sigmoid = jax.nn.sigmoid(gate_part)
    grad_gate = grad_hidden * up_part * gate_sigmoid * (1.0 + gate_part * (1.0 - gate_sigmoid))
    grad_up_part = grad_hidden * (gate_part * gate_sigmoid)
    grad_gate_up = jnp.concatenate([grad_gate, grad_up_part], axis=-1).astype(jnp.bfloat16)
    grad_up = jnp.einsum(
        "secd,secf->edf", received, grad_gate_up, preferred_element_type=jnp.float32
    )
    grad_rows = jnp.einsum(
        "secf,edf->secd", grad_gate_up, expert_up, preferred_element_type=jnp.float32
    ).astype(jnp.bfloat16)
    grad_back = lax.all_to_all(grad_rows, "expert", split_axis=0, concat_axis=0, tiled=True)
    grad_choice = grad_back.reshape(expert_count * capacity, D)[targets].reshape(
        row_count, TOP_K, D
    )
    grad_second = grad_second + jnp.sum(grad_choice, axis=1, dtype=jnp.float32)
    unit_second = middle * inv_second
    pull_second = grad_second * gain_ffn.astype(jnp.float32)
    grad_gain_ffn = jnp.sum(grad_second * unit_second, axis=0)
    grad_middle = upstream + inv_second * (
        pull_second - unit_second * jnp.mean(pull_second * unit_second, axis=1, keepdims=True)
    )
    grad_branch = grad_middle.astype(jnp.bfloat16)
    grad_out_weight = jnp.einsum(
        "tc,td->cd", attn_mixed, grad_branch, preferred_element_type=jnp.float32
    )
    grad_mixed = jnp.einsum(
        "td,cd->tc", grad_branch, out_weight, preferred_element_type=jnp.float32
    )
    grad_mixed = grad_mixed.astype(jnp.bfloat16).reshape(row_count, KV_HEADS, groups, HEAD)
    scores = attention_scores(queries, key_rot, causal)
    soft_probs = jnp.exp(scores - log_total)
    grad_values = jnp.einsum(
        "kgts,tkgh->skh",
        soft_probs.astype(jnp.bfloat16),
        grad_mixed,
        preferred_element_type=jnp.float32,
    )
    grad_probs = jnp.einsum(
        "tkgh,skh->kgts", grad_mixed, values, preferred_element_type=jnp.float32
    )
    grad_scores = soft_probs * (
        grad_probs - jnp.sum(soft_probs * grad_probs, axis=-1, keepdims=True)
    )
    grad_scores = grad_scores.astype(jnp.bfloat16)
    grad_query = (
        jnp.einsum("kgts,skh->tkgh", grad_scores, key_rot, preferred_element_type=jnp.float32)
        * score_scale
    )
    grad_key = (
        jnp.einsum("kgts,tkgh->skh", grad_scores, queries, preferred_element_type=jnp.float32)
        * score_scale
    )
    grad_query = unrotate(grad_query, cosine[:, None, None, :], sine_table[:, None, None, :])
    grad_key = unrotate(grad_key, cosine[:, None, :], sine_table[:, None, :])
    grad_qkv = jnp.concatenate(
        [
            grad_query.reshape(row_count, q_width),
            grad_key.reshape(row_count, k_width),
            grad_values.reshape(row_count, k_width),
        ],
        axis=1,
    ).astype(jnp.bfloat16)
    grad_qkv_weight = jnp.einsum(
        "tc,tq->cq", normed_first, grad_qkv, preferred_element_type=jnp.float32
    )
    grad_first = jnp.einsum("tq,cq->tc", grad_qkv, qkv_weight, preferred_element_type=jnp.float32)
    unit_first = inputs * inv_first
    pull_first = grad_first * gain_attn.astype(jnp.float32)
    grad_gain_attn = jnp.sum(grad_first * unit_first, axis=0)
    grad_inputs = grad_middle + inv_first * (
        pull_first - unit_first * jnp.mean(pull_first * unit_first, axis=1, keepdims=True)
    )
    dense_grads = (grad_gain_attn, grad_qkv_weight, grad_out_weight, grad_gain_ffn, grad_router)
    expert_grads = (grad_up, grad_down)
    return (grad_inputs, dense_grads, expert_grads)


def add_pair(left_part, right_part):
    return left_part + right_part


def per_device(
    tokens,
    segments,
    routes,
    cotangent,
    gain_attn,
    attn_in,
    attn_out,
    gain_ffn,
    router,
    expert_in,
    expert_out,
):
    local_experts = expert_in.shape[0]
    group_count = lax.axis_size("expert")
    expert_count = local_experts * group_count
    micro_count = tokens.shape[0]
    row_count = tokens.shape[1]
    capacity = (row_count * TOP_K * 5 // (4 * expert_count) + 7) // 8 * 8
    shapes = (expert_count, capacity, group_count, local_experts)
    outputs = []
    grad_list = []
    dense_total = None
    expert_total = None
    for micro_index in range(micro_count):
        dense_set = dense_fetch(gain_attn, attn_in, attn_out, gain_ffn, router)
        expert_set = expert_fetch(expert_in, expert_out)
        result, saved_state = forward_micro(
            tokens[micro_index],
            segments[micro_index, 0],
            routes[micro_index],
            dense_set,
            expert_set,
            shapes,
        )
        dense_set = dense_fetch(gain_attn, attn_in, attn_out, gain_ffn, router)
        expert_set = expert_fetch(expert_in, expert_out)
        grad_inputs, dense_grads, expert_grads = backward_micro(
            saved_state, cotangent[micro_index], dense_set, expert_set, shapes
        )
        dense_grads = dense_reduce(dense_grads)
        expert_grads = expert_reduce(expert_grads)
        if dense_total is None:
            dense_total = dense_grads
            expert_total = expert_grads
        else:
            dense_total = jax.tree.map(add_pair, dense_total, dense_grads)
            expert_total = jax.tree.map(add_pair, expert_total, expert_grads)
        outputs.append(result)
        grad_list.append(grad_inputs)
    return (
        jnp.stack(outputs, axis=0),
        jnp.stack(grad_list, axis=0),
        dense_total[0],
        dense_total[1],
        dense_total[2],
        dense_total[3],
        dense_total[4],
        expert_total[0],
        expert_total[1],
    )


NN = (((1,), (0,)), ((), ()))
NT = (((1,), (1,)), ((), ()))
TN = (((0,), (0,)), ((), ()))


def mm(a, b, dims=NN):
    return lax.dot_general(a, b, dims, preferred_element_type=jnp.float32)


class Place:
    def __init__(self, n):
        self.n = n
        d = self.d = lax.axis_index("dp")
        e = self.e = lax.axis_index("expert")
        c, x, y = lax.rem(e, 2), lax.rem(lax.div(e, 2), 2), lax.div(e, 4)
        self.sib = (d, e + 1 - 2 * c)
        self.nx = (d, e + 2 - 4 * x)
        self.ny = (d, e + 4 - 8 * y)
        self.diag = self.nx[1] + 4 - 8 * y
        self.c, self.x, self.y = c, x, y
        self.below = (d - 1, e)
        self.above = (d + 1, e)
        self.has_below = d > 0
        self.has_above = d < n - 1

    def meet(self, everyone=False):
        barrier = pltpu.get_barrier_semaphore()
        d, n = self.d, self.n
        if everyone:
            others = n - 1 + 3

            @pl.loop(1, n)
            def _(k):
                pl.semaphore_signal(barrier, inc=1, device_id=(lax.rem(d + k, n), self.e), device_id_type=MESH)
        else:
            others = 3 + jnp.minimum(d, 1) + jnp.minimum(n - 1 - d, 1)

            @pl.when(self.has_below)
            def _():
                pl.semaphore_signal(barrier, inc=1, device_id=self.below, device_id_type=MESH)

            @pl.when(self.has_above)
            def _():
                pl.semaphore_signal(barrier, inc=1, device_id=self.above, device_id_type=MESH)

        for dev in (self.sib, self.nx, self.ny):
            pl.semaphore_signal(barrier, inc=1, device_id=dev, device_id_type=MESH)
        pl.semaphore_wait(barrier, others)

    def far(self, i):
        n, d = self.n, self.d
        low = d < n - d
        m = jnp.where(low, d, n - 1 - d)
        t = jnp.where(i < n - 1 - m, n - 1 - i, jnp.where(i < n - 1, i - (n - 1 - m), m))
        return jnp.where(low, t, n - 1 - t)

    def near(self, i):
        return self.far(self.n - 1 - i)


def send(src, dst, ss, rs, dev):
    return pltpu.make_async_remote_copy(src, dst, ss, rs, device_id=dev, device_id_type=MESH)


class Gather:
    def __init__(self, at, own, buf, send_sem, recv_z, recv_x, recv_y, recv_d):
        self.at, self.own, self.buf = at, own, buf
        self.ss, self.rz, self.rx, self.ry, self.rd = send_sem, recv_z, recv_x, recv_y, recv_d
        rows = own.shape[0]
        self.A, self.B = pl.ds(0, rows // 2), pl.ds(rows // 2, rows // 2)

    def source(self, zz, own):
        return self.own if own else self.buf.at[zz, 0]

    def down(self, zz, own=False):
        return send(self.source(zz, own), self.buf.at[zz, 0], self.ss.at[zz, 0], self.rz.at[zz], self.at.below)

    def up(self, zz, own=False):
        return send(self.source(zz, own), self.buf.at[zz, 0], self.ss.at[zz, 1], self.rz.at[zz], self.at.above)

    def to_x(self, zz, own=False):
        return send(self.source(zz, own), self.buf.at[zz, 1], self.ss.at[zz, 2], self.rx.at[zz], self.at.nx)

    def to_y(self, zz, own=False):
        return send(self.source(zz, own), self.buf.at[zz, 2], self.ss.at[zz, 3], self.ry.at[zz], self.at.ny)

    def turn_y(self, zz):
        return send(self.buf.at[zz, 1, self.A], self.buf.at[zz, 3, self.A], self.ss.at[zz, 4], self.rd.at[zz, 0], self.at.ny)

    def turn_x(self, zz):
        return send(self.buf.at[zz, 2, self.B], self.buf.at[zz, 3, self.B], self.ss.at[zz, 5], self.rd.at[zz, 1], self.at.nx)

    def begin(self):
        self.begin_z()
        self.begin_xy()

    def begin_z(self):
        d = self.at.d

        @pl.when(self.at.has_below)
        def _():
            self.down(d, True).start()

        @pl.when(self.at.has_above)
        def _():
            self.up(d, True).start()

    def begin_xy(self):
        self.to_x(self.at.d, True).start()
        self.to_y(self.at.d, True).start()

    def column_z(self, zz):
        d = self.at.d

        @pl.when(zz < d)
        def _():
            self.up(zz).wait_recv()

            @pl.when(self.at.has_above)
            def _():
                self.up(zz).start()

        @pl.when(zz > d)
        def _():
            self.down(zz).wait_recv()

            @pl.when(self.at.has_below)
            def _():
                self.down(zz).start()

    def column_xy(self, zz):
        self.to_x(zz).start()
        self.to_y(zz).start()

    def column(self, zz):
        self.column_z(zz)
        self.column_xy(zz)

    def plane(self, zz):
        self.to_x(zz).wait_recv()
        self.turn_y(zz).start()
        self.to_y(zz).wait_recv()
        self.turn_x(zz).start()

    def corner(self, zz):
        self.turn_y(zz).wait_recv()
        self.turn_x(zz).wait_recv()

    def finish(self):
        d = self.at.d

        @pl.loop(0, self.at.n)
        def _(zz):
            for copy in (self.to_x, self.to_y, self.turn_y, self.turn_x):
                copy(zz).wait_send()

            @pl.when((d > 0) & (zz >= d))
            def _():
                self.down(zz).wait_send()

            @pl.when(self.at.has_above & (zz <= d))
            def _():
                self.up(zz).wait_send()


def gather_sems(n):
    D_ = pltpu.SemaphoreType.DMA
    return [D_((n, 6)), D_((n,)), D_((n,)), D_((n,)), D_((n, 2))]


def add_rows(dst, src):
    rows = dst.shape[0]
    step = 16

    @pl.loop(0, rows // step)
    def _(r):
        w = pl.ds(pl.multiple_of(r * step, step), step)
        dst[w, :] = (dst[w, :].astype(jnp.float32) + src[w, :].astype(jnp.float32)).astype(dst.dtype)


class Reduce:
    def __init__(self, at, buf, total, r1, r2, rz, ss_1, sr_1, ss_2, sr_2, ss_z, sr_z, start=None):
        self.start = start
        self.at, self.buf, self.total = at, buf, total
        self.r1, self.r2, self.rz = r1, r2, rz
        self.sems = (ss_1, sr_1, ss_2, sr_2, ss_z, sr_z)
        rows = total.shape[0]
        self.A, self.B = pl.ds(0, rows // 2), pl.ds(rows // 2, rows // 2)

    def first(self, zz, k):
        ss, sr = self.sems[0], self.sems[1]
        slot, part, dev = ((3, self.A, self.at.nx), (3, self.B, self.at.ny), (1, self.A, self.at.nx), (2, self.B, self.at.ny))[k]
        return send(self.buf.at[zz, slot, part], self.r1.at[zz, k], ss.at[zz, k], sr.at[zz, k], dev)

    def second(self, zz, k):
        ss, sr = self.sems[2], self.sems[3]
        slot, part, dev = ((2, self.A, self.at.ny), (1, self.B, self.at.nx))[k]
        return send(self.buf.at[zz, slot, part], self.r2.at[zz, k], ss.at[zz, k], sr.at[zz, k], dev)

    def down(self, zz):
        return send(self.buf.at[zz, 0], self.rz.at[zz], self.sems[4].at[zz], self.sems[5].at[zz], self.at.below)

    def up(self, zz):
        slot = jnp.where(zz == self.at.d + 1, self.at.n, zz)
        return send(self.buf.at[zz, 0], self.rz.at[slot], self.sems[4].at[zz], self.sems[5].at[slot], self.at.above)

    def arrive(self, slot):
        return send(self.buf.at[0, 0], self.rz.at[slot], self.sems[4].at[0], self.sems[5].at[slot], self.at.nx)

    def s1(self, zz):
        self.corners(zz)
        self.sides(zz)

    def corners(self, zz):
        self.first(zz, 0).start()
        self.first(zz, 1).start()

    def sides(self, zz):
        self.first(zz, 2).start()
        self.first(zz, 3).start()

    def turn(self, zz):
        self.first(zz, 0).wait_recv()
        add_rows(self.buf.at[zz, 2, self.A], self.r1.at[zz, 0])
        self.second(zz, 0).start()
        self.first(zz, 1).wait_recv()
        add_rows(self.buf.at[zz, 1, self.B], self.r1.at[zz, 1])
        self.second(zz, 1).start()

    def take_sides(self, zz):
        self.first(zz, 2).wait_recv()
        add_rows(self.buf.at[zz, 0, self.A], self.r1.at[zz, 2])
        self.first(zz, 3).wait_recv()
        add_rows(self.buf.at[zz, 0, self.B], self.r1.at[zz, 3])

    def s2(self, zz):
        self.turn(zz)
        self.take_sides(zz)

    def step(self, j):
        at = self.at
        if j < at.n:
            self.turn(at.far(j))
            self.sides(at.far(j))
            if j + 2 < at.n:
                self.corners(at.far(j + 2))
        if j >= 1:
            self.take_sides(at.far(j - 1))
            self.s3(at.far(j - 1))
            self.lines(j - 1)

    def s3(self, zz):
        self.second(zz, 0).wait_recv()
        add_rows(self.buf.at[zz, 0, self.A], self.r2.at[zz, 0])
        self.second(zz, 1).wait_recv()
        add_rows(self.buf.at[zz, 0, self.B], self.r2.at[zz, 1])

    def push(self, zz):
        d = self.at.d

        @pl.when(zz < d)
        def _():
            self.down(zz).start()

        @pl.when(zz > d)
        def _():
            self.up(zz).start()

    def line_head(self, zz):
        @pl.when(jnp.logical_not(self.passes(zz)))
        def _():
            self.push(zz)

    def passes(self, zz):
        d = self.at.d
        return ((zz < d) & self.at.has_above) | ((zz > d) & self.at.has_below)

    def line_rest(self, zz):
        @pl.when(self.passes(zz))
        def _():
            self.arrive(zz).wait_recv()
            add_rows(self.buf.at[zz, 0], self.rz.at[zz])
            self.push(zz)

    def lines(self, j):
        n = self.at.n
        if j < n - 1:
            self.line_head(self.at.far(j))
        if 0 <= j - 1 < n - 2:
            self.line_rest(self.at.far(j - 1))
        if j == n - 2:
            self.line_rest(self.at.far(j))

    def last(self):
        d, n, rows, step = self.at.d, self.at.n, self.total.shape[0], 16

        def over(fn):
            @pl.loop(0, rows // step)
            def _(r):
                fn(pl.ds(pl.multiple_of(r * step, step), step))

        def own(w):
            first = self.buf[d, 0, w, :].astype(jnp.float32)
            self.total[w, :] = first if self.start is None else first + self.start[w, :]

        def more(slot):
            def fn(w):
                self.total[w, :] += self.rz[slot, w, :].astype(jnp.float32)

            self.arrive(slot).wait_recv()
            over(fn)

        over(own)

        @pl.when(self.at.has_above)
        def _():
            more(d)

        @pl.when(self.at.has_below)
        def _():
            more(n)

    def finish(self):
        d = self.at.d

        @pl.loop(0, self.at.n)
        def _(zz):
            for k in range(4):
                self.first(zz, k).wait_send()
            for k in range(2):
                self.second(zz, k).wait_send()

            @pl.when(zz != d)
            def _():
                self.arrive(zz)
                send(self.buf.at[zz, 0], self.rz.at[zz], self.sems[4].at[zz], self.sems[5].at[zz], self.at.nx).wait_send()


def reduce_scratch(n, rows, cols):
    D_ = pltpu.SemaphoreType.DMA
    V = lambda *s: pltpu.VMEM(s, jnp.bfloat16)
    return [V(n, 4, rows // 2, cols), V(n, 2, rows // 2, cols), V(n + 1, rows, cols),
            D_((n, 4)), D_((n, 4)), D_((n, 2)), D_((n, 2)), D_((n,)), D_((n + 1,))]


def expert_kernel(n, experts, x_ref, cot_ref, up_ref, down_ref, mid_ref,
                  out_ref, gx_ref, gup_ref, gdown_ref,
                  xb, cb, gg, mixed, gb, wup, wdown, pick_ref, place_ref, *rest):
    f32, bf16 = jnp.float32, jnp.bfloat16
    at = Place(n)
    d = at.d
    gather = Gather(at, x_ref, xb, *rest[:5])
    grads = Reduce(at, gb, gx_ref, *rest[5:14])
    outs = Reduce(at, gg, out_ref, *rest[14:23], start=mid_ref)
    load_sem, core_ss, core_sr, free = rest[23:]
    rows = x_ref.shape[0]
    f2 = up_ref.shape[1]
    f = f2 // 2
    held = f // 128
    loads = [
        pltpu.make_async_copy(x_ref, xb.at[d, 0], load_sem.at[0]),
        pltpu.make_async_copy(up_ref, wup.at[0], load_sem.at[1]),
        pltpu.make_async_copy(down_ref, wdown.at[0], load_sem.at[2]),
        pltpu.make_async_copy(cot_ref, cb, load_sem.at[3]),
    ]
    for load in loads:
        load.start()
    at.meet()
    gather.begin()
    swaps = [
        send(up_ref, wup.at[1], core_ss.at[0], core_sr.at[0], at.sib),
        send(down_ref, wdown.at[1], core_ss.at[1], core_sr.at[1], at.sib),
    ]
    for swap in swaps:
        swap.start()
    for h, owner in ((0, at.e), (1, at.sib[1])):
        for j in range(held):
            expert, cols = owner * held + j, slice((h * held + j) * 128, (h * held + j + 1) * 128)
            gate_row = lax.broadcasted_iota(jnp.int32, (128, 128), 0)
            pick_ref[:, cols] = ((gate_row == expert) | (gate_row == expert + experts)).astype(bf16)
            place_ref[cols, :] = (lane_tile(128) == expert).astype(bf16)
    gather.plane(at.near(0))
    gather.column(at.near(1))
    for load in loads:
        load.wait()
    for swap in swaps:
        swap.wait_recv()

    def tokens(ref, zz, p, lo, width):
        return ref[zz, pl.ds(2 * p, 2), :, pl.ds(lo, width)].reshape(2 * rows, width)

    def half(zz, p):
        pair = pl.ds(2 * p, 2)
        x = tokens(xb, zz, p, 0, D)
        cot = tokens(cb, zz, p, 0, D)
        mix = mm(tokens(xb, zz, p, D, 128), pick_ref[...])
        sums = jnp.zeros((2 * rows, 128), f32)
        for h in range(2):
            gate_up = mm(x, wup[h])
            back = mm(cot, wdown[h], NT)
            for j in range(held):
                k = h * held + j
                gate = gate_up[:, j * 256 : j * 256 + 128]
                up = gate_up[:, j * 256 + 128 : j * 256 + 256]
                b = back[:, j * 128 : (j + 1) * 128]
                m = mix[:, k * 128 : (k + 1) * 128]
                sig = 1.0 / (1.0 + jnp.exp(-gate))
                act = gate * sig
                hidden = (act * up).astype(bf16).astype(f32)
                prod = hidden * b
                high = prod.astype(bf16)
                low = (prod - high.astype(f32)).astype(bf16)
                sel = place_ref[k * 128 : (k + 1) * 128, :]
                sums += mm(high, sel) + mm(low, sel)
                mixed[zz, pair, :, pl.ds(k * 128, 128)] = (m * hidden).astype(bf16).reshape(2, rows, 128)
                gh = m * b
                gg[zz, pair, :, pl.ds(k * 256, 128)] = (
                    (gh * up * sig * (1.0 + gate * (1.0 - sig))).astype(bf16).reshape(2, rows, 128))
                gg[zz, pair, :, pl.ds(k * 256 + 128, 128)] = (gh * act).astype(bf16).reshape(2, rows, 128)
        for q in range(D // 512):
            cols = pl.ds(q * 512, 512)
            part = mm(tokens(gg, zz, p, 0, f2), wup[0, cols, :], NT) + mm(tokens(gg, zz, p, f2, f2), wup[1, cols, :], NT)
            gb[zz, pair, :, cols] = part.astype(bf16).reshape(2, rows, 512)
        gb[zz, pair, :, pl.ds(D, 128)] = sums.astype(bf16).reshape(2, rows, 128)

    @pl.loop(0, n)
    def _(i):
        zz = at.near(i)
        half(zz, 0)

        @pl.when(i + 2 < n)
        def _():
            gather.column(at.near(i + 2))

        @pl.when(i + 1 < n)
        def _():
            gather.plane(at.near(i + 1))

        gather.corner(zz)
        half(zz, 1)
        grads.s1(zz)

        @pl.when(i >= 1)
        def _():
            grads.s2(at.near(i - 1))

        @pl.when(i >= 2)
        def _():
            grads.s3(at.near(i - 2))
            grads.line_head(at.near(i - 2))

    pl.semaphore_signal(free.at[0], inc=1, device_id=at.sib, device_id_type=MESH)

    def grad_up(h, more):
        @pl.loop(0, D // 256)
        def _(q):
            cols = pl.ds(pl.multiple_of(q * 256, 256), 256)
            xs = xb[:, :, :, cols].reshape(n * 4 * rows, 256)
            part = mm(xs, gg[:, :, :, pl.ds(h * f2, f2)].reshape(n * 4 * rows, f2), TN)
            if more:
                part += wup[h, cols, :].astype(f32)
            wup[h, cols, :] = part.astype(bf16)

    def grad_down(h):
        for q in range(D // 512):
            cols = pl.ds(q * 512, 512)
            part = mm(mixed[:, :, :, pl.ds(h * f, f)].reshape(n * 4 * rows, f), cb[:, :, :, cols].reshape(n * 4 * rows, 512), TN)
            if h == 0:
                gdown_ref[:, cols] = part + wdown[0, :, cols].astype(f32)
            else:
                wdown[1, :, cols] = part.astype(bf16)

    def output(zz):
        @pl.loop(0, 2)
        def _(p):
            for q in range(D // 512):
                cols = pl.ds(q * 512, 512)
                part = mm(tokens(mixed, zz, p, 0, f), wdown[0, :, cols]) + mm(tokens(mixed, zz, p, f, f), wdown[1, :, cols])
                gg[zz, pl.ds(2 * p, 2), :, cols] = part.astype(bf16).reshape(2, rows, 512)

    grad_up(1, False)
    pl.semaphore_wait(free.at[0], 1)
    up_swap = send(wup.at[1], wup.at[0], core_ss.at[2], core_sr.at[2], at.sib)
    for swap in swaps:
        swap.wait_send()
    up_swap.start()
    grads.s2(at.near(n - 1))
    grads.s3(at.near(n - 2))
    grads.line_head(at.near(n - 2))
    up_swap.wait_recv()
    grad_up(0, True)
    keep = pltpu.make_async_copy(wup.at[0], gup_ref, load_sem.at[0])
    keep.start()
    grads.s3(at.near(n - 1))
    grads.line_head(at.near(n - 1))
    for j in range(n):
        output(at.far(j))
        if j < 2:
            outs.corners(at.far(j))
    pl.semaphore_signal(free.at[1], inc=1, device_id=at.sib, device_id_type=MESH)
    grad_down(1)
    pl.semaphore_wait(free.at[1], 1)
    down_swap = send(wdown.at[1], wdown.at[0], core_ss.at[3], core_sr.at[3], at.sib)
    down_swap.start()
    for j in range(n + 1):
        outs.step(j)
        if j < n - 1:
            grads.line_rest(at.far(j))
    down_swap.wait_recv()
    grad_down(0)
    grads.last()
    outs.last()
    keep.wait()
    up_swap.wait_send()
    down_swap.wait_send()
    gather.finish()
    grads.finish()
    outs.finish()


def expert_layer(x, cot_all, up, down, middle, n, experts, cid):
    rows, wide = x.shape
    f2 = up.shape[1]
    f = f2 // 2
    bf16 = jnp.bfloat16
    V = lambda *s: pltpu.VMEM(s, bf16)
    D_ = pltpu.SemaphoreType.DMA
    any_, vm = pl.BlockSpec(memory_space=pl.ANY), pl.BlockSpec(memory_space=pltpu.VMEM)
    return pl.pallas_call(
        functools.partial(expert_kernel, n, experts),
        out_shape=(
            jax.ShapeDtypeStruct((rows, D), jnp.float32),
            jax.ShapeDtypeStruct((rows, wide), jnp.float32),
            jax.ShapeDtypeStruct((D, f2), bf16),
            jax.ShapeDtypeStruct((f, D), jnp.float32),
        ),
        in_specs=[any_, any_, any_, any_, vm],
        out_specs=[vm, vm, any_, vm],
        scratch_shapes=[V(n, 4, rows, wide), V(n, 4, rows, D), V(n, 4, rows, 2 * f2), V(n, 4, rows, 2 * f), V(n, 4, rows, wide),
                        V(2, D, f2), V(2, f, D), V(128, 2 * f), V(2 * f, 128)]
        + gather_sems(n) + reduce_scratch(n, rows, wide) + reduce_scratch(n, rows, D)
        + [D_((4,)), D_((4,)), D_((4,)), pltpu.SemaphoreType.REGULAR((2,))],
        compiler_params=pltpu.CompilerParams(collective_id=cid, has_side_effects=True, vmem_limit_bytes=63 << 20),
        name="expert_layer",
    )(x, cot_all, up, down, middle)


class GatherAll:
    def __init__(self, at, own, buf, send_sem, recv_z, recv_x, recv_y, recv_d, recv_s):
        self.at, self.own, self.buf = at, own, buf
        self.ss, self.rz, self.rx, self.ry, self.rd, self.rs = send_sem, recv_z, recv_x, recv_y, recv_d, recv_s
        cols = own.shape[1]
        half = (cols // 128 + 1) // 2 * 128
        self.A, self.B, self.F = pl.ds(0, half), pl.ds(half, cols - half), pl.ds(0, cols)

    def move(self, zz, e, cols, slot, sem, dev, own=False):
        dst = self.buf.at[zz * 8 + e, :, cols]
        return send(self.own.at[:, cols] if own else dst, dst, self.ss.at[zz, slot], sem, dev)

    def down(self, zz, own=False):
        return self.move(zz, self.at.e, self.F, 0, self.rz.at[zz], self.at.below, own)

    def up(self, zz, own=False):
        return self.move(zz, self.at.e, self.F, 1, self.rz.at[zz], self.at.above, own)

    def spread(self, zz, own=False):
        at = self.at
        return (self.move(zz, at.e, self.F, 2, self.rx.at[zz], at.nx, own),
                self.move(zz, at.e, self.F, 3, self.ry.at[zz], at.ny, own),
                self.move(zz, at.e, self.F, 4, self.rs.at[zz, 0], at.sib, own))

    def from_x(self, zz):
        at = self.at
        ex = at.nx[1]
        return (self.move(zz, ex, self.F, 2, self.rx.at[zz], at.nx),
                self.move(zz, ex, self.A, 5, self.rd.at[zz, 0], at.ny),
                self.move(zz, ex, self.F, 6, self.rs.at[zz, 1], at.sib))

    def from_y(self, zz):
        at = self.at
        ey = at.ny[1]
        return (self.move(zz, ey, self.F, 3, self.ry.at[zz], at.ny),
                self.move(zz, ey, self.B, 7, self.rd.at[zz, 1], at.nx),
                self.move(zz, ey, self.F, 8, self.rs.at[zz, 2], at.sib))

    def turned(self, zz):
        at = self.at
        return (self.move(zz, at.diag, self.A, 5, self.rd.at[zz, 0], at.ny),
                self.move(zz, at.diag, self.A, 9, self.rs.at[zz, 3], at.sib),
                self.move(zz, at.diag, self.B, 7, self.rd.at[zz, 1], at.nx),
                self.move(zz, at.diag, self.B, 10, self.rs.at[zz, 4], at.sib))

    def begin(self):
        d = self.at.d

        @pl.when(self.at.has_below)
        def _():
            self.down(d, True).start()

        @pl.when(self.at.has_above)
        def _():
            self.up(d, True).start()

        for copy in self.spread(d, True):
            copy.start()

    def column(self, zz):
        d = self.at.d

        @pl.when(zz < d)
        def _():
            self.up(zz).wait_recv()

            @pl.when(self.at.has_above)
            def _():
                self.up(zz).start()

        @pl.when(zz > d)
        def _():
            self.down(zz).wait_recv()

            @pl.when(self.at.has_below)
            def _():
                self.down(zz).start()

        for copy in self.spread(zz):
            copy.start()

    def plane(self, zz):
        for arrive, turn, share in (self.from_x(zz), self.from_y(zz)):
            arrive.wait_recv()
            turn.start()
            share.start()

    def corner(self, zz):
        a, share_a, b, share_b = self.turned(zz)
        a.wait_recv()
        share_a.start()
        b.wait_recv()
        share_b.start()

    def siblings(self):
        at = self.at
        es = at.sib[1]
        exs, eys, exys = es + at.nx[1] - at.e, es + at.ny[1] - at.e, es + at.diag - at.e

        @pl.loop(0, at.n)
        def _(zz):
            for e, cols, k in ((es, self.F, 0), (exs, self.F, 1), (eys, self.F, 2), (exys, self.A, 3), (exys, self.B, 4)):
                self.move(zz, e, cols, 4, self.rs.at[zz, k], at.sib).wait_recv()

    def finish(self):
        d = self.at.d

        @pl.loop(0, self.at.n)
        def _(zz):
            for group in (self.spread(zz), self.from_x(zz)[1:], self.from_y(zz)[1:], self.turned(zz)[1::2]):
                for copy in group:
                    copy.wait_send()

            @pl.when((d > 0) & (zz >= d))
            def _():
                self.down(zz).wait_send()

            @pl.when(self.at.has_above & (zz <= d))
            def _():
                self.up(zz).wait_send()


def lane_tile(rows):
    return lax.broadcasted_iota(jnp.int32, (rows, 128), 1)


def swap_halves(tile):
    front = lax.rem(lane_tile(tile.shape[0]), HEAD) < HEAD // 2
    return jnp.where(front, pltpu.roll(tile, 128 - HEAD // 2, 1), pltpu.roll(tile, HEAD // 2, 1))


def inverse_rms(v):
    return lax.rsqrt(jnp.mean(v * v, axis=1, keepdims=True) + norm_eps)


def rope_lanes(seg_ref, freq_ref, cos_ref, sin_ref):
    f32 = jnp.float32
    packs, rows = seg_ref.shape[0], seg_ref.shape[2]
    row = jnp.concatenate([seg_ref[i].astype(f32) + float(2 * rows * i) for i in range(packs)], axis=1)
    total = packs * rows
    across = jnp.broadcast_to(row, (total, total))
    same = across == jnp.transpose(across)
    source = lax.broadcasted_iota(jnp.int32, (total, total), 1)
    target = lax.broadcasted_iota(jnp.int32, (total, total), 0)
    start = jnp.min(jnp.where(same, source.astype(f32), float(total)), axis=1, keepdims=True)
    angle = (target.astype(f32) - start) * freq_ref[...]
    cos_ref[...] = jnp.cos(angle)
    front = lax.rem(source, HEAD) < HEAD // 2
    sine = jnp.sin(angle)
    sin_ref[...] = jnp.where(front, -sine, sine)
    return (same & (source <= target)).astype(f32)


def forward_kernel(n, experts, tok_ref, cot_ref, qkv_ref, proj_ref, tail_ref, ein_ref, seg_ref, route_ref, freq_ref,
                   w_all, cot_all, up_all, disp_ref, mid_ref, gates_ref, gain_ref, nf_ref, q_ref, k_ref, v_ref, p_ref, mixed_ref, cos_ref, sin_ref,
                   wv, pieces, dense_ref, *rest):
    f32, bf16 = jnp.float32, jnp.bfloat16
    at = Place(n)
    d = at.d
    dense = GatherAll(at, dense_ref, wv, *rest[:6])
    cot = Gather(at, cot_ref, cot_all, *rest[6:11])
    load_sem, a2a_ss, a2a_sr = rest[11:]
    q_width, k_width = HEADS * HEAD, KV_HEADS * HEAD
    groups = HEADS // KV_HEADS
    held, share = ein_ref.shape[:2]
    f = FF // n
    qkv_width = q_width + 2 * k_width
    dense_ref[:, :qkv_width] = qkv_ref[...]
    dense_ref[:, qkv_width : qkv_width + D] = proj_ref[...]
    dense_ref[:, qkv_width + D :] = tail_ref[...]
    loads = [
        pltpu.make_async_copy(dense_ref, wv.at[d * 8 + at.e], load_sem.at[0]),
        pltpu.make_async_copy(cot_ref, cot_all.at[d, 0], load_sem.at[1]),
    ]
    for load in loads:
        load.start()

    def rows_of(z):
        return up_all.at[pl.ds(pl.multiple_of(z * share, share), share), :]

    own_piece = pltpu.make_async_copy(pieces.at[d], rows_of(d), load_sem.at[2])

    def exchange(k):
        to = lax.rem(d + k, n)
        return send(pieces.at[to], rows_of(d), a2a_ss.at[k], a2a_sr.at[d], (to, at.e))

    at.meet(True)
    dense.begin()
    for q in range(n):
        for j in range(2 * held):
            lo = (j % 2) * FF + q * f
            pieces[q, :, j * f : (j + 1) * f] = ein_ref[j // 2, :, lo : lo + f]
    own_piece.start()
    allowed = rope_lanes(seg_ref, freq_ref, cos_ref, sin_ref)
    for i in range(1, n):
        dense.column(at.near(i))
        if i == n - 1:
            cot.begin_z()
            for k in range(1, n):
                exchange(k).start()
        dense.plane(at.near(i - 1))
        if i >= 2:
            dense.corner(at.near(i - 2))
    cot.begin_xy()
    dense.plane(at.near(n - 1))
    if n > 1:
        dense.corner(at.near(n - 2))
        cot.column(at.near(1))
    dense.corner(at.near(n - 1))
    for i in range(2, n):
        cot.column(at.near(i))
    for load in loads:
        load.wait()
    dense.siblings()
    keep = pltpu.make_async_copy(wv, w_all, load_sem.at[0])
    keep.start()

    def weight(lo, width):
        return wv[:, :, lo : lo + width].reshape(D, width)

    tail_at = q_width + 2 * k_width + D
    turned = jnp.transpose(weight(tail_at, 128).astype(f32))
    gain_ref[0:1, :] = turned[experts : experts + 1, :]
    gain_ref[1:2, :] = turned[experts + 1 : experts + 2, :]
    x = tok_ref[...].astype(f32)
    nf_ref[...] = (x * inverse_rms(x) * gain_ref[0:1, :]).astype(bf16)
    cos, sin = cos_ref[...], sin_ref[...]
    for q in range((q_width + 2 * k_width) // 512):
        lo = q * 512
        part = mm(nf_ref[...], weight(lo, 512))
        for t in range(4):
            tile = part[:, t * 128 : (t + 1) * 128]
            col = lo + t * 128
            if col < q_width + k_width:
                tile = tile * cos + swap_halves(tile) * sin
            ref, base = (q_ref, 0) if col < q_width else (k_ref, q_width) if col < q_width + k_width else (v_ref, q_width + k_width)
            ref[:, col - base : col - base + 128] = tile.astype(bf16)
    cot.plane(at.near(0))
    allowed = jnp.concatenate([allowed] * groups, axis=0) > 0
    for g in range(KV_HEADS):
        qs = jnp.concatenate([q_ref[:, (g * groups + j) * HEAD : (g * groups + j + 1) * HEAD] for j in range(groups)], axis=0)
        ks, vs = k_ref[:, g * HEAD : (g + 1) * HEAD], v_ref[:, g * HEAD : (g + 1) * HEAD]
        scores = jnp.where(allowed, mm(qs, ks, NT) * HEAD ** (-0.5), neg_large)
        raised = jnp.exp(scores - jnp.max(scores, axis=1, keepdims=True))
        probs = raised / jnp.sum(raised, axis=1, keepdims=True)
        p_ref[g] = probs
        out = mm(probs.astype(bf16), vs).astype(bf16)
        rows = out.shape[0] // groups
        for j in range(groups):
            mixed_ref[:, (g * groups + j) * HEAD : (g * groups + j + 1) * HEAD] = out[j * rows : (j + 1) * rows]
    for q in range(D // 512):
        lo = q * 512
        mid_ref[:, lo : lo + 512] = tok_ref[:, lo : lo + 512].astype(f32) + mm(mixed_ref[...], weight(q_width + 2 * k_width + lo, 512))
    mid = mid_ref[...]
    disp_ref[:, :D] = (mid * inverse_rms(mid) * gain_ref[1:2, :]).astype(bf16)
    logits = mm(disp_ref[:, :D], weight(tail_at, 128))
    lanes = lane_tile(mid.shape[0])
    chosen = jnp.zeros(lanes.shape, f32)
    for k in range(TOP_K):
        chosen += (route_ref[:, k : k + 1] == lanes).astype(f32)
    masked = jnp.where(chosen > 0, logits, neg_large)
    raised = jnp.where(chosen > 0, jnp.exp(masked - jnp.max(masked, axis=1, keepdims=True)), 0.0)
    gates = raised / jnp.sum(raised, axis=1, keepdims=True)
    gates_ref[...] = gates
    high = gates.astype(bf16).astype(f32)
    low = (gates - high).astype(bf16).astype(f32)
    disp_ref[:, D:] = (high + pltpu.roll(low, experts, 1)).astype(bf16)

    for i in range(1, n):
        cot.plane(at.near(i))
        cot.corner(at.near(i - 1))
    cot.corner(at.near(n - 1))
    own_piece.wait()
    for k in range(1, n):
        exchange(k).wait_send()
        source = lax.rem(d + k, n)
        send(pieces.at[0], rows_of(source), a2a_ss.at[k], a2a_sr.at[source], (source, at.e)).wait_recv()
    keep.wait()
    dense.finish()
    cot.finish()


def forward_layer(tok, cot, attn_in, attn_out, tail, ein, segments, routes, n, experts, cid):
    f32, bf16 = jnp.float32, jnp.bfloat16
    rows = tok.shape[0]
    shard = attn_in.shape[0]
    held, share = ein.shape[:2]
    q_width, k_width = HEADS * HEAD, KV_HEADS * HEAD
    wide = q_width + 2 * k_width + D + 128
    groups = HEADS // KV_HEADS
    half = HEAD // 2
    freq = jnp.tile(rope_base ** (-jnp.arange(half, dtype=f32) / half), 128 // half)[None, :]
    D_ = pltpu.SemaphoreType.DMA
    V = lambda *s: pltpu.VMEM(s, bf16)
    any_, vm = pl.BlockSpec(memory_space=pl.ANY), pl.BlockSpec(memory_space=pltpu.VMEM)
    S = jax.ShapeDtypeStruct
    return pl.pallas_call(
        functools.partial(forward_kernel, n, experts),
        out_shape=(
            S((n * 8, shard, wide), bf16), S((n, 4, rows, D), bf16), S((D, 2 * held * (FF // n)), bf16),
            S((rows, D + 128), bf16), S((rows, D), f32), S((rows, 128), f32), S((8, D), f32), S((rows, D), bf16),
            S((rows, q_width), bf16), S((rows, k_width), bf16), S((rows, k_width), bf16),
            S((KV_HEADS, groups * rows, rows), f32), S((rows, q_width), bf16), S((rows, 128), f32), S((rows, 128), f32),
        ),
        in_specs=[vm, any_] + [vm] * 7,
        out_specs=[any_] * 3 + [vm] * 12,
        scratch_shapes=[V(n * 8, shard, wide), V(n, share, 2 * held * (FF // n)), V(shard, wide)]
        + [D_((n, 11)), D_((n,)), D_((n,)), D_((n,)), D_((n, 2)), D_((n, 5))] + gather_sems(n)
        + [D_((3,)), D_((n,)), D_((n,))],
        compiler_params=pltpu.CompilerParams(collective_id=cid, has_side_effects=True, vmem_limit_bytes=60 << 20),
        name="forward_layer",
    )(tok, cot, attn_in, attn_out, tail, ein, segments, routes, freq)


def backward_kernel(n, experts, gs_ref, tok_ref, cot_ref, mid_ref, gates_ref, gain_ref, nf_ref, disp_ref, q_ref, k_ref, v_ref, p_ref,
                    mixed_ref, cos_ref, sin_ref, w_ref, gup_ref,
                    gtok_ref, gout_ref, gin_ref, gtail_ref, arrived,
                    wv, pout, pin, tot_out, tot_in, pair, gq, gl, sums, gb, gm, flat, *rest):
    f32, bf16 = jnp.float32, jnp.bfloat16
    at = Place(n)
    d, c = at.d, at.c
    outs = Reduce(at, pout, tot_out, *rest[:9])
    ins = Reduce(at, pin, tot_in, *rest[9:18])
    load_sem, pair_ss, pair_sr, a2a_ss, a2a_sr, end_ss, end_sr = rest[18:]
    q_width, k_width = HEADS * HEAD, KV_HEADS * HEAD
    groups = HEADS // KV_HEADS
    qkv_width = q_width + 2 * k_width
    tail_at = qkv_width + D
    rows = tok_ref.shape[0]
    shard = w_ref.shape[1]
    share = D // n
    f = FF // n
    loads = []
    for i, (lo, width) in enumerate(((tail_at, 128), (qkv_width, D), (0, qkv_width))):
        loads.append(pltpu.make_async_copy(w_ref.at[:, :, pl.ds(lo, width)], wv.at[:, :, pl.ds(lo, width)], load_sem.at[i]))
    for load in loads:
        load.start()
    own_share = pltpu.make_async_copy(gup_ref.at[pl.ds(pl.multiple_of(d * share, share), share), :], arrived.at[d], load_sem.at[3])
    own_share.start()

    def exchange(k):
        to = lax.rem(d + k, n)
        return send(gup_ref.at[pl.ds(pl.multiple_of(to * share, share), share), :], arrived.at[d], a2a_ss.at[k], a2a_sr.at[d], (to, at.e))

    swaps = [send(src, pair.at[i], pair_ss.at[i], pair_sr.at[i], at.sib)
             for i, src in enumerate((mixed_ref, nf_ref, disp_ref.at[:, pl.ds(0, D)], gb))]
    swap_q = send(gq.at[0], gq.at[1], pair_ss.at[4], pair_sr.at[4], at.sib)
    swap_l = send(gl.at[0], gl.at[1], pair_ss.at[5], pair_sr.at[5], at.sib)
    swap_s = send(sums.at[0], sums.at[1], pair_ss.at[6], pair_sr.at[6], at.sib)
    at.meet(True)
    for i in range(3):
        swaps[i].start()
    for k in range(1, n):
        exchange(k).start()

    def weight(lo, width):
        return wv[:, :, lo : lo + width].reshape(D, width)

    loads[0].wait()
    mid = mid_ref[...]
    inv_second = inverse_rms(mid)
    unit = mid * inv_second
    gates, gg = gates_ref[...], gs_ref[:, D:]
    gl[0] = (gates * (gg - jnp.sum(gates * gg, axis=1, keepdims=True))).astype(bf16)
    swap_l.start()
    grad_second = mm(gl[0], weight(tail_at, 128), NT) + gs_ref[:, :D]
    pull = grad_second * gain_ref[1:2, :]
    sums[0, 1:2, :] = jnp.sum(grad_second * unit, axis=0, keepdims=True)
    grad_middle = cot_ref[...].astype(f32) + inv_second * (pull - unit * jnp.mean(pull * unit, axis=1, keepdims=True))
    gtok_ref[...] = grad_middle
    gb[...] = grad_middle.astype(bf16)
    swaps[3].start()
    loads[1].wait()
    for q in range(q_width // 512):
        gm[:, q * 512 : (q + 1) * 512] = mm(gb[...], wv[:, :, qkv_width : qkv_width + D].reshape(D, D)[q * 512 : (q + 1) * 512], NT).astype(bf16)

    def both(own, other, cols):
        return jnp.concatenate([own[:, cols], other[:, cols]], axis=0)

    def store(buf, zz, lo, value):
        blocks = value.astype(bf16).reshape(4, 2 * shard, value.shape[1])
        for a in range(4):
            slot = 2 * lax.rem(a // 2 + at.y, 2) + lax.rem(a % 2 + at.x, 2)
            buf[zz, slot, :, lo : lo + value.shape[1]] = blocks[a]

    def row_cols(zz):
        return pl.ds(pl.multiple_of(zz * share, 128), share)

    half_out, half_in = D // 2, qkv_width // 2
    swaps[0].wait_recv()
    swaps[3].wait_recv()

    @pl.loop(0, n)
    def _(j):
        zz = at.far(j)
        branch = both(gb, pair.at[3], pl.ds(pl.multiple_of(c * half_out, 128), half_out))
        store(pout, zz, 0, mm(both(mixed_ref, pair.at[0], row_cols(zz)), branch, TN))
        outs.s1(zz)

    scale = HEAD ** (-0.5)
    for g in range(KV_HEADS):
        heads = [slice((g * groups + j) * HEAD, (g * groups + j + 1) * HEAD) for j in range(groups)]
        kv = slice(g * HEAD, (g + 1) * HEAD)
        qs = jnp.concatenate([q_ref[:, h] for h in heads], axis=0)
        ms = jnp.concatenate([gm[:, h] for h in heads], axis=0)
        ks, vs = k_ref[:, kv], v_ref[:, kv]
        probs = p_ref[g]
        grad_values = mm(probs.astype(bf16), ms, TN)
        grad_probs = mm(ms, vs, NT)
        grad_scores = (probs * (grad_probs - jnp.sum(probs * grad_probs, axis=1, keepdims=True))).astype(bf16)
        grad_query = mm(grad_scores, ks) * scale
        for j, h in enumerate(heads):
            flat[:, h] = grad_query[j * rows : (j + 1) * rows]
        flat[:, q_width + kv.start : q_width + kv.stop] = mm(grad_scores, qs, TN) * scale
        flat[:, q_width + k_width + kv.start : q_width + k_width + kv.stop] = grad_values
    for j in range(n):
        outs.s2(at.far(j))
    cos, sin = cos_ref[...], sin_ref[...]
    for t in range(qkv_width // 128):
        tile = flat[:, t * 128 : (t + 1) * 128]
        if t * 128 < q_width + k_width:
            tile = tile * cos - swap_halves(tile) * sin
        gq[0, :, t * 128 : (t + 1) * 128] = tile.astype(bf16)
    swap_q.start()
    loads[2].wait()
    x = tok_ref[...].astype(f32)
    inv_first = inverse_rms(x)
    unit = x * inv_first
    grad_first = jnp.concatenate(
        [mm(gq[0], wv[8 * i : 8 * (i + 1), :, :qkv_width].reshape(8 * shard, qkv_width), NT) for i in range(n)], axis=1)
    pull = grad_first * gain_ref[0:1, :]
    sums[0, 0:1, :] = jnp.sum(grad_first * unit, axis=0, keepdims=True)
    sums[0, 2:, :] = jnp.zeros((6, D), f32)
    swap_s.start()
    gtok_ref[...] += inv_first * (pull - unit * jnp.mean(pull * unit, axis=1, keepdims=True))
    for i in (1, 2):
        swaps[i].wait_recv()
    swap_l.wait_recv()
    swap_q.wait_recv()
    swap_s.wait_recv()
    gains = sums[0] + sums[1]
    high = gains.astype(bf16)
    low = (gains - high.astype(f32)).astype(bf16)
    swap_s.wait_send()
    sums[0] = high.astype(f32)
    sums[1] = low.astype(f32)
    line = lax.rem(lax.broadcasted_iota(jnp.int32, (16, 128), 0), 8)
    where = (((line == 0) & (lane_tile(16) == experts)) | ((line == 1) & (lane_tile(16) == experts + 1))).astype(bf16)

    @pl.loop(0, n)
    def _(j):
        zz = at.far(j)
        cols = row_cols(zz)
        normed = both(nf_ref, pair.at[1], cols)
        for q in range(2):
            part = pl.ds(pl.multiple_of(c * half_in + q * (half_in // 2), 128), half_in // 2)
            grad = jnp.concatenate([gq[0, :, part], gq[1, :, part]], axis=0)
            store(pin, zz, q * (half_in // 2), mm(normed, grad, TN))
        tail = mm(both(disp_ref, pair.at[2], cols), jnp.concatenate([gl[0], gl[1]], axis=0), TN)
        rows_now = jnp.concatenate([sums[0, :, cols], sums[1, :, cols]], axis=0).astype(bf16)
        store(pin, zz, half_in, tail + mm(rows_now, where, TN))

        @pl.when(j < 2)
        def _():
            ins.corners(zz)

    for j in range(n + 1):
        ins.step(j)
        if j < n:
            outs.s3(at.far(j))
            outs.lines(j)
    outs.last()
    mine, theirs = pl.ds(pl.multiple_of(c * shard, 8), shard), pl.ds(pl.multiple_of((1 - c) * shard, 8), shard)
    cols_out, cols_in = pl.ds(pl.multiple_of(c * half_out, 128), half_out), pl.ds(pl.multiple_of(c * half_in, 128), half_in)
    end_out = send(tot_out.at[theirs, :], gout_ref.at[:, cols_out], end_ss.at[0], end_sr.at[0], at.sib)
    end_out.start()
    gout_ref[:, cols_out] = tot_out[mine, :]
    ins.last()
    end_in = send(tot_in.at[theirs, pl.ds(0, half_in)], gin_ref.at[:, cols_in], end_ss.at[1], end_sr.at[1], at.sib)
    end_in.start()
    gin_ref[:, cols_in] = tot_in[mine, :half_in]
    gtail_ref[...] = tot_in[mine, half_in:]
    own_share.wait()
    for k in range(1, n):
        exchange(k).wait_send()
        source = lax.rem(d + k, n)
        send(gup_ref.at[pl.ds(0, share), :], arrived.at[source], a2a_ss.at[k], a2a_sr.at[source], (source, at.e)).wait_recv()

    end_out.wait()
    end_in.wait()
    for swap in swaps + [swap_q, swap_l]:
        swap.wait_send()
    outs.finish()
    ins.finish()


def backward_layer(gs, tok, cot, mid, gates, gain, nf, disp, q, k, v, p, mixed, cos, sin, w_all, gup, n, experts, cid):
    f32, bf16 = jnp.float32, jnp.bfloat16
    rows = tok.shape[0]
    shard, wide = w_all.shape[1:]
    qkv_width = (HEADS + 2 * KV_HEADS) * HEAD
    share = D // n
    D_ = pltpu.SemaphoreType.DMA
    V = lambda *s: pltpu.VMEM(s, bf16)
    W = lambda *s: pltpu.VMEM(s, f32)
    any_, vm = pl.BlockSpec(memory_space=pl.ANY), pl.BlockSpec(memory_space=pltpu.VMEM)
    S = jax.ShapeDtypeStruct
    width_out, width_in = D // 2, qkv_width // 2 + 128
    return pl.pallas_call(
        functools.partial(backward_kernel, n, experts),
        out_shape=(S((rows, D), f32), S((shard, D), f32), S((shard, qkv_width), f32), S((shard, 128), f32), S((n, share, gup.shape[1]), bf16)),
        in_specs=[vm] * 15 + [any_, any_],
        out_specs=[vm] * 4 + [any_],
        scratch_shapes=[V(n * 8, shard, wide), V(n, 4, 2 * shard, width_out), V(n, 4, 2 * shard, width_in),
                        W(2 * shard, width_out), W(2 * shard, width_in),
                        V(4, rows, D), V(2, rows, qkv_width), V(2, rows, 128), W(2, 8, D), V(rows, D), V(rows, D), W(rows, qkv_width)]
        + reduce_scratch(n, 2 * shard, width_out) + reduce_scratch(n, 2 * shard, width_in)
        + [D_((4,)), D_((7,)), D_((7,)), D_((n,)), D_((n,)), D_((2,)), D_((2,))],
        compiler_params=pltpu.CompilerParams(collective_id=cid, has_side_effects=True, vmem_limit_bytes=62 << 20),
        name="backward_layer",
    )(gs, tok, cot, mid, gates, gain, nf, disp, q, k, v, p, mixed, cos, sin, w_all, gup)


def results_kernel(experts, arrived, tok_in, down_in, out_in, qkv_in, tail_in,
                   up_ref, tok_ref, down_ref, proj_ref, qkv_ref, router_ref, gains_ref):
    n, width = arrived.shape[0], arrived.shape[2]
    f = FF // n
    for q in range(n):
        for j in range(width // f):
            lo = (j % 2) * FF + q * f
            up_ref[j // 2, :, lo : lo + f] = arrived[q, :, j * f : (j + 1) * f].astype(jnp.float32)

    @pl.when(pl.program_id(0) == 0)
    def _():
        tok_ref[...] = tok_in[...]
        down_ref[...] = down_in[...]
        proj_ref[...] = out_in[...]
        qkv_ref[...] = qkv_in[...]
        router_ref[...] = tail_in[:, :experts]
        turned = jnp.transpose(jnp.concatenate([tail_in[...], jnp.zeros((128 - tail_in.shape[0], 128), jnp.float32)], axis=0))
        gains_ref[...] = turned[experts : experts + 8, : tail_in.shape[0]]


def results(arrived, tok, down, proj, qkv, tail, held, experts):
    n, share, width = arrived.shape
    f32 = jnp.float32
    steps = 4
    rows = share // steps
    whole = lambda a: pl.BlockSpec(a.shape, lambda i: (0,) * len(a.shape))
    shapes = [jax.ShapeDtypeStruct(a.shape, f32) for a in (tok, down, proj, qkv)]
    shapes += [jax.ShapeDtypeStruct((tail.shape[0], experts), f32), jax.ShapeDtypeStruct((8, tail.shape[0]), f32)]
    return pl.pallas_call(
        functools.partial(results_kernel, experts),
        grid=(steps,),
        out_shape=[jax.ShapeDtypeStruct((held, share, 2 * FF), f32)] + shapes,
        in_specs=[pl.BlockSpec((n, rows, width), lambda i: (0, i, 0))] + [whole(a) for a in (tok, down, proj, qkv, tail)],
        out_specs=[pl.BlockSpec((held, rows, 2 * FF), lambda i: (0, i, 0))] + [whole(a) for a in shapes],
        compiler_params=pltpu.CompilerParams(vmem_limit_bytes=62 << 20),
        name="results",
    )(arrived, tok, down, proj, qkv, tail)


def per_device_fast(n, tokens, segments, routes, cotangent, gain_attn, attn_in, attn_out, gain_ffn, router, expert_in, expert_out):
    f32, bf16 = jnp.float32, jnp.bfloat16
    micro, rows = tokens.shape[:2]
    total = micro * rows
    held = expert_in.shape[0]
    experts = held * 8
    f = FF // n
    shard = attn_in.shape[0]
    x = tokens.reshape(total, D)
    cot = cotangent.reshape(total, D)
    tail = jnp.concatenate([router, gain_attn[:, None], gain_ffn[:, None], jnp.zeros((shard, 126 - experts), bf16)], axis=1)
    w_all, cot_all, up, disp, middle, gates, gain, nf, q, k, v, p, mixed, cos, sin = forward_layer(
        x, cot, attn_in, attn_out, tail, expert_in, segments, routes.reshape(total, TOP_K), n, experts, 0)
    out, grad_sum, grad_up, grad_down = expert_layer(disp, cot_all, up, expert_out.reshape(held * f, D), middle, n, experts, 1)
    grad_tokens, grad_out, grad_in, grad_tail, grad_up = backward_layer(
        grad_sum, x, cot, middle, gates, gain, nf, disp, q, k, v, p, mixed, cos, sin, w_all, grad_up, n, experts, 2)
    grad_up, grad_tokens, grad_down, grad_out, grad_in, grad_router, grad_gains = results(
        grad_up, grad_tokens, grad_down, grad_out, grad_in, grad_tail, held, experts)
    return (
        out.astype(bf16).reshape(micro, rows, D),
        grad_tokens.reshape(micro, rows, D),
        grad_gains[0],
        grad_in,
        grad_out,
        grad_gains[1],
        grad_router,
        grad_up,
        grad_down.reshape(held, f, D),
    )


def solution(mesh):
    placed = (
        P(None, ("dp", "expert"), None),
        P(None, ("dp", "expert"), None),
        P(None, ("dp", "expert"), None),
        P(None, ("dp", "expert"), None),
        P(("dp", "expert")),
        P(("dp", "expert"), None),
        P(("dp", "expert"), None),
        P(("dp", "expert")),
        P(("dp", "expert"), None),
        P("expert", "dp", None),
        P("expert", "dp", None),
    )
    fast = mesh.shape["expert"] == 8 and FF // mesh.shape["dp"] == 128
    body = functools.partial(per_device_fast, mesh.shape["dp"]) if fast else per_device
    return jax.shard_map(
        body,
        mesh=mesh,
        in_specs=placed,
        out_specs=(
            P(None, ("dp", "expert"), None),
            P(None, ("dp", "expert"), None),
            P(("dp", "expert")),
            P(("dp", "expert"), None),
            P(("dp", "expert"), None),
            P(("dp", "expert")),
            P(("dp", "expert"), None),
            P("expert", "dp", None),
            P("expert", "dp", None),
        ),
        check_vma=False,
    )
```

```python
import functools

import jax
import jax.numpy as jnp
from jax import lax
from jax.experimental import pallas as pl
from jax.experimental.pallas import tpu as pltpu
from jax.sharding import PartitionSpec as P

MESH = pl.DeviceIdType.MESH

D = 1536
HEADS = 24
KV_HEADS = 8
HEAD = 64
FF = 512
TOP_K = 8


norm_eps = 1e-06
rope_base = 10000.0
neg_large = -1e30
highest = lax.Precision.HIGHEST


def rope_tables(segment, half_width):
    row_count = segment.shape[0]
    places = jnp.arange(row_count, dtype=jnp.int32)
    same_seq = segment[:, None] == segment[None, :]
    seq_start = jnp.min(jnp.where(same_seq, places[None, :], row_count), axis=1)
    offset = (places - seq_start).astype(jnp.float32)
    frequencies = rope_base ** (-jnp.arange(half_width, dtype=jnp.float32) / half_width)
    angles = offset[:, None] * frequencies[None, :]
    causal = same_seq & (places[None, :] <= places[:, None])
    return (jnp.cos(angles), jnp.sin(angles), causal)


def rotate(operand, cosine, sine_table):
    half_width = operand.shape[-1] // 2
    front_part = operand[..., :half_width]
    back_part = operand[..., half_width:]
    return jnp.concatenate(
        [
            front_part * cosine - back_part * sine_table,
            back_part * cosine + front_part * sine_table,
        ],
        axis=-1,
    )


def unrotate(gradient, cosine, sine_table):
    half_width = gradient.shape[-1] // 2
    front_part = gradient[..., :half_width]
    back_part = gradient[..., half_width:]
    return jnp.concatenate(
        [
            front_part * cosine + back_part * sine_table,
            back_part * cosine - front_part * sine_table,
        ],
        axis=-1,
    )


def slot_targets(route_now, expert_count, capacity):
    flat_ids = route_now.reshape(-1)
    onehot = (flat_ids[:, None] == jnp.arange(expert_count, dtype=jnp.int32)[None, :]).astype(
        jnp.int32
    )
    earlier = jnp.cumsum(onehot, axis=0) - onehot
    slot_index = jnp.sum(earlier * onehot, axis=1)
    return flat_ids * capacity + slot_index


def dense_fetch(gain_attn, attn_in, attn_out, gain_ffn, router):
    return (
        lax.all_gather(gain_attn, ("dp", "expert"), axis=0, tiled=True),
        lax.all_gather(attn_in, ("dp", "expert"), axis=0, tiled=True),
        lax.all_gather(attn_out, ("dp", "expert"), axis=0, tiled=True),
        lax.all_gather(gain_ffn, ("dp", "expert"), axis=0, tiled=True),
        lax.all_gather(router, ("dp", "expert"), axis=0, tiled=True),
    )


def expert_fetch(expert_in, expert_out):
    return (
        lax.all_gather(expert_in, "dp", axis=1, tiled=True),
        lax.all_gather(expert_out, "dp", axis=1, tiled=True),
    )


def dense_reduce(grad_set):
    return (
        lax.psum_scatter(grad_set[0], ("dp", "expert"), scatter_dimension=0, tiled=True),
        lax.psum_scatter(grad_set[1], ("dp", "expert"), scatter_dimension=0, tiled=True),
        lax.psum_scatter(grad_set[2], ("dp", "expert"), scatter_dimension=0, tiled=True),
        lax.psum_scatter(grad_set[3], ("dp", "expert"), scatter_dimension=0, tiled=True),
        lax.psum_scatter(grad_set[4], ("dp", "expert"), scatter_dimension=0, tiled=True),
    )


def expert_reduce(grad_set):
    return (
        lax.psum_scatter(grad_set[0], "dp", scatter_dimension=1, tiled=True),
        lax.psum_scatter(grad_set[1], "dp", scatter_dimension=1, tiled=True),
    )


def attention_scores(queries, key_rot, causal):
    score_scale = HEAD ** (-0.5)
    scores = (
        jnp.einsum("tkgh,skh->kgts", queries, key_rot, preferred_element_type=jnp.float32)
        * score_scale
    )
    return jnp.where(causal[None, None], scores, neg_large)


def forward_micro(tokens_now, segment, route_now, dense_set, expert_set, shapes):
    expert_count, capacity, group_count, local_experts = shapes
    gain_attn, qkv_weight, out_weight, gain_ffn, router_weight = dense_set
    expert_up, expert_down = expert_set
    row_count = tokens_now.shape[0]
    groups = HEADS // KV_HEADS
    q_width = HEADS * HEAD
    k_width = KV_HEADS * HEAD
    inputs = tokens_now.astype(jnp.float32)
    inv_first = lax.rsqrt(jnp.mean(inputs * inputs, axis=1, keepdims=True) + norm_eps)
    normed_first = (inputs * inv_first * gain_attn.astype(jnp.float32)).astype(jnp.bfloat16)
    qkv_full = jnp.dot(normed_first, qkv_weight, preferred_element_type=jnp.float32)
    cosine, sine_table, causal = rope_tables(segment, HEAD // 2)
    queries = rotate(
        qkv_full[:, :q_width].reshape(row_count, KV_HEADS, groups, HEAD),
        cosine[:, None, None, :],
        sine_table[:, None, None, :],
    ).astype(jnp.bfloat16)
    key_rot = rotate(
        qkv_full[:, q_width : q_width + k_width].reshape(row_count, KV_HEADS, HEAD),
        cosine[:, None, :],
        sine_table[:, None, :],
    ).astype(jnp.bfloat16)
    values = (
        qkv_full[:, q_width + k_width :].reshape(row_count, KV_HEADS, HEAD).astype(jnp.bfloat16)
    )
    scores = attention_scores(queries, key_rot, causal)
    score_peak = jnp.max(scores, axis=-1, keepdims=True)
    exp_scores = jnp.exp(scores - score_peak)
    exp_total = jnp.sum(exp_scores, axis=-1, keepdims=True)
    log_total = score_peak + jnp.log(exp_total)
    soft_probs = (exp_scores / exp_total).astype(jnp.bfloat16)
    attn_mixed = jnp.einsum(
        "kgts,skh->tkgh", soft_probs, values, preferred_element_type=jnp.float32
    )
    attn_mixed = attn_mixed.reshape(row_count, q_width).astype(jnp.bfloat16)
    middle = inputs + jnp.dot(attn_mixed, out_weight, preferred_element_type=jnp.float32)
    inv_second = lax.rsqrt(jnp.mean(middle * middle, axis=1, keepdims=True) + norm_eps)
    normed_second = (middle * inv_second * gain_ffn.astype(jnp.float32)).astype(jnp.bfloat16)
    logits = jnp.dot(normed_second, router_weight, preferred_element_type=jnp.float32)
    chosen = (
        route_now[:, :, None] == jnp.arange(expert_count, dtype=jnp.int32)[None, None, :]
    ).astype(jnp.float32)
    picked_logits = jnp.sum(chosen * logits[:, None, :], axis=-1)
    gate_values = jax.nn.softmax(picked_logits, axis=-1)
    targets = slot_targets(route_now, expert_count, capacity)
    source_rows = jnp.repeat(normed_second, TOP_K, axis=0)
    buffer = jnp.zeros((expert_count * capacity, D), jnp.bfloat16).at[targets].set(source_rows)
    send_rows = buffer.reshape(group_count, local_experts, capacity, D)
    received = lax.all_to_all(send_rows, "expert", split_axis=0, concat_axis=0, tiled=True)
    gate_up = jnp.einsum("secd,edf->secf", received, expert_up, preferred_element_type=jnp.float32)
    hidden = (jax.nn.silu(gate_up[..., :FF]) * gate_up[..., FF:]).astype(jnp.bfloat16)
    expert_result = jnp.einsum(
        "secf,efd->secd", hidden, expert_down, preferred_element_type=jnp.float32
    ).astype(jnp.bfloat16)
    returned = lax.all_to_all(expert_result, "expert", split_axis=0, concat_axis=0, tiled=True)
    picked = returned.reshape(expert_count * capacity, D)[targets].reshape(row_count, TOP_K, D)
    moe_sum = jnp.einsum(
        "tk,tkd->td", gate_values, picked, precision=highest, preferred_element_type=jnp.float32
    )
    result = (middle + moe_sum).astype(jnp.bfloat16)
    saved_state = (
        inputs,
        inv_first,
        normed_first,
        queries,
        key_rot,
        values,
        log_total,
        causal,
        cosine,
        sine_table,
        attn_mixed,
        middle,
        inv_second,
        normed_second,
        chosen,
        gate_values,
        targets,
        received,
        gate_up,
        hidden,
        picked,
    )
    return (result, saved_state)


def backward_micro(saved_state, cotan_now, dense_set, expert_set, shapes):
    expert_count, capacity, group_count, local_experts = shapes
    (
        inputs,
        inv_first,
        normed_first,
        queries,
        key_rot,
        values,
        log_total,
        causal,
        cosine,
        sine_table,
        attn_mixed,
        middle,
        inv_second,
        normed_second,
        chosen,
        gate_values,
        targets,
        received,
        gate_up,
        hidden,
        picked,
    ) = saved_state
    gain_attn, qkv_weight, out_weight, gain_ffn, router_weight = dense_set
    expert_up, expert_down = expert_set
    row_count = inputs.shape[0]
    groups = HEADS // KV_HEADS
    q_width = HEADS * HEAD
    k_width = KV_HEADS * HEAD
    score_scale = HEAD ** (-0.5)
    upstream = cotan_now.astype(jnp.float32)
    grad_gates = jnp.einsum(
        "td,tkd->tk", upstream, picked, precision=highest, preferred_element_type=jnp.float32
    )
    grad_picked = gate_values * (
        grad_gates - jnp.sum(gate_values * grad_gates, axis=-1, keepdims=True)
    )
    grad_logits = jnp.sum(chosen * grad_picked[:, :, None], axis=1).astype(jnp.bfloat16)
    grad_router = jnp.einsum(
        "td,te->de", normed_second, grad_logits, preferred_element_type=jnp.float32
    )
    grad_second = jnp.einsum(
        "te,de->td", grad_logits, router_weight, preferred_element_type=jnp.float32
    )
    grad_slots = (
        (gate_values[:, :, None] * upstream[:, None, :])
        .astype(jnp.bfloat16)
        .reshape(row_count * TOP_K, D)
    )
    grad_buffer = jnp.zeros((expert_count * capacity, D), jnp.bfloat16).at[targets].set(grad_slots)
    grad_buffer = grad_buffer.reshape(group_count, local_experts, capacity, D)
    grad_result = lax.all_to_all(grad_buffer, "expert", split_axis=0, concat_axis=0, tiled=True)
    grad_hidden = jnp.einsum(
        "secd,efd->secf", grad_result, expert_down, preferred_element_type=jnp.float32
    )
    grad_down = jnp.einsum(
        "secf,secd->efd", hidden, grad_result, preferred_element_type=jnp.float32
    )
    gate_part = gate_up[..., :FF]
    up_part = gate_up[..., FF:]
    gate_sigmoid = jax.nn.sigmoid(gate_part)
    grad_gate = grad_hidden * up_part * gate_sigmoid * (1.0 + gate_part * (1.0 - gate_sigmoid))
    grad_up_part = grad_hidden * (gate_part * gate_sigmoid)
    grad_gate_up = jnp.concatenate([grad_gate, grad_up_part], axis=-1).astype(jnp.bfloat16)
    grad_up = jnp.einsum(
        "secd,secf->edf", received, grad_gate_up, preferred_element_type=jnp.float32
    )
    grad_rows = jnp.einsum(
        "secf,edf->secd", grad_gate_up, expert_up, preferred_element_type=jnp.float32
    ).astype(jnp.bfloat16)
    grad_back = lax.all_to_all(grad_rows, "expert", split_axis=0, concat_axis=0, tiled=True)
    grad_choice = grad_back.reshape(expert_count * capacity, D)[targets].reshape(
        row_count, TOP_K, D
    )
    grad_second = grad_second + jnp.sum(grad_choice, axis=1, dtype=jnp.float32)
    unit_second = middle * inv_second
    pull_second = grad_second * gain_ffn.astype(jnp.float32)
    grad_gain_ffn = jnp.sum(grad_second * unit_second, axis=0)
    grad_middle = upstream + inv_second * (
        pull_second - unit_second * jnp.mean(pull_second * unit_second, axis=1, keepdims=True)
    )
    grad_branch = grad_middle.astype(jnp.bfloat16)
    grad_out_weight = jnp.einsum(
        "tc,td->cd", attn_mixed, grad_branch, preferred_element_type=jnp.float32
    )
    grad_mixed = jnp.einsum(
        "td,cd->tc", grad_branch, out_weight, preferred_element_type=jnp.float32
    )
    grad_mixed = grad_mixed.astype(jnp.bfloat16).reshape(row_count, KV_HEADS, groups, HEAD)
    scores = attention_scores(queries, key_rot, causal)
    soft_probs = jnp.exp(scores - log_total)
    grad_values = jnp.einsum(
        "kgts,tkgh->skh",
        soft_probs.astype(jnp.bfloat16),
        grad_mixed,
        preferred_element_type=jnp.float32,
    )
    grad_probs = jnp.einsum(
        "tkgh,skh->kgts", grad_mixed, values, preferred_element_type=jnp.float32
    )
    grad_scores = soft_probs * (
        grad_probs - jnp.sum(soft_probs * grad_probs, axis=-1, keepdims=True)
    )
    grad_scores = grad_scores.astype(jnp.bfloat16)
    grad_query = (
        jnp.einsum("kgts,skh->tkgh", grad_scores, key_rot, preferred_element_type=jnp.float32)
        * score_scale
    )
    grad_key = (
        jnp.einsum("kgts,tkgh->skh", grad_scores, queries, preferred_element_type=jnp.float32)
        * score_scale
    )
    grad_query = unrotate(grad_query, cosine[:, None, None, :], sine_table[:, None, None, :])
    grad_key = unrotate(grad_key, cosine[:, None, :], sine_table[:, None, :])
    grad_qkv = jnp.concatenate(
        [
            grad_query.reshape(row_count, q_width),
            grad_key.reshape(row_count, k_width),
            grad_values.reshape(row_count, k_width),
        ],
        axis=1,
    ).astype(jnp.bfloat16)
    grad_qkv_weight = jnp.einsum(
        "tc,tq->cq", normed_first, grad_qkv, preferred_element_type=jnp.float32
    )
    grad_first = jnp.einsum("tq,cq->tc", grad_qkv, qkv_weight, preferred_element_type=jnp.float32)
    unit_first = inputs * inv_first
    pull_first = grad_first * gain_attn.astype(jnp.float32)
    grad_gain_attn = jnp.sum(grad_first * unit_first, axis=0)
    grad_inputs = grad_middle + inv_first * (
        pull_first - unit_first * jnp.mean(pull_first * unit_first, axis=1, keepdims=True)
    )
    dense_grads = (grad_gain_attn, grad_qkv_weight, grad_out_weight, grad_gain_ffn, grad_router)
    expert_grads = (grad_up, grad_down)
    return (grad_inputs, dense_grads, expert_grads)


def add_pair(left_part, right_part):
    return left_part + right_part


def per_device(
    tokens,
    segments,
    routes,
    cotangent,
    gain_attn,
    attn_in,
    attn_out,
    gain_ffn,
    router,
    expert_in,
    expert_out,
):
    local_experts = expert_in.shape[0]
    group_count = lax.axis_size("expert")
    expert_count = local_experts * group_count
    micro_count = tokens.shape[0]
    row_count = tokens.shape[1]
    capacity = (row_count * TOP_K * 5 // (4 * expert_count) + 7) // 8 * 8
    shapes = (expert_count, capacity, group_count, local_experts)
    outputs = []
    grad_list = []
    dense_total = None
    expert_total = None
    for micro_index in range(micro_count):
        dense_set = dense_fetch(gain_attn, attn_in, attn_out, gain_ffn, router)
        expert_set = expert_fetch(expert_in, expert_out)
        result, saved_state = forward_micro(
            tokens[micro_index],
            segments[micro_index, 0],
            routes[micro_index],
            dense_set,
            expert_set,
            shapes,
        )
        dense_set = dense_fetch(gain_attn, attn_in, attn_out, gain_ffn, router)
        expert_set = expert_fetch(expert_in, expert_out)
        grad_inputs, dense_grads, expert_grads = backward_micro(
            saved_state, cotangent[micro_index], dense_set, expert_set, shapes
        )
        dense_grads = dense_reduce(dense_grads)
        expert_grads = expert_reduce(expert_grads)
        if dense_total is None:
            dense_total = dense_grads
            expert_total = expert_grads
        else:
            dense_total = jax.tree.map(add_pair, dense_total, dense_grads)
            expert_total = jax.tree.map(add_pair, expert_total, expert_grads)
        outputs.append(result)
        grad_list.append(grad_inputs)
    return (
        jnp.stack(outputs, axis=0),
        jnp.stack(grad_list, axis=0),
        dense_total[0],
        dense_total[1],
        dense_total[2],
        dense_total[3],
        dense_total[4],
        expert_total[0],
        expert_total[1],
    )


NN = (((1,), (0,)), ((), ()))
NT = (((1,), (1,)), ((), ()))
TN = (((0,), (0,)), ((), ()))


def mm(a, b, dims=NN):
    return lax.dot_general(a, b, dims, preferred_element_type=jnp.float32)


class Place:
    def __init__(self, n):
        self.n = n
        d = self.d = lax.axis_index("dp")
        e = self.e = lax.axis_index("expert")
        c, x, y = lax.rem(e, 2), lax.rem(lax.div(e, 2), 2), lax.div(e, 4)
        self.sib = (d, e + 1 - 2 * c)
        self.nx = (d, e + 2 - 4 * x)
        self.ny = (d, e + 4 - 8 * y)
        self.diag = self.nx[1] + 4 - 8 * y
        self.c, self.x, self.y = c, x, y
        self.below = (d - 1, e)
        self.above = (d + 1, e)
        self.has_below = d > 0
        self.has_above = d < n - 1

    def meet(self, everyone=False):
        barrier = pltpu.get_barrier_semaphore()
        d, n = self.d, self.n
        if everyone:
            others = n - 1 + 3

            @pl.loop(1, n)
            def _(k):
                pl.semaphore_signal(barrier, inc=1, device_id=(lax.rem(d + k, n), self.e), device_id_type=MESH)
        else:
            others = 3 + jnp.minimum(d, 1) + jnp.minimum(n - 1 - d, 1)

            @pl.when(self.has_below)
            def _():
                pl.semaphore_signal(barrier, inc=1, device_id=self.below, device_id_type=MESH)

            @pl.when(self.has_above)
            def _():
                pl.semaphore_signal(barrier, inc=1, device_id=self.above, device_id_type=MESH)

        for dev in (self.sib, self.nx, self.ny):
            pl.semaphore_signal(barrier, inc=1, device_id=dev, device_id_type=MESH)
        pl.semaphore_wait(barrier, others)

    def far(self, i):
        n, d = self.n, self.d
        low = d < n - d
        m = jnp.where(low, d, n - 1 - d)
        t = jnp.where(i < n - 1 - m, n - 1 - i, jnp.where(i < n - 1, i - (n - 1 - m), m))
        return jnp.where(low, t, n - 1 - t)

    def near(self, i):
        return self.far(self.n - 1 - i)


def send(src, dst, ss, rs, dev):
    return pltpu.make_async_remote_copy(src, dst, ss, rs, device_id=dev, device_id_type=MESH)


class Gather:
    def __init__(self, at, own, buf, send_sem, recv_z, recv_x, recv_y, recv_d, rows=None):
        self.at, self.own, self.buf = at, own, buf
        self.ss, self.rz, self.rx, self.ry, self.rd = send_sem, recv_z, recv_x, recv_y, recv_d
        rows = rows or own.shape[0]
        self.F, self.A, self.B = pl.ds(0, rows), pl.ds(0, rows // 2), pl.ds(rows // 2, rows // 2)

    def source(self, zz, own):
        return self.own.at[self.F] if own else self.buf.at[zz, 0, self.F]

    def down(self, zz, own=False):
        return send(self.source(zz, own), self.buf.at[zz, 0, self.F], self.ss.at[zz, 0], self.rz.at[zz], self.at.below)

    def up(self, zz, own=False):
        return send(self.source(zz, own), self.buf.at[zz, 0, self.F], self.ss.at[zz, 1], self.rz.at[zz], self.at.above)

    def to_x(self, zz, own=False):
        return send(self.source(zz, own), self.buf.at[zz, 1, self.F], self.ss.at[zz, 2], self.rx.at[zz], self.at.nx)

    def to_y(self, zz, own=False):
        return send(self.source(zz, own), self.buf.at[zz, 2, self.F], self.ss.at[zz, 3], self.ry.at[zz], self.at.ny)

    def turn_y(self, zz):
        return send(self.buf.at[zz, 1, self.A], self.buf.at[zz, 3, self.A], self.ss.at[zz, 4], self.rd.at[zz, 0], self.at.ny)

    def turn_x(self, zz):
        return send(self.buf.at[zz, 2, self.B], self.buf.at[zz, 3, self.B], self.ss.at[zz, 5], self.rd.at[zz, 1], self.at.nx)

    def begin(self):
        self.begin_z()
        self.begin_xy()

    def begin_z(self):
        d = self.at.d

        @pl.when(self.at.has_below)
        def _():
            self.down(d, True).start()

        @pl.when(self.at.has_above)
        def _():
            self.up(d, True).start()

    def begin_xy(self):
        self.to_x(self.at.d, True).start()
        self.to_y(self.at.d, True).start()

    def column_z(self, zz):
        d = self.at.d

        @pl.when(zz < d)
        def _():
            self.up(zz).wait_recv()

            @pl.when(self.at.has_above)
            def _():
                self.up(zz).start()

        @pl.when(zz > d)
        def _():
            self.down(zz).wait_recv()

            @pl.when(self.at.has_below)
            def _():
                self.down(zz).start()

    def column_xy(self, zz):
        self.to_x(zz).start()
        self.to_y(zz).start()

    def column(self, zz):
        self.column_z(zz)
        self.column_xy(zz)

    def plane(self, zz):
        self.to_x(zz).wait_recv()
        self.turn_y(zz).start()
        self.to_y(zz).wait_recv()
        self.turn_x(zz).start()

    def corner(self, zz):
        self.turn_y(zz).wait_recv()
        self.turn_x(zz).wait_recv()

    def finish(self):
        d = self.at.d

        @pl.loop(0, self.at.n)
        def _(zz):
            for copy in (self.to_x, self.to_y, self.turn_y, self.turn_x):
                copy(zz).wait_send()

            @pl.when((d > 0) & (zz >= d))
            def _():
                self.down(zz).wait_send()

            @pl.when(self.at.has_above & (zz <= d))
            def _():
                self.up(zz).wait_send()


class LineGather:
    def __init__(self, at, own, buf, lo, ss, sr, zs, zr):
        self.at, self.own, self.buf = at, own, buf
        self.ss, self.sr, self.zs, self.zr = ss, sr, zs, zr
        rows = own.shape[0] - lo
        self.P, self.A, self.B = pl.ds(lo, rows), pl.ds(lo, rows // 2), pl.ds(lo + rows // 2, rows // 2)

    def inside(self, k):
        at, buf, d = self.at, self.buf, self.at.d
        src, slot, part, dev = (
            (self.own.at[self.P], 1, self.P, at.nx), (self.own.at[self.P], 2, self.P, at.ny),
            (buf.at[d, 1, self.A], 3, self.A, at.ny), (buf.at[d, 2, self.B], 3, self.B, at.nx))[k]
        return send(src, buf.at[d, slot, part], self.ss.at[k], self.sr.at[k], dev)

    def along(self, zz, up):
        part = self.buf.at[zz, :, self.P]
        return send(part, part, self.zs.at[zz, up], self.zr.at[zz], self.at.above if up else self.at.below)

    def begin(self):
        self.inside(0).start()
        self.inside(1).start()

    def plane(self):
        self.inside(0).wait_recv()
        self.inside(2).start()
        self.inside(1).wait_recv()
        self.inside(3).start()

    def corner(self):
        self.inside(2).wait_recv()
        self.inside(3).wait_recv()

        @pl.when(self.at.has_below)
        def _():
            self.along(self.at.d, 0).start()

        @pl.when(self.at.has_above)
        def _():
            self.along(self.at.d, 1).start()

    def line(self, zz):
        self.along(zz, 0).wait_recv()

        @pl.when((zz < self.at.d) & self.at.has_above)
        def _():
            self.along(zz, 1).start()

        @pl.when((zz > self.at.d) & self.at.has_below)
        def _():
            self.along(zz, 0).start()

    def finish(self):
        d = self.at.d
        for k in range(4):
            self.inside(k).wait_send()

        @pl.loop(0, self.at.n)
        def _(zz):
            @pl.when(self.at.has_below & (zz >= d))
            def _():
                self.along(zz, 0).wait_send()

            @pl.when(self.at.has_above & (zz <= d))
            def _():
                self.along(zz, 1).wait_send()


def line_gather_sems(n):
    D_ = pltpu.SemaphoreType.DMA
    return [D_((4,)), D_((4,)), D_((n, 2)), D_((n,))]


def gather_sems(n):
    D_ = pltpu.SemaphoreType.DMA
    return [D_((n, 6)), D_((n,)), D_((n,)), D_((n,)), D_((n, 2))]


def add_rows(dst, src):
    rows = dst.shape[0]
    step = 16

    @pl.loop(0, rows // step)
    def _(r):
        w = pl.ds(pl.multiple_of(r * step, step), step)
        dst[w, :] = (dst[w, :].astype(jnp.float32) + src[w, :].astype(jnp.float32)).astype(dst.dtype)


class Reduce:
    def __init__(self, at, buf, total, r1, r2, rz, ss_1, sr_1, ss_2, sr_2, ss_z, sr_z, start=None):
        self.start = start
        self.at, self.buf, self.total = at, buf, total
        self.r1, self.r2, self.rz = r1, r2, rz
        self.sems = (ss_1, sr_1, ss_2, sr_2, ss_z, sr_z)
        rows = total.shape[0]
        self.A, self.B = pl.ds(0, rows // 2), pl.ds(rows // 2, rows // 2)

    def first(self, zz, k):
        ss, sr = self.sems[0], self.sems[1]
        slot, part, dev = ((3, self.A, self.at.nx), (3, self.B, self.at.ny), (1, self.A, self.at.nx), (2, self.B, self.at.ny))[k]
        return send(self.buf.at[zz, slot, part], self.r1.at[zz, k], ss.at[zz, k], sr.at[zz, k], dev)

    def second(self, zz, k):
        ss, sr = self.sems[2], self.sems[3]
        slot, part, dev = ((2, self.A, self.at.ny), (1, self.B, self.at.nx))[k]
        return send(self.buf.at[zz, slot, part], self.r2.at[zz, k], ss.at[zz, k], sr.at[zz, k], dev)

    def down(self, zz):
        return send(self.buf.at[zz, 0], self.rz.at[zz], self.sems[4].at[zz], self.sems[5].at[zz], self.at.below)

    def up(self, zz):
        slot = jnp.where(zz == self.at.d + 1, self.at.n, zz)
        return send(self.buf.at[zz, 0], self.rz.at[slot], self.sems[4].at[zz], self.sems[5].at[slot], self.at.above)

    def arrive(self, slot):
        return send(self.buf.at[0, 0], self.rz.at[slot], self.sems[4].at[0], self.sems[5].at[slot], self.at.nx)

    def s1(self, zz):
        self.corners(zz)
        self.sides(zz)

    def corners(self, zz):
        self.first(zz, 0).start()
        self.first(zz, 1).start()

    def sides(self, zz):
        self.first(zz, 2).start()
        self.first(zz, 3).start()

    def turn(self, zz):
        self.first(zz, 0).wait_recv()
        add_rows(self.buf.at[zz, 2, self.A], self.r1.at[zz, 0])
        self.second(zz, 0).start()
        self.first(zz, 1).wait_recv()
        add_rows(self.buf.at[zz, 1, self.B], self.r1.at[zz, 1])
        self.second(zz, 1).start()

    def take_sides(self, zz):
        self.first(zz, 2).wait_recv()
        add_rows(self.buf.at[zz, 0, self.A], self.r1.at[zz, 2])
        self.first(zz, 3).wait_recv()
        add_rows(self.buf.at[zz, 0, self.B], self.r1.at[zz, 3])

    def s2(self, zz):
        self.turn(zz)
        self.take_sides(zz)

    def step(self, j):
        at = self.at
        if j < at.n:
            self.turn(at.far(j))
            self.sides(at.far(j))
            if j + 2 < at.n:
                self.corners(at.far(j + 2))
        if j >= 1:
            self.take_sides(at.far(j - 1))
            self.s3(at.far(j - 1))
            self.lines(j - 1)

    def s3(self, zz):
        self.second(zz, 0).wait_recv()
        add_rows(self.buf.at[zz, 0, self.A], self.r2.at[zz, 0])
        self.second(zz, 1).wait_recv()
        add_rows(self.buf.at[zz, 0, self.B], self.r2.at[zz, 1])

    def push(self, zz):
        d = self.at.d

        @pl.when(zz < d)
        def _():
            self.down(zz).start()

        @pl.when(zz > d)
        def _():
            self.up(zz).start()

    def line_head(self, zz):
        @pl.when(jnp.logical_not(self.passes(zz)))
        def _():
            self.push(zz)

    def passes(self, zz):
        d = self.at.d
        return ((zz < d) & self.at.has_above) | ((zz > d) & self.at.has_below)

    def line_rest(self, zz):
        @pl.when(self.passes(zz))
        def _():
            self.arrive(zz).wait_recv()
            add_rows(self.buf.at[zz, 0], self.rz.at[zz])
            self.push(zz)

    def lines(self, j):
        n = self.at.n
        if j < n - 1:
            self.line_head(self.at.far(j))
        if 0 <= j - 1 < n - 2:
            self.line_rest(self.at.far(j - 1))
        if j == n - 2:
            self.line_rest(self.at.far(j))

    def last(self):
        d, n, rows, step = self.at.d, self.at.n, self.total.shape[0], 16

        def over(fn):
            @pl.loop(0, rows // step)
            def _(r):
                fn(pl.ds(pl.multiple_of(r * step, step), step))

        def own(w):
            first = self.buf[d, 0, w, :].astype(jnp.float32)
            self.total[w, :] = first if self.start is None else first + self.start[w, :]

        def more(slot):
            def fn(w):
                self.total[w, :] += self.rz[slot, w, :].astype(jnp.float32)

            self.arrive(slot).wait_recv()
            over(fn)

        over(own)

        @pl.when(self.at.has_above)
        def _():
            more(d)

        @pl.when(self.at.has_below)
        def _():
            more(n)

    def finish(self):
        d = self.at.d

        @pl.loop(0, self.at.n)
        def _(zz):
            for k in range(4):
                self.first(zz, k).wait_send()
            for k in range(2):
                self.second(zz, k).wait_send()

            @pl.when(zz != d)
            def _():
                self.arrive(zz)
                send(self.buf.at[zz, 0], self.rz.at[zz], self.sems[4].at[zz], self.sems[5].at[zz], self.at.nx).wait_send()


def reduce_scratch(n, rows, cols):
    D_ = pltpu.SemaphoreType.DMA
    V = lambda *s: pltpu.VMEM(s, jnp.bfloat16)
    return [V(n, 4, rows // 2, cols), V(n, 2, rows // 2, cols), V(n + 1, rows, cols),
            D_((n, 4)), D_((n, 4)), D_((n, 2)), D_((n, 2)), D_((n,)), D_((n + 1,))]


def expert_kernel(n, experts, x_ref, cot_ref, up_ref, down_ref, mid_ref,
                  out_ref, gx_ref, gup_ref, gdown_out,
                  gdown_ref, xb, cb, gg, mixed, gb, wup, wdown, pick_ref, place_ref, *rest):
    f32, bf16 = jnp.float32, jnp.bfloat16
    at = Place(n)
    d = at.d
    lo = x_ref.shape[0] * 3 // 4
    gather = Gather(at, x_ref, xb, *rest[:5], rows=lo)
    tail = LineGather(at, x_ref, xb, lo, *rest[-4:])
    grads = Reduce(at, gb, gx_ref, *rest[5:14])
    outs = Reduce(at, gg, out_ref, *rest[14:23], start=mid_ref)
    load_sem, core_ss, core_sr, free = rest[23:-4]
    rows = x_ref.shape[0]
    f2 = up_ref.shape[1]
    f = f2 // 2
    held = f // 128
    loads = [
        pltpu.make_async_copy(x_ref, xb.at[d, 0], load_sem.at[0]),
        pltpu.make_async_copy(up_ref, wup.at[0], load_sem.at[1]),
        pltpu.make_async_copy(down_ref, wdown.at[0], load_sem.at[2]),
        pltpu.make_async_copy(cot_ref, cb, load_sem.at[3]),
    ]
    for load in loads:
        load.start()
    at.meet()
    gather.begin_z()
    tail.begin()
    gather.begin_xy()
    swaps = [
        send(up_ref, wup.at[1], core_ss.at[0], core_sr.at[0], at.sib),
        send(down_ref, wdown.at[1], core_ss.at[1], core_sr.at[1], at.sib),
    ]
    for swap in swaps:
        swap.start()
    for h, owner in ((0, at.e), (1, at.sib[1])):
        for j in range(held):
            expert, cols = owner * held + j, slice((h * held + j) * 128, (h * held + j + 1) * 128)
            gate_row = lax.broadcasted_iota(jnp.int32, (128, 128), 0)
            pick_ref[:, cols] = ((gate_row == expert) | (gate_row == expert + experts)).astype(bf16)
            place_ref[cols, :] = (lane_tile(128) == expert).astype(bf16)
    loads[0].wait()
    tail.plane()
    tail.corner()
    gather.plane(at.near(0))
    gather.column(at.near(1))
    for load in loads[1:]:
        load.wait()
    for swap in swaps:
        swap.wait_recv()

    def tokens(ref, zz, p, lo, width):
        return ref[zz, pl.ds(2 * p, 2), :, pl.ds(lo, width)].reshape(2 * rows, width)

    def half(zz, p):
        pair = pl.ds(2 * p, 2)
        x = tokens(xb, zz, p, 0, D)
        cot = tokens(cb, zz, p, 0, D)
        mix = mm(tokens(xb, zz, p, D, 128), pick_ref[...])
        sums = jnp.zeros((2 * rows, 128), f32)
        for h in range(2):
            gate_up = mm(x, wup[h])
            back = mm(cot, wdown[h], NT)
            for j in range(held):
                k = h * held + j
                gate = gate_up[:, j * 256 : j * 256 + 128]
                up = gate_up[:, j * 256 + 128 : j * 256 + 256]
                b = back[:, j * 128 : (j + 1) * 128]
                m = mix[:, k * 128 : (k + 1) * 128]
                sig = 1.0 / (1.0 + jnp.exp(-gate))
                act = gate * sig
                hidden = (act * up).astype(bf16).astype(f32)
                prod = hidden * b
                high = prod.astype(bf16)
                low = (prod - high.astype(f32)).astype(bf16)
                sel = place_ref[k * 128 : (k + 1) * 128, :]
                sums += mm(high, sel) + mm(low, sel)
                mixed[zz, pair, :, pl.ds(k * 128, 128)] = (m * hidden).astype(bf16).reshape(2, rows, 128)
                gh = m * b
                gg[zz, pair, :, pl.ds(k * 256, 128)] = (
                    (gh * up * sig * (1.0 + gate * (1.0 - sig))).astype(bf16).reshape(2, rows, 128))
                gg[zz, pair, :, pl.ds(k * 256 + 128, 128)] = (gh * act).astype(bf16).reshape(2, rows, 128)
        for q in range(D // 512):
            cols = pl.ds(q * 512, 512)
            part = mm(tokens(gg, zz, p, 0, f2), wup[0, cols, :], NT) + mm(tokens(gg, zz, p, f2, f2), wup[1, cols, :], NT)
            gb[zz, pair, :, cols] = part.astype(bf16).reshape(2, rows, 512)
        gb[zz, pair, :, pl.ds(D, 128)] = sums.astype(bf16).reshape(2, rows, 128)

    @pl.loop(0, n)
    def _(i):
        zz = at.near(i)
        half(zz, 0)

        @pl.when(i + 2 < n)
        def _():
            gather.column(at.near(i + 2))

        @pl.when(i + 1 < n)
        def _():
            tail.line(at.near(i + 1))
            gather.plane(at.near(i + 1))

        gather.corner(zz)
        half(zz, 1)
        grads.s1(zz)

        @pl.when(i >= 1)
        def _():
            grads.s2(at.near(i - 1))

        @pl.when(i >= 2)
        def _():
            grads.s3(at.near(i - 2))
            grads.line_head(at.near(i - 2))

    pl.semaphore_signal(free.at[0], inc=1, device_id=at.sib, device_id_type=MESH)

    def grad_up(h, more):
        @pl.loop(0, D // 256)
        def _(q):
            cols = pl.ds(pl.multiple_of(q * 256, 256), 256)
            xs = xb[:, :, :, cols].reshape(n * 4 * rows, 256)
            part = mm(xs, gg[:, :, :, pl.ds(h * f2, f2)].reshape(n * 4 * rows, f2), TN)
            if more:
                part += wup[h, cols, :].astype(f32)
            wup[h, cols, :] = part.astype(bf16)

    def grad_down(h):
        for q in range(D // 512):
            cols = pl.ds(q * 512, 512)
            part = mm(mixed[:, :, :, pl.ds(h * f, f)].reshape(n * 4 * rows, f), cb[:, :, :, cols].reshape(n * 4 * rows, 512), TN)
            if h == 0:
                gdown_ref[:, cols] = part + wdown[0, :, cols].astype(f32)
            else:
                wdown[1, :, cols] = part.astype(bf16)

    def output(zz):
        @pl.loop(0, 2)
        def _(p):
            for q in range(D // 512):
                cols = pl.ds(q * 512, 512)
                part = mm(tokens(mixed, zz, p, 0, f), wdown[0, :, cols]) + mm(tokens(mixed, zz, p, f, f), wdown[1, :, cols])
                gg[zz, pl.ds(2 * p, 2), :, cols] = part.astype(bf16).reshape(2, rows, 512)

    grad_up(1, False)
    pl.semaphore_wait(free.at[0], 1)
    up_swap = send(wup.at[1], wup.at[0], core_ss.at[2], core_sr.at[2], at.sib)
    for swap in swaps:
        swap.wait_send()
    up_swap.start()
    grads.s2(at.near(n - 1))
    grads.s3(at.near(n - 2))
    grads.line_head(at.near(n - 2))
    up_swap.wait_recv()
    grad_up(0, True)
    keep = pltpu.make_async_copy(wup.at[0], gup_ref, load_sem.at[0])
    keep_down = pltpu.make_async_copy(gdown_ref, gdown_out, load_sem.at[1])
    keep.start()
    grads.s3(at.near(n - 1))
    grads.line_head(at.near(n - 1))
    for j in range(n):
        output(at.far(j))
        if j < 2:
            outs.corners(at.far(j))
    pl.semaphore_signal(free.at[1], inc=1, device_id=at.sib, device_id_type=MESH)
    grad_down(1)
    pl.semaphore_wait(free.at[1], 1)
    down_swap = send(wdown.at[1], wdown.at[0], core_ss.at[3], core_sr.at[3], at.sib)
    down_swap.start()
    for j in range(n + 1):
        if j == n:
            grads.last()
        outs.step(j)
        if j < n - 1:
            grads.line_rest(at.far(j))
        if j == 0:
            down_swap.wait_recv()
            grad_down(0)
            keep_down.start()
    outs.last()
    keep_down.wait()
    keep.wait()
    up_swap.wait_send()
    down_swap.wait_send()
    gather.finish()
    tail.finish()
    grads.finish()
    outs.finish()


def expert_layer(x, cot_all, up, down, middle, n, experts, cid):
    rows, wide = x.shape
    f2 = up.shape[1]
    f = f2 // 2
    bf16 = jnp.bfloat16
    V = lambda *s: pltpu.VMEM(s, bf16)
    D_ = pltpu.SemaphoreType.DMA
    any_, vm = pl.BlockSpec(memory_space=pl.ANY), pl.BlockSpec(memory_space=pltpu.VMEM)
    return pl.pallas_call(
        functools.partial(expert_kernel, n, experts),
        out_shape=(
            jax.ShapeDtypeStruct((rows, D), jnp.float32),
            jax.ShapeDtypeStruct((rows, wide), jnp.float32),
            jax.ShapeDtypeStruct((D, f2), bf16),
            jax.ShapeDtypeStruct((f, D), jnp.float32),
        ),
        in_specs=[any_, any_, any_, any_, vm],
        out_specs=[vm, vm, any_, any_],
        scratch_shapes=[pltpu.VMEM((f, D), jnp.float32), V(n, 4, rows, wide), V(n, 4, rows, D), V(n, 4, rows, 2 * f2), V(n, 4, rows, 2 * f), V(n, 4, rows, wide),
                        V(2, D, f2), V(2, f, D), V(128, 2 * f), V(2 * f, 128)]
        + gather_sems(n) + reduce_scratch(n, rows, wide) + reduce_scratch(n, rows, D)
        + [D_((4,)), D_((4,)), D_((4,)), pltpu.SemaphoreType.REGULAR((2,))] + line_gather_sems(n),
        compiler_params=pltpu.CompilerParams(collective_id=cid, has_side_effects=True, vmem_limit_bytes=63 << 20),
        name="expert_layer",
    )(x, cot_all, up, down, middle)


class GatherAll:
    def __init__(self, at, own, buf, send_sem, recv_z, recv_x, recv_y, recv_d, recv_s):
        self.at, self.own, self.buf = at, own, buf
        self.ss, self.rz, self.rx, self.ry, self.rd, self.rs = send_sem, recv_z, recv_x, recv_y, recv_d, recv_s
        cols = own.shape[1]
        half = (cols // 128 + 1) // 2 * 128
        self.A, self.B, self.F = pl.ds(0, half), pl.ds(half, cols - half), pl.ds(0, cols)

    def move(self, zz, e, cols, slot, sem, dev, own=False):
        dst = self.buf.at[zz * 8 + e, :, cols]
        return send(self.own.at[:, cols] if own else dst, dst, self.ss.at[zz, slot], sem, dev)

    def down(self, zz, own=False):
        return self.move(zz, self.at.e, self.F, 0, self.rz.at[zz], self.at.below, own)

    def up(self, zz, own=False):
        return self.move(zz, self.at.e, self.F, 1, self.rz.at[zz], self.at.above, own)

    def spread(self, zz, own=False):
        at = self.at
        return (self.move(zz, at.e, self.F, 2, self.rx.at[zz], at.nx, own),
                self.move(zz, at.e, self.F, 3, self.ry.at[zz], at.ny, own),
                self.move(zz, at.e, self.F, 4, self.rs.at[zz, 0], at.sib, own))

    def from_x(self, zz):
        at = self.at
        ex = at.nx[1]
        return (self.move(zz, ex, self.F, 2, self.rx.at[zz], at.nx),
                self.move(zz, ex, self.A, 5, self.rd.at[zz, 0], at.ny),
                self.move(zz, ex, self.F, 6, self.rs.at[zz, 1], at.sib))

    def from_y(self, zz):
        at = self.at
        ey = at.ny[1]
        return (self.move(zz, ey, self.F, 3, self.ry.at[zz], at.ny),
                self.move(zz, ey, self.B, 7, self.rd.at[zz, 1], at.nx),
                self.move(zz, ey, self.F, 8, self.rs.at[zz, 2], at.sib))

    def turned(self, zz):
        at = self.at
        return (self.move(zz, at.diag, self.A, 5, self.rd.at[zz, 0], at.ny),
                self.move(zz, at.diag, self.A, 9, self.rs.at[zz, 3], at.sib),
                self.move(zz, at.diag, self.B, 7, self.rd.at[zz, 1], at.nx),
                self.move(zz, at.diag, self.B, 10, self.rs.at[zz, 4], at.sib))

    def begin(self):
        d = self.at.d

        @pl.when(self.at.has_below)
        def _():
            self.down(d, True).start()

        @pl.when(self.at.has_above)
        def _():
            self.up(d, True).start()

        for copy in self.spread(d, True):
            copy.start()

    def column(self, zz):
        d = self.at.d

        @pl.when(zz < d)
        def _():
            self.up(zz).wait_recv()

            @pl.when(self.at.has_above)
            def _():
                self.up(zz).start()

        @pl.when(zz > d)
        def _():
            self.down(zz).wait_recv()

            @pl.when(self.at.has_below)
            def _():
                self.down(zz).start()

        for copy in self.spread(zz):
            copy.start()

    def plane(self, zz):
        for arrive, turn, share in (self.from_x(zz), self.from_y(zz)):
            arrive.wait_recv()
            turn.start()
            share.start()

    def corner(self, zz):
        a, share_a, b, share_b = self.turned(zz)
        a.wait_recv()
        share_a.start()
        b.wait_recv()
        share_b.start()

    def siblings(self):
        at = self.at
        es = at.sib[1]
        exs, eys, exys = es + at.nx[1] - at.e, es + at.ny[1] - at.e, es + at.diag - at.e

        @pl.loop(0, at.n)
        def _(zz):
            for e, cols, k in ((es, self.F, 0), (exs, self.F, 1), (eys, self.F, 2), (exys, self.A, 3), (exys, self.B, 4)):
                self.move(zz, e, cols, 4, self.rs.at[zz, k], at.sib).wait_recv()

    def finish(self):
        d = self.at.d

        @pl.loop(0, self.at.n)
        def _(zz):
            for group in (self.spread(zz), self.from_x(zz)[1:], self.from_y(zz)[1:], self.turned(zz)[1::2]):
                for copy in group:
                    copy.wait_send()

            @pl.when((d > 0) & (zz >= d))
            def _():
                self.down(zz).wait_send()

            @pl.when(self.at.has_above & (zz <= d))
            def _():
                self.up(zz).wait_send()


def lane_tile(rows):
    return lax.broadcasted_iota(jnp.int32, (rows, 128), 1)


def swap_halves(tile):
    front = lax.rem(lane_tile(tile.shape[0]), HEAD) < HEAD // 2
    return jnp.where(front, pltpu.roll(tile, 128 - HEAD // 2, 1), pltpu.roll(tile, HEAD // 2, 1))


def inverse_rms(v):
    return lax.rsqrt(jnp.mean(v * v, axis=1, keepdims=True) + norm_eps)


def rope_lanes(seg_ref, freq_ref, cos_ref, sin_ref):
    f32 = jnp.float32
    packs, rows = seg_ref.shape[0], seg_ref.shape[2]
    row = jnp.concatenate([seg_ref[i].astype(f32) + float(2 * rows * i) for i in range(packs)], axis=1)
    total = packs * rows
    across = jnp.broadcast_to(row, (total, total))
    same = across == jnp.transpose(across)
    source = lax.broadcasted_iota(jnp.int32, (total, total), 1)
    target = lax.broadcasted_iota(jnp.int32, (total, total), 0)
    start = jnp.min(jnp.where(same, source.astype(f32), float(total)), axis=1, keepdims=True)
    angle = (target.astype(f32) - start) * freq_ref[...]
    cos_ref[...] = jnp.cos(angle)
    front = lax.rem(source, HEAD) < HEAD // 2
    sine = jnp.sin(angle)
    sin_ref[...] = jnp.where(front, -sine, sine)
    return (same & (source <= target)).astype(f32)


def forward_kernel(n, experts, tok_ref, cot_ref, qkv_ref, proj_ref, tail_ref, ein_ref, seg_ref, route_ref, freq_ref,
                   w_all, cot_all, up_all, disp_out, mid_out, gates_out, gain_out, nf_out, q_out, k_out, v_out, p_out, mixed_out, cos_out, sin_out,
                   disp_ref, mid_ref, gates_ref, gain_ref, nf_ref, q_ref, k_ref, v_ref, p_ref, mixed_ref, cos_ref, sin_ref,
                   wv, pieces, dense_ref, *rest):
    f32, bf16 = jnp.float32, jnp.bfloat16
    at = Place(n)
    d = at.d
    dense = GatherAll(at, dense_ref, wv, *rest[:6])
    cot = Gather(at, cot_ref, cot_all, *rest[6:11])
    load_sem, a2a_ss, a2a_sr, keep_sem = rest[11:]
    q_width, k_width = HEADS * HEAD, KV_HEADS * HEAD
    groups = HEADS // KV_HEADS
    held, share = ein_ref.shape[:2]
    f = FF // n
    qkv_width = q_width + 2 * k_width
    dense_ref[:, :qkv_width] = qkv_ref[...]
    dense_ref[:, qkv_width : qkv_width + D] = proj_ref[...]
    dense_ref[:, qkv_width + D :] = tail_ref[...]
    loads = [
        pltpu.make_async_copy(dense_ref, wv.at[d * 8 + at.e], load_sem.at[0]),
        pltpu.make_async_copy(cot_ref, cot_all.at[d, 0], load_sem.at[1]),
    ]
    for load in loads:
        load.start()

    def rows_of(z):
        return up_all.at[pl.ds(pl.multiple_of(z * share, share), share), :]

    own_piece = pltpu.make_async_copy(pieces.at[d], rows_of(d), load_sem.at[2])

    def exchange(k):
        to = lax.rem(d + k, n)
        return send(pieces.at[to], rows_of(d), a2a_ss.at[k], a2a_sr.at[d], (to, at.e))

    at.meet(True)
    dense.begin()
    for q in range(n):
        for j in range(2 * held):
            lo = (j % 2) * FF + q * f
            pieces[q, :, j * f : (j + 1) * f] = ein_ref[j // 2, :, lo : lo + f]
    own_piece.start()
    allowed = rope_lanes(seg_ref, freq_ref, cos_ref, sin_ref)
    for i in range(1, n):
        dense.column(at.near(i))
        if i == n - 1:
            cot.begin_z()
            for k in range(1, n):
                exchange(k).start()
        dense.plane(at.near(i - 1))
        if i >= 2:
            dense.corner(at.near(i - 2))
    cot.begin_xy()
    dense.plane(at.near(n - 1))
    if n > 1:
        dense.corner(at.near(n - 2))
        cot.column(at.near(1))
    dense.corner(at.near(n - 1))
    for i in range(2, n):
        cot.column(at.near(i))
    for load in loads:
        load.wait()
    dense.siblings()
    keep = pltpu.make_async_copy(wv, w_all, load_sem.at[0])
    keep.start()

    def weight(lo, width):
        return wv[:, :, lo : lo + width].reshape(D, width)

    tail_at = q_width + 2 * k_width + D
    turned = jnp.transpose(weight(tail_at, 128).astype(f32))
    gain_ref[0:1, :] = turned[experts : experts + 1, :]
    gain_ref[1:2, :] = turned[experts + 1 : experts + 2, :]
    x = tok_ref[...].astype(f32)
    nf_ref[...] = (x * inverse_rms(x) * gain_ref[0:1, :]).astype(bf16)
    cos, sin = cos_ref[...], sin_ref[...]
    for q in range((q_width + 2 * k_width) // 512):
        lo = q * 512
        part = mm(nf_ref[...], weight(lo, 512))
        for t in range(4):
            tile = part[:, t * 128 : (t + 1) * 128]
            col = lo + t * 128
            if col < q_width + k_width:
                tile = tile * cos + swap_halves(tile) * sin
            ref, base = (q_ref, 0) if col < q_width else (k_ref, q_width) if col < q_width + k_width else (v_ref, q_width + k_width)
            ref[:, col - base : col - base + 128] = tile.astype(bf16)
    cot.plane(at.near(0))
    allowed = jnp.concatenate([allowed] * groups, axis=0) > 0
    for g in range(KV_HEADS):
        qs = jnp.concatenate([q_ref[:, (g * groups + j) * HEAD : (g * groups + j + 1) * HEAD] for j in range(groups)], axis=0)
        ks, vs = k_ref[:, g * HEAD : (g + 1) * HEAD], v_ref[:, g * HEAD : (g + 1) * HEAD]
        scores = jnp.where(allowed, mm(qs, ks, NT) * HEAD ** (-0.5), neg_large)
        raised = jnp.exp(scores - jnp.max(scores, axis=1, keepdims=True))
        probs = raised / jnp.sum(raised, axis=1, keepdims=True)
        p_ref[g] = probs
        out = mm(probs.astype(bf16), vs).astype(bf16)
        rows = out.shape[0] // groups
        for j in range(groups):
            mixed_ref[:, (g * groups + j) * HEAD : (g * groups + j + 1) * HEAD] = out[j * rows : (j + 1) * rows]
    for q in range(D // 512):
        lo = q * 512
        mid_ref[:, lo : lo + 512] = tok_ref[:, lo : lo + 512].astype(f32) + mm(mixed_ref[...], weight(q_width + 2 * k_width + lo, 512))
    mid = mid_ref[...]
    disp_ref[:, :D] = (mid * inverse_rms(mid) * gain_ref[1:2, :]).astype(bf16)
    logits = mm(disp_ref[:, :D], weight(tail_at, 128))
    lanes = lane_tile(mid.shape[0])
    chosen = jnp.zeros(lanes.shape, f32)
    for k in range(TOP_K):
        chosen += (route_ref[:, k : k + 1] == lanes).astype(f32)
    masked = jnp.where(chosen > 0, logits, neg_large)
    raised = jnp.where(chosen > 0, jnp.exp(masked - jnp.max(masked, axis=1, keepdims=True)), 0.0)
    gates = raised / jnp.sum(raised, axis=1, keepdims=True)
    gates_ref[...] = gates
    high = gates.astype(bf16).astype(f32)
    low = (gates - high).astype(bf16).astype(f32)
    disp_ref[:, D:] = (high + pltpu.roll(low, experts, 1)).astype(bf16)

    keeps = [pltpu.make_async_copy(src, dst, keep_sem.at[i]) for i, (src, dst) in enumerate((
        (disp_ref, disp_out), (mid_ref, mid_out), (gates_ref, gates_out), (gain_ref, gain_out), (nf_ref, nf_out), (q_ref, q_out),
        (k_ref, k_out), (v_ref, v_out), (p_ref, p_out), (mixed_ref, mixed_out), (cos_ref, cos_out), (sin_ref, sin_out)))]
    for copy in keeps:
        copy.start()
    for i in range(1, n):
        cot.plane(at.near(i))
        cot.corner(at.near(i - 1))
    cot.corner(at.near(n - 1))
    own_piece.wait()
    for k in range(1, n):
        exchange(k).wait_send()
        source = lax.rem(d + k, n)
        send(pieces.at[0], rows_of(source), a2a_ss.at[k], a2a_sr.at[source], (source, at.e)).wait_recv()
    keep.wait()
    dense.finish()
    cot.finish()
    for copy in keeps:
        copy.wait()


def forward_layer(tok, cot, attn_in, attn_out, tail, ein, segments, routes, n, experts, cid):
    f32, bf16 = jnp.float32, jnp.bfloat16
    rows = tok.shape[0]
    shard = attn_in.shape[0]
    held, share = ein.shape[:2]
    q_width, k_width = HEADS * HEAD, KV_HEADS * HEAD
    wide = q_width + 2 * k_width + D + 128
    groups = HEADS // KV_HEADS
    half = HEAD // 2
    freq = jnp.tile(rope_base ** (-jnp.arange(half, dtype=f32) / half), 128 // half)[None, :]
    D_ = pltpu.SemaphoreType.DMA
    V = lambda *s: pltpu.VMEM(s, bf16)
    any_, vm = pl.BlockSpec(memory_space=pl.ANY), pl.BlockSpec(memory_space=pltpu.VMEM)
    S = jax.ShapeDtypeStruct
    saved = (
        S((rows, D + 128), bf16), S((rows, D), f32), S((rows, 128), f32), S((8, D), f32), S((rows, D), bf16),
        S((rows, q_width), bf16), S((rows, k_width), bf16), S((rows, k_width), bf16),
        S((KV_HEADS, groups * rows, rows), f32), S((rows, q_width), bf16), S((rows, 128), f32), S((rows, 128), f32),
    )
    return pl.pallas_call(
        functools.partial(forward_kernel, n, experts),
        out_shape=(S((n * 8, shard, wide), bf16), S((n, 4, rows, D), bf16), S((D, 2 * held * (FF // n)), bf16)) + saved,
        in_specs=[vm, any_] + [vm] * 7,
        out_specs=[any_] * 15,
        scratch_shapes=[pltpu.VMEM(a.shape, a.dtype) for a in saved]
        + [V(n * 8, shard, wide), V(n, share, 2 * held * (FF // n)), V(shard, wide)]
        + [D_((n, 11)), D_((n,)), D_((n,)), D_((n,)), D_((n, 2)), D_((n, 5))] + gather_sems(n)
        + [D_((3,)), D_((n,)), D_((n,)), D_((len(saved),))],
        compiler_params=pltpu.CompilerParams(collective_id=cid, has_side_effects=True, vmem_limit_bytes=60 << 20),
        name="forward_layer",
    )(tok, cot, attn_in, attn_out, tail, ein, segments, routes, freq)


def backward_kernel(n, experts, gs_in, tok_in, cot_in, mid_in, gates_in, gain_in, nf_in, disp_in, q_in, k_in, v_in, p_in, mixed_in, cos_in, sin_in, w_ref, gup_ref,
                    gtok_ref, gout_ref, gin_ref, gtail_ref, arrived,
                    gs_ref, tok_ref, cot_ref, mid_ref, gates_ref, gain_ref, nf_ref, disp_ref, q_ref, k_ref, v_ref, p_ref, mixed_ref, cos_ref, sin_ref,
                    wv, pout, pin, tot_out, tot_in, pair, gq, gl, sums, gb, gm, flat, *rest):
    f32, bf16 = jnp.float32, jnp.bfloat16
    at = Place(n)
    d, c = at.d, at.c
    outs = Reduce(at, pout, tot_out, *rest[:9])
    ins = Reduce(at, pin, tot_in, *rest[9:18])
    load_sem, pair_ss, pair_sr, a2a_ss, a2a_sr, end_ss, end_sr, in_sem = rest[18:]
    q_width, k_width = HEADS * HEAD, KV_HEADS * HEAD
    groups = HEADS // KV_HEADS
    qkv_width = q_width + 2 * k_width
    tail_at = qkv_width + D
    rows = tok_ref.shape[0]
    shard = w_ref.shape[1]
    share = D // n
    f = FF // n
    fetched = [pltpu.make_async_copy(src, dst, in_sem.at[i]) for i, (src, dst) in enumerate((
        (mid_in, mid_ref), (gates_in, gates_ref), (gs_in, gs_ref), (gain_in, gain_ref), (cot_in, cot_ref), (mixed_in, mixed_ref), (nf_in, nf_ref), (disp_in, disp_ref), (q_in, q_ref), (k_in, k_ref), (v_in, v_ref), (p_in, p_ref), (tok_in, tok_ref), (cos_in, cos_ref), (sin_in, sin_ref)))]
    for copy in fetched[:8]:
        copy.start()
    loads = []
    for i, (lo, width) in enumerate(((tail_at, 128), (qkv_width, D), (0, qkv_width))):
        loads.append(pltpu.make_async_copy(w_ref.at[:, :, pl.ds(lo, width)], wv.at[:, :, pl.ds(lo, width)], load_sem.at[i]))
    for load in loads:
        load.start()
    for copy in fetched[8:]:
        copy.start()
    own_share = pltpu.make_async_copy(gup_ref.at[pl.ds(pl.multiple_of(d * share, share), share), :], arrived.at[d], load_sem.at[3])
    own_share.start()

    def exchange(k):
        to = lax.rem(d + k, n)
        return send(gup_ref.at[pl.ds(pl.multiple_of(to * share, share), share), :], arrived.at[d], a2a_ss.at[k], a2a_sr.at[d], (to, at.e))

    swaps = [send(src, pair.at[i], pair_ss.at[i], pair_sr.at[i], at.sib)
             for i, src in enumerate((mixed_ref, nf_ref, disp_ref.at[:, pl.ds(0, D)], gb))]
    swap_q = send(gq.at[0], gq.at[1], pair_ss.at[4], pair_sr.at[4], at.sib)
    swap_l = send(gl.at[0], gl.at[1], pair_ss.at[5], pair_sr.at[5], at.sib)
    swap_s = send(sums.at[0], sums.at[1], pair_ss.at[6], pair_sr.at[6], at.sib)
    at.meet(True)
    for k in range(1, n):
        exchange(k).start()
    for copy in fetched[:8]:
        copy.wait()
    for i in range(3):
        swaps[i].start()

    def weight(lo, width):
        return wv[:, :, lo : lo + width].reshape(D, width)

    loads[0].wait()
    mid = mid_ref[...]
    inv_second = inverse_rms(mid)
    unit = mid * inv_second
    gates, gg = gates_ref[...], gs_ref[:, D:]
    gl[0] = (gates * (gg - jnp.sum(gates * gg, axis=1, keepdims=True))).astype(bf16)
    swap_l.start()
    grad_second = mm(gl[0], weight(tail_at, 128), NT) + gs_ref[:, :D]
    pull = grad_second * gain_ref[1:2, :]
    sums[0, 1:2, :] = jnp.sum(grad_second * unit, axis=0, keepdims=True)
    grad_middle = cot_ref[...].astype(f32) + inv_second * (pull - unit * jnp.mean(pull * unit, axis=1, keepdims=True))
    gtok_ref[...] = grad_middle
    gb[...] = grad_middle.astype(bf16)
    swaps[3].start()
    loads[1].wait()
    for q in range(q_width // 512):
        gm[:, q * 512 : (q + 1) * 512] = mm(gb[...], wv[:, :, qkv_width : qkv_width + D].reshape(D, D)[q * 512 : (q + 1) * 512], NT).astype(bf16)

    def both(own, other, cols):
        return jnp.concatenate([own[:, cols], other[:, cols]], axis=0)

    def store(buf, zz, lo, value):
        blocks = value.astype(bf16).reshape(4, 2 * shard, value.shape[1])
        for a in range(4):
            slot = 2 * lax.rem(a // 2 + at.y, 2) + lax.rem(a % 2 + at.x, 2)
            buf[zz, slot, :, lo : lo + value.shape[1]] = blocks[a]

    def row_cols(zz):
        return pl.ds(pl.multiple_of(zz * share, 128), share)

    half_out, half_in = D // 2, qkv_width // 2
    swaps[0].wait_recv()
    swaps[3].wait_recv()

    @pl.loop(0, n)
    def _(j):
        zz = at.far(j)
        branch = both(gb, pair.at[3], pl.ds(pl.multiple_of(c * half_out, 128), half_out))
        store(pout, zz, 0, mm(both(mixed_ref, pair.at[0], row_cols(zz)), branch, TN))
        outs.s1(zz)

    for copy in fetched[8:]:
        copy.wait()
    scale = HEAD ** (-0.5)
    for g in range(KV_HEADS):
        heads = [slice((g * groups + j) * HEAD, (g * groups + j + 1) * HEAD) for j in range(groups)]
        kv = slice(g * HEAD, (g + 1) * HEAD)
        qs = jnp.concatenate([q_ref[:, h] for h in heads], axis=0)
        ms = jnp.concatenate([gm[:, h] for h in heads], axis=0)
        ks, vs = k_ref[:, kv], v_ref[:, kv]
        probs = p_ref[g]
        grad_values = mm(probs.astype(bf16), ms, TN)
        grad_probs = mm(ms, vs, NT)
        grad_scores = (probs * (grad_probs - jnp.sum(probs * grad_probs, axis=1, keepdims=True))).astype(bf16)
        grad_query = mm(grad_scores, ks) * scale
        for j, h in enumerate(heads):
            flat[:, h] = grad_query[j * rows : (j + 1) * rows]
        flat[:, q_width + kv.start : q_width + kv.stop] = mm(grad_scores, qs, TN) * scale
        flat[:, q_width + k_width + kv.start : q_width + k_width + kv.stop] = grad_values
    for j in range(n):
        outs.s2(at.far(j))
    cos, sin = cos_ref[...], sin_ref[...]
    for t in range(qkv_width // 128):
        tile = flat[:, t * 128 : (t + 1) * 128]
        if t * 128 < q_width + k_width:
            tile = tile * cos - swap_halves(tile) * sin
        gq[0, :, t * 128 : (t + 1) * 128] = tile.astype(bf16)
    swap_q.start()
    loads[2].wait()
    x = tok_ref[...].astype(f32)
    inv_first = inverse_rms(x)
    unit = x * inv_first
    grad_first = jnp.concatenate(
        [mm(gq[0], wv[8 * i : 8 * (i + 1), :, :qkv_width].reshape(8 * shard, qkv_width), NT) for i in range(n)], axis=1)
    pull = grad_first * gain_ref[0:1, :]
    sums[0, 0:1, :] = jnp.sum(grad_first * unit, axis=0, keepdims=True)
    sums[0, 2:, :] = jnp.zeros((6, D), f32)
    swap_s.start()
    gtok_ref[...] += inv_first * (pull - unit * jnp.mean(pull * unit, axis=1, keepdims=True))
    for i in (1, 2):
        swaps[i].wait_recv()
    swap_l.wait_recv()
    swap_q.wait_recv()
    swap_s.wait_recv()
    gains = sums[0] + sums[1]
    high = gains.astype(bf16)
    low = (gains - high.astype(f32)).astype(bf16)
    swap_s.wait_send()
    sums[0] = high.astype(f32)
    sums[1] = low.astype(f32)
    line = lax.rem(lax.broadcasted_iota(jnp.int32, (16, 128), 0), 8)
    where = (((line == 0) & (lane_tile(16) == experts)) | ((line == 1) & (lane_tile(16) == experts + 1))).astype(bf16)

    @pl.loop(0, n)
    def _(j):
        zz = at.far(j)
        cols = row_cols(zz)
        normed = both(nf_ref, pair.at[1], cols)
        for q in range(2):
            part = pl.ds(pl.multiple_of(c * half_in + q * (half_in // 2), 128), half_in // 2)
            grad = jnp.concatenate([gq[0, :, part], gq[1, :, part]], axis=0)
            store(pin, zz, q * (half_in // 2), mm(normed, grad, TN))
        tail = mm(both(disp_ref, pair.at[2], cols), jnp.concatenate([gl[0], gl[1]], axis=0), TN)
        rows_now = jnp.concatenate([sums[0, :, cols], sums[1, :, cols]], axis=0).astype(bf16)
        store(pin, zz, half_in, tail + mm(rows_now, where, TN))

        @pl.when(j < 2)
        def _():
            ins.corners(zz)

    for j in range(n + 1):
        ins.step(j)
        if j < n:
            outs.s3(at.far(j))
            outs.lines(j)
    outs.last()
    mine, theirs = pl.ds(pl.multiple_of(c * shard, 8), shard), pl.ds(pl.multiple_of((1 - c) * shard, 8), shard)
    cols_out, cols_in = pl.ds(pl.multiple_of(c * half_out, 128), half_out), pl.ds(pl.multiple_of(c * half_in, 128), half_in)
    end_out = send(tot_out.at[theirs, :], gout_ref.at[:, cols_out], end_ss.at[0], end_sr.at[0], at.sib)
    end_out.start()
    gout_ref[:, cols_out] = tot_out[mine, :]
    ins.last()
    end_in = send(tot_in.at[theirs, pl.ds(0, half_in)], gin_ref.at[:, cols_in], end_ss.at[1], end_sr.at[1], at.sib)
    end_in.start()
    gin_ref[:, cols_in] = tot_in[mine, :half_in]
    gtail_ref[...] = tot_in[mine, half_in:]
    own_share.wait()
    for k in range(1, n):
        exchange(k).wait_send()
        source = lax.rem(d + k, n)
        send(gup_ref.at[pl.ds(0, share), :], arrived.at[source], a2a_ss.at[k], a2a_sr.at[source], (source, at.e)).wait_recv()

    end_out.wait()
    end_in.wait()
    for swap in swaps + [swap_q, swap_l]:
        swap.wait_send()
    outs.finish()
    ins.finish()


def backward_layer(gs, tok, cot, mid, gates, gain, nf, disp, q, k, v, p, mixed, cos, sin, w_all, gup, n, experts, cid):
    f32, bf16 = jnp.float32, jnp.bfloat16
    rows = tok.shape[0]
    shard, wide = w_all.shape[1:]
    qkv_width = (HEADS + 2 * KV_HEADS) * HEAD
    share = D // n
    D_ = pltpu.SemaphoreType.DMA
    V = lambda *s: pltpu.VMEM(s, bf16)
    W = lambda *s: pltpu.VMEM(s, f32)
    any_, vm = pl.BlockSpec(memory_space=pl.ANY), pl.BlockSpec(memory_space=pltpu.VMEM)
    S = jax.ShapeDtypeStruct
    width_out, width_in = D // 2, qkv_width // 2 + 128
    return pl.pallas_call(
        functools.partial(backward_kernel, n, experts),
        out_shape=(S((rows, D), f32), S((shard, D), f32), S((shard, qkv_width), f32), S((shard, 128), f32), S((n, share, gup.shape[1]), bf16)),
        in_specs=[any_] * 17,
        out_specs=[vm] * 4 + [any_],
        scratch_shapes=[pltpu.VMEM(a.shape, a.dtype) for a in (gs, tok, cot, mid, gates, gain, nf, disp, q, k, v, p, mixed, cos, sin)]
        + [V(n * 8, shard, wide), V(n, 4, 2 * shard, width_out), V(n, 4, 2 * shard, width_in),
                        W(2 * shard, width_out), W(2 * shard, width_in),
                        V(4, rows, D), V(2, rows, qkv_width), V(2, rows, 128), W(2, 8, D), V(rows, D), V(rows, D), W(rows, qkv_width)]
        + reduce_scratch(n, 2 * shard, width_out) + reduce_scratch(n, 2 * shard, width_in)
        + [D_((4,)), D_((7,)), D_((7,)), D_((n,)), D_((n,)), D_((2,)), D_((2,)), D_((15,))],
        compiler_params=pltpu.CompilerParams(collective_id=cid, has_side_effects=True, vmem_limit_bytes=62 << 20),
        name="backward_layer",
    )(gs, tok, cot, mid, gates, gain, nf, disp, q, k, v, p, mixed, cos, sin, w_all, gup)


def results_kernel(experts, arrived, tok_in, down_in, out_in, qkv_in, tail_in,
                   up_ref, tok_ref, down_ref, proj_ref, qkv_ref, router_ref, gains_ref):
    n, width = arrived.shape[0], arrived.shape[2]
    f = FF // n
    for q in range(n):
        for j in range(width // f):
            lo = (j % 2) * FF + q * f
            up_ref[j // 2, :, lo : lo + f] = arrived[q, :, j * f : (j + 1) * f].astype(jnp.float32)

    tok_ref[...] = tok_in[...]
    down_ref[...] = down_in[...]

    @pl.when(pl.program_id(0) == 0)
    def _():
        proj_ref[...] = out_in[...]
        qkv_ref[...] = qkv_in[...]
        router_ref[...] = tail_in[:, :experts]
        turned = jnp.transpose(jnp.concatenate([tail_in[...], jnp.zeros((128 - tail_in.shape[0], 128), jnp.float32)], axis=0))
        gains_ref[...] = turned[experts : experts + 8, : tail_in.shape[0]]


def results(arrived, tok, down, proj, qkv, tail, held, experts):
    n, share, width = arrived.shape
    f32 = jnp.float32
    steps = 4
    rows = share // steps
    whole = lambda a: pl.BlockSpec(a.shape, lambda i: (0,) * len(a.shape))
    part = lambda a: pl.BlockSpec((a.shape[0] // steps, a.shape[1]), lambda i: (i, 0))
    shapes = [jax.ShapeDtypeStruct(a.shape, f32) for a in (tok, down, proj, qkv)]
    shapes += [jax.ShapeDtypeStruct((tail.shape[0], experts), f32), jax.ShapeDtypeStruct((8, tail.shape[0]), f32)]
    return pl.pallas_call(
        functools.partial(results_kernel, experts),
        grid=(steps,),
        out_shape=[jax.ShapeDtypeStruct((held, share, 2 * FF), f32)] + shapes,
        in_specs=[pl.BlockSpec((n, rows, width), lambda i: (0, i, 0))] + [part(a) for a in (tok, down)] + [whole(a) for a in (proj, qkv, tail)],
        out_specs=[pl.BlockSpec((held, rows, 2 * FF), lambda i: (0, i, 0))] + [part(a) for a in (tok, down)] + [whole(a) for a in shapes[2:]],
        compiler_params=pltpu.CompilerParams(vmem_limit_bytes=62 << 20),
        name="results",
    )(arrived, tok, down, proj, qkv, tail)


def per_device_fast(n, tokens, segments, routes, cotangent, gain_attn, attn_in, attn_out, gain_ffn, router, expert_in, expert_out):
    f32, bf16 = jnp.float32, jnp.bfloat16
    micro, rows = tokens.shape[:2]
    total = micro * rows
    held = expert_in.shape[0]
    experts = held * 8
    f = FF // n
    shard = attn_in.shape[0]
    x = tokens.reshape(total, D)
    cot = cotangent.reshape(total, D)
    tail = jnp.concatenate([router, gain_attn[:, None], gain_ffn[:, None], jnp.zeros((shard, 126 - experts), bf16)], axis=1)
    w_all, cot_all, up, disp, middle, gates, gain, nf, q, k, v, p, mixed, cos, sin = forward_layer(
        x, cot, attn_in, attn_out, tail, expert_in, segments, routes.reshape(total, TOP_K), n, experts, 0)
    out, grad_sum, grad_up, grad_down = expert_layer(disp, cot_all, up, expert_out.reshape(held * f, D), middle, n, experts, 1)
    grad_tokens, grad_out, grad_in, grad_tail, grad_up = backward_layer(
        grad_sum, x, cot, middle, gates, gain, nf, disp, q, k, v, p, mixed, cos, sin, w_all, grad_up, n, experts, 2)
    grad_up, grad_tokens, grad_down, grad_out, grad_in, grad_router, grad_gains = results(
        grad_up, grad_tokens, grad_down, grad_out, grad_in, grad_tail, held, experts)
    return (
        out.astype(bf16).reshape(micro, rows, D),
        grad_tokens.reshape(micro, rows, D),
        grad_gains[0],
        grad_in,
        grad_out,
        grad_gains[1],
        grad_router,
        grad_up,
        grad_down.reshape(held, f, D),
    )


def solution(mesh):
    placed = (
        P(None, ("dp", "expert"), None),
        P(None, ("dp", "expert"), None),
        P(None, ("dp", "expert"), None),
        P(None, ("dp", "expert"), None),
        P(("dp", "expert")),
        P(("dp", "expert"), None),
        P(("dp", "expert"), None),
        P(("dp", "expert")),
        P(("dp", "expert"), None),
        P("expert", "dp", None),
        P("expert", "dp", None),
    )
    fast = mesh.shape["expert"] == 8 and FF // mesh.shape["dp"] == 128
    body = functools.partial(per_device_fast, mesh.shape["dp"]) if fast else per_device
    return jax.shard_map(
        body,
        mesh=mesh,
        in_specs=placed,
        out_specs=(
            P(None, ("dp", "expert"), None),
            P(None, ("dp", "expert"), None),
            P(("dp", "expert")),
            P(("dp", "expert"), None),
            P(("dp", "expert"), None),
            P(("dp", "expert")),
            P(("dp", "expert"), None),
            P("expert", "dp", None),
            P("expert", "dp", None),
        ),
        check_vma=False,
    )
```

```python
import functools

import jax
import jax.numpy as jnp
from jax import lax
from jax.experimental import pallas as pl
from jax.experimental.pallas import tpu as pltpu
from jax.sharding import PartitionSpec as P

MESH = pl.DeviceIdType.MESH

D = 1536
HEADS = 24
KV_HEADS = 8
HEAD = 64
FF = 512
TOP_K = 8


norm_eps = 1e-06
rope_base = 10000.0
neg_large = -1e30
highest = lax.Precision.HIGHEST


def rope_tables(segment, half_width):
    row_count = segment.shape[0]
    places = jnp.arange(row_count, dtype=jnp.int32)
    same_seq = segment[:, None] == segment[None, :]
    seq_start = jnp.min(jnp.where(same_seq, places[None, :], row_count), axis=1)
    offset = (places - seq_start).astype(jnp.float32)
    frequencies = rope_base ** (-jnp.arange(half_width, dtype=jnp.float32) / half_width)
    angles = offset[:, None] * frequencies[None, :]
    causal = same_seq & (places[None, :] <= places[:, None])
    return (jnp.cos(angles), jnp.sin(angles), causal)


def rotate(operand, cosine, sine_table):
    half_width = operand.shape[-1] // 2
    front_part = operand[..., :half_width]
    back_part = operand[..., half_width:]
    return jnp.concatenate(
        [
            front_part * cosine - back_part * sine_table,
            back_part * cosine + front_part * sine_table,
        ],
        axis=-1,
    )


def unrotate(gradient, cosine, sine_table):
    half_width = gradient.shape[-1] // 2
    front_part = gradient[..., :half_width]
    back_part = gradient[..., half_width:]
    return jnp.concatenate(
        [
            front_part * cosine + back_part * sine_table,
            back_part * cosine - front_part * sine_table,
        ],
        axis=-1,
    )


def slot_targets(route_now, expert_count, capacity):
    flat_ids = route_now.reshape(-1)
    onehot = (flat_ids[:, None] == jnp.arange(expert_count, dtype=jnp.int32)[None, :]).astype(
        jnp.int32
    )
    earlier = jnp.cumsum(onehot, axis=0) - onehot
    slot_index = jnp.sum(earlier * onehot, axis=1)
    return flat_ids * capacity + slot_index


def dense_fetch(gain_attn, attn_in, attn_out, gain_ffn, router):
    return (
        lax.all_gather(gain_attn, ("dp", "expert"), axis=0, tiled=True),
        lax.all_gather(attn_in, ("dp", "expert"), axis=0, tiled=True),
        lax.all_gather(attn_out, ("dp", "expert"), axis=0, tiled=True),
        lax.all_gather(gain_ffn, ("dp", "expert"), axis=0, tiled=True),
        lax.all_gather(router, ("dp", "expert"), axis=0, tiled=True),
    )


def expert_fetch(expert_in, expert_out):
    return (
        lax.all_gather(expert_in, "dp", axis=1, tiled=True),
        lax.all_gather(expert_out, "dp", axis=1, tiled=True),
    )


def dense_reduce(grad_set):
    return (
        lax.psum_scatter(grad_set[0], ("dp", "expert"), scatter_dimension=0, tiled=True),
        lax.psum_scatter(grad_set[1], ("dp", "expert"), scatter_dimension=0, tiled=True),
        lax.psum_scatter(grad_set[2], ("dp", "expert"), scatter_dimension=0, tiled=True),
        lax.psum_scatter(grad_set[3], ("dp", "expert"), scatter_dimension=0, tiled=True),
        lax.psum_scatter(grad_set[4], ("dp", "expert"), scatter_dimension=0, tiled=True),
    )


def expert_reduce(grad_set):
    return (
        lax.psum_scatter(grad_set[0], "dp", scatter_dimension=1, tiled=True),
        lax.psum_scatter(grad_set[1], "dp", scatter_dimension=1, tiled=True),
    )


def attention_scores(queries, key_rot, causal):
    score_scale = HEAD ** (-0.5)
    scores = (
        jnp.einsum("tkgh,skh->kgts", queries, key_rot, preferred_element_type=jnp.float32)
        * score_scale
    )
    return jnp.where(causal[None, None], scores, neg_large)


def forward_micro(tokens_now, segment, route_now, dense_set, expert_set, shapes):
    expert_count, capacity, group_count, local_experts = shapes
    gain_attn, qkv_weight, out_weight, gain_ffn, router_weight = dense_set
    expert_up, expert_down = expert_set
    row_count = tokens_now.shape[0]
    groups = HEADS // KV_HEADS
    q_width = HEADS * HEAD
    k_width = KV_HEADS * HEAD
    inputs = tokens_now.astype(jnp.float32)
    inv_first = lax.rsqrt(jnp.mean(inputs * inputs, axis=1, keepdims=True) + norm_eps)
    normed_first = (inputs * inv_first * gain_attn.astype(jnp.float32)).astype(jnp.bfloat16)
    qkv_full = jnp.dot(normed_first, qkv_weight, preferred_element_type=jnp.float32)
    cosine, sine_table, causal = rope_tables(segment, HEAD // 2)
    queries = rotate(
        qkv_full[:, :q_width].reshape(row_count, KV_HEADS, groups, HEAD),
        cosine[:, None, None, :],
        sine_table[:, None, None, :],
    ).astype(jnp.bfloat16)
    key_rot = rotate(
        qkv_full[:, q_width : q_width + k_width].reshape(row_count, KV_HEADS, HEAD),
        cosine[:, None, :],
        sine_table[:, None, :],
    ).astype(jnp.bfloat16)
    values = (
        qkv_full[:, q_width + k_width :].reshape(row_count, KV_HEADS, HEAD).astype(jnp.bfloat16)
    )
    scores = attention_scores(queries, key_rot, causal)
    score_peak = jnp.max(scores, axis=-1, keepdims=True)
    exp_scores = jnp.exp(scores - score_peak)
    exp_total = jnp.sum(exp_scores, axis=-1, keepdims=True)
    log_total = score_peak + jnp.log(exp_total)
    soft_probs = (exp_scores / exp_total).astype(jnp.bfloat16)
    attn_mixed = jnp.einsum(
        "kgts,skh->tkgh", soft_probs, values, preferred_element_type=jnp.float32
    )
    attn_mixed = attn_mixed.reshape(row_count, q_width).astype(jnp.bfloat16)
    middle = inputs + jnp.dot(attn_mixed, out_weight, preferred_element_type=jnp.float32)
    inv_second = lax.rsqrt(jnp.mean(middle * middle, axis=1, keepdims=True) + norm_eps)
    normed_second = (middle * inv_second * gain_ffn.astype(jnp.float32)).astype(jnp.bfloat16)
    logits = jnp.dot(normed_second, router_weight, preferred_element_type=jnp.float32)
    chosen = (
        route_now[:, :, None] == jnp.arange(expert_count, dtype=jnp.int32)[None, None, :]
    ).astype(jnp.float32)
    picked_logits = jnp.sum(chosen * logits[:, None, :], axis=-1)
    gate_values = jax.nn.softmax(picked_logits, axis=-1)
    targets = slot_targets(route_now, expert_count, capacity)
    source_rows = jnp.repeat(normed_second, TOP_K, axis=0)
    buffer = jnp.zeros((expert_count * capacity, D), jnp.bfloat16).at[targets].set(source_rows)
    send_rows = buffer.reshape(group_count, local_experts, capacity, D)
    received = lax.all_to_all(send_rows, "expert", split_axis=0, concat_axis=0, tiled=True)
    gate_up = jnp.einsum("secd,edf->secf", received, expert_up, preferred_element_type=jnp.float32)
    hidden = (jax.nn.silu(gate_up[..., :FF]) * gate_up[..., FF:]).astype(jnp.bfloat16)
    expert_result = jnp.einsum(
        "secf,efd->secd", hidden, expert_down, preferred_element_type=jnp.float32
    ).astype(jnp.bfloat16)
    returned = lax.all_to_all(expert_result, "expert", split_axis=0, concat_axis=0, tiled=True)
    picked = returned.reshape(expert_count * capacity, D)[targets].reshape(row_count, TOP_K, D)
    moe_sum = jnp.einsum(
        "tk,tkd->td", gate_values, picked, precision=highest, preferred_element_type=jnp.float32
    )
    result = (middle + moe_sum).astype(jnp.bfloat16)
    saved_state = (
        inputs,
        inv_first,
        normed_first,
        queries,
        key_rot,
        values,
        log_total,
        causal,
        cosine,
        sine_table,
        attn_mixed,
        middle,
        inv_second,
        normed_second,
        chosen,
        gate_values,
        targets,
        received,
        gate_up,
        hidden,
        picked,
    )
    return (result, saved_state)


def backward_micro(saved_state, cotan_now, dense_set, expert_set, shapes):
    expert_count, capacity, group_count, local_experts = shapes
    (
        inputs,
        inv_first,
        normed_first,
        queries,
        key_rot,
        values,
        log_total,
        causal,
        cosine,
        sine_table,
        attn_mixed,
        middle,
        inv_second,
        normed_second,
        chosen,
        gate_values,
        targets,
        received,
        gate_up,
        hidden,
        picked,
    ) = saved_state
    gain_attn, qkv_weight, out_weight, gain_ffn, router_weight = dense_set
    expert_up, expert_down = expert_set
    row_count = inputs.shape[0]
    groups = HEADS // KV_HEADS
    q_width = HEADS * HEAD
    k_width = KV_HEADS * HEAD
    score_scale = HEAD ** (-0.5)
    upstream = cotan_now.astype(jnp.float32)
    grad_gates = jnp.einsum(
        "td,tkd->tk", upstream, picked, precision=highest, preferred_element_type=jnp.float32
    )
    grad_picked = gate_values * (
        grad_gates - jnp.sum(gate_values * grad_gates, axis=-1, keepdims=True)
    )
    grad_logits = jnp.sum(chosen * grad_picked[:, :, None], axis=1).astype(jnp.bfloat16)
    grad_router = jnp.einsum(
        "td,te->de", normed_second, grad_logits, preferred_element_type=jnp.float32
    )
    grad_second = jnp.einsum(
        "te,de->td", grad_logits, router_weight, preferred_element_type=jnp.float32
    )
    grad_slots = (
        (gate_values[:, :, None] * upstream[:, None, :])
        .astype(jnp.bfloat16)
        .reshape(row_count * TOP_K, D)
    )
    grad_buffer = jnp.zeros((expert_count * capacity, D), jnp.bfloat16).at[targets].set(grad_slots)
    grad_buffer = grad_buffer.reshape(group_count, local_experts, capacity, D)
    grad_result = lax.all_to_all(grad_buffer, "expert", split_axis=0, concat_axis=0, tiled=True)
    grad_hidden = jnp.einsum(
        "secd,efd->secf", grad_result, expert_down, preferred_element_type=jnp.float32
    )
    grad_down = jnp.einsum(
        "secf,secd->efd", hidden, grad_result, preferred_element_type=jnp.float32
    )
    gate_part = gate_up[..., :FF]
    up_part = gate_up[..., FF:]
    gate_sigmoid = jax.nn.sigmoid(gate_part)
    grad_gate = grad_hidden * up_part * gate_sigmoid * (1.0 + gate_part * (1.0 - gate_sigmoid))
    grad_up_part = grad_hidden * (gate_part * gate_sigmoid)
    grad_gate_up = jnp.concatenate([grad_gate, grad_up_part], axis=-1).astype(jnp.bfloat16)
    grad_up = jnp.einsum(
        "secd,secf->edf", received, grad_gate_up, preferred_element_type=jnp.float32
    )
    grad_rows = jnp.einsum(
        "secf,edf->secd", grad_gate_up, expert_up, preferred_element_type=jnp.float32
    ).astype(jnp.bfloat16)
    grad_back = lax.all_to_all(grad_rows, "expert", split_axis=0, concat_axis=0, tiled=True)
    grad_choice = grad_back.reshape(expert_count * capacity, D)[targets].reshape(
        row_count, TOP_K, D
    )
    grad_second = grad_second + jnp.sum(grad_choice, axis=1, dtype=jnp.float32)
    unit_second = middle * inv_second
    pull_second = grad_second * gain_ffn.astype(jnp.float32)
    grad_gain_ffn = jnp.sum(grad_second * unit_second, axis=0)
    grad_middle = upstream + inv_second * (
        pull_second - unit_second * jnp.mean(pull_second * unit_second, axis=1, keepdims=True)
    )
    grad_branch = grad_middle.astype(jnp.bfloat16)
    grad_out_weight = jnp.einsum(
        "tc,td->cd", attn_mixed, grad_branch, preferred_element_type=jnp.float32
    )
    grad_mixed = jnp.einsum(
        "td,cd->tc", grad_branch, out_weight, preferred_element_type=jnp.float32
    )
    grad_mixed = grad_mixed.astype(jnp.bfloat16).reshape(row_count, KV_HEADS, groups, HEAD)
    scores = attention_scores(queries, key_rot, causal)
    soft_probs = jnp.exp(scores - log_total)
    grad_values = jnp.einsum(
        "kgts,tkgh->skh",
        soft_probs.astype(jnp.bfloat16),
        grad_mixed,
        preferred_element_type=jnp.float32,
    )
    grad_probs = jnp.einsum(
        "tkgh,skh->kgts", grad_mixed, values, preferred_element_type=jnp.float32
    )
    grad_scores = soft_probs * (
        grad_probs - jnp.sum(soft_probs * grad_probs, axis=-1, keepdims=True)
    )
    grad_scores = grad_scores.astype(jnp.bfloat16)
    grad_query = (
        jnp.einsum("kgts,skh->tkgh", grad_scores, key_rot, preferred_element_type=jnp.float32)
        * score_scale
    )
    grad_key = (
        jnp.einsum("kgts,tkgh->skh", grad_scores, queries, preferred_element_type=jnp.float32)
        * score_scale
    )
    grad_query = unrotate(grad_query, cosine[:, None, None, :], sine_table[:, None, None, :])
    grad_key = unrotate(grad_key, cosine[:, None, :], sine_table[:, None, :])
    grad_qkv = jnp.concatenate(
        [
            grad_query.reshape(row_count, q_width),
            grad_key.reshape(row_count, k_width),
            grad_values.reshape(row_count, k_width),
        ],
        axis=1,
    ).astype(jnp.bfloat16)
    grad_qkv_weight = jnp.einsum(
        "tc,tq->cq", normed_first, grad_qkv, preferred_element_type=jnp.float32
    )
    grad_first = jnp.einsum("tq,cq->tc", grad_qkv, qkv_weight, preferred_element_type=jnp.float32)
    unit_first = inputs * inv_first
    pull_first = grad_first * gain_attn.astype(jnp.float32)
    grad_gain_attn = jnp.sum(grad_first * unit_first, axis=0)
    grad_inputs = grad_middle + inv_first * (
        pull_first - unit_first * jnp.mean(pull_first * unit_first, axis=1, keepdims=True)
    )
    dense_grads = (grad_gain_attn, grad_qkv_weight, grad_out_weight, grad_gain_ffn, grad_router)
    expert_grads = (grad_up, grad_down)
    return (grad_inputs, dense_grads, expert_grads)


def add_pair(left_part, right_part):
    return left_part + right_part


def per_device(
    tokens,
    segments,
    routes,
    cotangent,
    gain_attn,
    attn_in,
    attn_out,
    gain_ffn,
    router,
    expert_in,
    expert_out,
):
    local_experts = expert_in.shape[0]
    group_count = lax.axis_size("expert")
    expert_count = local_experts * group_count
    micro_count = tokens.shape[0]
    row_count = tokens.shape[1]
    capacity = (row_count * TOP_K * 5 // (4 * expert_count) + 7) // 8 * 8
    shapes = (expert_count, capacity, group_count, local_experts)
    outputs = []
    grad_list = []
    dense_total = None
    expert_total = None
    for micro_index in range(micro_count):
        dense_set = dense_fetch(gain_attn, attn_in, attn_out, gain_ffn, router)
        expert_set = expert_fetch(expert_in, expert_out)
        result, saved_state = forward_micro(
            tokens[micro_index],
            segments[micro_index, 0],
            routes[micro_index],
            dense_set,
            expert_set,
            shapes,
        )
        dense_set = dense_fetch(gain_attn, attn_in, attn_out, gain_ffn, router)
        expert_set = expert_fetch(expert_in, expert_out)
        grad_inputs, dense_grads, expert_grads = backward_micro(
            saved_state, cotangent[micro_index], dense_set, expert_set, shapes
        )
        dense_grads = dense_reduce(dense_grads)
        expert_grads = expert_reduce(expert_grads)
        if dense_total is None:
            dense_total = dense_grads
            expert_total = expert_grads
        else:
            dense_total = jax.tree.map(add_pair, dense_total, dense_grads)
            expert_total = jax.tree.map(add_pair, expert_total, expert_grads)
        outputs.append(result)
        grad_list.append(grad_inputs)
    return (
        jnp.stack(outputs, axis=0),
        jnp.stack(grad_list, axis=0),
        dense_total[0],
        dense_total[1],
        dense_total[2],
        dense_total[3],
        dense_total[4],
        expert_total[0],
        expert_total[1],
    )


NN = (((1,), (0,)), ((), ()))
NT = (((1,), (1,)), ((), ()))
TN = (((0,), (0,)), ((), ()))


def mm(a, b, dims=NN):
    return lax.dot_general(a, b, dims, preferred_element_type=jnp.float32)


class Place:
    def __init__(self, n):
        self.n = n
        d = self.d = lax.axis_index("dp")
        e = self.e = lax.axis_index("expert")
        c, x, y = lax.rem(e, 2), lax.rem(lax.div(e, 2), 2), lax.div(e, 4)
        self.sib = (d, e + 1 - 2 * c)
        self.nx = (d, e + 2 - 4 * x)
        self.ny = (d, e + 4 - 8 * y)
        self.diag = self.nx[1] + 4 - 8 * y
        self.c, self.x, self.y = c, x, y
        self.below = (d - 1, e)
        self.above = (d + 1, e)
        self.has_below = d > 0
        self.has_above = d < n - 1

    def meet(self, everyone=False):
        barrier = pltpu.get_barrier_semaphore()
        d, n = self.d, self.n
        if everyone:
            others = n - 1 + 3

            @pl.loop(1, n)
            def _(k):
                pl.semaphore_signal(barrier, inc=1, device_id=(lax.rem(d + k, n), self.e), device_id_type=MESH)
        else:
            others = 3 + jnp.minimum(d, 1) + jnp.minimum(n - 1 - d, 1)

            @pl.when(self.has_below)
            def _():
                pl.semaphore_signal(barrier, inc=1, device_id=self.below, device_id_type=MESH)

            @pl.when(self.has_above)
            def _():
                pl.semaphore_signal(barrier, inc=1, device_id=self.above, device_id_type=MESH)

        for dev in (self.sib, self.nx, self.ny):
            pl.semaphore_signal(barrier, inc=1, device_id=dev, device_id_type=MESH)
        pl.semaphore_wait(barrier, others)

    def far(self, i):
        n, d = self.n, self.d
        low = d < n - d
        m = jnp.where(low, d, n - 1 - d)
        t = jnp.where(i < n - 1 - m, n - 1 - i, jnp.where(i < n - 1, i - (n - 1 - m), m))
        return jnp.where(low, t, n - 1 - t)

    def near(self, i):
        return self.far(self.n - 1 - i)


def send(src, dst, ss, rs, dev):
    return pltpu.make_async_remote_copy(src, dst, ss, rs, device_id=dev, device_id_type=MESH)


class Gather:
    def __init__(self, at, own, buf, send_sem, recv_z, recv_x, recv_y, recv_d, rows=None):
        self.at, self.own, self.buf = at, own, buf
        self.ss, self.rz, self.rx, self.ry, self.rd = send_sem, recv_z, recv_x, recv_y, recv_d
        rows = rows or own.shape[0]
        self.F, self.A, self.B = pl.ds(0, rows), pl.ds(0, rows // 2), pl.ds(rows // 2, rows // 2)

    def source(self, zz, own):
        return self.own.at[self.F] if own else self.buf.at[zz, 0, self.F]

    def down(self, zz, own=False):
        return send(self.source(zz, own), self.buf.at[zz, 0, self.F], self.ss.at[zz, 0], self.rz.at[zz], self.at.below)

    def up(self, zz, own=False):
        return send(self.source(zz, own), self.buf.at[zz, 0, self.F], self.ss.at[zz, 1], self.rz.at[zz], self.at.above)

    def to_x(self, zz, own=False):
        return send(self.source(zz, own), self.buf.at[zz, 1, self.F], self.ss.at[zz, 2], self.rx.at[zz], self.at.nx)

    def to_y(self, zz, own=False):
        return send(self.source(zz, own), self.buf.at[zz, 2, self.F], self.ss.at[zz, 3], self.ry.at[zz], self.at.ny)

    def turn_y(self, zz):
        return send(self.buf.at[zz, 1, self.A], self.buf.at[zz, 3, self.A], self.ss.at[zz, 4], self.rd.at[zz, 0], self.at.ny)

    def turn_x(self, zz):
        return send(self.buf.at[zz, 2, self.B], self.buf.at[zz, 3, self.B], self.ss.at[zz, 5], self.rd.at[zz, 1], self.at.nx)

    def begin(self):
        self.begin_z()
        self.begin_xy()

    def begin_z(self):
        d = self.at.d

        @pl.when(self.at.has_below)
        def _():
            self.down(d, True).start()

        @pl.when(self.at.has_above)
        def _():
            self.up(d, True).start()

    def begin_xy(self):
        self.to_x(self.at.d, True).start()
        self.to_y(self.at.d, True).start()

    def column_z(self, zz):
        d = self.at.d

        @pl.when(zz < d)
        def _():
            self.up(zz).wait_recv()

            @pl.when(self.at.has_above)
            def _():
                self.up(zz).start()

        @pl.when(zz > d)
        def _():
            self.down(zz).wait_recv()

            @pl.when(self.at.has_below)
            def _():
                self.down(zz).start()

    def column_xy(self, zz):
        self.to_x(zz).start()
        self.to_y(zz).start()

    def column(self, zz):
        self.column_z(zz)
        self.column_xy(zz)

    def plane(self, zz):
        self.to_x(zz).wait_recv()
        self.turn_y(zz).start()
        self.to_y(zz).wait_recv()
        self.turn_x(zz).start()

    def corner(self, zz):
        self.turn_y(zz).wait_recv()
        self.turn_x(zz).wait_recv()

    def finish(self):
        d = self.at.d

        @pl.loop(0, self.at.n)
        def _(zz):
            for copy in (self.to_x, self.to_y, self.turn_y, self.turn_x):
                copy(zz).wait_send()

            @pl.when((d > 0) & (zz >= d))
            def _():
                self.down(zz).wait_send()

            @pl.when(self.at.has_above & (zz <= d))
            def _():
                self.up(zz).wait_send()


class LineGather:
    def __init__(self, at, own, buf, lo, ss, sr, zs, zr):
        self.at, self.own, self.buf = at, own, buf
        self.ss, self.sr, self.zs, self.zr = ss, sr, zs, zr
        rows = own.shape[0] - lo
        self.P, self.A, self.B = pl.ds(lo, rows), pl.ds(lo, rows // 2), pl.ds(lo + rows // 2, rows // 2)

    def inside(self, k):
        at, buf, d = self.at, self.buf, self.at.d
        src, slot, part, dev = (
            (self.own.at[self.P], 1, self.P, at.nx), (self.own.at[self.P], 2, self.P, at.ny),
            (buf.at[d, 1, self.A], 3, self.A, at.ny), (buf.at[d, 2, self.B], 3, self.B, at.nx))[k]
        return send(src, buf.at[d, slot, part], self.ss.at[k], self.sr.at[k], dev)

    def along(self, zz, up):
        part = self.buf.at[zz, :, self.P]
        return send(part, part, self.zs.at[zz, up], self.zr.at[zz], self.at.above if up else self.at.below)

    def begin(self):
        self.inside(0).start()
        self.inside(1).start()

    def plane(self):
        self.inside(0).wait_recv()
        self.inside(2).start()
        self.inside(1).wait_recv()
        self.inside(3).start()

    def corner(self):
        self.inside(2).wait_recv()
        self.inside(3).wait_recv()

        @pl.when(self.at.has_below)
        def _():
            self.along(self.at.d, 0).start()

        @pl.when(self.at.has_above)
        def _():
            self.along(self.at.d, 1).start()

    def line(self, zz):
        self.along(zz, 0).wait_recv()

        @pl.when((zz < self.at.d) & self.at.has_above)
        def _():
            self.along(zz, 1).start()

        @pl.when((zz > self.at.d) & self.at.has_below)
        def _():
            self.along(zz, 0).start()

    def finish(self):
        d = self.at.d
        for k in range(4):
            self.inside(k).wait_send()

        @pl.loop(0, self.at.n)
        def _(zz):
            @pl.when(self.at.has_below & (zz >= d))
            def _():
                self.along(zz, 0).wait_send()

            @pl.when(self.at.has_above & (zz <= d))
            def _():
                self.along(zz, 1).wait_send()


def line_gather_sems(n):
    D_ = pltpu.SemaphoreType.DMA
    return [D_((4,)), D_((4,)), D_((n, 2)), D_((n,))]


def gather_sems(n):
    D_ = pltpu.SemaphoreType.DMA
    return [D_((n, 6)), D_((n,)), D_((n,)), D_((n,)), D_((n, 2))]


def add_rows(dst, src):
    rows = dst.shape[0]
    step = 16

    @pl.loop(0, rows // step)
    def _(r):
        w = pl.ds(pl.multiple_of(r * step, step), step)
        dst[w, :] = (dst[w, :].astype(jnp.float32) + src[w, :].astype(jnp.float32)).astype(dst.dtype)


class Reduce:
    def __init__(self, at, buf, total, r1, r2, rz, ss_1, sr_1, ss_2, sr_2, ss_z, sr_z, start=None):
        self.start = start
        self.at, self.buf, self.total = at, buf, total
        self.r1, self.r2, self.rz = r1, r2, rz
        self.sems = (ss_1, sr_1, ss_2, sr_2, ss_z, sr_z)
        rows = total.shape[0]
        self.A, self.B = pl.ds(0, rows // 2), pl.ds(rows // 2, rows // 2)

    def first(self, zz, k):
        ss, sr = self.sems[0], self.sems[1]
        slot, part, dev = ((3, self.A, self.at.nx), (3, self.B, self.at.ny), (1, self.A, self.at.nx), (2, self.B, self.at.ny))[k]
        return send(self.buf.at[zz, slot, part], self.r1.at[zz, k], ss.at[zz, k], sr.at[zz, k], dev)

    def second(self, zz, k):
        ss, sr = self.sems[2], self.sems[3]
        slot, part, dev = ((2, self.A, self.at.ny), (1, self.B, self.at.nx))[k]
        return send(self.buf.at[zz, slot, part], self.r2.at[zz, k], ss.at[zz, k], sr.at[zz, k], dev)

    def down(self, zz):
        return send(self.buf.at[zz, 0], self.rz.at[zz], self.sems[4].at[zz], self.sems[5].at[zz], self.at.below)

    def up(self, zz):
        slot = jnp.where(zz == self.at.d + 1, self.at.n, zz)
        return send(self.buf.at[zz, 0], self.rz.at[slot], self.sems[4].at[zz], self.sems[5].at[slot], self.at.above)

    def arrive(self, slot):
        return send(self.buf.at[0, 0], self.rz.at[slot], self.sems[4].at[0], self.sems[5].at[slot], self.at.nx)

    def s1(self, zz):
        self.corners(zz)
        self.sides(zz)

    def corners(self, zz):
        self.first(zz, 0).start()
        self.first(zz, 1).start()

    def sides(self, zz):
        self.first(zz, 2).start()
        self.first(zz, 3).start()

    def turn(self, zz):
        self.first(zz, 0).wait_recv()
        add_rows(self.buf.at[zz, 2, self.A], self.r1.at[zz, 0])
        self.second(zz, 0).start()
        self.first(zz, 1).wait_recv()
        add_rows(self.buf.at[zz, 1, self.B], self.r1.at[zz, 1])
        self.second(zz, 1).start()

    def take_sides(self, zz):
        self.first(zz, 2).wait_recv()
        add_rows(self.buf.at[zz, 0, self.A], self.r1.at[zz, 2])
        self.first(zz, 3).wait_recv()
        add_rows(self.buf.at[zz, 0, self.B], self.r1.at[zz, 3])

    def s2(self, zz):
        self.turn(zz)
        self.take_sides(zz)

    def step(self, j):
        at = self.at
        if j < at.n:
            self.turn(at.far(j))
            self.sides(at.far(j))
            if j + 2 < at.n:
                self.corners(at.far(j + 2))
        if j >= 1:
            self.take_sides(at.far(j - 1))
            self.s3(at.far(j - 1))
            self.lines(j - 1)

    def s3(self, zz):
        self.second(zz, 0).wait_recv()
        add_rows(self.buf.at[zz, 0, self.A], self.r2.at[zz, 0])
        self.second(zz, 1).wait_recv()
        add_rows(self.buf.at[zz, 0, self.B], self.r2.at[zz, 1])

    def push(self, zz):
        d = self.at.d

        @pl.when(zz < d)
        def _():
            self.down(zz).start()

        @pl.when(zz > d)
        def _():
            self.up(zz).start()

    def line_head(self, zz):
        @pl.when(jnp.logical_not(self.passes(zz)))
        def _():
            self.push(zz)

    def passes(self, zz):
        d = self.at.d
        return ((zz < d) & self.at.has_above) | ((zz > d) & self.at.has_below)

    def line_rest(self, zz):
        @pl.when(self.passes(zz))
        def _():
            self.arrive(zz).wait_recv()
            add_rows(self.buf.at[zz, 0], self.rz.at[zz])
            self.push(zz)

    def lines(self, j):
        n = self.at.n
        if j < n - 1:
            self.line_head(self.at.far(j))
        if 0 <= j - 1 < n - 2:
            self.line_rest(self.at.far(j - 1))
        if j == n - 2:
            self.line_rest(self.at.far(j))

    def last(self):
        d, n, rows, step = self.at.d, self.at.n, self.total.shape[0], 16

        def over(fn):
            @pl.loop(0, rows // step)
            def _(r):
                fn(pl.ds(pl.multiple_of(r * step, step), step))

        def own(w):
            first = self.buf[d, 0, w, :].astype(jnp.float32)
            self.total[w, :] = first if self.start is None else first + self.start[w, :]

        def more(slot):
            def fn(w):
                self.total[w, :] += self.rz[slot, w, :].astype(jnp.float32)

            self.arrive(slot).wait_recv()
            over(fn)

        over(own)

        @pl.when(self.at.has_above)
        def _():
            more(d)

        @pl.when(self.at.has_below)
        def _():
            more(n)

    def finish(self):
        d = self.at.d

        @pl.loop(0, self.at.n)
        def _(zz):
            for k in range(4):
                self.first(zz, k).wait_send()
            for k in range(2):
                self.second(zz, k).wait_send()

            @pl.when(zz != d)
            def _():
                self.arrive(zz)
                send(self.buf.at[zz, 0], self.rz.at[zz], self.sems[4].at[zz], self.sems[5].at[zz], self.at.nx).wait_send()


def reduce_scratch(n, rows, cols):
    D_ = pltpu.SemaphoreType.DMA
    V = lambda *s: pltpu.VMEM(s, jnp.bfloat16)
    return [V(n, 4, rows // 2, cols), V(n, 2, rows // 2, cols), V(n + 1, rows, cols),
            D_((n, 4)), D_((n, 4)), D_((n, 2)), D_((n, 2)), D_((n,)), D_((n + 1,))]


def expert_kernel(n, experts, x_ref, cot_ref, up_ref, down_ref, mid_ref,
                  out_ref, gx_ref, gup_ref, gdown_out,
                  gdown_ref, xb, cb, gg, mixed, gb, wup, wdown, pick_ref, place_ref, *rest):
    f32, bf16 = jnp.float32, jnp.bfloat16
    at = Place(n)
    d = at.d
    lo = x_ref.shape[0] * 3 // 4
    gather = Gather(at, x_ref, xb, *rest[:5], rows=lo)
    tail = LineGather(at, x_ref, xb, lo, *rest[-4:])
    grads = Reduce(at, gb, gx_ref, *rest[5:14])
    outs = Reduce(at, gg, out_ref, *rest[14:23], start=mid_ref)
    load_sem, core_ss, core_sr, free = rest[23:-4]
    rows = x_ref.shape[0]
    f2 = up_ref.shape[1]
    f = f2 // 2
    held = f // 128
    loads = [
        pltpu.make_async_copy(x_ref, xb.at[d, 0], load_sem.at[0]),
        pltpu.make_async_copy(up_ref, wup.at[0], load_sem.at[1]),
        pltpu.make_async_copy(down_ref, wdown.at[0], load_sem.at[2]),
        pltpu.make_async_copy(cot_ref, cb, load_sem.at[3]),
    ]
    for load in loads:
        load.start()
    at.meet()
    gather.begin_z()
    tail.begin()
    gather.begin_xy()
    swaps = [
        send(up_ref, wup.at[1], core_ss.at[0], core_sr.at[0], at.sib),
        send(down_ref, wdown.at[1], core_ss.at[1], core_sr.at[1], at.sib),
    ]
    for swap in swaps:
        swap.start()
    for h, owner in ((0, at.e), (1, at.sib[1])):
        for j in range(held):
            expert, cols = owner * held + j, slice((h * held + j) * 128, (h * held + j + 1) * 128)
            gate_row = lax.broadcasted_iota(jnp.int32, (128, 128), 0)
            pick_ref[:, cols] = ((gate_row == expert) | (gate_row == expert + experts)).astype(bf16)
            place_ref[cols, :] = (lane_tile(128) == expert).astype(bf16)
    loads[0].wait()
    tail.plane()
    tail.corner()
    gather.plane(at.near(0))
    gather.column(at.near(1))
    for load in loads[1:]:
        load.wait()
    for swap in swaps:
        swap.wait_recv()

    def tokens(ref, zz, p, lo, width):
        return ref[zz, pl.ds(2 * p, 2), :, pl.ds(lo, width)].reshape(2 * rows, width)

    def half(zz, p):
        pair = pl.ds(2 * p, 2)
        x = tokens(xb, zz, p, 0, D)
        cot = tokens(cb, zz, p, 0, D)
        mix = mm(tokens(xb, zz, p, D, 128), pick_ref[...])
        sums = jnp.zeros((2 * rows, 128), f32)
        for h in range(2):
            gate_up = mm(x, wup[h])
            back = mm(cot, wdown[h], NT)
            for j in range(held):
                k = h * held + j
                gate = gate_up[:, j * 256 : j * 256 + 128]
                up = gate_up[:, j * 256 + 128 : j * 256 + 256]
                b = back[:, j * 128 : (j + 1) * 128]
                m = mix[:, k * 128 : (k + 1) * 128]
                sig = 1.0 / (1.0 + jnp.exp(-gate))
                act = gate * sig
                hidden = (act * up).astype(bf16).astype(f32)
                prod = hidden * b
                high = prod.astype(bf16)
                low = (prod - high.astype(f32)).astype(bf16)
                sel = place_ref[k * 128 : (k + 1) * 128, :]
                sums += mm(high, sel) + mm(low, sel)
                mixed[zz, pair, :, pl.ds(k * 128, 128)] = (m * hidden).astype(bf16).reshape(2, rows, 128)
                gh = m * b
                gg[zz, pair, :, pl.ds(k * 256, 128)] = (
                    (gh * up * sig * (1.0 + gate * (1.0 - sig))).astype(bf16).reshape(2, rows, 128))
                gg[zz, pair, :, pl.ds(k * 256 + 128, 128)] = (gh * act).astype(bf16).reshape(2, rows, 128)
        for q in range(D // 512):
            cols = pl.ds(q * 512, 512)
            part = mm(tokens(gg, zz, p, 0, f2), wup[0, cols, :], NT) + mm(tokens(gg, zz, p, f2, f2), wup[1, cols, :], NT)
            gb[zz, pair, :, cols] = part.astype(bf16).reshape(2, rows, 512)
        gb[zz, pair, :, pl.ds(D, 128)] = sums.astype(bf16).reshape(2, rows, 128)

    @pl.loop(0, n)
    def _(i):
        zz = at.near(i)
        half(zz, 0)

        @pl.when(i + 2 < n)
        def _():
            gather.column(at.near(i + 2))

        @pl.when(i + 1 < n)
        def _():
            tail.line(at.near(i + 1))
            gather.plane(at.near(i + 1))

        gather.corner(zz)
        half(zz, 1)
        grads.s1(zz)

        @pl.when(i >= 1)
        def _():
            grads.s2(at.near(i - 1))

        @pl.when(i >= 2)
        def _():
            grads.s3(at.near(i - 2))
            grads.line_head(at.near(i - 2))

    pl.semaphore_signal(free.at[0], inc=1, device_id=at.sib, device_id_type=MESH)

    def grad_up(h, more):
        @pl.loop(0, D // 256)
        def _(q):
            cols = pl.ds(pl.multiple_of(q * 256, 256), 256)
            xs = xb[:, :, :, cols].reshape(n * 4 * rows, 256)
            part = mm(xs, gg[:, :, :, pl.ds(h * f2, f2)].reshape(n * 4 * rows, f2), TN)
            if more:
                part += wup[h, cols, :].astype(f32)
            wup[h, cols, :] = part.astype(bf16)

    def grad_down(h):
        for q in range(D // 512):
            cols = pl.ds(q * 512, 512)
            part = mm(mixed[:, :, :, pl.ds(h * f, f)].reshape(n * 4 * rows, f), cb[:, :, :, cols].reshape(n * 4 * rows, 512), TN)
            if h == 0:
                gdown_ref[:, cols] = part + wdown[0, :, cols].astype(f32)
            else:
                wdown[1, :, cols] = part.astype(bf16)

    def output(zz):
        @pl.loop(0, 2)
        def _(p):
            for q in range(D // 512):
                cols = pl.ds(q * 512, 512)
                part = mm(tokens(mixed, zz, p, 0, f), wdown[0, :, cols]) + mm(tokens(mixed, zz, p, f, f), wdown[1, :, cols])
                gg[zz, pl.ds(2 * p, 2), :, cols] = part.astype(bf16).reshape(2, rows, 512)

    grad_up(1, False)
    pl.semaphore_wait(free.at[0], 1)
    up_swap = send(wup.at[1], wup.at[0], core_ss.at[2], core_sr.at[2], at.sib)
    for swap in swaps:
        swap.wait_send()
    up_swap.start()
    grads.s2(at.near(n - 1))
    grads.s3(at.near(n - 2))
    grads.line_head(at.near(n - 2))
    up_swap.wait_recv()
    grad_up(0, True)
    keep = pltpu.make_async_copy(wup.at[0], gup_ref, load_sem.at[0])
    keep_down = pltpu.make_async_copy(gdown_ref, gdown_out, load_sem.at[1])
    keep.start()
    grads.s3(at.near(n - 1))
    grads.line_head(at.near(n - 1))
    for j in range(n):
        output(at.far(j))
        if j < 2:
            outs.corners(at.far(j))
    pl.semaphore_signal(free.at[1], inc=1, device_id=at.sib, device_id_type=MESH)
    grad_down(1)
    pl.semaphore_wait(free.at[1], 1)
    down_swap = send(wdown.at[1], wdown.at[0], core_ss.at[3], core_sr.at[3], at.sib)
    down_swap.start()
    for j in range(n + 1):
        if j == n:
            grads.last()
        outs.step(j)
        if j < n - 1:
            grads.line_rest(at.far(j))
        if j == 0:
            down_swap.wait_recv()
            grad_down(0)
            keep_down.start()
    outs.last()
    keep_down.wait()
    keep.wait()
    up_swap.wait_send()
    down_swap.wait_send()
    gather.finish()
    tail.finish()
    grads.finish()
    outs.finish()


def expert_layer(x, cot_all, up, down, middle, n, experts, cid):
    rows, wide = x.shape
    f2 = up.shape[1]
    f = f2 // 2
    bf16 = jnp.bfloat16
    V = lambda *s: pltpu.VMEM(s, bf16)
    D_ = pltpu.SemaphoreType.DMA
    any_, vm = pl.BlockSpec(memory_space=pl.ANY), pl.BlockSpec(memory_space=pltpu.VMEM)
    return pl.pallas_call(
        functools.partial(expert_kernel, n, experts),
        out_shape=(
            jax.ShapeDtypeStruct((rows, D), jnp.float32),
            jax.ShapeDtypeStruct((rows, wide), jnp.float32),
            jax.ShapeDtypeStruct((D, f2), bf16),
            jax.ShapeDtypeStruct((f, D), jnp.float32),
        ),
        in_specs=[any_, any_, any_, any_, vm],
        out_specs=[vm, vm, any_, any_],
        scratch_shapes=[pltpu.VMEM((f, D), jnp.float32), V(n, 4, rows, wide), V(n, 4, rows, D), V(n, 4, rows, 2 * f2), V(n, 4, rows, 2 * f), V(n, 4, rows, wide),
                        V(2, D, f2), V(2, f, D), V(128, 2 * f), V(2 * f, 128)]
        + gather_sems(n) + reduce_scratch(n, rows, wide) + reduce_scratch(n, rows, D)
        + [D_((4,)), D_((4,)), D_((4,)), pltpu.SemaphoreType.REGULAR((2,))] + line_gather_sems(n),
        compiler_params=pltpu.CompilerParams(collective_id=cid, has_side_effects=True, vmem_limit_bytes=63 << 20),
        name="expert_layer",
    )(x, cot_all, up, down, middle)


class GatherAll:
    def __init__(self, at, own, buf, send_sem, recv_z, recv_x, recv_y, recv_d, recv_s):
        self.at, self.own, self.buf = at, own, buf
        self.ss, self.rz, self.rx, self.ry, self.rd, self.rs = send_sem, recv_z, recv_x, recv_y, recv_d, recv_s
        cols = own.shape[1]
        half = (cols // 128 + 1) // 2 * 128
        self.A, self.B, self.F = pl.ds(0, half), pl.ds(half, cols - half), pl.ds(0, cols)

    def move(self, zz, e, cols, slot, sem, dev, own=False):
        dst = self.buf.at[zz * 8 + e, :, cols]
        return send(self.own.at[:, cols] if own else dst, dst, self.ss.at[zz, slot], sem, dev)

    def down(self, zz, own=False):
        return self.move(zz, self.at.e, self.F, 0, self.rz.at[zz], self.at.below, own)

    def up(self, zz, own=False):
        return self.move(zz, self.at.e, self.F, 1, self.rz.at[zz], self.at.above, own)

    def spread(self, zz, own=False):
        at = self.at
        return (self.move(zz, at.e, self.F, 2, self.rx.at[zz], at.nx, own),
                self.move(zz, at.e, self.F, 3, self.ry.at[zz], at.ny, own),
                self.move(zz, at.e, self.F, 4, self.rs.at[zz, 0], at.sib, own))

    def from_x(self, zz):
        at = self.at
        ex = at.nx[1]
        return (self.move(zz, ex, self.F, 2, self.rx.at[zz], at.nx),
                self.move(zz, ex, self.A, 5, self.rd.at[zz, 0], at.ny),
                self.move(zz, ex, self.F, 6, self.rs.at[zz, 1], at.sib))

    def from_y(self, zz):
        at = self.at
        ey = at.ny[1]
        return (self.move(zz, ey, self.F, 3, self.ry.at[zz], at.ny),
                self.move(zz, ey, self.B, 7, self.rd.at[zz, 1], at.nx),
                self.move(zz, ey, self.F, 8, self.rs.at[zz, 2], at.sib))

    def turned(self, zz):
        at = self.at
        return (self.move(zz, at.diag, self.A, 5, self.rd.at[zz, 0], at.ny),
                self.move(zz, at.diag, self.A, 9, self.rs.at[zz, 3], at.sib),
                self.move(zz, at.diag, self.B, 7, self.rd.at[zz, 1], at.nx),
                self.move(zz, at.diag, self.B, 10, self.rs.at[zz, 4], at.sib))

    def begin(self):
        d = self.at.d

        @pl.when(self.at.has_below)
        def _():
            self.down(d, True).start()

        @pl.when(self.at.has_above)
        def _():
            self.up(d, True).start()

        for copy in self.spread(d, True):
            copy.start()

    def column(self, zz):
        d = self.at.d

        @pl.when(zz < d)
        def _():
            self.up(zz).wait_recv()

            @pl.when(self.at.has_above)
            def _():
                self.up(zz).start()

        @pl.when(zz > d)
        def _():
            self.down(zz).wait_recv()

            @pl.when(self.at.has_below)
            def _():
                self.down(zz).start()

        for copy in self.spread(zz):
            copy.start()

    def plane(self, zz):
        for arrive, turn, share in (self.from_x(zz), self.from_y(zz)):
            arrive.wait_recv()
            turn.start()
            share.start()

    def corner(self, zz):
        a, share_a, b, share_b = self.turned(zz)
        a.wait_recv()
        share_a.start()
        b.wait_recv()
        share_b.start()

    def siblings(self):
        at = self.at
        es = at.sib[1]
        exs, eys, exys = es + at.nx[1] - at.e, es + at.ny[1] - at.e, es + at.diag - at.e

        @pl.loop(0, at.n)
        def _(zz):
            for e, cols, k in ((es, self.F, 0), (exs, self.F, 1), (eys, self.F, 2), (exys, self.A, 3), (exys, self.B, 4)):
                self.move(zz, e, cols, 4, self.rs.at[zz, k], at.sib).wait_recv()

    def finish(self):
        d = self.at.d

        @pl.loop(0, self.at.n)
        def _(zz):
            for group in (self.spread(zz), self.from_x(zz)[1:], self.from_y(zz)[1:], self.turned(zz)[1::2]):
                for copy in group:
                    copy.wait_send()

            @pl.when((d > 0) & (zz >= d))
            def _():
                self.down(zz).wait_send()

            @pl.when(self.at.has_above & (zz <= d))
            def _():
                self.up(zz).wait_send()


def lane_tile(rows):
    return lax.broadcasted_iota(jnp.int32, (rows, 128), 1)


def swap_halves(tile):
    front = lax.rem(lane_tile(tile.shape[0]), HEAD) < HEAD // 2
    return jnp.where(front, pltpu.roll(tile, 128 - HEAD // 2, 1), pltpu.roll(tile, HEAD // 2, 1))


def inverse_rms(v):
    return lax.rsqrt(jnp.mean(v * v, axis=1, keepdims=True) + norm_eps)


def rope_lanes(seg_ref, freq_ref, cos_ref, sin_ref):
    f32 = jnp.float32
    packs, rows = seg_ref.shape[0], seg_ref.shape[2]
    row = jnp.concatenate([seg_ref[i].astype(f32) + float(2 * rows * i) for i in range(packs)], axis=1)
    total = packs * rows
    across = jnp.broadcast_to(row, (total, total))
    same = across == jnp.transpose(across)
    source = lax.broadcasted_iota(jnp.int32, (total, total), 1)
    target = lax.broadcasted_iota(jnp.int32, (total, total), 0)
    start = jnp.min(jnp.where(same, source.astype(f32), float(total)), axis=1, keepdims=True)
    angle = (target.astype(f32) - start) * freq_ref[...]
    cos_ref[...] = jnp.cos(angle)
    front = lax.rem(source, HEAD) < HEAD // 2
    sine = jnp.sin(angle)
    sin_ref[...] = jnp.where(front, -sine, sine)
    return (same & (source <= target)).astype(f32)


def forward_kernel(n, experts, tok_ref, cot_ref, qkv_ref, proj_ref, tail_ref, ein_ref, seg_ref, route_ref, freq_ref,
                   w_all, cot_all, up_all, disp_out, mid_out, gates_out, gain_out, nf_out, q_out, k_out, v_out, p_out, mixed_out, cos_out, sin_out,
                   disp_ref, mid_ref, gates_ref, gain_ref, nf_ref, q_ref, k_ref, v_ref, p_ref, mixed_ref, cos_ref, sin_ref,
                   wv, pieces, dense_ref, *rest):
    f32, bf16 = jnp.float32, jnp.bfloat16
    at = Place(n)
    d = at.d
    dense = GatherAll(at, dense_ref, wv, *rest[:6])
    cot = Gather(at, cot_ref, cot_all, *rest[6:11])
    load_sem, a2a_ss, a2a_sr, keep_sem = rest[11:]
    q_width, k_width = HEADS * HEAD, KV_HEADS * HEAD
    groups = HEADS // KV_HEADS
    held, share = ein_ref.shape[:2]
    f = FF // n
    qkv_width = q_width + 2 * k_width
    dense_ref[:, :qkv_width] = qkv_ref[...]
    dense_ref[:, qkv_width : qkv_width + D] = proj_ref[...]
    dense_ref[:, qkv_width + D :] = tail_ref[...]
    loads = [
        pltpu.make_async_copy(dense_ref, wv.at[d * 8 + at.e], load_sem.at[0]),
        pltpu.make_async_copy(cot_ref, cot_all.at[d, 0], load_sem.at[1]),
    ]
    for load in loads:
        load.start()

    def rows_of(z):
        return up_all.at[pl.ds(pl.multiple_of(z * share, share), share), :]

    own_piece = pltpu.make_async_copy(pieces.at[d], rows_of(d), load_sem.at[2])

    parts = 3
    third = share // parts

    def third_of(z, r):
        return up_all.at[pl.ds(pl.multiple_of(z * share + r * third, third), third), :]

    def exchange(k, r):
        to = lax.rem(d + k, n)
        return send(pieces.at[to, pl.ds(r * third, third), :], third_of(d, r), a2a_ss.at[k, r], a2a_sr.at[d, r], (to, at.e))

    def exchange_part(r):
        for k in range(1, n):
            exchange(k, r).start()

    at.meet(True)
    dense.begin()
    for q in range(n):
        for j in range(2 * held):
            lo = (j % 2) * FF + q * f
            pieces[q, :, j * f : (j + 1) * f] = ein_ref[j // 2, :, lo : lo + f]
    own_piece.start()
    allowed = rope_lanes(seg_ref, freq_ref, cos_ref, sin_ref)
    for i in range(1, n):
        dense.column(at.near(i))
        if i == n - 1:
            cot.begin_z()
            exchange_part(0)
        dense.plane(at.near(i - 1))
        if i >= 2:
            dense.corner(at.near(i - 2))
    cot.begin_xy()
    dense.plane(at.near(n - 1))
    dense.corner(at.near(n - 2))
    cot.column(at.near(1))
    cot.column(at.near(2))
    exchange_part(1)
    exchange_part(2)
    dense.corner(at.near(n - 1))
    for load in loads:
        load.wait()
    dense.siblings()
    keep = pltpu.make_async_copy(wv, w_all, load_sem.at[0])
    keep.start()

    def weight(lo, width):
        return wv[:, :, lo : lo + width].reshape(D, width)

    tail_at = q_width + 2 * k_width + D
    turned = jnp.transpose(weight(tail_at, 128).astype(f32))
    gain_ref[0:1, :] = turned[experts : experts + 1, :]
    gain_ref[1:2, :] = turned[experts + 1 : experts + 2, :]
    x = tok_ref[...].astype(f32)
    nf_ref[...] = (x * inverse_rms(x) * gain_ref[0:1, :]).astype(bf16)
    cos, sin = cos_ref[...], sin_ref[...]
    for q in range((q_width + 2 * k_width) // 512):
        lo = q * 512
        part = mm(nf_ref[...], weight(lo, 512))
        for t in range(4):
            tile = part[:, t * 128 : (t + 1) * 128]
            col = lo + t * 128
            if col < q_width + k_width:
                tile = tile * cos + swap_halves(tile) * sin
            ref, base = (q_ref, 0) if col < q_width else (k_ref, q_width) if col < q_width + k_width else (v_ref, q_width + k_width)
            ref[:, col - base : col - base + 128] = tile.astype(bf16)
    cot.plane(at.near(0))
    allowed = jnp.concatenate([allowed] * groups, axis=0) > 0
    for g in range(KV_HEADS):
        qs = jnp.concatenate([q_ref[:, (g * groups + j) * HEAD : (g * groups + j + 1) * HEAD] for j in range(groups)], axis=0)
        ks, vs = k_ref[:, g * HEAD : (g + 1) * HEAD], v_ref[:, g * HEAD : (g + 1) * HEAD]
        scores = jnp.where(allowed, mm(qs, ks, NT) * HEAD ** (-0.5), neg_large)
        raised = jnp.exp(scores - jnp.max(scores, axis=1, keepdims=True))
        probs = raised / jnp.sum(raised, axis=1, keepdims=True)
        p_ref[g] = probs
        out = mm(probs.astype(bf16), vs).astype(bf16)
        rows = out.shape[0] // groups
        for j in range(groups):
            mixed_ref[:, (g * groups + j) * HEAD : (g * groups + j + 1) * HEAD] = out[j * rows : (j + 1) * rows]
    for q in range(D // 512):
        lo = q * 512
        mid_ref[:, lo : lo + 512] = tok_ref[:, lo : lo + 512].astype(f32) + mm(mixed_ref[...], weight(q_width + 2 * k_width + lo, 512))
    mid = mid_ref[...]
    disp_ref[:, :D] = (mid * inverse_rms(mid) * gain_ref[1:2, :]).astype(bf16)
    logits = mm(disp_ref[:, :D], weight(tail_at, 128))
    lanes = lane_tile(mid.shape[0])
    chosen = jnp.zeros(lanes.shape, f32)
    for k in range(TOP_K):
        chosen += (route_ref[:, k : k + 1] == lanes).astype(f32)
    masked = jnp.where(chosen > 0, logits, neg_large)
    raised = jnp.where(chosen > 0, jnp.exp(masked - jnp.max(masked, axis=1, keepdims=True)), 0.0)
    gates = raised / jnp.sum(raised, axis=1, keepdims=True)
    gates_ref[...] = gates
    high = gates.astype(bf16).astype(f32)
    low = (gates - high).astype(bf16).astype(f32)
    disp_ref[:, D:] = (high + pltpu.roll(low, experts, 1)).astype(bf16)

    keeps = [pltpu.make_async_copy(src, dst, keep_sem.at[i]) for i, (src, dst) in enumerate((
        (disp_ref, disp_out), (mid_ref, mid_out), (gates_ref, gates_out), (gain_ref, gain_out), (nf_ref, nf_out), (q_ref, q_out),
        (k_ref, k_out), (v_ref, v_out), (p_ref, p_out), (mixed_ref, mixed_out), (cos_ref, cos_out), (sin_ref, sin_out)))]
    for copy in keeps:
        copy.start()
    for i in range(1, n):
        cot.plane(at.near(i))
        cot.corner(at.near(i - 1))
        if i + 2 < n:
            cot.column(at.near(i + 2))
    cot.corner(at.near(n - 1))
    own_piece.wait()
    for k in range(1, n):
        source = lax.rem(d + k, n)
        for r in range(parts):
            exchange(k, r).wait_send()
            send(pieces.at[0, pl.ds(r * third, third), :], third_of(source, r), a2a_ss.at[k, r], a2a_sr.at[source, r], (source, at.e)).wait_recv()
    keep.wait()
    dense.finish()
    cot.finish()
    for copy in keeps:
        copy.wait()


def forward_layer(tok, cot, attn_in, attn_out, tail, ein, segments, routes, n, experts, cid):
    f32, bf16 = jnp.float32, jnp.bfloat16
    rows = tok.shape[0]
    shard = attn_in.shape[0]
    held, share = ein.shape[:2]
    q_width, k_width = HEADS * HEAD, KV_HEADS * HEAD
    wide = q_width + 2 * k_width + D + 128
    groups = HEADS // KV_HEADS
    half = HEAD // 2
    freq = jnp.tile(rope_base ** (-jnp.arange(half, dtype=f32) / half), 128 // half)[None, :]
    D_ = pltpu.SemaphoreType.DMA
    V = lambda *s: pltpu.VMEM(s, bf16)
    any_, vm = pl.BlockSpec(memory_space=pl.ANY), pl.BlockSpec(memory_space=pltpu.VMEM)
    S = jax.ShapeDtypeStruct
    saved = (
        S((rows, D + 128), bf16), S((rows, D), f32), S((rows, 128), f32), S((8, D), f32), S((rows, D), bf16),
        S((rows, q_width), bf16), S((rows, k_width), bf16), S((rows, k_width), bf16),
        S((KV_HEADS, groups * rows, rows), f32), S((rows, q_width), bf16), S((rows, 128), f32), S((rows, 128), f32),
    )
    return pl.pallas_call(
        functools.partial(forward_kernel, n, experts),
        out_shape=(S((n * 8, shard, wide), bf16), S((n, 4, rows, D), bf16), S((D, 2 * held * (FF // n)), bf16)) + saved,
        in_specs=[vm, any_] + [vm] * 7,
        out_specs=[any_] * 15,
        scratch_shapes=[pltpu.VMEM(a.shape, a.dtype) for a in saved]
        + [V(n * 8, shard, wide), V(n, share, 2 * held * (FF // n)), V(shard, wide)]
        + [D_((n, 11)), D_((n,)), D_((n,)), D_((n,)), D_((n, 2)), D_((n, 5))] + gather_sems(n)
        + [D_((3,)), D_((n, 3)), D_((n, 3)), D_((len(saved),))],
        compiler_params=pltpu.CompilerParams(collective_id=cid, has_side_effects=True, vmem_limit_bytes=60 << 20),
        name="forward_layer",
    )(tok, cot, attn_in, attn_out, tail, ein, segments, routes, freq)


def backward_kernel(n, experts, gs_in, tok_in, cot_in, mid_in, gates_in, gain_in, nf_in, disp_in, q_in, k_in, v_in, p_in, mixed_in, cos_in, sin_in, w_ref, gup_ref,
                    gtok_ref, gout_ref, gin_ref, gtail_ref, arrived,
                    gs_ref, tok_ref, cot_ref, mid_ref, gates_ref, gain_ref, nf_ref, disp_ref, q_ref, k_ref, v_ref, p_ref, mixed_ref, cos_ref, sin_ref,
                    wv, pout, pin, tot_out, tot_in, pair, gq, gl, sums, gb, gm, flat, *rest):
    f32, bf16 = jnp.float32, jnp.bfloat16
    at = Place(n)
    d, c = at.d, at.c
    outs = Reduce(at, pout, tot_out, *rest[:9])
    ins = Reduce(at, pin, tot_in, *rest[9:18])
    load_sem, pair_ss, pair_sr, a2a_ss, a2a_sr, end_ss, end_sr, in_sem = rest[18:]
    q_width, k_width = HEADS * HEAD, KV_HEADS * HEAD
    groups = HEADS // KV_HEADS
    qkv_width = q_width + 2 * k_width
    tail_at = qkv_width + D
    rows = tok_ref.shape[0]
    shard = w_ref.shape[1]
    share = D // n
    f = FF // n
    fetched = [pltpu.make_async_copy(src, dst, in_sem.at[i]) for i, (src, dst) in enumerate((
        (mid_in, mid_ref), (gates_in, gates_ref), (gs_in, gs_ref), (gain_in, gain_ref), (cot_in, cot_ref), (mixed_in, mixed_ref), (nf_in, nf_ref), (disp_in, disp_ref), (q_in, q_ref), (k_in, k_ref), (v_in, v_ref), (p_in, p_ref), (tok_in, tok_ref), (cos_in, cos_ref), (sin_in, sin_ref)))]
    for copy in fetched[:8]:
        copy.start()
    loads = []
    for i, (lo, width) in enumerate(((tail_at, 128), (qkv_width, D), (0, qkv_width))):
        loads.append(pltpu.make_async_copy(w_ref.at[:, :, pl.ds(lo, width)], wv.at[:, :, pl.ds(lo, width)], load_sem.at[i]))
    for load in loads:
        load.start()
    for copy in fetched[8:]:
        copy.start()
    own_share = pltpu.make_async_copy(gup_ref.at[pl.ds(pl.multiple_of(d * share, share), share), :], arrived.at[d], load_sem.at[3])
    own_share.start()

    def exchange(k):
        to = lax.rem(d + k, n)
        return send(gup_ref.at[pl.ds(pl.multiple_of(to * share, share), share), :], arrived.at[d], a2a_ss.at[k], a2a_sr.at[d], (to, at.e))

    swaps = [send(src, pair.at[i], pair_ss.at[i], pair_sr.at[i], at.sib)
             for i, src in enumerate((mixed_ref, nf_ref, disp_ref.at[:, pl.ds(0, D)], gb))]
    swap_q = send(gq.at[0], gq.at[1], pair_ss.at[4], pair_sr.at[4], at.sib)
    swap_l = send(gl.at[0], gl.at[1], pair_ss.at[5], pair_sr.at[5], at.sib)
    swap_s = send(sums.at[0], sums.at[1], pair_ss.at[6], pair_sr.at[6], at.sib)
    at.meet(True)
    for k in range(1, n):
        exchange(k).start()
    for copy in fetched[:8]:
        copy.wait()
    for i in range(3):
        swaps[i].start()

    def weight(lo, width):
        return wv[:, :, lo : lo + width].reshape(D, width)

    loads[0].wait()
    mid = mid_ref[...]
    inv_second = inverse_rms(mid)
    unit = mid * inv_second
    gates, gg = gates_ref[...], gs_ref[:, D:]
    gl[0] = (gates * (gg - jnp.sum(gates * gg, axis=1, keepdims=True))).astype(bf16)
    swap_l.start()
    grad_second = mm(gl[0], weight(tail_at, 128), NT) + gs_ref[:, :D]
    pull = grad_second * gain_ref[1:2, :]
    sums[0, 1:2, :] = jnp.sum(grad_second * unit, axis=0, keepdims=True)
    grad_middle = cot_ref[...].astype(f32) + inv_second * (pull - unit * jnp.mean(pull * unit, axis=1, keepdims=True))
    gtok_ref[...] = grad_middle
    gb[...] = grad_middle.astype(bf16)
    swaps[3].start()
    loads[1].wait()
    for q in range(q_width // 512):
        gm[:, q * 512 : (q + 1) * 512] = mm(gb[...], wv[:, :, qkv_width : qkv_width + D].reshape(D, D)[q * 512 : (q + 1) * 512], NT).astype(bf16)

    def both(own, other, cols):
        return jnp.concatenate([own[:, cols], other[:, cols]], axis=0)

    def store(buf, zz, lo, value):
        blocks = value.astype(bf16).reshape(4, 2 * shard, value.shape[1])
        for a in range(4):
            slot = 2 * lax.rem(a // 2 + at.y, 2) + lax.rem(a % 2 + at.x, 2)
            buf[zz, slot, :, lo : lo + value.shape[1]] = blocks[a]

    def row_cols(zz):
        return pl.ds(pl.multiple_of(zz * share, 128), share)

    half_out, half_in = D // 2, qkv_width // 2
    swaps[0].wait_recv()
    swaps[3].wait_recv()

    @pl.loop(0, n)
    def _(j):
        zz = at.far(j)
        branch = both(gb, pair.at[3], pl.ds(pl.multiple_of(c * half_out, 128), half_out))
        store(pout, zz, 0, mm(both(mixed_ref, pair.at[0], row_cols(zz)), branch, TN))
        outs.s1(zz)

    for copy in fetched[8:]:
        copy.wait()
    scale = HEAD ** (-0.5)
    for g in range(KV_HEADS):
        heads = [slice((g * groups + j) * HEAD, (g * groups + j + 1) * HEAD) for j in range(groups)]
        kv = slice(g * HEAD, (g + 1) * HEAD)
        qs = jnp.concatenate([q_ref[:, h] for h in heads], axis=0)
        ms = jnp.concatenate([gm[:, h] for h in heads], axis=0)
        ks, vs = k_ref[:, kv], v_ref[:, kv]
        probs = p_ref[g]
        grad_values = mm(probs.astype(bf16), ms, TN)
        grad_probs = mm(ms, vs, NT)
        grad_scores = (probs * (grad_probs - jnp.sum(probs * grad_probs, axis=1, keepdims=True))).astype(bf16)
        grad_query = mm(grad_scores, ks) * scale
        for j, h in enumerate(heads):
            flat[:, h] = grad_query[j * rows : (j + 1) * rows]
        flat[:, q_width + kv.start : q_width + kv.stop] = mm(grad_scores, qs, TN) * scale
        flat[:, q_width + k_width + kv.start : q_width + k_width + kv.stop] = grad_values
    for j in range(n):
        outs.s2(at.far(j))
    cos, sin = cos_ref[...], sin_ref[...]
    for t in range(qkv_width // 128):
        tile = flat[:, t * 128 : (t + 1) * 128]
        if t * 128 < q_width + k_width:
            tile = tile * cos - swap_halves(tile) * sin
        gq[0, :, t * 128 : (t + 1) * 128] = tile.astype(bf16)
    swap_q.start()
    loads[2].wait()
    x = tok_ref[...].astype(f32)
    inv_first = inverse_rms(x)
    unit = x * inv_first
    grad_first = jnp.concatenate(
        [mm(gq[0], wv[8 * i : 8 * (i + 1), :, :qkv_width].reshape(8 * shard, qkv_width), NT) for i in range(n)], axis=1)
    pull = grad_first * gain_ref[0:1, :]
    sums[0, 0:1, :] = jnp.sum(grad_first * unit, axis=0, keepdims=True)
    sums[0, 2:, :] = jnp.zeros((6, D), f32)
    swap_s.start()
    gtok_ref[...] += inv_first * (pull - unit * jnp.mean(pull * unit, axis=1, keepdims=True))
    for i in (1, 2):
        swaps[i].wait_recv()
    swap_l.wait_recv()
    swap_q.wait_recv()
    swap_s.wait_recv()
    gains = sums[0] + sums[1]
    high = gains.astype(bf16)
    low = (gains - high.astype(f32)).astype(bf16)
    swap_s.wait_send()
    sums[0] = high.astype(f32)
    sums[1] = low.astype(f32)
    line = lax.rem(lax.broadcasted_iota(jnp.int32, (16, 128), 0), 8)
    where = (((line == 0) & (lane_tile(16) == experts)) | ((line == 1) & (lane_tile(16) == experts + 1))).astype(bf16)

    @pl.loop(0, n)
    def _(j):
        zz = at.far(j)
        cols = row_cols(zz)
        normed = both(nf_ref, pair.at[1], cols)
        for q in range(2):
            part = pl.ds(pl.multiple_of(c * half_in + q * (half_in // 2), 128), half_in // 2)
            grad = jnp.concatenate([gq[0, :, part], gq[1, :, part]], axis=0)
            store(pin, zz, q * (half_in // 2), mm(normed, grad, TN))
        tail = mm(both(disp_ref, pair.at[2], cols), jnp.concatenate([gl[0], gl[1]], axis=0), TN)
        rows_now = jnp.concatenate([sums[0, :, cols], sums[1, :, cols]], axis=0).astype(bf16)
        store(pin, zz, half_in, tail + mm(rows_now, where, TN))

        @pl.when(j < 2)
        def _():
            ins.corners(zz)

    for j in range(n + 1):
        ins.step(j)
        if j < n:
            outs.s3(at.far(j))
            outs.lines(j)
    outs.last()
    mine, theirs = pl.ds(pl.multiple_of(c * shard, 8), shard), pl.ds(pl.multiple_of((1 - c) * shard, 8), shard)
    cols_out, cols_in = pl.ds(pl.multiple_of(c * half_out, 128), half_out), pl.ds(pl.multiple_of(c * half_in, 128), half_in)
    end_out = send(tot_out.at[theirs, :], gout_ref.at[:, cols_out], end_ss.at[0], end_sr.at[0], at.sib)
    end_out.start()
    gout_ref[:, cols_out] = tot_out[mine, :]
    ins.last()
    end_in = send(tot_in.at[theirs, pl.ds(0, half_in)], gin_ref.at[:, cols_in], end_ss.at[1], end_sr.at[1], at.sib)
    end_in.start()
    gin_ref[:, cols_in] = tot_in[mine, :half_in]
    gtail_ref[...] = tot_in[mine, half_in:]
    own_share.wait()
    for k in range(1, n):
        exchange(k).wait_send()
        source = lax.rem(d + k, n)
        send(gup_ref.at[pl.ds(0, share), :], arrived.at[source], a2a_ss.at[k], a2a_sr.at[source], (source, at.e)).wait_recv()

    end_out.wait()
    end_in.wait()
    for swap in swaps + [swap_q, swap_l]:
        swap.wait_send()
    outs.finish()
    ins.finish()


def backward_layer(gs, tok, cot, mid, gates, gain, nf, disp, q, k, v, p, mixed, cos, sin, w_all, gup, n, experts, cid):
    f32, bf16 = jnp.float32, jnp.bfloat16
    rows = tok.shape[0]
    shard, wide = w_all.shape[1:]
    qkv_width = (HEADS + 2 * KV_HEADS) * HEAD
    share = D // n
    D_ = pltpu.SemaphoreType.DMA
    V = lambda *s: pltpu.VMEM(s, bf16)
    W = lambda *s: pltpu.VMEM(s, f32)
    any_, vm = pl.BlockSpec(memory_space=pl.ANY), pl.BlockSpec(memory_space=pltpu.VMEM)
    S = jax.ShapeDtypeStruct
    width_out, width_in = D // 2, qkv_width // 2 + 128
    return pl.pallas_call(
        functools.partial(backward_kernel, n, experts),
        out_shape=(S((rows, D), f32), S((shard, D), f32), S((shard, qkv_width), f32), S((shard, 128), f32), S((n, share, gup.shape[1]), bf16)),
        in_specs=[any_] * 17,
        out_specs=[vm] * 4 + [any_],
        scratch_shapes=[pltpu.VMEM(a.shape, a.dtype) for a in (gs, tok, cot, mid, gates, gain, nf, disp, q, k, v, p, mixed, cos, sin)]
        + [V(n * 8, shard, wide), V(n, 4, 2 * shard, width_out), V(n, 4, 2 * shard, width_in),
                        W(2 * shard, width_out), W(2 * shard, width_in),
                        V(4, rows, D), V(2, rows, qkv_width), V(2, rows, 128), W(2, 8, D), V(rows, D), V(rows, D), W(rows, qkv_width)]
        + reduce_scratch(n, 2 * shard, width_out) + reduce_scratch(n, 2 * shard, width_in)
        + [D_((4,)), D_((7,)), D_((7,)), D_((n,)), D_((n,)), D_((2,)), D_((2,)), D_((15,))],
        compiler_params=pltpu.CompilerParams(collective_id=cid, has_side_effects=True, vmem_limit_bytes=62 << 20),
        name="backward_layer",
    )(gs, tok, cot, mid, gates, gain, nf, disp, q, k, v, p, mixed, cos, sin, w_all, gup)


def results_kernel(experts, arrived, tok_in, down_in, out_in, qkv_in, tail_in,
                   up_ref, tok_ref, down_ref, proj_ref, qkv_ref, router_ref, gains_ref):
    n, width = arrived.shape[0], arrived.shape[2]
    f = FF // n
    for q in range(n):
        for j in range(width // f):
            lo = (j % 2) * FF + q * f
            up_ref[j // 2, :, lo : lo + f] = arrived[q, :, j * f : (j + 1) * f].astype(jnp.float32)

    tok_ref[...] = tok_in[...]
    down_ref[...] = down_in[...]

    @pl.when(pl.program_id(0) == 0)
    def _():
        proj_ref[...] = out_in[...]
        qkv_ref[...] = qkv_in[...]
        router_ref[...] = tail_in[:, :experts]
        turned = jnp.transpose(jnp.concatenate([tail_in[...], jnp.zeros((128 - tail_in.shape[0], 128), jnp.float32)], axis=0))
        gains_ref[...] = turned[experts : experts + 8, : tail_in.shape[0]]


def results(arrived, tok, down, proj, qkv, tail, held, experts):
    n, share, width = arrived.shape
    f32 = jnp.float32
    steps = 4
    rows = share // steps
    whole = lambda a: pl.BlockSpec(a.shape, lambda i: (0,) * len(a.shape))
    part = lambda a: pl.BlockSpec((a.shape[0] // steps, a.shape[1]), lambda i: (i, 0))
    shapes = [jax.ShapeDtypeStruct(a.shape, f32) for a in (tok, down, proj, qkv)]
    shapes += [jax.ShapeDtypeStruct((tail.shape[0], experts), f32), jax.ShapeDtypeStruct((8, tail.shape[0]), f32)]
    return pl.pallas_call(
        functools.partial(results_kernel, experts),
        grid=(steps,),
        out_shape=[jax.ShapeDtypeStruct((held, share, 2 * FF), f32)] + shapes,
        in_specs=[pl.BlockSpec((n, rows, width), lambda i: (0, i, 0))] + [part(a) for a in (tok, down)] + [whole(a) for a in (proj, qkv, tail)],
        out_specs=[pl.BlockSpec((held, rows, 2 * FF), lambda i: (0, i, 0))] + [part(a) for a in (tok, down)] + [whole(a) for a in shapes[2:]],
        compiler_params=pltpu.CompilerParams(vmem_limit_bytes=62 << 20),
        name="results",
    )(arrived, tok, down, proj, qkv, tail)


def per_device_fast(n, tokens, segments, routes, cotangent, gain_attn, attn_in, attn_out, gain_ffn, router, expert_in, expert_out):
    f32, bf16 = jnp.float32, jnp.bfloat16
    micro, rows = tokens.shape[:2]
    total = micro * rows
    held = expert_in.shape[0]
    experts = held * 8
    f = FF // n
    shard = attn_in.shape[0]
    x = tokens.reshape(total, D)
    cot = cotangent.reshape(total, D)
    tail = jnp.concatenate([router, gain_attn[:, None], gain_ffn[:, None], jnp.zeros((shard, 126 - experts), bf16)], axis=1)
    w_all, cot_all, up, disp, middle, gates, gain, nf, q, k, v, p, mixed, cos, sin = forward_layer(
        x, cot, attn_in, attn_out, tail, expert_in, segments, routes.reshape(total, TOP_K), n, experts, 0)
    out, grad_sum, grad_up, grad_down = expert_layer(disp, cot_all, up, expert_out.reshape(held * f, D), middle, n, experts, 1)
    grad_tokens, grad_out, grad_in, grad_tail, grad_up = backward_layer(
        grad_sum, x, cot, middle, gates, gain, nf, disp, q, k, v, p, mixed, cos, sin, w_all, grad_up, n, experts, 2)
    grad_up, grad_tokens, grad_down, grad_out, grad_in, grad_router, grad_gains = results(
        grad_up, grad_tokens, grad_down, grad_out, grad_in, grad_tail, held, experts)
    return (
        out.astype(bf16).reshape(micro, rows, D),
        grad_tokens.reshape(micro, rows, D),
        grad_gains[0],
        grad_in,
        grad_out,
        grad_gains[1],
        grad_router,
        grad_up,
        grad_down.reshape(held, f, D),
    )


def solution(mesh):
    placed = (
        P(None, ("dp", "expert"), None),
        P(None, ("dp", "expert"), None),
        P(None, ("dp", "expert"), None),
        P(None, ("dp", "expert"), None),
        P(("dp", "expert")),
        P(("dp", "expert"), None),
        P(("dp", "expert"), None),
        P(("dp", "expert")),
        P(("dp", "expert"), None),
        P("expert", "dp", None),
        P("expert", "dp", None),
    )
    fast = mesh.shape["expert"] == 8 and FF // mesh.shape["dp"] == 128
    body = functools.partial(per_device_fast, mesh.shape["dp"]) if fast else per_device
    return jax.shard_map(
        body,
        mesh=mesh,
        in_specs=placed,
        out_specs=(
            P(None, ("dp", "expert"), None),
            P(None, ("dp", "expert"), None),
            P(("dp", "expert")),
            P(("dp", "expert"), None),
            P(("dp", "expert"), None),
            P(("dp", "expert")),
            P(("dp", "expert"), None),
            P("expert", "dp", None),
            P("expert", "dp", None),
        ),
        check_vma=False,
    )
```

```python
import functools

import jax
import jax.numpy as jnp
import numpy as np
from jax import lax
from jax.experimental import pallas as pl
from jax.experimental.pallas import tpu as pltpu
from jax.sharding import PartitionSpec as P

MESH = pl.DeviceIdType.MESH

D = 1536
HEADS = 24
KV_HEADS = 8
HEAD = 64
FF = 512
TOP_K = 8


norm_eps = 1e-06
rope_base = 10000.0
neg_large = -1e30
highest = lax.Precision.HIGHEST


def rope_tables(segment, half_width):
    row_count = segment.shape[0]
    places = jnp.arange(row_count, dtype=jnp.int32)
    same_seq = segment[:, None] == segment[None, :]
    seq_start = jnp.min(jnp.where(same_seq, places[None, :], row_count), axis=1)
    offset = (places - seq_start).astype(jnp.float32)
    frequencies = rope_base ** (-jnp.arange(half_width, dtype=jnp.float32) / half_width)
    angles = offset[:, None] * frequencies[None, :]
    causal = same_seq & (places[None, :] <= places[:, None])
    return (jnp.cos(angles), jnp.sin(angles), causal)


def rotate(operand, cosine, sine_table):
    half_width = operand.shape[-1] // 2
    front_part = operand[..., :half_width]
    back_part = operand[..., half_width:]
    return jnp.concatenate(
        [
            front_part * cosine - back_part * sine_table,
            back_part * cosine + front_part * sine_table,
        ],
        axis=-1,
    )


def unrotate(gradient, cosine, sine_table):
    half_width = gradient.shape[-1] // 2
    front_part = gradient[..., :half_width]
    back_part = gradient[..., half_width:]
    return jnp.concatenate(
        [
            front_part * cosine + back_part * sine_table,
            back_part * cosine - front_part * sine_table,
        ],
        axis=-1,
    )


def slot_targets(route_now, expert_count, capacity):
    flat_ids = route_now.reshape(-1)
    onehot = (flat_ids[:, None] == jnp.arange(expert_count, dtype=jnp.int32)[None, :]).astype(
        jnp.int32
    )
    earlier = jnp.cumsum(onehot, axis=0) - onehot
    slot_index = jnp.sum(earlier * onehot, axis=1)
    return flat_ids * capacity + slot_index


def dense_fetch(gain_attn, attn_in, attn_out, gain_ffn, router):
    return (
        lax.all_gather(gain_attn, ("dp", "expert"), axis=0, tiled=True),
        lax.all_gather(attn_in, ("dp", "expert"), axis=0, tiled=True),
        lax.all_gather(attn_out, ("dp", "expert"), axis=0, tiled=True),
        lax.all_gather(gain_ffn, ("dp", "expert"), axis=0, tiled=True),
        lax.all_gather(router, ("dp", "expert"), axis=0, tiled=True),
    )


def expert_fetch(expert_in, expert_out):
    return (
        lax.all_gather(expert_in, "dp", axis=1, tiled=True),
        lax.all_gather(expert_out, "dp", axis=1, tiled=True),
    )


def dense_reduce(grad_set):
    return (
        lax.psum_scatter(grad_set[0], ("dp", "expert"), scatter_dimension=0, tiled=True),
        lax.psum_scatter(grad_set[1], ("dp", "expert"), scatter_dimension=0, tiled=True),
        lax.psum_scatter(grad_set[2], ("dp", "expert"), scatter_dimension=0, tiled=True),
        lax.psum_scatter(grad_set[3], ("dp", "expert"), scatter_dimension=0, tiled=True),
        lax.psum_scatter(grad_set[4], ("dp", "expert"), scatter_dimension=0, tiled=True),
    )


def expert_reduce(grad_set):
    return (
        lax.psum_scatter(grad_set[0], "dp", scatter_dimension=1, tiled=True),
        lax.psum_scatter(grad_set[1], "dp", scatter_dimension=1, tiled=True),
    )


def attention_scores(queries, key_rot, causal):
    score_scale = HEAD ** (-0.5)
    scores = (
        jnp.einsum("tkgh,skh->kgts", queries, key_rot, preferred_element_type=jnp.float32)
        * score_scale
    )
    return jnp.where(causal[None, None], scores, neg_large)


def forward_micro(tokens_now, segment, route_now, dense_set, expert_set, shapes):
    expert_count, capacity, group_count, local_experts = shapes
    gain_attn, qkv_weight, out_weight, gain_ffn, router_weight = dense_set
    expert_up, expert_down = expert_set
    row_count = tokens_now.shape[0]
    groups = HEADS // KV_HEADS
    q_width = HEADS * HEAD
    k_width = KV_HEADS * HEAD
    inputs = tokens_now.astype(jnp.float32)
    inv_first = lax.rsqrt(jnp.mean(inputs * inputs, axis=1, keepdims=True) + norm_eps)
    normed_first = (inputs * inv_first * gain_attn.astype(jnp.float32)).astype(jnp.bfloat16)
    qkv_full = jnp.dot(normed_first, qkv_weight, preferred_element_type=jnp.float32)
    cosine, sine_table, causal = rope_tables(segment, HEAD // 2)
    queries = rotate(
        qkv_full[:, :q_width].reshape(row_count, KV_HEADS, groups, HEAD),
        cosine[:, None, None, :],
        sine_table[:, None, None, :],
    ).astype(jnp.bfloat16)
    key_rot = rotate(
        qkv_full[:, q_width : q_width + k_width].reshape(row_count, KV_HEADS, HEAD),
        cosine[:, None, :],
        sine_table[:, None, :],
    ).astype(jnp.bfloat16)
    values = (
        qkv_full[:, q_width + k_width :].reshape(row_count, KV_HEADS, HEAD).astype(jnp.bfloat16)
    )
    scores = attention_scores(queries, key_rot, causal)
    score_peak = jnp.max(scores, axis=-1, keepdims=True)
    exp_scores = jnp.exp(scores - score_peak)
    exp_total = jnp.sum(exp_scores, axis=-1, keepdims=True)
    log_total = score_peak + jnp.log(exp_total)
    soft_probs = (exp_scores / exp_total).astype(jnp.bfloat16)
    attn_mixed = jnp.einsum(
        "kgts,skh->tkgh", soft_probs, values, preferred_element_type=jnp.float32
    )
    attn_mixed = attn_mixed.reshape(row_count, q_width).astype(jnp.bfloat16)
    middle = inputs + jnp.dot(attn_mixed, out_weight, preferred_element_type=jnp.float32)
    inv_second = lax.rsqrt(jnp.mean(middle * middle, axis=1, keepdims=True) + norm_eps)
    normed_second = (middle * inv_second * gain_ffn.astype(jnp.float32)).astype(jnp.bfloat16)
    logits = jnp.dot(normed_second, router_weight, preferred_element_type=jnp.float32)
    chosen = (
        route_now[:, :, None] == jnp.arange(expert_count, dtype=jnp.int32)[None, None, :]
    ).astype(jnp.float32)
    picked_logits = jnp.sum(chosen * logits[:, None, :], axis=-1)
    gate_values = jax.nn.softmax(picked_logits, axis=-1)
    targets = slot_targets(route_now, expert_count, capacity)
    source_rows = jnp.repeat(normed_second, TOP_K, axis=0)
    buffer = jnp.zeros((expert_count * capacity, D), jnp.bfloat16).at[targets].set(source_rows)
    send_rows = buffer.reshape(group_count, local_experts, capacity, D)
    received = lax.all_to_all(send_rows, "expert", split_axis=0, concat_axis=0, tiled=True)
    gate_up = jnp.einsum("secd,edf->secf", received, expert_up, preferred_element_type=jnp.float32)
    hidden = (jax.nn.silu(gate_up[..., :FF]) * gate_up[..., FF:]).astype(jnp.bfloat16)
    expert_result = jnp.einsum(
        "secf,efd->secd", hidden, expert_down, preferred_element_type=jnp.float32
    ).astype(jnp.bfloat16)
    returned = lax.all_to_all(expert_result, "expert", split_axis=0, concat_axis=0, tiled=True)
    picked = returned.reshape(expert_count * capacity, D)[targets].reshape(row_count, TOP_K, D)
    moe_sum = jnp.einsum(
        "tk,tkd->td", gate_values, picked, precision=highest, preferred_element_type=jnp.float32
    )
    result = (middle + moe_sum).astype(jnp.bfloat16)
    saved_state = (
        inputs,
        inv_first,
        normed_first,
        queries,
        key_rot,
        values,
        log_total,
        causal,
        cosine,
        sine_table,
        attn_mixed,
        middle,
        inv_second,
        normed_second,
        chosen,
        gate_values,
        targets,
        received,
        gate_up,
        hidden,
        picked,
    )
    return (result, saved_state)


def backward_micro(saved_state, cotan_now, dense_set, expert_set, shapes):
    expert_count, capacity, group_count, local_experts = shapes
    (
        inputs,
        inv_first,
        normed_first,
        queries,
        key_rot,
        values,
        log_total,
        causal,
        cosine,
        sine_table,
        attn_mixed,
        middle,
        inv_second,
        normed_second,
        chosen,
        gate_values,
        targets,
        received,
        gate_up,
        hidden,
        picked,
    ) = saved_state
    gain_attn, qkv_weight, out_weight, gain_ffn, router_weight = dense_set
    expert_up, expert_down = expert_set
    row_count = inputs.shape[0]
    groups = HEADS // KV_HEADS
    q_width = HEADS * HEAD
    k_width = KV_HEADS * HEAD
    score_scale = HEAD ** (-0.5)
    upstream = cotan_now.astype(jnp.float32)
    grad_gates = jnp.einsum(
        "td,tkd->tk", upstream, picked, precision=highest, preferred_element_type=jnp.float32
    )
    grad_picked = gate_values * (
        grad_gates - jnp.sum(gate_values * grad_gates, axis=-1, keepdims=True)
    )
    grad_logits = jnp.sum(chosen * grad_picked[:, :, None], axis=1).astype(jnp.bfloat16)
    grad_router = jnp.einsum(
        "td,te->de", normed_second, grad_logits, preferred_element_type=jnp.float32
    )
    grad_second = jnp.einsum(
        "te,de->td", grad_logits, router_weight, preferred_element_type=jnp.float32
    )
    grad_slots = (
        (gate_values[:, :, None] * upstream[:, None, :])
        .astype(jnp.bfloat16)
        .reshape(row_count * TOP_K, D)
    )
    grad_buffer = jnp.zeros((expert_count * capacity, D), jnp.bfloat16).at[targets].set(grad_slots)
    grad_buffer = grad_buffer.reshape(group_count, local_experts, capacity, D)
    grad_result = lax.all_to_all(grad_buffer, "expert", split_axis=0, concat_axis=0, tiled=True)
    grad_hidden = jnp.einsum(
        "secd,efd->secf", grad_result, expert_down, preferred_element_type=jnp.float32
    )
    grad_down = jnp.einsum(
        "secf,secd->efd", hidden, grad_result, preferred_element_type=jnp.float32
    )
    gate_part = gate_up[..., :FF]
    up_part = gate_up[..., FF:]
    gate_sigmoid = jax.nn.sigmoid(gate_part)
    grad_gate = grad_hidden * up_part * gate_sigmoid * (1.0 + gate_part * (1.0 - gate_sigmoid))
    grad_up_part = grad_hidden * (gate_part * gate_sigmoid)
    grad_gate_up = jnp.concatenate([grad_gate, grad_up_part], axis=-1).astype(jnp.bfloat16)
    grad_up = jnp.einsum(
        "secd,secf->edf", received, grad_gate_up, preferred_element_type=jnp.float32
    )
    grad_rows = jnp.einsum(
        "secf,edf->secd", grad_gate_up, expert_up, preferred_element_type=jnp.float32
    ).astype(jnp.bfloat16)
    grad_back = lax.all_to_all(grad_rows, "expert", split_axis=0, concat_axis=0, tiled=True)
    grad_choice = grad_back.reshape(expert_count * capacity, D)[targets].reshape(
        row_count, TOP_K, D
    )
    grad_second = grad_second + jnp.sum(grad_choice, axis=1, dtype=jnp.float32)
    unit_second = middle * inv_second
    pull_second = grad_second * gain_ffn.astype(jnp.float32)
    grad_gain_ffn = jnp.sum(grad_second * unit_second, axis=0)
    grad_middle = upstream + inv_second * (
        pull_second - unit_second * jnp.mean(pull_second * unit_second, axis=1, keepdims=True)
    )
    grad_branch = grad_middle.astype(jnp.bfloat16)
    grad_out_weight = jnp.einsum(
        "tc,td->cd", attn_mixed, grad_branch, preferred_element_type=jnp.float32
    )
    grad_mixed = jnp.einsum(
        "td,cd->tc", grad_branch, out_weight, preferred_element_type=jnp.float32
    )
    grad_mixed = grad_mixed.astype(jnp.bfloat16).reshape(row_count, KV_HEADS, groups, HEAD)
    scores = attention_scores(queries, key_rot, causal)
    soft_probs = jnp.exp(scores - log_total)
    grad_values = jnp.einsum(
        "kgts,tkgh->skh",
        soft_probs.astype(jnp.bfloat16),
        grad_mixed,
        preferred_element_type=jnp.float32,
    )
    grad_probs = jnp.einsum(
        "tkgh,skh->kgts", grad_mixed, values, preferred_element_type=jnp.float32
    )
    grad_scores = soft_probs * (
        grad_probs - jnp.sum(soft_probs * grad_probs, axis=-1, keepdims=True)
    )
    grad_scores = grad_scores.astype(jnp.bfloat16)
    grad_query = (
        jnp.einsum("kgts,skh->tkgh", grad_scores, key_rot, preferred_element_type=jnp.float32)
        * score_scale
    )
    grad_key = (
        jnp.einsum("kgts,tkgh->skh", grad_scores, queries, preferred_element_type=jnp.float32)
        * score_scale
    )
    grad_query = unrotate(grad_query, cosine[:, None, None, :], sine_table[:, None, None, :])
    grad_key = unrotate(grad_key, cosine[:, None, :], sine_table[:, None, :])
    grad_qkv = jnp.concatenate(
        [
            grad_query.reshape(row_count, q_width),
            grad_key.reshape(row_count, k_width),
            grad_values.reshape(row_count, k_width),
        ],
        axis=1,
    ).astype(jnp.bfloat16)
    grad_qkv_weight = jnp.einsum(
        "tc,tq->cq", normed_first, grad_qkv, preferred_element_type=jnp.float32
    )
    grad_first = jnp.einsum("tq,cq->tc", grad_qkv, qkv_weight, preferred_element_type=jnp.float32)
    unit_first = inputs * inv_first
    pull_first = grad_first * gain_attn.astype(jnp.float32)
    grad_gain_attn = jnp.sum(grad_first * unit_first, axis=0)
    grad_inputs = grad_middle + inv_first * (
        pull_first - unit_first * jnp.mean(pull_first * unit_first, axis=1, keepdims=True)
    )
    dense_grads = (grad_gain_attn, grad_qkv_weight, grad_out_weight, grad_gain_ffn, grad_router)
    expert_grads = (grad_up, grad_down)
    return (grad_inputs, dense_grads, expert_grads)


def add_pair(left_part, right_part):
    return left_part + right_part


def per_device(
    tokens,
    segments,
    routes,
    cotangent,
    gain_attn,
    attn_in,
    attn_out,
    gain_ffn,
    router,
    expert_in,
    expert_out,
):
    local_experts = expert_in.shape[0]
    group_count = lax.axis_size("expert")
    expert_count = local_experts * group_count
    micro_count = tokens.shape[0]
    row_count = tokens.shape[1]
    capacity = (row_count * TOP_K * 5 // (4 * expert_count) + 7) // 8 * 8
    shapes = (expert_count, capacity, group_count, local_experts)
    outputs = []
    grad_list = []
    dense_total = None
    expert_total = None
    for micro_index in range(micro_count):
        dense_set = dense_fetch(gain_attn, attn_in, attn_out, gain_ffn, router)
        expert_set = expert_fetch(expert_in, expert_out)
        result, saved_state = forward_micro(
            tokens[micro_index],
            segments[micro_index, 0],
            routes[micro_index],
            dense_set,
            expert_set,
            shapes,
        )
        dense_set = dense_fetch(gain_attn, attn_in, attn_out, gain_ffn, router)
        expert_set = expert_fetch(expert_in, expert_out)
        grad_inputs, dense_grads, expert_grads = backward_micro(
            saved_state, cotangent[micro_index], dense_set, expert_set, shapes
        )
        dense_grads = dense_reduce(dense_grads)
        expert_grads = expert_reduce(expert_grads)
        if dense_total is None:
            dense_total = dense_grads
            expert_total = expert_grads
        else:
            dense_total = jax.tree.map(add_pair, dense_total, dense_grads)
            expert_total = jax.tree.map(add_pair, expert_total, expert_grads)
        outputs.append(result)
        grad_list.append(grad_inputs)
    return (
        jnp.stack(outputs, axis=0),
        jnp.stack(grad_list, axis=0),
        dense_total[0],
        dense_total[1],
        dense_total[2],
        dense_total[3],
        dense_total[4],
        expert_total[0],
        expert_total[1],
    )


NN = (((1,), (0,)), ((), ()))
NT = (((1,), (1,)), ((), ()))
TN = (((0,), (0,)), ((), ()))


def mm(a, b, dims=NN):
    return lax.dot_general(a, b, dims, preferred_element_type=jnp.float32)


class Place:
    def __init__(self, n):
        self.n = n
        d = self.d = lax.axis_index("dp")
        e = self.e = lax.axis_index("expert")
        c, x, y = lax.rem(e, 2), lax.rem(lax.div(e, 2), 2), lax.div(e, 4)
        self.sib = (d, e + 1 - 2 * c)
        self.nx = (d, e + 2 - 4 * x)
        self.ny = (d, e + 4 - 8 * y)
        self.diag = self.nx[1] + 4 - 8 * y
        self.c, self.x, self.y = c, x, y
        self.below = (d - 1, e)
        self.above = (d + 1, e)
        self.has_below = d > 0
        self.has_above = d < n - 1

    def meet(self, everyone=False):
        barrier = pltpu.get_barrier_semaphore()
        d, n = self.d, self.n
        if everyone:
            others = n - 1 + 3

            @pl.loop(1, n)
            def _(k):
                pl.semaphore_signal(barrier, inc=1, device_id=(lax.rem(d + k, n), self.e), device_id_type=MESH)
        else:
            others = 3 + jnp.minimum(d, 1) + jnp.minimum(n - 1 - d, 1)

            @pl.when(self.has_below)
            def _():
                pl.semaphore_signal(barrier, inc=1, device_id=self.below, device_id_type=MESH)

            @pl.when(self.has_above)
            def _():
                pl.semaphore_signal(barrier, inc=1, device_id=self.above, device_id_type=MESH)

        for dev in (self.sib, self.nx, self.ny):
            pl.semaphore_signal(barrier, inc=1, device_id=dev, device_id_type=MESH)
        pl.semaphore_wait(barrier, others)

    def far(self, i):
        n, d = self.n, self.d
        low = d < n - d
        m = jnp.where(low, d, n - 1 - d)
        t = jnp.where(i < n - 1 - m, n - 1 - i, jnp.where(i < n - 1, i - (n - 1 - m), m))
        return jnp.where(low, t, n - 1 - t)

    def near(self, i):
        return self.far(self.n - 1 - i)


def send(src, dst, ss, rs, dev):
    return pltpu.make_async_remote_copy(src, dst, ss, rs, device_id=dev, device_id_type=MESH)


class Gather:
    def __init__(self, at, own, buf, send_sem, recv_z, recv_x, recv_y, recv_d, rows=None):
        self.at, self.own, self.buf = at, own, buf
        self.ss, self.rz, self.rx, self.ry, self.rd = send_sem, recv_z, recv_x, recv_y, recv_d
        rows = rows or own.shape[0]
        self.F, self.A, self.B = pl.ds(0, rows), pl.ds(0, rows // 2), pl.ds(rows // 2, rows // 2)

    def source(self, zz, own):
        return self.own.at[self.F] if own else self.buf.at[zz, 0, self.F]

    def down(self, zz, own=False):
        return send(self.source(zz, own), self.buf.at[zz, 0, self.F], self.ss.at[zz, 0], self.rz.at[zz], self.at.below)

    def up(self, zz, own=False):
        return send(self.source(zz, own), self.buf.at[zz, 0, self.F], self.ss.at[zz, 1], self.rz.at[zz], self.at.above)

    def to_x(self, zz, own=False):
        return send(self.source(zz, own), self.buf.at[zz, 1, self.F], self.ss.at[zz, 2], self.rx.at[zz], self.at.nx)

    def to_y(self, zz, own=False):
        return send(self.source(zz, own), self.buf.at[zz, 2, self.F], self.ss.at[zz, 3], self.ry.at[zz], self.at.ny)

    def turn_y(self, zz):
        return send(self.buf.at[zz, 1, self.A], self.buf.at[zz, 3, self.A], self.ss.at[zz, 4], self.rd.at[zz, 0], self.at.ny)

    def turn_x(self, zz):
        return send(self.buf.at[zz, 2, self.B], self.buf.at[zz, 3, self.B], self.ss.at[zz, 5], self.rd.at[zz, 1], self.at.nx)

    def begin(self):
        self.begin_z()
        self.begin_xy()

    def begin_z(self):
        d = self.at.d

        @pl.when(self.at.has_below)
        def _():
            self.down(d, True).start()

        @pl.when(self.at.has_above)
        def _():
            self.up(d, True).start()

    def begin_xy(self):
        self.to_x(self.at.d, True).start()
        self.to_y(self.at.d, True).start()

    def column_z(self, zz):
        d = self.at.d

        @pl.when(zz < d)
        def _():
            self.up(zz).wait_recv()

            @pl.when(self.at.has_above)
            def _():
                self.up(zz).start()

        @pl.when(zz > d)
        def _():
            self.down(zz).wait_recv()

            @pl.when(self.at.has_below)
            def _():
                self.down(zz).start()

    def column_xy(self, zz):
        self.to_x(zz).start()
        self.to_y(zz).start()

    def column(self, zz):
        self.column_z(zz)
        self.column_xy(zz)

    def plane(self, zz):
        self.to_x(zz).wait_recv()
        self.turn_y(zz).start()
        self.to_y(zz).wait_recv()
        self.turn_x(zz).start()

    def corner(self, zz):
        self.turn_y(zz).wait_recv()
        self.turn_x(zz).wait_recv()

    def finish(self):
        d = self.at.d

        @pl.loop(0, self.at.n)
        def _(zz):
            for copy in (self.to_x, self.to_y, self.turn_y, self.turn_x):
                copy(zz).wait_send()

            @pl.when((d > 0) & (zz >= d))
            def _():
                self.down(zz).wait_send()

            @pl.when(self.at.has_above & (zz <= d))
            def _():
                self.up(zz).wait_send()


class LineGather:
    def __init__(self, at, own, buf, lo, ss, sr, zs, zr):
        self.at, self.own, self.buf = at, own, buf
        self.ss, self.sr, self.zs, self.zr = ss, sr, zs, zr
        rows = own.shape[0] - lo
        self.P, self.A, self.B = pl.ds(lo, rows), pl.ds(lo, rows // 2), pl.ds(lo + rows // 2, rows // 2)

    def inside(self, k):
        at, buf, d = self.at, self.buf, self.at.d
        src, slot, part, dev = (
            (self.own.at[self.P], 1, self.P, at.nx), (self.own.at[self.P], 2, self.P, at.ny),
            (buf.at[d, 1, self.A], 3, self.A, at.ny), (buf.at[d, 2, self.B], 3, self.B, at.nx))[k]
        return send(src, buf.at[d, slot, part], self.ss.at[k], self.sr.at[k], dev)

    def along(self, zz, up):
        part = self.buf.at[zz, :, self.P]
        return send(part, part, self.zs.at[zz, up], self.zr.at[zz], self.at.above if up else self.at.below)

    def begin(self):
        self.inside(0).start()
        self.inside(1).start()

    def plane(self):
        self.inside(0).wait_recv()
        self.inside(2).start()
        self.inside(1).wait_recv()
        self.inside(3).start()

    def corner(self):
        self.inside(2).wait_recv()
        self.inside(3).wait_recv()

        @pl.when(self.at.has_below)
        def _():
            self.along(self.at.d, 0).start()

        @pl.when(self.at.has_above)
        def _():
            self.along(self.at.d, 1).start()

    def line(self, zz):
        self.along(zz, 0).wait_recv()

        @pl.when((zz < self.at.d) & self.at.has_above)
        def _():
            self.along(zz, 1).start()

        @pl.when((zz > self.at.d) & self.at.has_below)
        def _():
            self.along(zz, 0).start()

    def finish(self):
        d = self.at.d
        for k in range(4):
            self.inside(k).wait_send()

        @pl.loop(0, self.at.n)
        def _(zz):
            @pl.when(self.at.has_below & (zz >= d))
            def _():
                self.along(zz, 0).wait_send()

            @pl.when(self.at.has_above & (zz <= d))
            def _():
                self.along(zz, 1).wait_send()


def line_gather_sems(n):
    D_ = pltpu.SemaphoreType.DMA
    return [D_((4,)), D_((4,)), D_((n, 2)), D_((n,))]


def gather_sems(n):
    D_ = pltpu.SemaphoreType.DMA
    return [D_((n, 6)), D_((n,)), D_((n,)), D_((n,)), D_((n, 2))]


def add_rows(dst, src):
    rows = dst.shape[0]
    step = 16

    @pl.loop(0, rows // step)
    def _(r):
        w = pl.ds(pl.multiple_of(r * step, step), step)
        dst[w, :] = (dst[w, :].astype(jnp.float32) + src[w, :].astype(jnp.float32)).astype(dst.dtype)


class Reduce:
    def __init__(self, at, buf, total, r1, r2, rz, ss_1, sr_1, ss_2, sr_2, ss_z, sr_z, start=None):
        self.start = start
        self.at, self.buf, self.total = at, buf, total
        self.r1, self.r2, self.rz = r1, r2, rz
        self.sems = (ss_1, sr_1, ss_2, sr_2, ss_z, sr_z)
        rows = total.shape[0]
        self.A, self.B = pl.ds(0, rows // 2), pl.ds(rows // 2, rows // 2)

    def first(self, zz, k):
        ss, sr = self.sems[0], self.sems[1]
        slot, part, dev = ((3, self.A, self.at.nx), (3, self.B, self.at.ny), (1, self.A, self.at.nx), (2, self.B, self.at.ny))[k]
        return send(self.buf.at[zz, slot, part], self.r1.at[zz, k], ss.at[zz, k], sr.at[zz, k], dev)

    def second(self, zz, k):
        ss, sr = self.sems[2], self.sems[3]
        slot, part, dev = ((2, self.A, self.at.ny), (1, self.B, self.at.nx))[k]
        return send(self.buf.at[zz, slot, part], self.r2.at[zz, k], ss.at[zz, k], sr.at[zz, k], dev)

    def down(self, zz):
        return send(self.buf.at[zz, 0], self.rz.at[zz], self.sems[4].at[zz], self.sems[5].at[zz], self.at.below)

    def up(self, zz):
        slot = jnp.where(zz == self.at.d + 1, self.at.n, zz)
        return send(self.buf.at[zz, 0], self.rz.at[slot], self.sems[4].at[zz], self.sems[5].at[slot], self.at.above)

    def arrive(self, slot):
        return send(self.buf.at[0, 0], self.rz.at[slot], self.sems[4].at[0], self.sems[5].at[slot], self.at.nx)

    def s1(self, zz):
        self.corners(zz)
        self.sides(zz)

    def corners(self, zz):
        self.first(zz, 0).start()
        self.first(zz, 1).start()

    def sides(self, zz):
        self.first(zz, 2).start()
        self.first(zz, 3).start()

    def turn(self, zz):
        self.first(zz, 0).wait_recv()
        add_rows(self.buf.at[zz, 2, self.A], self.r1.at[zz, 0])
        self.second(zz, 0).start()
        self.first(zz, 1).wait_recv()
        add_rows(self.buf.at[zz, 1, self.B], self.r1.at[zz, 1])
        self.second(zz, 1).start()

    def take_sides(self, zz):
        self.first(zz, 2).wait_recv()
        add_rows(self.buf.at[zz, 0, self.A], self.r1.at[zz, 2])
        self.first(zz, 3).wait_recv()
        add_rows(self.buf.at[zz, 0, self.B], self.r1.at[zz, 3])

    def s2(self, zz):
        self.turn(zz)
        self.take_sides(zz)

    def step(self, j):
        at = self.at
        if j < at.n:
            self.turn(at.far(j))
            self.sides(at.far(j))
            if j + 2 < at.n:
                self.corners(at.far(j + 2))
        if j >= 1:
            self.take_sides(at.far(j - 1))
            self.s3(at.far(j - 1))
            self.lines(j - 1)

    def s3(self, zz):
        self.second(zz, 0).wait_recv()
        add_rows(self.buf.at[zz, 0, self.A], self.r2.at[zz, 0])
        self.second(zz, 1).wait_recv()
        add_rows(self.buf.at[zz, 0, self.B], self.r2.at[zz, 1])

    def push(self, zz):
        d = self.at.d

        @pl.when(zz < d)
        def _():
            self.down(zz).start()

        @pl.when(zz > d)
        def _():
            self.up(zz).start()

    def line_head(self, zz):
        @pl.when(jnp.logical_not(self.passes(zz)))
        def _():
            self.push(zz)

    def passes(self, zz):
        d = self.at.d
        return ((zz < d) & self.at.has_above) | ((zz > d) & self.at.has_below)

    def line_rest(self, zz):
        @pl.when(self.passes(zz))
        def _():
            self.arrive(zz).wait_recv()
            add_rows(self.buf.at[zz, 0], self.rz.at[zz])
            self.push(zz)

    def lines(self, j):
        n = self.at.n
        if j < n - 1:
            self.line_head(self.at.far(j))
        if 0 <= j - 1 < n - 2:
            self.line_rest(self.at.far(j - 1))
        if j == n - 2:
            self.line_rest(self.at.far(j))

    def last(self):
        d, n, rows, step = self.at.d, self.at.n, self.total.shape[0], 16

        def over(fn):
            @pl.loop(0, rows // step)
            def _(r):
                fn(pl.ds(pl.multiple_of(r * step, step), step))

        def own(w):
            first = self.buf[d, 0, w, :].astype(jnp.float32)
            self.total[w, :] = first if self.start is None else first + self.start[w, :]

        def more(slot):
            def fn(w):
                self.total[w, :] += self.rz[slot, w, :].astype(jnp.float32)

            self.arrive(slot).wait_recv()
            over(fn)

        over(own)

        @pl.when(self.at.has_above)
        def _():
            more(d)

        @pl.when(self.at.has_below)
        def _():
            more(n)

    def finish(self):
        d = self.at.d

        @pl.loop(0, self.at.n)
        def _(zz):
            for k in range(4):
                self.first(zz, k).wait_send()
            for k in range(2):
                self.second(zz, k).wait_send()

            @pl.when(zz != d)
            def _():
                self.arrive(zz)
                send(self.buf.at[zz, 0], self.rz.at[zz], self.sems[4].at[zz], self.sems[5].at[zz], self.at.nx).wait_send()


def reduce_scratch(n, rows, cols):
    D_ = pltpu.SemaphoreType.DMA
    V = lambda *s: pltpu.VMEM(s, jnp.bfloat16)
    return [V(n, 4, rows // 2, cols), V(n, 2, rows // 2, cols), V(n + 1, rows, cols),
            D_((n, 4)), D_((n, 4)), D_((n, 2)), D_((n, 2)), D_((n,)), D_((n + 1,))]


def expert_kernel(n, experts, x_ref, cot_ref, up_ref, down_ref, mid_ref,
                  out_ref, gx_ref, gup_ref, gdown_out,
                  gdown_ref, xb, cb, gg, mixed, gb, wup, wdown, pick_ref, place_ref, *rest):
    f32, bf16 = jnp.float32, jnp.bfloat16
    at = Place(n)
    d = at.d
    lo = x_ref.shape[0] * 3 // 4
    gather = Gather(at, x_ref, xb, *rest[:5], rows=lo)
    tail = LineGather(at, x_ref, xb, lo, *rest[-4:])
    grads = Reduce(at, gb, gx_ref, *rest[5:14])
    outs = Reduce(at, gg, out_ref, *rest[14:23], start=mid_ref)
    load_sem, core_ss, core_sr, free = rest[23:-4]
    rows = x_ref.shape[0]
    f2 = up_ref.shape[1]
    f = f2 // 2
    held = f // 128
    loads = [
        pltpu.make_async_copy(x_ref, xb.at[d, 0], load_sem.at[0]),
        pltpu.make_async_copy(up_ref, wup.at[0], load_sem.at[1]),
        pltpu.make_async_copy(down_ref, wdown.at[0], load_sem.at[2]),
        pltpu.make_async_copy(cot_ref, cb, load_sem.at[3]),
    ]
    for load in loads:
        load.start()
    at.meet()
    gather.begin_z()
    tail.begin()
    gather.begin_xy()
    swaps = [
        send(up_ref, wup.at[1], core_ss.at[0], core_sr.at[0], at.sib),
        send(down_ref, wdown.at[1], core_ss.at[1], core_sr.at[1], at.sib),
    ]
    for swap in swaps:
        swap.start()
    for h, owner in ((0, at.e), (1, at.sib[1])):
        for j in range(held):
            expert, cols = owner * held + j, slice((h * held + j) * 128, (h * held + j + 1) * 128)
            gate_row = lax.broadcasted_iota(jnp.int32, (128, 128), 0)
            pick_ref[:, cols] = ((gate_row == expert) | (gate_row == expert + experts)).astype(bf16)
            place_ref[cols, :] = (lane_tile(128) == expert).astype(bf16)
    loads[0].wait()
    tail.plane()
    tail.corner()
    gather.plane(at.near(0))
    gather.column(at.near(1))
    for load in loads[1:]:
        load.wait()
    for swap in swaps:
        swap.wait_recv()

    def tokens(ref, zz, p, lo, width):
        return ref[zz, pl.ds(2 * p, 2), :, pl.ds(lo, width)].reshape(2 * rows, width)

    def half(zz, p):
        pair = pl.ds(2 * p, 2)
        x = tokens(xb, zz, p, 0, D)
        cot = tokens(cb, zz, p, 0, D)
        mix = mm(tokens(xb, zz, p, D, 128), pick_ref[...])
        sums = jnp.zeros((2 * rows, 128), f32)
        for h in range(2):
            gate_up = mm(x, wup[h])
            back = mm(cot, wdown[h], NT)
            for j in range(held):
                k = h * held + j
                gate = gate_up[:, j * 256 : j * 256 + 128]
                up = gate_up[:, j * 256 + 128 : j * 256 + 256]
                b = back[:, j * 128 : (j + 1) * 128]
                m = mix[:, k * 128 : (k + 1) * 128]
                sig = 1.0 / (1.0 + jnp.exp(-gate))
                act = gate * sig
                hidden = (act * up).astype(bf16).astype(f32)
                prod = hidden * b
                high = prod.astype(bf16)
                low = (prod - high.astype(f32)).astype(bf16)
                sel = place_ref[k * 128 : (k + 1) * 128, :]
                sums += mm(high, sel) + mm(low, sel)
                mixed[zz, pair, :, pl.ds(k * 128, 128)] = (m * hidden).astype(bf16).reshape(2, rows, 128)
                gh = m * b
                gg[zz, pair, :, pl.ds(k * 256, 128)] = (
                    (gh * up * sig * (1.0 + gate * (1.0 - sig))).astype(bf16).reshape(2, rows, 128))
                gg[zz, pair, :, pl.ds(k * 256 + 128, 128)] = (gh * act).astype(bf16).reshape(2, rows, 128)
        for q in range(D // 512):
            cols = pl.ds(q * 512, 512)
            part = mm(tokens(gg, zz, p, 0, f2), wup[0, cols, :], NT) + mm(tokens(gg, zz, p, f2, f2), wup[1, cols, :], NT)
            gb[zz, pair, :, cols] = part.astype(bf16).reshape(2, rows, 512)
        gb[zz, pair, :, pl.ds(D, 128)] = sums.astype(bf16).reshape(2, rows, 128)

    @pl.loop(0, n)
    def _(i):
        zz = at.near(i)
        half(zz, 0)

        @pl.when(i + 2 < n)
        def _():
            gather.column(at.near(i + 2))

        @pl.when(i + 1 < n)
        def _():
            tail.line(at.near(i + 1))
            gather.plane(at.near(i + 1))

        gather.corner(zz)
        half(zz, 1)
        grads.s1(zz)

        @pl.when(i >= 1)
        def _():
            grads.s2(at.near(i - 1))

        @pl.when(i >= 2)
        def _():
            grads.s3(at.near(i - 2))
            grads.line_head(at.near(i - 2))

    pl.semaphore_signal(free.at[0], inc=1, device_id=at.sib, device_id_type=MESH)

    def grad_up(h, more):
        @pl.loop(0, D // 256)
        def _(q):
            cols = pl.ds(pl.multiple_of(q * 256, 256), 256)
            xs = xb[:, :, :, cols].reshape(n * 4 * rows, 256)
            part = mm(xs, gg[:, :, :, pl.ds(h * f2, f2)].reshape(n * 4 * rows, f2), TN)
            if more:
                part += wup[h, cols, :].astype(f32)
            wup[h, cols, :] = part.astype(bf16)

    def grad_down(h):
        for q in range(D // 512):
            cols = pl.ds(q * 512, 512)
            part = mm(mixed[:, :, :, pl.ds(h * f, f)].reshape(n * 4 * rows, f), cb[:, :, :, cols].reshape(n * 4 * rows, 512), TN)
            if h == 0:
                gdown_ref[:, cols] = part + wdown[0, :, cols].astype(f32)
            else:
                wdown[1, :, cols] = part.astype(bf16)

    def output(zz):
        @pl.loop(0, 2)
        def _(p):
            for q in range(D // 512):
                cols = pl.ds(q * 512, 512)
                part = mm(tokens(mixed, zz, p, 0, f), wdown[0, :, cols]) + mm(tokens(mixed, zz, p, f, f), wdown[1, :, cols])
                gg[zz, pl.ds(2 * p, 2), :, cols] = part.astype(bf16).reshape(2, rows, 512)

    grad_up(1, False)
    pl.semaphore_wait(free.at[0], 1)
    up_swap = send(wup.at[1], wup.at[0], core_ss.at[2], core_sr.at[2], at.sib)
    for swap in swaps:
        swap.wait_send()
    up_swap.start()
    grads.s2(at.near(n - 1))
    grads.s3(at.near(n - 2))
    grads.line_head(at.near(n - 2))
    up_swap.wait_recv()
    grad_up(0, True)
    keep = pltpu.make_async_copy(wup.at[0], gup_ref, load_sem.at[0])
    keep_down = pltpu.make_async_copy(gdown_ref, gdown_out, load_sem.at[1])
    keep.start()
    grads.s3(at.near(n - 1))
    grads.line_head(at.near(n - 1))
    for j in range(n):
        output(at.far(j))
        if j < 2:
            outs.corners(at.far(j))
    pl.semaphore_signal(free.at[1], inc=1, device_id=at.sib, device_id_type=MESH)
    grad_down(1)
    pl.semaphore_wait(free.at[1], 1)
    down_swap = send(wdown.at[1], wdown.at[0], core_ss.at[3], core_sr.at[3], at.sib)
    down_swap.start()
    for j in range(n + 1):
        if j == n:
            grads.last()
        outs.step(j)
        if j < n - 1:
            grads.line_rest(at.far(j))
        if j == 0:
            down_swap.wait_recv()
            grad_down(0)
            keep_down.start()
    outs.last()
    keep_down.wait()
    keep.wait()
    up_swap.wait_send()
    down_swap.wait_send()
    gather.finish()
    tail.finish()
    grads.finish()
    outs.finish()


def expert_layer(x, cot_all, up, down, middle, n, experts, cid):
    rows, wide = x.shape
    f2 = up.shape[1]
    f = f2 // 2
    bf16 = jnp.bfloat16
    V = lambda *s: pltpu.VMEM(s, bf16)
    D_ = pltpu.SemaphoreType.DMA
    any_, vm = pl.BlockSpec(memory_space=pl.ANY), pl.BlockSpec(memory_space=pltpu.VMEM)
    return pl.pallas_call(
        functools.partial(expert_kernel, n, experts),
        out_shape=(
            jax.ShapeDtypeStruct((rows, D), jnp.float32),
            jax.ShapeDtypeStruct((rows, wide), jnp.float32),
            jax.ShapeDtypeStruct((D, f2), bf16),
            jax.ShapeDtypeStruct((f, D), jnp.float32),
        ),
        in_specs=[any_, any_, any_, any_, vm],
        out_specs=[vm, vm, any_, any_],
        scratch_shapes=[pltpu.VMEM((f, D), jnp.float32), V(n, 4, rows, wide), V(n, 4, rows, D), V(n, 4, rows, 2 * f2), V(n, 4, rows, 2 * f), V(n, 4, rows, wide),
                        V(2, D, f2), V(2, f, D), V(128, 2 * f), V(2 * f, 128)]
        + gather_sems(n) + reduce_scratch(n, rows, wide) + reduce_scratch(n, rows, D)
        + [D_((4,)), D_((4,)), D_((4,)), pltpu.SemaphoreType.REGULAR((2,))] + line_gather_sems(n),
        compiler_params=pltpu.CompilerParams(collective_id=cid, has_side_effects=True, vmem_limit_bytes=63 << 20),
        name="expert_layer",
    )(x, cot_all, up, down, middle)


class GatherAll:
    def __init__(self, at, own, buf, send_sem, recv_z, recv_x, recv_y, recv_d, recv_s):
        self.at, self.own, self.buf = at, own, buf
        self.ss, self.rz, self.rx, self.ry, self.rd, self.rs = send_sem, recv_z, recv_x, recv_y, recv_d, recv_s
        cols = own.shape[1]
        half = (cols // 128 + 1) // 2 * 128
        self.A, self.B, self.F = pl.ds(0, half), pl.ds(half, cols - half), pl.ds(0, cols)

    def move(self, zz, e, cols, slot, sem, dev, own=False):
        dst = self.buf.at[zz * 8 + e, :, cols]
        return send(self.own.at[:, cols] if own else dst, dst, self.ss.at[zz, slot], sem, dev)

    def down(self, zz, own=False):
        return self.move(zz, self.at.e, self.F, 0, self.rz.at[zz], self.at.below, own)

    def up(self, zz, own=False):
        return self.move(zz, self.at.e, self.F, 1, self.rz.at[zz], self.at.above, own)

    def spread(self, zz, own=False):
        at = self.at
        return (self.move(zz, at.e, self.F, 2, self.rx.at[zz], at.nx, own),
                self.move(zz, at.e, self.F, 3, self.ry.at[zz], at.ny, own),
                self.move(zz, at.e, self.F, 4, self.rs.at[zz, 0], at.sib, own))

    def from_x(self, zz):
        at = self.at
        ex = at.nx[1]
        return (self.move(zz, ex, self.F, 2, self.rx.at[zz], at.nx),
                self.move(zz, ex, self.A, 5, self.rd.at[zz, 0], at.ny),
                self.move(zz, ex, self.F, 6, self.rs.at[zz, 1], at.sib))

    def from_y(self, zz):
        at = self.at
        ey = at.ny[1]
        return (self.move(zz, ey, self.F, 3, self.ry.at[zz], at.ny),
                self.move(zz, ey, self.B, 7, self.rd.at[zz, 1], at.nx),
                self.move(zz, ey, self.F, 8, self.rs.at[zz, 2], at.sib))

    def turned(self, zz):
        at = self.at
        return (self.move(zz, at.diag, self.A, 5, self.rd.at[zz, 0], at.ny),
                self.move(zz, at.diag, self.A, 9, self.rs.at[zz, 3], at.sib),
                self.move(zz, at.diag, self.B, 7, self.rd.at[zz, 1], at.nx),
                self.move(zz, at.diag, self.B, 10, self.rs.at[zz, 4], at.sib))

    def begin(self):
        d = self.at.d

        @pl.when(self.at.has_below)
        def _():
            self.down(d, True).start()

        @pl.when(self.at.has_above)
        def _():
            self.up(d, True).start()

        for copy in self.spread(d, True):
            copy.start()

    def column(self, zz):
        d = self.at.d

        @pl.when(zz < d)
        def _():
            self.up(zz).wait_recv()

            @pl.when(self.at.has_above)
            def _():
                self.up(zz).start()

        @pl.when(zz > d)
        def _():
            self.down(zz).wait_recv()

            @pl.when(self.at.has_below)
            def _():
                self.down(zz).start()

        for copy in self.spread(zz):
            copy.start()

    def plane(self, zz):
        for arrive, turn, share in (self.from_x(zz), self.from_y(zz)):
            arrive.wait_recv()
            turn.start()
            share.start()

    def corner(self, zz):
        a, share_a, b, share_b = self.turned(zz)
        a.wait_recv()
        share_a.start()
        b.wait_recv()
        share_b.start()

    def siblings(self):
        at = self.at
        es = at.sib[1]
        exs, eys, exys = es + at.nx[1] - at.e, es + at.ny[1] - at.e, es + at.diag - at.e

        @pl.loop(0, at.n)
        def _(zz):
            for e, cols, k in ((es, self.F, 0), (exs, self.F, 1), (eys, self.F, 2), (exys, self.A, 3), (exys, self.B, 4)):
                self.move(zz, e, cols, 4, self.rs.at[zz, k], at.sib).wait_recv()

    def finish(self):
        d = self.at.d

        @pl.loop(0, self.at.n)
        def _(zz):
            for group in (self.spread(zz), self.from_x(zz)[1:], self.from_y(zz)[1:], self.turned(zz)[1::2]):
                for copy in group:
                    copy.wait_send()

            @pl.when((d > 0) & (zz >= d))
            def _():
                self.down(zz).wait_send()

            @pl.when(self.at.has_above & (zz <= d))
            def _():
                self.up(zz).wait_send()


def lane_tile(rows):
    return lax.broadcasted_iota(jnp.int32, (rows, 128), 1)


def swap_halves(tile):
    front = lax.rem(lane_tile(tile.shape[0]), HEAD) < HEAD // 2
    return jnp.where(front, pltpu.roll(tile, 128 - HEAD // 2, 1), pltpu.roll(tile, HEAD // 2, 1))


def inverse_rms(v):
    return lax.rsqrt(jnp.mean(v * v, axis=1, keepdims=True) + norm_eps)


def rope_lanes(seg_ref, freq_ref, cos_ref, sin_ref):
    f32 = jnp.float32
    packs, rows = seg_ref.shape[0], seg_ref.shape[2]
    row = jnp.concatenate([seg_ref[i].astype(f32) + float(2 * rows * i) for i in range(packs)], axis=1)
    total = packs * rows
    across = jnp.broadcast_to(row, (total, total))
    same = across == jnp.transpose(across)
    source = lax.broadcasted_iota(jnp.int32, (total, total), 1)
    target = lax.broadcasted_iota(jnp.int32, (total, total), 0)
    start = jnp.min(jnp.where(same, source.astype(f32), float(total)), axis=1, keepdims=True)
    angle = (target.astype(f32) - start) * freq_ref[...]
    cos_ref[...] = jnp.cos(angle)
    front = lax.rem(source, HEAD) < HEAD // 2
    sine = jnp.sin(angle)
    sin_ref[...] = jnp.where(front, -sine, sine)
    return (same & (source <= target)).astype(f32)


def forward_kernel(n, experts, tok_ref, cot_ref, qkv_ref, proj_ref, router_ref, gain_a_ref, gain_f_ref, ein_ref, seg_ref, route_ref, freq_ref,
                   w_all, cot_all, up_all, disp_out, mid_out, gates_out, gain_out, nf_out, q_out, k_out, v_out, p_out, mixed_out, cos_out, sin_out,
                   disp_ref, mid_ref, gates_ref, gain_ref, nf_ref, q_ref, k_ref, v_ref, p_ref, mixed_ref, cos_ref, sin_ref,
                   wv, pieces, dense_ref, small_ref, *rest):
    f32, bf16 = jnp.float32, jnp.bfloat16
    at = Place(n)
    d = at.d
    dense = GatherAll(at, dense_ref, wv, *rest[:6])
    cot = Gather(at, cot_ref, cot_all, *rest[6:11])
    load_sem, a2a_ss, a2a_sr, keep_sem = rest[11:]
    q_width, k_width = HEADS * HEAD, KV_HEADS * HEAD
    groups = HEADS // KV_HEADS
    held, share = ein_ref.shape[:2]
    f = FF // n
    qkv_width = q_width + 2 * k_width
    dense_ref[:, :qkv_width] = qkv_ref[...]
    dense_ref[:, qkv_width : qkv_width + D] = proj_ref[...]
    shard = dense_ref.shape[0]
    small_ref[...] = jnp.zeros(small_ref.shape, f32)
    small_ref[:experts, :shard] = router_ref[...].astype(f32)
    small_ref[experts : experts + 1, :shard] = gain_a_ref[...].astype(f32)
    small_ref[experts + 1 : experts + 2, :shard] = gain_f_ref[...].astype(f32)
    dense_ref[:, qkv_width + D :] = jnp.transpose(small_ref[...])[:shard].astype(bf16)
    loads = [
        pltpu.make_async_copy(dense_ref, wv.at[d * 8 + at.e], load_sem.at[0]),
        pltpu.make_async_copy(cot_ref, cot_all.at[d, 0], load_sem.at[1]),
    ]
    for load in loads:
        load.start()

    def rows_of(z):
        return up_all.at[pl.ds(pl.multiple_of(z * share, share), share), :]

    own_piece = pltpu.make_async_copy(pieces.at[d], rows_of(d), load_sem.at[2])

    parts = 3
    third = share // parts

    def third_of(z, r):
        return up_all.at[pl.ds(pl.multiple_of(z * share + r * third, third), third), :]

    def exchange(k, r):
        to = lax.rem(d + k, n)
        return send(pieces.at[to, pl.ds(r * third, third), :], third_of(d, r), a2a_ss.at[k, r], a2a_sr.at[d, r], (to, at.e))

    def exchange_part(r):
        for k in range(1, n):
            exchange(k, r).start()

    at.meet(True)
    dense.begin()
    for q in range(n):
        for j in range(2 * held):
            lo = (j % 2) * FF + q * f
            pieces[q, :, j * f : (j + 1) * f] = ein_ref[j // 2, :, lo : lo + f]
    own_piece.start()
    allowed = rope_lanes(seg_ref, freq_ref, cos_ref, sin_ref)
    for i in range(1, n):
        dense.column(at.near(i))
        if i == n - 1:
            cot.begin_z()
            exchange_part(0)
        dense.plane(at.near(i - 1))
        if i >= 2:
            dense.corner(at.near(i - 2))
    cot.begin_xy()
    dense.plane(at.near(n - 1))
    dense.corner(at.near(n - 2))
    cot.column(at.near(1))
    cot.column(at.near(2))
    exchange_part(1)
    exchange_part(2)
    dense.corner(at.near(n - 1))
    for load in loads:
        load.wait()
    dense.siblings()
    keep = pltpu.make_async_copy(wv, w_all, load_sem.at[0])
    keep.start()

    def weight(lo, width):
        return wv[:, :, lo : lo + width].reshape(D, width)

    tail_at = q_width + 2 * k_width + D
    turned = jnp.transpose(weight(tail_at, 128).astype(f32))
    gain_ref[0:1, :] = turned[experts : experts + 1, :]
    gain_ref[1:2, :] = turned[experts + 1 : experts + 2, :]
    x = tok_ref[...].astype(f32)
    nf_ref[...] = (x * inverse_rms(x) * gain_ref[0:1, :]).astype(bf16)
    cos, sin = cos_ref[...], sin_ref[...]
    for q in range((q_width + 2 * k_width) // 512):
        lo = q * 512
        part = mm(nf_ref[...], weight(lo, 512))
        for t in range(4):
            tile = part[:, t * 128 : (t + 1) * 128]
            col = lo + t * 128
            if col < q_width + k_width:
                tile = tile * cos + swap_halves(tile) * sin
            ref, base = (q_ref, 0) if col < q_width else (k_ref, q_width) if col < q_width + k_width else (v_ref, q_width + k_width)
            ref[:, col - base : col - base + 128] = tile.astype(bf16)
    cot.plane(at.near(0))
    allowed = jnp.concatenate([allowed] * groups, axis=0) > 0
    for g in range(KV_HEADS):
        qs = jnp.concatenate([q_ref[:, (g * groups + j) * HEAD : (g * groups + j + 1) * HEAD] for j in range(groups)], axis=0)
        ks, vs = k_ref[:, g * HEAD : (g + 1) * HEAD], v_ref[:, g * HEAD : (g + 1) * HEAD]
        scores = jnp.where(allowed, mm(qs, ks, NT) * HEAD ** (-0.5), neg_large)
        raised = jnp.exp(scores - jnp.max(scores, axis=1, keepdims=True))
        probs = raised / jnp.sum(raised, axis=1, keepdims=True)
        p_ref[g] = probs
        out = mm(probs.astype(bf16), vs).astype(bf16)
        rows = out.shape[0] // groups
        for j in range(groups):
            mixed_ref[:, (g * groups + j) * HEAD : (g * groups + j + 1) * HEAD] = out[j * rows : (j + 1) * rows]
    for q in range(D // 512):
        lo = q * 512
        mid_ref[:, lo : lo + 512] = tok_ref[:, lo : lo + 512].astype(f32) + mm(mixed_ref[...], weight(q_width + 2 * k_width + lo, 512))
    mid = mid_ref[...]
    disp_ref[:, :D] = (mid * inverse_rms(mid) * gain_ref[1:2, :]).astype(bf16)
    logits = mm(disp_ref[:, :D], weight(tail_at, 128))
    hits = []
    for i in range(route_ref.shape[0]):
        expert = lax.broadcasted_iota(jnp.int32, (128, route_ref.shape[2]), 0)
        hits.append(sum((route_ref[i, k : k + 1, :] == expert).astype(f32) for k in range(TOP_K)))
    chosen = jnp.transpose(jnp.concatenate(hits, axis=1))
    masked = jnp.where(chosen > 0, logits, neg_large)
    raised = jnp.where(chosen > 0, jnp.exp(masked - jnp.max(masked, axis=1, keepdims=True)), 0.0)
    gates = raised / jnp.sum(raised, axis=1, keepdims=True)
    gates_ref[...] = gates
    high = gates.astype(bf16).astype(f32)
    low = (gates - high).astype(bf16).astype(f32)
    disp_ref[:, D:] = (high + pltpu.roll(low, experts, 1)).astype(bf16)

    keeps = [pltpu.make_async_copy(src, dst, keep_sem.at[i]) for i, (src, dst) in enumerate((
        (disp_ref, disp_out), (mid_ref, mid_out), (gates_ref, gates_out), (gain_ref, gain_out), (nf_ref, nf_out), (q_ref, q_out),
        (k_ref, k_out), (v_ref, v_out), (p_ref, p_out), (mixed_ref, mixed_out), (cos_ref, cos_out), (sin_ref, sin_out)))]
    for copy in keeps:
        copy.start()
    for i in range(1, n):
        cot.plane(at.near(i))
        cot.corner(at.near(i - 1))
        if i + 2 < n:
            cot.column(at.near(i + 2))
    cot.corner(at.near(n - 1))
    own_piece.wait()
    for k in range(1, n):
        source = lax.rem(d + k, n)
        for r in range(parts):
            exchange(k, r).wait_send()
            send(pieces.at[0, pl.ds(r * third, third), :], third_of(source, r), a2a_ss.at[k, r], a2a_sr.at[source, r], (source, at.e)).wait_recv()
    keep.wait()
    dense.finish()
    cot.finish()
    for copy in keeps:
        copy.wait()


def forward_layer(tok, cot, attn_in, attn_out, router, gain_attn, gain_ffn, ein, segments, routes, n, experts, cid):
    f32, bf16 = jnp.float32, jnp.bfloat16
    rows = tok.shape[0]
    shard = attn_in.shape[0]
    held, share = ein.shape[:2]
    q_width, k_width = HEADS * HEAD, KV_HEADS * HEAD
    wide = q_width + 2 * k_width + D + 128
    groups = HEADS // KV_HEADS
    half = HEAD // 2
    freq = np.tile(np.float32(rope_base) ** (-np.arange(half, dtype=np.float32) / np.float32(half)), 128 // half)[None, :]
    D_ = pltpu.SemaphoreType.DMA
    V = lambda *s: pltpu.VMEM(s, bf16)
    any_, vm = pl.BlockSpec(memory_space=pl.ANY), pl.BlockSpec(memory_space=pltpu.VMEM)
    S = jax.ShapeDtypeStruct
    saved = (
        S((rows, D + 128), bf16), S((rows, D), f32), S((rows, 128), f32), S((8, D), f32), S((rows, D), bf16),
        S((rows, q_width), bf16), S((rows, k_width), bf16), S((rows, k_width), bf16),
        S((KV_HEADS, groups * rows, rows), f32), S((rows, q_width), bf16), S((rows, 128), f32), S((rows, 128), f32),
    )
    return pl.pallas_call(
        functools.partial(forward_kernel, n, experts),
        out_shape=(S((n * 8, shard, wide), bf16), S((n, 4, rows, D), bf16), S((D, 2 * held * (FF // n)), bf16)) + saved,
        in_specs=[vm, any_] + [vm] * 9,
        out_specs=[any_] * 15,
        scratch_shapes=[pltpu.VMEM(a.shape, a.dtype) for a in saved]
        + [V(n * 8, shard, wide), V(n, share, 2 * held * (FF // n)), V(shard, wide), pltpu.VMEM((128, 128), f32)]
        + [D_((n, 11)), D_((n,)), D_((n,)), D_((n,)), D_((n, 2)), D_((n, 5))] + gather_sems(n)
        + [D_((3,)), D_((n, 3)), D_((n, 3)), D_((len(saved),))],
        compiler_params=pltpu.CompilerParams(collective_id=cid, has_side_effects=True, vmem_limit_bytes=60 << 20),
        name="forward_layer",
    )(tok, cot, attn_in, attn_out, router.T, gain_attn[None, :], gain_ffn[None, :], ein, segments, routes.transpose(0, 2, 1), freq)


def backward_kernel(n, experts, gs_in, tok_in, cot_in, mid_in, gates_in, gain_in, nf_in, disp_in, q_in, k_in, v_in, p_in, mixed_in, cos_in, sin_in, w_ref, gup_ref,
                    gtok_ref, gout_ref, gin_ref, gtail_ref, arrived,
                    gs_ref, tok_ref, cot_ref, mid_ref, gates_ref, gain_ref, nf_ref, disp_ref, q_ref, k_ref, v_ref, p_ref, mixed_ref, cos_ref, sin_ref,
                    wv, pout, pin, tot_out, tot_in, pair, gq, gl, sums, gb, gm, flat, *rest):
    f32, bf16 = jnp.float32, jnp.bfloat16
    at = Place(n)
    d, c = at.d, at.c
    outs = Reduce(at, pout, tot_out, *rest[:9])
    ins = Reduce(at, pin, tot_in, *rest[9:18])
    load_sem, pair_ss, pair_sr, a2a_ss, a2a_sr, end_ss, end_sr, in_sem = rest[18:]
    q_width, k_width = HEADS * HEAD, KV_HEADS * HEAD
    groups = HEADS // KV_HEADS
    qkv_width = q_width + 2 * k_width
    tail_at = qkv_width + D
    rows = tok_ref.shape[0]
    shard = w_ref.shape[1]
    share = D // n
    f = FF // n
    fetched = [pltpu.make_async_copy(src, dst, in_sem.at[i]) for i, (src, dst) in enumerate((
        (mid_in, mid_ref), (gates_in, gates_ref), (gs_in, gs_ref), (gain_in, gain_ref), (cot_in, cot_ref), (mixed_in, mixed_ref), (nf_in, nf_ref), (disp_in, disp_ref), (q_in, q_ref), (k_in, k_ref), (v_in, v_ref), (p_in, p_ref), (tok_in, tok_ref), (cos_in, cos_ref), (sin_in, sin_ref)))]
    for copy in fetched[:8]:
        copy.start()
    loads = []
    for i, (lo, width) in enumerate(((tail_at, 128), (qkv_width, D), (0, qkv_width))):
        loads.append(pltpu.make_async_copy(w_ref.at[:, :, pl.ds(lo, width)], wv.at[:, :, pl.ds(lo, width)], load_sem.at[i]))
    for load in loads:
        load.start()
    for copy in fetched[8:]:
        copy.start()
    own_share = pltpu.make_async_copy(gup_ref.at[pl.ds(pl.multiple_of(d * share, share), share), :], arrived.at[d], load_sem.at[3])
    own_share.start()

    def exchange(k):
        to = lax.rem(d + k, n)
        return send(gup_ref.at[pl.ds(pl.multiple_of(to * share, share), share), :], arrived.at[d], a2a_ss.at[k], a2a_sr.at[d], (to, at.e))

    swaps = [send(src, pair.at[i], pair_ss.at[i], pair_sr.at[i], at.sib)
             for i, src in enumerate((mixed_ref, nf_ref, disp_ref.at[:, pl.ds(0, D)], gb))]
    swap_q = send(gq.at[0], gq.at[1], pair_ss.at[4], pair_sr.at[4], at.sib)
    swap_l = send(gl.at[0], gl.at[1], pair_ss.at[5], pair_sr.at[5], at.sib)
    swap_s = send(sums.at[0], sums.at[1], pair_ss.at[6], pair_sr.at[6], at.sib)
    at.meet(True)
    for k in range(1, n):
        exchange(k).start()
    for copy in fetched[:8]:
        copy.wait()
    for i in range(3):
        swaps[i].start()

    def weight(lo, width):
        return wv[:, :, lo : lo + width].reshape(D, width)

    loads[0].wait()
    mid = mid_ref[...]
    inv_second = inverse_rms(mid)
    unit = mid * inv_second
    gates, gg = gates_ref[...], gs_ref[:, D:]
    gl[0] = (gates * (gg - jnp.sum(gates * gg, axis=1, keepdims=True))).astype(bf16)
    swap_l.start()
    grad_second = mm(gl[0], weight(tail_at, 128), NT) + gs_ref[:, :D]
    pull = grad_second * gain_ref[1:2, :]
    sums[0, 1:2, :] = jnp.sum(grad_second * unit, axis=0, keepdims=True)
    grad_middle = cot_ref[...].astype(f32) + inv_second * (pull - unit * jnp.mean(pull * unit, axis=1, keepdims=True))
    gtok_ref[...] = grad_middle
    gb[...] = grad_middle.astype(bf16)
    swaps[3].start()
    loads[1].wait()
    for q in range(q_width // 512):
        gm[:, q * 512 : (q + 1) * 512] = mm(gb[...], wv[:, :, qkv_width : qkv_width + D].reshape(D, D)[q * 512 : (q + 1) * 512], NT).astype(bf16)

    def both(own, other, cols):
        return jnp.concatenate([own[:, cols], other[:, cols]], axis=0)

    def store(buf, zz, lo, value):
        blocks = value.astype(bf16).reshape(4, 2 * shard, value.shape[1])
        for a in range(4):
            slot = 2 * lax.rem(a // 2 + at.y, 2) + lax.rem(a % 2 + at.x, 2)
            buf[zz, slot, :, lo : lo + value.shape[1]] = blocks[a]

    def row_cols(zz):
        return pl.ds(pl.multiple_of(zz * share, 128), share)

    half_out, half_in = D // 2, qkv_width // 2
    swaps[0].wait_recv()
    swaps[3].wait_recv()

    @pl.loop(0, n)
    def _(j):
        zz = at.far(j)
        branch = both(gb, pair.at[3], pl.ds(pl.multiple_of(c * half_out, 128), half_out))
        store(pout, zz, 0, mm(both(mixed_ref, pair.at[0], row_cols(zz)), branch, TN))
        outs.s1(zz)

    for copy in fetched[8:]:
        copy.wait()
    scale = HEAD ** (-0.5)
    for g in range(KV_HEADS):
        heads = [slice((g * groups + j) * HEAD, (g * groups + j + 1) * HEAD) for j in range(groups)]
        kv = slice(g * HEAD, (g + 1) * HEAD)
        qs = jnp.concatenate([q_ref[:, h] for h in heads], axis=0)
        ms = jnp.concatenate([gm[:, h] for h in heads], axis=0)
        ks, vs = k_ref[:, kv], v_ref[:, kv]
        probs = p_ref[g]
        grad_values = mm(probs.astype(bf16), ms, TN)
        grad_probs = mm(ms, vs, NT)
        grad_scores = (probs * (grad_probs - jnp.sum(probs * grad_probs, axis=1, keepdims=True))).astype(bf16)
        grad_query = mm(grad_scores, ks) * scale
        for j, h in enumerate(heads):
            flat[:, h] = grad_query[j * rows : (j + 1) * rows]
        flat[:, q_width + kv.start : q_width + kv.stop] = mm(grad_scores, qs, TN) * scale
        flat[:, q_width + k_width + kv.start : q_width + k_width + kv.stop] = grad_values
    for j in range(n):
        outs.s2(at.far(j))
    cos, sin = cos_ref[...], sin_ref[...]
    for t in range(qkv_width // 128):
        tile = flat[:, t * 128 : (t + 1) * 128]
        if t * 128 < q_width + k_width:
            tile = tile * cos - swap_halves(tile) * sin
        gq[0, :, t * 128 : (t + 1) * 128] = tile.astype(bf16)
    swap_q.start()
    loads[2].wait()
    x = tok_ref[...].astype(f32)
    inv_first = inverse_rms(x)
    unit = x * inv_first
    grad_first = jnp.concatenate(
        [mm(gq[0], wv[8 * i : 8 * (i + 1), :, :qkv_width].reshape(8 * shard, qkv_width), NT) for i in range(n)], axis=1)
    pull = grad_first * gain_ref[0:1, :]
    sums[0, 0:1, :] = jnp.sum(grad_first * unit, axis=0, keepdims=True)
    sums[0, 2:, :] = jnp.zeros((6, D), f32)
    swap_s.start()
    gtok_ref[...] += inv_first * (pull - unit * jnp.mean(pull * unit, axis=1, keepdims=True))
    for i in (1, 2):
        swaps[i].wait_recv()
    swap_l.wait_recv()
    swap_q.wait_recv()
    swap_s.wait_recv()
    gains = sums[0] + sums[1]
    high = gains.astype(bf16)
    low = (gains - high.astype(f32)).astype(bf16)
    swap_s.wait_send()
    sums[0] = high.astype(f32)
    sums[1] = low.astype(f32)
    line = lax.rem(lax.broadcasted_iota(jnp.int32, (16, 128), 0), 8)
    where = (((line == 0) & (lane_tile(16) == experts)) | ((line == 1) & (lane_tile(16) == experts + 1))).astype(bf16)

    @pl.loop(0, n)
    def _(j):
        zz = at.far(j)
        cols = row_cols(zz)
        normed = both(nf_ref, pair.at[1], cols)
        for q in range(2):
            part = pl.ds(pl.multiple_of(c * half_in + q * (half_in // 2), 128), half_in // 2)
            grad = jnp.concatenate([gq[0, :, part], gq[1, :, part]], axis=0)
            store(pin, zz, q * (half_in // 2), mm(normed, grad, TN))
        tail = mm(both(disp_ref, pair.at[2], cols), jnp.concatenate([gl[0], gl[1]], axis=0), TN)
        rows_now = jnp.concatenate([sums[0, :, cols], sums[1, :, cols]], axis=0).astype(bf16)
        store(pin, zz, half_in, tail + mm(rows_now, where, TN))

        @pl.when(j < 2)
        def _():
            ins.corners(zz)

    for j in range(n + 1):
        ins.step(j)
        if j < n:
            outs.s3(at.far(j))
            outs.lines(j)
    outs.last()
    mine, theirs = pl.ds(pl.multiple_of(c * shard, 8), shard), pl.ds(pl.multiple_of((1 - c) * shard, 8), shard)
    cols_out, cols_in = pl.ds(pl.multiple_of(c * half_out, 128), half_out), pl.ds(pl.multiple_of(c * half_in, 128), half_in)
    end_out = send(tot_out.at[theirs, :], gout_ref.at[:, cols_out], end_ss.at[0], end_sr.at[0], at.sib)
    end_out.start()
    gout_ref[:, cols_out] = tot_out[mine, :]
    ins.last()
    end_in = send(tot_in.at[theirs, pl.ds(0, half_in)], gin_ref.at[:, cols_in], end_ss.at[1], end_sr.at[1], at.sib)
    end_in.start()
    gin_ref[:, cols_in] = tot_in[mine, :half_in]
    gtail_ref[...] = tot_in[mine, half_in:]
    own_share.wait()
    for k in range(1, n):
        exchange(k).wait_send()
        source = lax.rem(d + k, n)
        send(gup_ref.at[pl.ds(0, share), :], arrived.at[source], a2a_ss.at[k], a2a_sr.at[source], (source, at.e)).wait_recv()

    end_out.wait()
    end_in.wait()
    for swap in swaps + [swap_q, swap_l]:
        swap.wait_send()
    outs.finish()
    ins.finish()


def backward_layer(gs, tok, cot, mid, gates, gain, nf, disp, q, k, v, p, mixed, cos, sin, w_all, gup, n, experts, cid):
    f32, bf16 = jnp.float32, jnp.bfloat16
    rows = tok.shape[0]
    shard, wide = w_all.shape[1:]
    qkv_width = (HEADS + 2 * KV_HEADS) * HEAD
    share = D // n
    D_ = pltpu.SemaphoreType.DMA
    V = lambda *s: pltpu.VMEM(s, bf16)
    W = lambda *s: pltpu.VMEM(s, f32)
    any_, vm = pl.BlockSpec(memory_space=pl.ANY), pl.BlockSpec(memory_space=pltpu.VMEM)
    S = jax.ShapeDtypeStruct
    width_out, width_in = D // 2, qkv_width // 2 + 128
    return pl.pallas_call(
        functools.partial(backward_kernel, n, experts),
        out_shape=(S((rows, D), f32), S((shard, D), f32), S((shard, qkv_width), f32), S((shard, 128), f32), S((n, share, gup.shape[1]), bf16)),
        in_specs=[any_] * 17,
        out_specs=[vm] * 4 + [any_],
        scratch_shapes=[pltpu.VMEM(a.shape, a.dtype) for a in (gs, tok, cot, mid, gates, gain, nf, disp, q, k, v, p, mixed, cos, sin)]
        + [V(n * 8, shard, wide), V(n, 4, 2 * shard, width_out), V(n, 4, 2 * shard, width_in),
                        W(2 * shard, width_out), W(2 * shard, width_in),
                        V(4, rows, D), V(2, rows, qkv_width), V(2, rows, 128), W(2, 8, D), V(rows, D), V(rows, D), W(rows, qkv_width)]
        + reduce_scratch(n, 2 * shard, width_out) + reduce_scratch(n, 2 * shard, width_in)
        + [D_((4,)), D_((7,)), D_((7,)), D_((n,)), D_((n,)), D_((2,)), D_((2,)), D_((15,))],
        compiler_params=pltpu.CompilerParams(collective_id=cid, has_side_effects=True, vmem_limit_bytes=62 << 20),
        name="backward_layer",
    )(gs, tok, cot, mid, gates, gain, nf, disp, q, k, v, p, mixed, cos, sin, w_all, gup)


def results_kernel(experts, arrived, tok_in, down_in, out_in, qkv_in, tail_in,
                   up_ref, tok_ref, down_ref, proj_ref, qkv_ref, router_ref, gains_ref):
    n, width = arrived.shape[0], arrived.shape[2]
    f = FF // n
    for q in range(n):
        for j in range(width // f):
            lo = (j % 2) * FF + q * f
            up_ref[j // 2, :, lo : lo + f] = arrived[q, :, j * f : (j + 1) * f].astype(jnp.float32)

    tok_ref[...] = tok_in[...]
    down_ref[...] = down_in[...]

    @pl.when(pl.program_id(0) == 0)
    def _():
        proj_ref[...] = out_in[...]
        qkv_ref[...] = qkv_in[...]
        turned = jnp.transpose(jnp.concatenate([tail_in[...], jnp.zeros((128 - tail_in.shape[0], 128), jnp.float32)], axis=0))
        router_ref[...] = turned[:experts, : tail_in.shape[0]]
        gains_ref[...] = turned[experts : experts + 8, : tail_in.shape[0]]


def results(arrived, tok, down, proj, qkv, tail, held, experts):
    n, share, width = arrived.shape
    f32 = jnp.float32
    steps = 4
    rows = share // steps
    whole = lambda a: pl.BlockSpec(a.shape, lambda i: (0,) * len(a.shape))
    part = lambda a: pl.BlockSpec((a.shape[0] // steps, a.shape[1]), lambda i: (i, 0))
    shapes = [jax.ShapeDtypeStruct(a.shape, f32) for a in (tok, down, proj, qkv)]
    shapes += [jax.ShapeDtypeStruct((experts, tail.shape[0]), f32), jax.ShapeDtypeStruct((8, tail.shape[0]), f32)]
    return pl.pallas_call(
        functools.partial(results_kernel, experts),
        grid=(steps,),
        out_shape=[jax.ShapeDtypeStruct((held, share, 2 * FF), f32)] + shapes,
        in_specs=[pl.BlockSpec((n, rows, width), lambda i: (0, i, 0))] + [part(a) for a in (tok, down)] + [whole(a) for a in (proj, qkv, tail)],
        out_specs=[pl.BlockSpec((held, rows, 2 * FF), lambda i: (0, i, 0))] + [part(a) for a in (tok, down)] + [whole(a) for a in shapes[2:]],
        compiler_params=pltpu.CompilerParams(vmem_limit_bytes=62 << 20),
        name="results",
    )(arrived, tok, down, proj, qkv, tail)


def per_device_fast(n, tokens, segments, routes, cotangent, gain_attn, attn_in, attn_out, gain_ffn, router, expert_in, expert_out):
    f32, bf16 = jnp.float32, jnp.bfloat16
    micro, rows = tokens.shape[:2]
    total = micro * rows
    held = expert_in.shape[0]
    experts = held * 8
    f = FF // n
    x = tokens.reshape(total, D)
    cot = cotangent.reshape(total, D)
    w_all, cot_all, up, disp, middle, gates, gain, nf, q, k, v, p, mixed, cos, sin = forward_layer(
        x, cot, attn_in, attn_out, router, gain_attn, gain_ffn, expert_in, segments, routes, n, experts, 0)
    out, grad_sum, grad_up, grad_down = expert_layer(disp, cot_all, up, expert_out.reshape(held * f, D), middle, n, experts, 1)
    grad_tokens, grad_out, grad_in, grad_tail, grad_up = backward_layer(
        grad_sum, x, cot, middle, gates, gain, nf, disp, q, k, v, p, mixed, cos, sin, w_all, grad_up, n, experts, 2)
    grad_up, grad_tokens, grad_down, grad_out, grad_in, grad_router, grad_gains = results(
        grad_up, grad_tokens, grad_down, grad_out, grad_in, grad_tail, held, experts)
    return (
        out.astype(bf16).reshape(micro, rows, D),
        grad_tokens.reshape(micro, rows, D),
        grad_gains[0],
        grad_in,
        grad_out,
        grad_gains[1],
        grad_router.T,
        grad_up,
        grad_down.reshape(held, f, D),
    )


def solution(mesh):
    placed = (
        P(None, ("dp", "expert"), None),
        P(None, ("dp", "expert"), None),
        P(None, ("dp", "expert"), None),
        P(None, ("dp", "expert"), None),
        P(("dp", "expert")),
        P(("dp", "expert"), None),
        P(("dp", "expert"), None),
        P(("dp", "expert")),
        P(("dp", "expert"), None),
        P("expert", "dp", None),
        P("expert", "dp", None),
    )
    fast = mesh.shape["expert"] == 8 and FF // mesh.shape["dp"] == 128
    body = functools.partial(per_device_fast, mesh.shape["dp"]) if fast else per_device
    return jax.shard_map(
        body,
        mesh=mesh,
        in_specs=placed,
        out_specs=(
            P(None, ("dp", "expert"), None),
            P(None, ("dp", "expert"), None),
            P(("dp", "expert")),
            P(("dp", "expert"), None),
            P(("dp", "expert"), None),
            P(("dp", "expert")),
            P(("dp", "expert"), None),
            P("expert", "dp", None),
            P("expert", "dp", None),
        ),
        check_vma=False,
    )
```

```python
import functools

import jax
import jax.numpy as jnp
import numpy as np
from jax import lax
from jax.experimental import pallas as pl
from jax.experimental.pallas import tpu as pltpu
from jax.sharding import PartitionSpec as P

MESH = pl.DeviceIdType.MESH

D = 1536
HEADS = 24
KV_HEADS = 8
HEAD = 64
FF = 512
TOP_K = 8


norm_eps = 1e-06
rope_base = 10000.0
neg_large = -1e30
highest = lax.Precision.HIGHEST


def rope_tables(segment, half_width):
    row_count = segment.shape[0]
    places = jnp.arange(row_count, dtype=jnp.int32)
    same_seq = segment[:, None] == segment[None, :]
    seq_start = jnp.min(jnp.where(same_seq, places[None, :], row_count), axis=1)
    offset = (places - seq_start).astype(jnp.float32)
    frequencies = rope_base ** (-jnp.arange(half_width, dtype=jnp.float32) / half_width)
    angles = offset[:, None] * frequencies[None, :]
    causal = same_seq & (places[None, :] <= places[:, None])
    return (jnp.cos(angles), jnp.sin(angles), causal)


def rotate(operand, cosine, sine_table):
    half_width = operand.shape[-1] // 2
    front_part = operand[..., :half_width]
    back_part = operand[..., half_width:]
    return jnp.concatenate(
        [
            front_part * cosine - back_part * sine_table,
            back_part * cosine + front_part * sine_table,
        ],
        axis=-1,
    )


def unrotate(gradient, cosine, sine_table):
    half_width = gradient.shape[-1] // 2
    front_part = gradient[..., :half_width]
    back_part = gradient[..., half_width:]
    return jnp.concatenate(
        [
            front_part * cosine + back_part * sine_table,
            back_part * cosine - front_part * sine_table,
        ],
        axis=-1,
    )


def slot_targets(route_now, expert_count, capacity):
    flat_ids = route_now.reshape(-1)
    onehot = (flat_ids[:, None] == jnp.arange(expert_count, dtype=jnp.int32)[None, :]).astype(
        jnp.int32
    )
    earlier = jnp.cumsum(onehot, axis=0) - onehot
    slot_index = jnp.sum(earlier * onehot, axis=1)
    return flat_ids * capacity + slot_index


def dense_fetch(gain_attn, attn_in, attn_out, gain_ffn, router):
    return (
        lax.all_gather(gain_attn, ("dp", "expert"), axis=0, tiled=True),
        lax.all_gather(attn_in, ("dp", "expert"), axis=0, tiled=True),
        lax.all_gather(attn_out, ("dp", "expert"), axis=0, tiled=True),
        lax.all_gather(gain_ffn, ("dp", "expert"), axis=0, tiled=True),
        lax.all_gather(router, ("dp", "expert"), axis=0, tiled=True),
    )


def expert_fetch(expert_in, expert_out):
    return (
        lax.all_gather(expert_in, "dp", axis=1, tiled=True),
        lax.all_gather(expert_out, "dp", axis=1, tiled=True),
    )


def dense_reduce(grad_set):
    return (
        lax.psum_scatter(grad_set[0], ("dp", "expert"), scatter_dimension=0, tiled=True),
        lax.psum_scatter(grad_set[1], ("dp", "expert"), scatter_dimension=0, tiled=True),
        lax.psum_scatter(grad_set[2], ("dp", "expert"), scatter_dimension=0, tiled=True),
        lax.psum_scatter(grad_set[3], ("dp", "expert"), scatter_dimension=0, tiled=True),
        lax.psum_scatter(grad_set[4], ("dp", "expert"), scatter_dimension=0, tiled=True),
    )


def expert_reduce(grad_set):
    return (
        lax.psum_scatter(grad_set[0], "dp", scatter_dimension=1, tiled=True),
        lax.psum_scatter(grad_set[1], "dp", scatter_dimension=1, tiled=True),
    )


def attention_scores(queries, key_rot, causal):
    score_scale = HEAD ** (-0.5)
    scores = (
        jnp.einsum("tkgh,skh->kgts", queries, key_rot, preferred_element_type=jnp.float32)
        * score_scale
    )
    return jnp.where(causal[None, None], scores, neg_large)


def forward_micro(tokens_now, segment, route_now, dense_set, expert_set, shapes):
    expert_count, capacity, group_count, local_experts = shapes
    gain_attn, qkv_weight, out_weight, gain_ffn, router_weight = dense_set
    expert_up, expert_down = expert_set
    row_count = tokens_now.shape[0]
    groups = HEADS // KV_HEADS
    q_width = HEADS * HEAD
    k_width = KV_HEADS * HEAD
    inputs = tokens_now.astype(jnp.float32)
    inv_first = lax.rsqrt(jnp.mean(inputs * inputs, axis=1, keepdims=True) + norm_eps)
    normed_first = (inputs * inv_first * gain_attn.astype(jnp.float32)).astype(jnp.bfloat16)
    qkv_full = jnp.dot(normed_first, qkv_weight, preferred_element_type=jnp.float32)
    cosine, sine_table, causal = rope_tables(segment, HEAD // 2)
    queries = rotate(
        qkv_full[:, :q_width].reshape(row_count, KV_HEADS, groups, HEAD),
        cosine[:, None, None, :],
        sine_table[:, None, None, :],
    ).astype(jnp.bfloat16)
    key_rot = rotate(
        qkv_full[:, q_width : q_width + k_width].reshape(row_count, KV_HEADS, HEAD),
        cosine[:, None, :],
        sine_table[:, None, :],
    ).astype(jnp.bfloat16)
    values = (
        qkv_full[:, q_width + k_width :].reshape(row_count, KV_HEADS, HEAD).astype(jnp.bfloat16)
    )
    scores = attention_scores(queries, key_rot, causal)
    score_peak = jnp.max(scores, axis=-1, keepdims=True)
    exp_scores = jnp.exp(scores - score_peak)
    exp_total = jnp.sum(exp_scores, axis=-1, keepdims=True)
    log_total = score_peak + jnp.log(exp_total)
    soft_probs = (exp_scores / exp_total).astype(jnp.bfloat16)
    attn_mixed = jnp.einsum(
        "kgts,skh->tkgh", soft_probs, values, preferred_element_type=jnp.float32
    )
    attn_mixed = attn_mixed.reshape(row_count, q_width).astype(jnp.bfloat16)
    middle = inputs + jnp.dot(attn_mixed, out_weight, preferred_element_type=jnp.float32)
    inv_second = lax.rsqrt(jnp.mean(middle * middle, axis=1, keepdims=True) + norm_eps)
    normed_second = (middle * inv_second * gain_ffn.astype(jnp.float32)).astype(jnp.bfloat16)
    logits = jnp.dot(normed_second, router_weight, preferred_element_type=jnp.float32)
    chosen = (
        route_now[:, :, None] == jnp.arange(expert_count, dtype=jnp.int32)[None, None, :]
    ).astype(jnp.float32)
    picked_logits = jnp.sum(chosen * logits[:, None, :], axis=-1)
    gate_values = jax.nn.softmax(picked_logits, axis=-1)
    targets = slot_targets(route_now, expert_count, capacity)
    source_rows = jnp.repeat(normed_second, TOP_K, axis=0)
    buffer = jnp.zeros((expert_count * capacity, D), jnp.bfloat16).at[targets].set(source_rows)
    send_rows = buffer.reshape(group_count, local_experts, capacity, D)
    received = lax.all_to_all(send_rows, "expert", split_axis=0, concat_axis=0, tiled=True)
    gate_up = jnp.einsum("secd,edf->secf", received, expert_up, preferred_element_type=jnp.float32)
    hidden = (jax.nn.silu(gate_up[..., :FF]) * gate_up[..., FF:]).astype(jnp.bfloat16)
    expert_result = jnp.einsum(
        "secf,efd->secd", hidden, expert_down, preferred_element_type=jnp.float32
    ).astype(jnp.bfloat16)
    returned = lax.all_to_all(expert_result, "expert", split_axis=0, concat_axis=0, tiled=True)
    picked = returned.reshape(expert_count * capacity, D)[targets].reshape(row_count, TOP_K, D)
    moe_sum = jnp.einsum(
        "tk,tkd->td", gate_values, picked, precision=highest, preferred_element_type=jnp.float32
    )
    result = (middle + moe_sum).astype(jnp.bfloat16)
    saved_state = (
        inputs,
        inv_first,
        normed_first,
        queries,
        key_rot,
        values,
        log_total,
        causal,
        cosine,
        sine_table,
        attn_mixed,
        middle,
        inv_second,
        normed_second,
        chosen,
        gate_values,
        targets,
        received,
        gate_up,
        hidden,
        picked,
    )
    return (result, saved_state)


def backward_micro(saved_state, cotan_now, dense_set, expert_set, shapes):
    expert_count, capacity, group_count, local_experts = shapes
    (
        inputs,
        inv_first,
        normed_first,
        queries,
        key_rot,
        values,
        log_total,
        causal,
        cosine,
        sine_table,
        attn_mixed,
        middle,
        inv_second,
        normed_second,
        chosen,
        gate_values,
        targets,
        received,
        gate_up,
        hidden,
        picked,
    ) = saved_state
    gain_attn, qkv_weight, out_weight, gain_ffn, router_weight = dense_set
    expert_up, expert_down = expert_set
    row_count = inputs.shape[0]
    groups = HEADS // KV_HEADS
    q_width = HEADS * HEAD
    k_width = KV_HEADS * HEAD
    score_scale = HEAD ** (-0.5)
    upstream = cotan_now.astype(jnp.float32)
    grad_gates = jnp.einsum(
        "td,tkd->tk", upstream, picked, precision=highest, preferred_element_type=jnp.float32
    )
    grad_picked = gate_values * (
        grad_gates - jnp.sum(gate_values * grad_gates, axis=-1, keepdims=True)
    )
    grad_logits = jnp.sum(chosen * grad_picked[:, :, None], axis=1).astype(jnp.bfloat16)
    grad_router = jnp.einsum(
        "td,te->de", normed_second, grad_logits, preferred_element_type=jnp.float32
    )
    grad_second = jnp.einsum(
        "te,de->td", grad_logits, router_weight, preferred_element_type=jnp.float32
    )
    grad_slots = (
        (gate_values[:, :, None] * upstream[:, None, :])
        .astype(jnp.bfloat16)
        .reshape(row_count * TOP_K, D)
    )
    grad_buffer = jnp.zeros((expert_count * capacity, D), jnp.bfloat16).at[targets].set(grad_slots)
    grad_buffer = grad_buffer.reshape(group_count, local_experts, capacity, D)
    grad_result = lax.all_to_all(grad_buffer, "expert", split_axis=0, concat_axis=0, tiled=True)
    grad_hidden = jnp.einsum(
        "secd,efd->secf", grad_result, expert_down, preferred_element_type=jnp.float32
    )
    grad_down = jnp.einsum(
        "secf,secd->efd", hidden, grad_result, preferred_element_type=jnp.float32
    )
    gate_part = gate_up[..., :FF]
    up_part = gate_up[..., FF:]
    gate_sigmoid = jax.nn.sigmoid(gate_part)
    grad_gate = grad_hidden * up_part * gate_sigmoid * (1.0 + gate_part * (1.0 - gate_sigmoid))
    grad_up_part = grad_hidden * (gate_part * gate_sigmoid)
    grad_gate_up = jnp.concatenate([grad_gate, grad_up_part], axis=-1).astype(jnp.bfloat16)
    grad_up = jnp.einsum(
        "secd,secf->edf", received, grad_gate_up, preferred_element_type=jnp.float32
    )
    grad_rows = jnp.einsum(
        "secf,edf->secd", grad_gate_up, expert_up, preferred_element_type=jnp.float32
    ).astype(jnp.bfloat16)
    grad_back = lax.all_to_all(grad_rows, "expert", split_axis=0, concat_axis=0, tiled=True)
    grad_choice = grad_back.reshape(expert_count * capacity, D)[targets].reshape(
        row_count, TOP_K, D
    )
    grad_second = grad_second + jnp.sum(grad_choice, axis=1, dtype=jnp.float32)
    unit_second = middle * inv_second
    pull_second = grad_second * gain_ffn.astype(jnp.float32)
    grad_gain_ffn = jnp.sum(grad_second * unit_second, axis=0)
    grad_middle = upstream + inv_second * (
        pull_second - unit_second * jnp.mean(pull_second * unit_second, axis=1, keepdims=True)
    )
    grad_branch = grad_middle.astype(jnp.bfloat16)
    grad_out_weight = jnp.einsum(
        "tc,td->cd", attn_mixed, grad_branch, preferred_element_type=jnp.float32
    )
    grad_mixed = jnp.einsum(
        "td,cd->tc", grad_branch, out_weight, preferred_element_type=jnp.float32
    )
    grad_mixed = grad_mixed.astype(jnp.bfloat16).reshape(row_count, KV_HEADS, groups, HEAD)
    scores = attention_scores(queries, key_rot, causal)
    soft_probs = jnp.exp(scores - log_total)
    grad_values = jnp.einsum(
        "kgts,tkgh->skh",
        soft_probs.astype(jnp.bfloat16),
        grad_mixed,
        preferred_element_type=jnp.float32,
    )
    grad_probs = jnp.einsum(
        "tkgh,skh->kgts", grad_mixed, values, preferred_element_type=jnp.float32
    )
    grad_scores = soft_probs * (
        grad_probs - jnp.sum(soft_probs * grad_probs, axis=-1, keepdims=True)
    )
    grad_scores = grad_scores.astype(jnp.bfloat16)
    grad_query = (
        jnp.einsum("kgts,skh->tkgh", grad_scores, key_rot, preferred_element_type=jnp.float32)
        * score_scale
    )
    grad_key = (
        jnp.einsum("kgts,tkgh->skh", grad_scores, queries, preferred_element_type=jnp.float32)
        * score_scale
    )
    grad_query = unrotate(grad_query, cosine[:, None, None, :], sine_table[:, None, None, :])
    grad_key = unrotate(grad_key, cosine[:, None, :], sine_table[:, None, :])
    grad_qkv = jnp.concatenate(
        [
            grad_query.reshape(row_count, q_width),
            grad_key.reshape(row_count, k_width),
            grad_values.reshape(row_count, k_width),
        ],
        axis=1,
    ).astype(jnp.bfloat16)
    grad_qkv_weight = jnp.einsum(
        "tc,tq->cq", normed_first, grad_qkv, preferred_element_type=jnp.float32
    )
    grad_first = jnp.einsum("tq,cq->tc", grad_qkv, qkv_weight, preferred_element_type=jnp.float32)
    unit_first = inputs * inv_first
    pull_first = grad_first * gain_attn.astype(jnp.float32)
    grad_gain_attn = jnp.sum(grad_first * unit_first, axis=0)
    grad_inputs = grad_middle + inv_first * (
        pull_first - unit_first * jnp.mean(pull_first * unit_first, axis=1, keepdims=True)
    )
    dense_grads = (grad_gain_attn, grad_qkv_weight, grad_out_weight, grad_gain_ffn, grad_router)
    expert_grads = (grad_up, grad_down)
    return (grad_inputs, dense_grads, expert_grads)


def add_pair(left_part, right_part):
    return left_part + right_part


def per_device(
    tokens,
    segments,
    routes,
    cotangent,
    gain_attn,
    attn_in,
    attn_out,
    gain_ffn,
    router,
    expert_in,
    expert_out,
):
    local_experts = expert_in.shape[0]
    group_count = lax.axis_size("expert")
    expert_count = local_experts * group_count
    micro_count = tokens.shape[0]
    row_count = tokens.shape[1]
    capacity = (row_count * TOP_K * 5 // (4 * expert_count) + 7) // 8 * 8
    shapes = (expert_count, capacity, group_count, local_experts)
    outputs = []
    grad_list = []
    dense_total = None
    expert_total = None
    for micro_index in range(micro_count):
        dense_set = dense_fetch(gain_attn, attn_in, attn_out, gain_ffn, router)
        expert_set = expert_fetch(expert_in, expert_out)
        result, saved_state = forward_micro(
            tokens[micro_index],
            segments[micro_index, 0],
            routes[micro_index],
            dense_set,
            expert_set,
            shapes,
        )
        dense_set = dense_fetch(gain_attn, attn_in, attn_out, gain_ffn, router)
        expert_set = expert_fetch(expert_in, expert_out)
        grad_inputs, dense_grads, expert_grads = backward_micro(
            saved_state, cotangent[micro_index], dense_set, expert_set, shapes
        )
        dense_grads = dense_reduce(dense_grads)
        expert_grads = expert_reduce(expert_grads)
        if dense_total is None:
            dense_total = dense_grads
            expert_total = expert_grads
        else:
            dense_total = jax.tree.map(add_pair, dense_total, dense_grads)
            expert_total = jax.tree.map(add_pair, expert_total, expert_grads)
        outputs.append(result)
        grad_list.append(grad_inputs)
    return (
        jnp.stack(outputs, axis=0),
        jnp.stack(grad_list, axis=0),
        dense_total[0],
        dense_total[1],
        dense_total[2],
        dense_total[3],
        dense_total[4],
        expert_total[0],
        expert_total[1],
    )


NN = (((1,), (0,)), ((), ()))
NT = (((1,), (1,)), ((), ()))
TN = (((0,), (0,)), ((), ()))


def mm(a, b, dims=NN):
    return lax.dot_general(a, b, dims, preferred_element_type=jnp.float32)


class Place:
    def __init__(self, n):
        self.n = n
        d = self.d = lax.axis_index("dp")
        e = self.e = lax.axis_index("expert")
        c, x, y = lax.rem(e, 2), lax.rem(lax.div(e, 2), 2), lax.div(e, 4)
        self.sib = (d, e + 1 - 2 * c)
        self.nx = (d, e + 2 - 4 * x)
        self.ny = (d, e + 4 - 8 * y)
        self.diag = self.nx[1] + 4 - 8 * y
        self.c, self.x, self.y = c, x, y
        self.below = (d - 1, e)
        self.above = (d + 1, e)
        self.has_below = d > 0
        self.has_above = d < n - 1

    def meet(self, everyone=False):
        barrier = pltpu.get_barrier_semaphore()
        d, n = self.d, self.n
        if everyone:
            others = n - 1 + 3

            @pl.loop(1, n)
            def _(k):
                pl.semaphore_signal(barrier, inc=1, device_id=(lax.rem(d + k, n), self.e), device_id_type=MESH)
        else:
            others = 3 + jnp.minimum(d, 1) + jnp.minimum(n - 1 - d, 1)

            @pl.when(self.has_below)
            def _():
                pl.semaphore_signal(barrier, inc=1, device_id=self.below, device_id_type=MESH)

            @pl.when(self.has_above)
            def _():
                pl.semaphore_signal(barrier, inc=1, device_id=self.above, device_id_type=MESH)

        for dev in (self.sib, self.nx, self.ny):
            pl.semaphore_signal(barrier, inc=1, device_id=dev, device_id_type=MESH)
        pl.semaphore_wait(barrier, others)

    def far(self, i):
        n, d = self.n, self.d
        low = d < n - d
        m = jnp.where(low, d, n - 1 - d)
        t = jnp.where(i < n - 1 - m, n - 1 - i, jnp.where(i < n - 1, i - (n - 1 - m), m))
        return jnp.where(low, t, n - 1 - t)

    def near(self, i):
        return self.far(self.n - 1 - i)


def send(src, dst, ss, rs, dev):
    return pltpu.make_async_remote_copy(src, dst, ss, rs, device_id=dev, device_id_type=MESH)


class Gather:
    def __init__(self, at, own, buf, send_sem, recv_z, recv_x, recv_y, recv_d, rows=None):
        self.at, self.own, self.buf = at, own, buf
        self.ss, self.rz, self.rx, self.ry, self.rd = send_sem, recv_z, recv_x, recv_y, recv_d
        rows = rows or own.shape[0]
        self.F, self.A, self.B = pl.ds(0, rows), pl.ds(0, rows // 2), pl.ds(rows // 2, rows // 2)

    def source(self, zz, own):
        return self.own.at[self.F] if own else self.buf.at[zz, 0, self.F]

    def down(self, zz, own=False):
        return send(self.source(zz, own), self.buf.at[zz, 0, self.F], self.ss.at[zz, 0], self.rz.at[zz], self.at.below)

    def up(self, zz, own=False):
        return send(self.source(zz, own), self.buf.at[zz, 0, self.F], self.ss.at[zz, 1], self.rz.at[zz], self.at.above)

    def to_x(self, zz, own=False):
        return send(self.source(zz, own), self.buf.at[zz, 1, self.F], self.ss.at[zz, 2], self.rx.at[zz], self.at.nx)

    def to_y(self, zz, own=False):
        return send(self.source(zz, own), self.buf.at[zz, 2, self.F], self.ss.at[zz, 3], self.ry.at[zz], self.at.ny)

    def turn_y(self, zz):
        return send(self.buf.at[zz, 1, self.A], self.buf.at[zz, 3, self.A], self.ss.at[zz, 4], self.rd.at[zz, 0], self.at.ny)

    def turn_x(self, zz):
        return send(self.buf.at[zz, 2, self.B], self.buf.at[zz, 3, self.B], self.ss.at[zz, 5], self.rd.at[zz, 1], self.at.nx)

    def begin(self):
        self.begin_z()
        self.begin_xy()

    def begin_z(self):
        d = self.at.d

        @pl.when(self.at.has_below)
        def _():
            self.down(d, True).start()

        @pl.when(self.at.has_above)
        def _():
            self.up(d, True).start()

    def begin_xy(self):
        self.to_x(self.at.d, True).start()
        self.to_y(self.at.d, True).start()

    def column_z(self, zz):
        d = self.at.d

        @pl.when(zz < d)
        def _():
            self.up(zz).wait_recv()

            @pl.when(self.at.has_above)
            def _():
                self.up(zz).start()

        @pl.when(zz > d)
        def _():
            self.down(zz).wait_recv()

            @pl.when(self.at.has_below)
            def _():
                self.down(zz).start()

    def column_xy(self, zz):
        self.to_x(zz).start()
        self.to_y(zz).start()

    def column(self, zz):
        self.column_z(zz)
        self.column_xy(zz)

    def plane(self, zz):
        self.to_x(zz).wait_recv()
        self.turn_y(zz).start()
        self.to_y(zz).wait_recv()
        self.turn_x(zz).start()

    def corner(self, zz):
        self.turn_y(zz).wait_recv()
        self.turn_x(zz).wait_recv()

    def finish(self):
        d = self.at.d

        @pl.loop(0, self.at.n)
        def _(zz):
            for copy in (self.to_x, self.to_y, self.turn_y, self.turn_x):
                copy(zz).wait_send()

            @pl.when((d > 0) & (zz >= d))
            def _():
                self.down(zz).wait_send()

            @pl.when(self.at.has_above & (zz <= d))
            def _():
                self.up(zz).wait_send()


class LineGather:
    def __init__(self, at, own, buf, lo, ss, sr, zs, zr):
        self.at, self.own, self.buf = at, own, buf
        self.ss, self.sr, self.zs, self.zr = ss, sr, zs, zr
        rows = own.shape[0] - lo
        self.P, self.A, self.B = pl.ds(lo, rows), pl.ds(lo, rows // 2), pl.ds(lo + rows // 2, rows // 2)

    def inside(self, k):
        at, buf, d = self.at, self.buf, self.at.d
        src, slot, part, dev = (
            (self.own.at[self.P], 1, self.P, at.nx), (self.own.at[self.P], 2, self.P, at.ny),
            (buf.at[d, 1, self.A], 3, self.A, at.ny), (buf.at[d, 2, self.B], 3, self.B, at.nx))[k]
        return send(src, buf.at[d, slot, part], self.ss.at[k], self.sr.at[k], dev)

    def along(self, zz, up):
        part = self.buf.at[zz, :, self.P]
        return send(part, part, self.zs.at[zz, up], self.zr.at[zz], self.at.above if up else self.at.below)

    def begin(self):
        self.inside(0).start()
        self.inside(1).start()

    def plane(self):
        self.inside(0).wait_recv()
        self.inside(2).start()
        self.inside(1).wait_recv()
        self.inside(3).start()

    def corner(self):
        self.inside(2).wait_recv()
        self.inside(3).wait_recv()

        @pl.when(self.at.has_below)
        def _():
            self.along(self.at.d, 0).start()

        @pl.when(self.at.has_above)
        def _():
            self.along(self.at.d, 1).start()

    def line(self, zz):
        self.along(zz, 0).wait_recv()

        @pl.when((zz < self.at.d) & self.at.has_above)
        def _():
            self.along(zz, 1).start()

        @pl.when((zz > self.at.d) & self.at.has_below)
        def _():
            self.along(zz, 0).start()

    def finish(self):
        d = self.at.d
        for k in range(4):
            self.inside(k).wait_send()

        @pl.loop(0, self.at.n)
        def _(zz):
            @pl.when(self.at.has_below & (zz >= d))
            def _():
                self.along(zz, 0).wait_send()

            @pl.when(self.at.has_above & (zz <= d))
            def _():
                self.along(zz, 1).wait_send()


def line_gather_sems(n):
    D_ = pltpu.SemaphoreType.DMA
    return [D_((4,)), D_((4,)), D_((n, 2)), D_((n,))]


def gather_sems(n):
    D_ = pltpu.SemaphoreType.DMA
    return [D_((n, 6)), D_((n,)), D_((n,)), D_((n,)), D_((n, 2))]


def add_rows(dst, src):
    rows = dst.shape[0]
    step = 32 if rows % 32 == 0 else 48 if rows % 48 == 0 else 16

    @pl.loop(0, rows // step)
    def _(r):
        w = pl.ds(pl.multiple_of(r * step, step), step)
        dst[w, :] = (dst[w, :].astype(jnp.float32) + src[w, :].astype(jnp.float32)).astype(dst.dtype)


class Reduce:
    def __init__(self, at, buf, total, r1, r2, rz, ss_1, sr_1, ss_2, sr_2, ss_z, sr_z, start=None):
        self.start = start
        self.at, self.buf, self.total = at, buf, total
        self.r1, self.r2, self.rz = r1, r2, rz
        self.sems = (ss_1, sr_1, ss_2, sr_2, ss_z, sr_z)
        rows = total.shape[0]
        self.A, self.B = pl.ds(0, rows // 2), pl.ds(rows // 2, rows // 2)

    def first(self, zz, k):
        ss, sr = self.sems[0], self.sems[1]
        slot, part, dev = ((3, self.A, self.at.nx), (3, self.B, self.at.ny), (1, self.A, self.at.nx), (2, self.B, self.at.ny))[k]
        return send(self.buf.at[zz, slot, part], self.r1.at[zz, k], ss.at[zz, k], sr.at[zz, k], dev)

    def second(self, zz, k):
        ss, sr = self.sems[2], self.sems[3]
        slot, part, dev = ((2, self.A, self.at.ny), (1, self.B, self.at.nx))[k]
        return send(self.buf.at[zz, slot, part], self.r2.at[zz, k], ss.at[zz, k], sr.at[zz, k], dev)

    def down(self, zz):
        return send(self.buf.at[zz, 0], self.rz.at[zz], self.sems[4].at[zz], self.sems[5].at[zz], self.at.below)

    def up(self, zz):
        slot = jnp.where(zz == self.at.d + 1, self.at.n, zz)
        return send(self.buf.at[zz, 0], self.rz.at[slot], self.sems[4].at[zz], self.sems[5].at[slot], self.at.above)

    def arrive(self, slot):
        return send(self.buf.at[0, 0], self.rz.at[slot], self.sems[4].at[0], self.sems[5].at[slot], self.at.nx)

    def s1(self, zz):
        self.corners(zz)
        self.sides(zz)

    def corners(self, zz):
        self.first(zz, 0).start()
        self.first(zz, 1).start()

    def sides(self, zz):
        self.first(zz, 2).start()
        self.first(zz, 3).start()

    def turn(self, zz):
        self.first(zz, 0).wait_recv()
        add_rows(self.buf.at[zz, 2, self.A], self.r1.at[zz, 0])
        self.second(zz, 0).start()
        self.first(zz, 1).wait_recv()
        add_rows(self.buf.at[zz, 1, self.B], self.r1.at[zz, 1])
        self.second(zz, 1).start()

    def take_sides(self, zz):
        self.first(zz, 2).wait_recv()
        add_rows(self.buf.at[zz, 0, self.A], self.r1.at[zz, 2])
        self.first(zz, 3).wait_recv()
        add_rows(self.buf.at[zz, 0, self.B], self.r1.at[zz, 3])

    def s2(self, zz):
        self.turn(zz)
        self.take_sides(zz)

    def step(self, j):
        at = self.at
        if j < at.n:
            self.turn(at.far(j))
            self.sides(at.far(j))
            if j + 2 < at.n:
                self.corners(at.far(j + 2))
        if j >= 1:
            self.take_sides(at.far(j - 1))
            self.s3(at.far(j - 1))
            self.lines(j - 1)

    def s3(self, zz):
        self.second(zz, 0).wait_recv()
        add_rows(self.buf.at[zz, 0, self.A], self.r2.at[zz, 0])
        self.second(zz, 1).wait_recv()
        add_rows(self.buf.at[zz, 0, self.B], self.r2.at[zz, 1])

    def push(self, zz):
        d = self.at.d

        @pl.when(zz < d)
        def _():
            self.down(zz).start()

        @pl.when(zz > d)
        def _():
            self.up(zz).start()

    def line_head(self, zz):
        @pl.when(jnp.logical_not(self.passes(zz)))
        def _():
            self.push(zz)

    def passes(self, zz):
        d = self.at.d
        return ((zz < d) & self.at.has_above) | ((zz > d) & self.at.has_below)

    def line_rest(self, zz):
        @pl.when(self.passes(zz))
        def _():
            self.arrive(zz).wait_recv()
            add_rows(self.buf.at[zz, 0], self.rz.at[zz])
            self.push(zz)

    def lines(self, j):
        n = self.at.n
        if j < n - 1:
            self.line_head(self.at.far(j))
        if 0 <= j - 1 < n - 2:
            self.line_rest(self.at.far(j - 1))
        if j == n - 2:
            self.line_rest(self.at.far(j))

    def last(self):
        d, n, rows, step = self.at.d, self.at.n, self.total.shape[0], 16

        def over(fn):
            @pl.loop(0, rows // step)
            def _(r):
                fn(pl.ds(pl.multiple_of(r * step, step), step))

        def own(w):
            first = self.buf[d, 0, w, :].astype(jnp.float32)
            self.total[w, :] = first if self.start is None else first + self.start[w, :]

        def more(slot):
            def fn(w):
                self.total[w, :] += self.rz[slot, w, :].astype(jnp.float32)

            self.arrive(slot).wait_recv()
            over(fn)

        over(own)

        @pl.when(self.at.has_above)
        def _():
            more(d)

        @pl.when(self.at.has_below)
        def _():
            more(n)

    def finish(self):
        d = self.at.d

        @pl.loop(0, self.at.n)
        def _(zz):
            for k in range(4):
                self.first(zz, k).wait_send()
            for k in range(2):
                self.second(zz, k).wait_send()

            @pl.when(zz != d)
            def _():
                self.arrive(zz)
                send(self.buf.at[zz, 0], self.rz.at[zz], self.sems[4].at[zz], self.sems[5].at[zz], self.at.nx).wait_send()


def reduce_scratch(n, rows, cols):
    D_ = pltpu.SemaphoreType.DMA
    V = lambda *s: pltpu.VMEM(s, jnp.bfloat16)
    return [V(n, 4, rows // 2, cols), V(n, 2, rows // 2, cols), V(n + 1, rows, cols),
            D_((n, 4)), D_((n, 4)), D_((n, 2)), D_((n, 2)), D_((n,)), D_((n + 1,))]


def expert_kernel(n, experts, x_ref, cot_ref, up_ref, down_ref, mid_ref,
                  out_ref, gx_ref, gup_ref, gdown_out,
                  gdown_ref, xb, cb, gg, mixed, gb, wup, wdown, pick_ref, place_ref, *rest):
    f32, bf16 = jnp.float32, jnp.bfloat16
    at = Place(n)
    d = at.d
    lo = x_ref.shape[0] * 3 // 4
    gather = Gather(at, x_ref, xb, *rest[:5], rows=lo)
    tail = LineGather(at, x_ref, xb, lo, *rest[-4:])
    grads = Reduce(at, gb, gx_ref, *rest[5:14])
    outs = Reduce(at, gg, out_ref, *rest[14:23], start=mid_ref)
    load_sem, core_ss, core_sr, free = rest[23:-4]
    rows = x_ref.shape[0]
    f2 = up_ref.shape[1]
    f = f2 // 2
    held = f // 128
    loads = [
        pltpu.make_async_copy(x_ref, xb.at[d, 0], load_sem.at[0]),
        pltpu.make_async_copy(up_ref, wup.at[0], load_sem.at[1]),
        pltpu.make_async_copy(down_ref, wdown.at[0], load_sem.at[2]),
        pltpu.make_async_copy(cot_ref, cb, load_sem.at[3]),
    ]
    for load in loads:
        load.start()
    at.meet()
    gather.begin_z()
    tail.begin()
    gather.begin_xy()
    swaps = [
        send(up_ref, wup.at[1], core_ss.at[0], core_sr.at[0], at.sib),
        send(down_ref, wdown.at[1], core_ss.at[1], core_sr.at[1], at.sib),
    ]
    for swap in swaps:
        swap.start()
    for h, owner in ((0, at.e), (1, at.sib[1])):
        for j in range(held):
            expert, cols = owner * held + j, slice((h * held + j) * 128, (h * held + j + 1) * 128)
            gate_row = lax.broadcasted_iota(jnp.int32, (128, 128), 0)
            pick_ref[:, cols] = ((gate_row == expert) | (gate_row == expert + experts)).astype(bf16)
            place_ref[cols, :] = (lane_tile(128) == expert).astype(bf16)
    loads[0].wait()
    tail.plane()
    tail.corner()
    gather.plane(at.near(0))
    gather.column(at.near(1))
    for load in loads[1:]:
        load.wait()
    for swap in swaps:
        swap.wait_recv()

    def tokens(ref, zz, p, lo, width):
        return ref[zz, pl.ds(2 * p, 2), :, pl.ds(lo, width)].reshape(2 * rows, width)

    def half(zz, p):
        pair = pl.ds(2 * p, 2)
        x = tokens(xb, zz, p, 0, D)
        cot = tokens(cb, zz, p, 0, D)
        mix = mm(tokens(xb, zz, p, D, 128), pick_ref[...])
        sums = jnp.zeros((2 * rows, 128), f32)
        for h in range(2):
            gate_up = mm(x, wup[h])
            back = mm(cot, wdown[h], NT)
            for j in range(held):
                k = h * held + j
                gate = gate_up[:, j * 256 : j * 256 + 128]
                up = gate_up[:, j * 256 + 128 : j * 256 + 256]
                b = back[:, j * 128 : (j + 1) * 128]
                m = mix[:, k * 128 : (k + 1) * 128]
                sig = 1.0 / (1.0 + jnp.exp(-gate))
                act = gate * sig
                hidden = (act * up).astype(bf16).astype(f32)
                prod = hidden * b
                high = prod.astype(bf16)
                low = (prod - high.astype(f32)).astype(bf16)
                sel = place_ref[k * 128 : (k + 1) * 128, :]
                sums += mm(high, sel) + mm(low, sel)
                mixed[zz, pair, :, pl.ds(k * 128, 128)] = (m * hidden).astype(bf16).reshape(2, rows, 128)
                gh = m * b
                gg[zz, pair, :, pl.ds(k * 256, 128)] = (
                    (gh * up * sig * (1.0 + gate * (1.0 - sig))).astype(bf16).reshape(2, rows, 128))
                gg[zz, pair, :, pl.ds(k * 256 + 128, 128)] = (gh * act).astype(bf16).reshape(2, rows, 128)
        for q in range(D // 512):
            cols = pl.ds(q * 512, 512)
            part = mm(tokens(gg, zz, p, 0, f2), wup[0, cols, :], NT) + mm(tokens(gg, zz, p, f2, f2), wup[1, cols, :], NT)
            gb[zz, pair, :, cols] = part.astype(bf16).reshape(2, rows, 512)
        gb[zz, pair, :, pl.ds(D, 128)] = sums.astype(bf16).reshape(2, rows, 128)

    @pl.loop(0, n)
    def _(i):
        zz = at.near(i)
        half(zz, 0)

        @pl.when(i + 2 < n)
        def _():
            gather.column(at.near(i + 2))

        @pl.when(i + 1 < n)
        def _():
            tail.line(at.near(i + 1))
            gather.plane(at.near(i + 1))

        gather.corner(zz)
        half(zz, 1)
        grads.s1(zz)

        @pl.when(i >= 1)
        def _():
            grads.s2(at.near(i - 1))

        @pl.when(i >= 2)
        def _():
            grads.s3(at.near(i - 2))
            grads.line_head(at.near(i - 2))

    pl.semaphore_signal(free.at[0], inc=1, device_id=at.sib, device_id_type=MESH)

    def grad_up(h, more):
        @pl.loop(0, D // 256)
        def _(q):
            cols = pl.ds(pl.multiple_of(q * 256, 256), 256)
            xs = xb[:, :, :, cols].reshape(n * 4 * rows, 256)
            part = mm(xs, gg[:, :, :, pl.ds(h * f2, f2)].reshape(n * 4 * rows, f2), TN)
            if more:
                part += wup[h, cols, :].astype(f32)
            wup[h, cols, :] = part.astype(bf16)

    def grad_down(h):
        for q in range(D // 512):
            cols = pl.ds(q * 512, 512)
            part = mm(mixed[:, :, :, pl.ds(h * f, f)].reshape(n * 4 * rows, f), cb[:, :, :, cols].reshape(n * 4 * rows, 512), TN)
            if h == 0:
                gdown_ref[:, cols] = part + wdown[0, :, cols].astype(f32)
            else:
                wdown[1, :, cols] = part.astype(bf16)

    def output(zz):
        @pl.loop(0, 2)
        def _(p):
            for q in range(D // 512):
                cols = pl.ds(q * 512, 512)
                part = mm(tokens(mixed, zz, p, 0, f), wdown[0, :, cols]) + mm(tokens(mixed, zz, p, f, f), wdown[1, :, cols])
                gg[zz, pl.ds(2 * p, 2), :, cols] = part.astype(bf16).reshape(2, rows, 512)

    grad_up(1, False)
    pl.semaphore_wait(free.at[0], 1)
    up_swap = send(wup.at[1], wup.at[0], core_ss.at[2], core_sr.at[2], at.sib)
    for swap in swaps:
        swap.wait_send()
    up_swap.start()
    grads.s2(at.near(n - 1))
    grads.s3(at.near(n - 2))
    grads.line_head(at.near(n - 2))
    up_swap.wait_recv()
    grad_up(0, True)
    keep = pltpu.make_async_copy(wup.at[0], gup_ref, load_sem.at[0])
    keep_down = pltpu.make_async_copy(gdown_ref, gdown_out, load_sem.at[1])
    keep.start()
    grads.s3(at.near(n - 1))
    grads.line_head(at.near(n - 1))
    for j in range(n):
        output(at.far(j))
        if j < 2:
            outs.corners(at.far(j))
    pl.semaphore_signal(free.at[1], inc=1, device_id=at.sib, device_id_type=MESH)
    grad_down(1)
    pl.semaphore_wait(free.at[1], 1)
    down_swap = send(wdown.at[1], wdown.at[0], core_ss.at[3], core_sr.at[3], at.sib)
    down_swap.start()
    for j in range(n + 1):
        if j == n:
            grads.last()
        outs.step(j)
        if j < n - 1:
            grads.line_rest(at.far(j))
        if j == 0:
            down_swap.wait_recv()
            grad_down(0)
            keep_down.start()
    outs.last()
    keep_down.wait()
    keep.wait()
    up_swap.wait_send()
    down_swap.wait_send()
    gather.finish()
    tail.finish()
    grads.finish()
    outs.finish()


def expert_layer(x, cot_all, up, down, middle, n, experts, cid):
    rows, wide = x.shape
    f2 = up.shape[1]
    f = f2 // 2
    bf16 = jnp.bfloat16
    V = lambda *s: pltpu.VMEM(s, bf16)
    D_ = pltpu.SemaphoreType.DMA
    any_, vm = pl.BlockSpec(memory_space=pl.ANY), pl.BlockSpec(memory_space=pltpu.VMEM)
    return pl.pallas_call(
        functools.partial(expert_kernel, n, experts),
        out_shape=(
            jax.ShapeDtypeStruct((rows, D), jnp.float32),
            jax.ShapeDtypeStruct((rows, wide), jnp.float32),
            jax.ShapeDtypeStruct((D, f2), bf16),
            jax.ShapeDtypeStruct((f, D), jnp.float32),
        ),
        in_specs=[any_, any_, any_, any_, vm],
        out_specs=[vm, vm, any_, any_],
        scratch_shapes=[pltpu.VMEM((f, D), jnp.float32), V(n, 4, rows, wide), V(n, 4, rows, D), V(n, 4, rows, 2 * f2), V(n, 4, rows, 2 * f), V(n, 4, rows, wide),
                        V(2, D, f2), V(2, f, D), V(128, 2 * f), V(2 * f, 128)]
        + gather_sems(n) + reduce_scratch(n, rows, wide) + reduce_scratch(n, rows, D)
        + [D_((4,)), D_((4,)), D_((4,)), pltpu.SemaphoreType.REGULAR((2,))] + line_gather_sems(n),
        compiler_params=pltpu.CompilerParams(collective_id=cid, has_side_effects=True, vmem_limit_bytes=63 << 20),
        name="expert_layer",
    )(x, cot_all, up, down, middle)


class GatherAll:
    def __init__(self, at, own, buf, send_sem, recv_z, recv_x, recv_y, recv_d, recv_s):
        self.at, self.own, self.buf = at, own, buf
        self.ss, self.rz, self.rx, self.ry, self.rd, self.rs = send_sem, recv_z, recv_x, recv_y, recv_d, recv_s
        cols = own.shape[1]
        half = (cols // 128 + 1) // 2 * 128
        self.A, self.B, self.F = pl.ds(0, half), pl.ds(half, cols - half), pl.ds(0, cols)

    def move(self, zz, e, cols, slot, sem, dev, own=False):
        dst = self.buf.at[zz * 8 + e, :, cols]
        return send(self.own.at[:, cols] if own else dst, dst, self.ss.at[zz, slot], sem, dev)

    def down(self, zz, own=False):
        return self.move(zz, self.at.e, self.F, 0, self.rz.at[zz], self.at.below, own)

    def up(self, zz, own=False):
        return self.move(zz, self.at.e, self.F, 1, self.rz.at[zz], self.at.above, own)

    def spread(self, zz, own=False):
        at = self.at
        return (self.move(zz, at.e, self.F, 2, self.rx.at[zz], at.nx, own),
                self.move(zz, at.e, self.F, 3, self.ry.at[zz], at.ny, own),
                self.move(zz, at.e, self.F, 4, self.rs.at[zz, 0], at.sib, own))

    def from_x(self, zz):
        at = self.at
        ex = at.nx[1]
        return (self.move(zz, ex, self.F, 2, self.rx.at[zz], at.nx),
                self.move(zz, ex, self.A, 5, self.rd.at[zz, 0], at.ny),
                self.move(zz, ex, self.F, 6, self.rs.at[zz, 1], at.sib))

    def from_y(self, zz):
        at = self.at
        ey = at.ny[1]
        return (self.move(zz, ey, self.F, 3, self.ry.at[zz], at.ny),
                self.move(zz, ey, self.B, 7, self.rd.at[zz, 1], at.nx),
                self.move(zz, ey, self.F, 8, self.rs.at[zz, 2], at.sib))

    def turned(self, zz):
        at = self.at
        return (self.move(zz, at.diag, self.A, 5, self.rd.at[zz, 0], at.ny),
                self.move(zz, at.diag, self.A, 9, self.rs.at[zz, 3], at.sib),
                self.move(zz, at.diag, self.B, 7, self.rd.at[zz, 1], at.nx),
                self.move(zz, at.diag, self.B, 10, self.rs.at[zz, 4], at.sib))

    def begin(self):
        d = self.at.d

        @pl.when(self.at.has_below)
        def _():
            self.down(d, True).start()

        @pl.when(self.at.has_above)
        def _():
            self.up(d, True).start()

        for copy in self.spread(d, True):
            copy.start()

    def column(self, zz):
        d = self.at.d

        @pl.when(zz < d)
        def _():
            self.up(zz).wait_recv()

            @pl.when(self.at.has_above)
            def _():
                self.up(zz).start()

        @pl.when(zz > d)
        def _():
            self.down(zz).wait_recv()

            @pl.when(self.at.has_below)
            def _():
                self.down(zz).start()

        for copy in self.spread(zz):
            copy.start()

    def plane(self, zz):
        for arrive, turn, share in (self.from_x(zz), self.from_y(zz)):
            arrive.wait_recv()
            turn.start()
            share.start()

    def corner(self, zz):
        a, share_a, b, share_b = self.turned(zz)
        a.wait_recv()
        share_a.start()
        b.wait_recv()
        share_b.start()

    def siblings(self):
        at = self.at
        es = at.sib[1]
        exs, eys, exys = es + at.nx[1] - at.e, es + at.ny[1] - at.e, es + at.diag - at.e

        @pl.loop(0, at.n)
        def _(zz):
            for e, cols, k in ((es, self.F, 0), (exs, self.F, 1), (eys, self.F, 2), (exys, self.A, 3), (exys, self.B, 4)):
                self.move(zz, e, cols, 4, self.rs.at[zz, k], at.sib).wait_recv()

    def finish(self):
        d = self.at.d

        @pl.loop(0, self.at.n)
        def _(zz):
            for group in (self.spread(zz), self.from_x(zz)[1:], self.from_y(zz)[1:], self.turned(zz)[1::2]):
                for copy in group:
                    copy.wait_send()

            @pl.when((d > 0) & (zz >= d))
            def _():
                self.down(zz).wait_send()

            @pl.when(self.at.has_above & (zz <= d))
            def _():
                self.up(zz).wait_send()


def lane_tile(rows):
    return lax.broadcasted_iota(jnp.int32, (rows, 128), 1)


def swap_halves(tile):
    front = lax.rem(lane_tile(tile.shape[0]), HEAD) < HEAD // 2
    return jnp.where(front, pltpu.roll(tile, 128 - HEAD // 2, 1), pltpu.roll(tile, HEAD // 2, 1))


def inverse_rms(v):
    return lax.rsqrt(jnp.mean(v * v, axis=1, keepdims=True) + norm_eps)


def rope_lanes(seg_ref, freq_ref, cos_ref, sin_ref):
    f32 = jnp.float32
    packs, rows = seg_ref.shape[0], seg_ref.shape[2]
    row = jnp.concatenate([seg_ref[i].astype(f32) + float(2 * rows * i) for i in range(packs)], axis=1)
    total = packs * rows
    across = jnp.broadcast_to(row, (total, total))
    same = across == jnp.transpose(across)
    source = lax.broadcasted_iota(jnp.int32, (total, total), 1)
    target = lax.broadcasted_iota(jnp.int32, (total, total), 0)
    start = jnp.min(jnp.where(same, source.astype(f32), float(total)), axis=1, keepdims=True)
    angle = (target.astype(f32) - start) * freq_ref[...]
    cos_ref[...] = jnp.cos(angle)
    front = lax.rem(source, HEAD) < HEAD // 2
    sine = jnp.sin(angle)
    sin_ref[...] = jnp.where(front, -sine, sine)
    return (same & (source <= target)).astype(f32)


def forward_kernel(n, experts, tok_ref, cot_ref, qkv_ref, proj_ref, router_ref, gain_a_ref, gain_f_ref, ein_ref, seg_ref, route_ref, freq_ref,
                   w_all, cot_all, up_all, disp_out, mid_out, gates_out, gain_out, nf_out, q_out, k_out, v_out, p_out, mixed_out, cos_out, sin_out,
                   disp_ref, mid_ref, gates_ref, gain_ref, nf_ref, q_ref, k_ref, v_ref, p_ref, mixed_ref, cos_ref, sin_ref,
                   wv, pieces, dense_ref, small_ref, *rest):
    f32, bf16 = jnp.float32, jnp.bfloat16
    at = Place(n)
    d = at.d
    dense = GatherAll(at, dense_ref, wv, *rest[:6])
    cot = Gather(at, cot_ref, cot_all, *rest[6:11])
    load_sem, a2a_ss, a2a_sr, keep_sem = rest[11:]
    q_width, k_width = HEADS * HEAD, KV_HEADS * HEAD
    groups = HEADS // KV_HEADS
    held, share = ein_ref.shape[:2]
    f = FF // n
    qkv_width = q_width + 2 * k_width
    dense_ref[:, :qkv_width] = qkv_ref[...]
    dense_ref[:, qkv_width : qkv_width + D] = proj_ref[...]
    shard = dense_ref.shape[0]
    small_ref[...] = jnp.zeros(small_ref.shape, f32)
    small_ref[:experts, :shard] = router_ref[...].astype(f32)
    small_ref[experts : experts + 1, :shard] = gain_a_ref[...].astype(f32)
    small_ref[experts + 1 : experts + 2, :shard] = gain_f_ref[...].astype(f32)
    dense_ref[:, qkv_width + D :] = jnp.transpose(small_ref[...])[:shard].astype(bf16)
    loads = [
        pltpu.make_async_copy(dense_ref, wv.at[d * 8 + at.e], load_sem.at[0]),
        pltpu.make_async_copy(cot_ref, cot_all.at[d, 0], load_sem.at[1]),
    ]
    for load in loads:
        load.start()

    def rows_of(z):
        return up_all.at[pl.ds(pl.multiple_of(z * share, share), share), :]

    own_piece = pltpu.make_async_copy(pieces.at[d], rows_of(d), load_sem.at[2])

    parts = 3
    third = share // parts

    def third_of(z, r):
        return up_all.at[pl.ds(pl.multiple_of(z * share + r * third, third), third), :]

    def exchange(k, r):
        to = lax.rem(d + k, n)
        return send(pieces.at[to, pl.ds(r * third, third), :], third_of(d, r), a2a_ss.at[k, r], a2a_sr.at[d, r], (to, at.e))

    def exchange_part(r):
        for k in range(1, n):
            exchange(k, r).start()

    at.meet(True)
    dense.begin()
    for q in range(n):
        for j in range(2 * held):
            lo = (j % 2) * FF + q * f
            pieces[q, :, j * f : (j + 1) * f] = ein_ref[j // 2, :, lo : lo + f]
    own_piece.start()
    allowed = rope_lanes(seg_ref, freq_ref, cos_ref, sin_ref)
    for i in range(1, n):
        dense.column(at.near(i))
        if i == n - 1:
            cot.begin_z()
            exchange_part(0)
        dense.plane(at.near(i - 1))
        if i >= 2:
            dense.corner(at.near(i - 2))
    cot.begin_xy()
    dense.plane(at.near(n - 1))
    dense.corner(at.near(n - 2))
    cot.column(at.near(1))
    cot.column(at.near(2))
    exchange_part(1)
    exchange_part(2)
    dense.corner(at.near(n - 1))
    for load in loads:
        load.wait()
    dense.siblings()
    keep = pltpu.make_async_copy(wv, w_all, load_sem.at[0])
    keep.start()

    def weight(lo, width):
        return wv[:, :, lo : lo + width].reshape(D, width)

    tail_at = q_width + 2 * k_width + D
    turned = jnp.transpose(weight(tail_at, 128).astype(f32))
    gain_ref[0:1, :] = turned[experts : experts + 1, :]
    gain_ref[1:2, :] = turned[experts + 1 : experts + 2, :]
    x = tok_ref[...].astype(f32)
    nf_ref[...] = (x * inverse_rms(x) * gain_ref[0:1, :]).astype(bf16)
    cos, sin = cos_ref[...], sin_ref[...]
    for q in range((q_width + 2 * k_width) // 512):
        lo = q * 512
        part = mm(nf_ref[...], weight(lo, 512))
        for t in range(4):
            tile = part[:, t * 128 : (t + 1) * 128]
            col = lo + t * 128
            if col < q_width + k_width:
                tile = tile * cos + swap_halves(tile) * sin
            ref, base = (q_ref, 0) if col < q_width else (k_ref, q_width) if col < q_width + k_width else (v_ref, q_width + k_width)
            ref[:, col - base : col - base + 128] = tile.astype(bf16)
    cot.plane(at.near(0))
    allowed = jnp.concatenate([allowed] * groups, axis=0) > 0
    for g in range(KV_HEADS):
        qs = jnp.concatenate([q_ref[:, (g * groups + j) * HEAD : (g * groups + j + 1) * HEAD] for j in range(groups)], axis=0)
        ks, vs = k_ref[:, g * HEAD : (g + 1) * HEAD], v_ref[:, g * HEAD : (g + 1) * HEAD]
        scores = jnp.where(allowed, mm(qs, ks, NT) * HEAD ** (-0.5), neg_large)
        raised = jnp.exp(scores - jnp.max(scores, axis=1, keepdims=True))
        probs = raised / jnp.sum(raised, axis=1, keepdims=True)
        p_ref[g] = probs
        out = mm(probs.astype(bf16), vs).astype(bf16)
        rows = out.shape[0] // groups
        for j in range(groups):
            mixed_ref[:, (g * groups + j) * HEAD : (g * groups + j + 1) * HEAD] = out[j * rows : (j + 1) * rows]
    for q in range(D // 512):
        lo = q * 512
        mid_ref[:, lo : lo + 512] = tok_ref[:, lo : lo + 512].astype(f32) + mm(mixed_ref[...], weight(q_width + 2 * k_width + lo, 512))
    mid = mid_ref[...]
    disp_ref[:, :D] = (mid * inverse_rms(mid) * gain_ref[1:2, :]).astype(bf16)
    logits = mm(disp_ref[:, :D], weight(tail_at, 128))
    hits = []
    for i in range(route_ref.shape[0]):
        expert = lax.broadcasted_iota(jnp.int32, (128, route_ref.shape[2]), 0)
        hits.append(sum((route_ref[i, k : k + 1, :] == expert).astype(f32) for k in range(TOP_K)))
    chosen = jnp.transpose(jnp.concatenate(hits, axis=1))
    masked = jnp.where(chosen > 0, logits, neg_large)
    raised = jnp.where(chosen > 0, jnp.exp(masked - jnp.max(masked, axis=1, keepdims=True)), 0.0)
    gates = raised / jnp.sum(raised, axis=1, keepdims=True)
    gates_ref[...] = gates
    high = gates.astype(bf16).astype(f32)
    low = (gates - high).astype(bf16).astype(f32)
    disp_ref[:, D:] = (high + pltpu.roll(low, experts, 1)).astype(bf16)

    keeps = [pltpu.make_async_copy(src, dst, keep_sem.at[i]) for i, (src, dst) in enumerate((
        (disp_ref, disp_out), (mid_ref, mid_out), (gates_ref, gates_out), (gain_ref, gain_out), (nf_ref, nf_out), (q_ref, q_out),
        (k_ref, k_out), (v_ref, v_out), (p_ref, p_out), (mixed_ref, mixed_out), (cos_ref, cos_out), (sin_ref, sin_out)))]
    for copy in keeps:
        copy.start()
    for i in range(1, n):
        cot.plane(at.near(i))
        cot.corner(at.near(i - 1))
        if i + 2 < n:
            cot.column(at.near(i + 2))
    cot.corner(at.near(n - 1))
    own_piece.wait()
    for k in range(1, n):
        source = lax.rem(d + k, n)
        for r in range(parts):
            exchange(k, r).wait_send()
            send(pieces.at[0, pl.ds(r * third, third), :], third_of(source, r), a2a_ss.at[k, r], a2a_sr.at[source, r], (source, at.e)).wait_recv()
    keep.wait()
    dense.finish()
    cot.finish()
    for copy in keeps:
        copy.wait()


def forward_layer(tok, cot, attn_in, attn_out, router, gain_attn, gain_ffn, ein, segments, routes, n, experts, cid):
    f32, bf16 = jnp.float32, jnp.bfloat16
    rows = tok.shape[0]
    shard = attn_in.shape[0]
    held, share = ein.shape[:2]
    q_width, k_width = HEADS * HEAD, KV_HEADS * HEAD
    wide = q_width + 2 * k_width + D + 128
    groups = HEADS // KV_HEADS
    half = HEAD // 2
    freq = np.tile(np.float32(rope_base) ** (-np.arange(half, dtype=np.float32) / np.float32(half)), 128 // half)[None, :]
    D_ = pltpu.SemaphoreType.DMA
    V = lambda *s: pltpu.VMEM(s, bf16)
    any_, vm = pl.BlockSpec(memory_space=pl.ANY), pl.BlockSpec(memory_space=pltpu.VMEM)
    S = jax.ShapeDtypeStruct
    saved = (
        S((rows, D + 128), bf16), S((rows, D), f32), S((rows, 128), f32), S((8, D), f32), S((rows, D), bf16),
        S((rows, q_width), bf16), S((rows, k_width), bf16), S((rows, k_width), bf16),
        S((KV_HEADS, groups * rows, rows), f32), S((rows, q_width), bf16), S((rows, 128), f32), S((rows, 128), f32),
    )
    return pl.pallas_call(
        functools.partial(forward_kernel, n, experts),
        out_shape=(S((n * 8, shard, wide), bf16), S((n, 4, rows, D), bf16), S((D, 2 * held * (FF // n)), bf16)) + saved,
        in_specs=[vm, any_] + [vm] * 9,
        out_specs=[any_] * 15,
        scratch_shapes=[pltpu.VMEM(a.shape, a.dtype) for a in saved]
        + [V(n * 8, shard, wide), V(n, share, 2 * held * (FF // n)), V(shard, wide), pltpu.VMEM((128, 128), f32)]
        + [D_((n, 11)), D_((n,)), D_((n,)), D_((n,)), D_((n, 2)), D_((n, 5))] + gather_sems(n)
        + [D_((3,)), D_((n, 3)), D_((n, 3)), D_((len(saved),))],
        compiler_params=pltpu.CompilerParams(collective_id=cid, has_side_effects=True, vmem_limit_bytes=60 << 20),
        name="forward_layer",
    )(tok, cot, attn_in, attn_out, router.T, gain_attn[None, :], gain_ffn[None, :], ein, segments, routes.transpose(0, 2, 1), freq)


def backward_kernel(n, experts, gs_in, tok_in, cot_in, mid_in, gates_in, gain_in, nf_in, disp_in, q_in, k_in, v_in, p_in, mixed_in, cos_in, sin_in, w_ref, gup_ref,
                    gtok_ref, gout_ref, gin_ref, gtail_ref, arrived,
                    gs_ref, tok_ref, cot_ref, mid_ref, gates_ref, gain_ref, nf_ref, disp_ref, q_ref, k_ref, v_ref, p_ref, mixed_ref, cos_ref, sin_ref,
                    wv, pout, pin, tot_out, tot_in, pair, gq, gl, sums, gb, gm, flat, *rest):
    f32, bf16 = jnp.float32, jnp.bfloat16
    at = Place(n)
    d, c = at.d, at.c
    outs = Reduce(at, pout, tot_out, *rest[:9])
    ins = Reduce(at, pin, tot_in, *rest[9:18])
    load_sem, pair_ss, pair_sr, a2a_ss, a2a_sr, end_ss, end_sr, in_sem = rest[18:]
    q_width, k_width = HEADS * HEAD, KV_HEADS * HEAD
    groups = HEADS // KV_HEADS
    qkv_width = q_width + 2 * k_width
    tail_at = qkv_width + D
    rows = tok_ref.shape[0]
    shard = w_ref.shape[1]
    share = D // n
    f = FF // n
    fetched = [pltpu.make_async_copy(src, dst, in_sem.at[i]) for i, (src, dst) in enumerate((
        (mid_in, mid_ref), (gates_in, gates_ref), (gs_in, gs_ref), (gain_in, gain_ref), (cot_in, cot_ref), (mixed_in, mixed_ref), (nf_in, nf_ref), (disp_in, disp_ref), (q_in, q_ref), (k_in, k_ref), (v_in, v_ref), (p_in, p_ref), (tok_in, tok_ref), (cos_in, cos_ref), (sin_in, sin_ref)))]
    for copy in fetched[:8]:
        copy.start()
    loads = []
    for i, (lo, width) in enumerate(((tail_at, 128), (qkv_width, D), (0, qkv_width))):
        loads.append(pltpu.make_async_copy(w_ref.at[:, :, pl.ds(lo, width)], wv.at[:, :, pl.ds(lo, width)], load_sem.at[i]))
    for load in loads:
        load.start()
    for copy in fetched[8:]:
        copy.start()
    own_share = pltpu.make_async_copy(gup_ref.at[pl.ds(pl.multiple_of(d * share, share), share), :], arrived.at[d], load_sem.at[3])
    own_share.start()

    def exchange(k):
        to = lax.rem(d + k, n)
        return send(gup_ref.at[pl.ds(pl.multiple_of(to * share, share), share), :], arrived.at[d], a2a_ss.at[k], a2a_sr.at[d], (to, at.e))

    swaps = [send(src, pair.at[i], pair_ss.at[i], pair_sr.at[i], at.sib)
             for i, src in enumerate((mixed_ref, nf_ref, disp_ref.at[:, pl.ds(0, D)], gb))]
    swap_q = send(gq.at[0], gq.at[1], pair_ss.at[4], pair_sr.at[4], at.sib)
    swap_l = send(gl.at[0], gl.at[1], pair_ss.at[5], pair_sr.at[5], at.sib)
    swap_s = send(sums.at[0], sums.at[1], pair_ss.at[6], pair_sr.at[6], at.sib)
    at.meet(True)
    for k in range(1, n):
        exchange(k).start()
    for copy in fetched[:8]:
        copy.wait()
    for i in range(3):
        swaps[i].start()

    def weight(lo, width):
        return wv[:, :, lo : lo + width].reshape(D, width)

    loads[0].wait()
    mid = mid_ref[...]
    inv_second = inverse_rms(mid)
    unit = mid * inv_second
    gates, gg = gates_ref[...], gs_ref[:, D:]
    gl[0] = (gates * (gg - jnp.sum(gates * gg, axis=1, keepdims=True))).astype(bf16)
    swap_l.start()
    grad_second = mm(gl[0], weight(tail_at, 128), NT) + gs_ref[:, :D]
    pull = grad_second * gain_ref[1:2, :]
    sums[0, 1:2, :] = jnp.sum(grad_second * unit, axis=0, keepdims=True)
    grad_middle = cot_ref[...].astype(f32) + inv_second * (pull - unit * jnp.mean(pull * unit, axis=1, keepdims=True))
    gtok_ref[...] = grad_middle
    gb[...] = grad_middle.astype(bf16)
    swaps[3].start()
    loads[1].wait()
    for q in range(q_width // 512):
        gm[:, q * 512 : (q + 1) * 512] = mm(gb[...], wv[:, :, qkv_width : qkv_width + D].reshape(D, D)[q * 512 : (q + 1) * 512], NT).astype(bf16)

    def both(own, other, cols):
        return jnp.concatenate([own[:, cols], other[:, cols]], axis=0)

    def store(buf, zz, lo, value):
        blocks = value.astype(bf16).reshape(4, 2 * shard, value.shape[1])
        for a in range(4):
            slot = 2 * lax.rem(a // 2 + at.y, 2) + lax.rem(a % 2 + at.x, 2)
            buf[zz, slot, :, lo : lo + value.shape[1]] = blocks[a]

    def row_cols(zz):
        return pl.ds(pl.multiple_of(zz * share, 128), share)

    half_out, half_in = D // 2, qkv_width // 2
    swaps[0].wait_recv()
    swaps[3].wait_recv()

    @pl.loop(0, n)
    def _(j):
        zz = at.far(j)
        branch = both(gb, pair.at[3], pl.ds(pl.multiple_of(c * half_out, 128), half_out))
        store(pout, zz, 0, mm(both(mixed_ref, pair.at[0], row_cols(zz)), branch, TN))
        outs.s1(zz)

    for copy in fetched[8:]:
        copy.wait()
    scale = HEAD ** (-0.5)
    for g in range(KV_HEADS):
        heads = [slice((g * groups + j) * HEAD, (g * groups + j + 1) * HEAD) for j in range(groups)]
        kv = slice(g * HEAD, (g + 1) * HEAD)
        qs = jnp.concatenate([q_ref[:, h] for h in heads], axis=0)
        ms = jnp.concatenate([gm[:, h] for h in heads], axis=0)
        ks, vs = k_ref[:, kv], v_ref[:, kv]
        probs = p_ref[g]
        grad_values = mm(probs.astype(bf16), ms, TN)
        grad_probs = mm(ms, vs, NT)
        grad_scores = (probs * (grad_probs - jnp.sum(probs * grad_probs, axis=1, keepdims=True))).astype(bf16)
        grad_query = mm(grad_scores, ks) * scale
        for j, h in enumerate(heads):
            flat[:, h] = grad_query[j * rows : (j + 1) * rows]
        flat[:, q_width + kv.start : q_width + kv.stop] = mm(grad_scores, qs, TN) * scale
        flat[:, q_width + k_width + kv.start : q_width + k_width + kv.stop] = grad_values
    for j in range(n):
        outs.s2(at.far(j))
    cos, sin = cos_ref[...], sin_ref[...]
    for t in range(qkv_width // 128):
        tile = flat[:, t * 128 : (t + 1) * 128]
        if t * 128 < q_width + k_width:
            tile = tile * cos - swap_halves(tile) * sin
        gq[0, :, t * 128 : (t + 1) * 128] = tile.astype(bf16)
    swap_q.start()
    loads[2].wait()
    x = tok_ref[...].astype(f32)
    inv_first = inverse_rms(x)
    unit = x * inv_first
    grad_first = jnp.concatenate(
        [mm(gq[0], wv[8 * i : 8 * (i + 1), :, :qkv_width].reshape(8 * shard, qkv_width), NT) for i in range(n)], axis=1)
    pull = grad_first * gain_ref[0:1, :]
    sums[0, 0:1, :] = jnp.sum(grad_first * unit, axis=0, keepdims=True)
    sums[0, 2:, :] = jnp.zeros((6, D), f32)
    swap_s.start()
    gtok_ref[...] += inv_first * (pull - unit * jnp.mean(pull * unit, axis=1, keepdims=True))
    for i in (1, 2):
        swaps[i].wait_recv()
    swap_l.wait_recv()
    swap_q.wait_recv()
    swap_s.wait_recv()
    gains = sums[0] + sums[1]
    high = gains.astype(bf16)
    low = (gains - high.astype(f32)).astype(bf16)
    swap_s.wait_send()
    sums[0] = high.astype(f32)
    sums[1] = low.astype(f32)
    line = lax.rem(lax.broadcasted_iota(jnp.int32, (16, 128), 0), 8)
    where = (((line == 0) & (lane_tile(16) == experts)) | ((line == 1) & (lane_tile(16) == experts + 1))).astype(bf16)

    @pl.loop(0, n)
    def _(j):
        zz = at.far(j)
        cols = row_cols(zz)
        normed = both(nf_ref, pair.at[1], cols)
        for q in range(2):
            part = pl.ds(pl.multiple_of(c * half_in + q * (half_in // 2), 128), half_in // 2)
            grad = jnp.concatenate([gq[0, :, part], gq[1, :, part]], axis=0)
            store(pin, zz, q * (half_in // 2), mm(normed, grad, TN))
        tail = mm(both(disp_ref, pair.at[2], cols), jnp.concatenate([gl[0], gl[1]], axis=0), TN)
        rows_now = jnp.concatenate([sums[0, :, cols], sums[1, :, cols]], axis=0).astype(bf16)
        store(pin, zz, half_in, tail + mm(rows_now, where, TN))

        @pl.when(j < 2)
        def _():
            ins.corners(zz)

    for j in range(n + 1):
        ins.step(j)
        if j < n:
            outs.s3(at.far(j))
            outs.lines(j)
    outs.last()
    mine, theirs = pl.ds(pl.multiple_of(c * shard, 8), shard), pl.ds(pl.multiple_of((1 - c) * shard, 8), shard)
    cols_out, cols_in = pl.ds(pl.multiple_of(c * half_out, 128), half_out), pl.ds(pl.multiple_of(c * half_in, 128), half_in)
    end_out = send(tot_out.at[theirs, :], gout_ref.at[:, cols_out], end_ss.at[0], end_sr.at[0], at.sib)
    end_out.start()
    gout_ref[:, cols_out] = tot_out[mine, :]
    ins.last()
    end_in = send(tot_in.at[theirs, pl.ds(0, half_in)], gin_ref.at[:, cols_in], end_ss.at[1], end_sr.at[1], at.sib)
    end_in.start()
    gin_ref[:, cols_in] = tot_in[mine, :half_in]
    gtail_ref[...] = tot_in[mine, half_in:]
    own_share.wait()
    for k in range(1, n):
        exchange(k).wait_send()
        source = lax.rem(d + k, n)
        send(gup_ref.at[pl.ds(0, share), :], arrived.at[source], a2a_ss.at[k], a2a_sr.at[source], (source, at.e)).wait_recv()

    end_out.wait()
    end_in.wait()
    for swap in swaps + [swap_q, swap_l]:
        swap.wait_send()
    outs.finish()
    ins.finish()


def backward_layer(gs, tok, cot, mid, gates, gain, nf, disp, q, k, v, p, mixed, cos, sin, w_all, gup, n, experts, cid):
    f32, bf16 = jnp.float32, jnp.bfloat16
    rows = tok.shape[0]
    shard, wide = w_all.shape[1:]
    qkv_width = (HEADS + 2 * KV_HEADS) * HEAD
    share = D // n
    D_ = pltpu.SemaphoreType.DMA
    V = lambda *s: pltpu.VMEM(s, bf16)
    W = lambda *s: pltpu.VMEM(s, f32)
    any_, vm = pl.BlockSpec(memory_space=pl.ANY), pl.BlockSpec(memory_space=pltpu.VMEM)
    S = jax.ShapeDtypeStruct
    width_out, width_in = D // 2, qkv_width // 2 + 128
    return pl.pallas_call(
        functools.partial(backward_kernel, n, experts),
        out_shape=(S((rows, D), f32), S((shard, D), f32), S((shard, qkv_width), f32), S((shard, 128), f32), S((n, share, gup.shape[1]), bf16)),
        in_specs=[any_] * 17,
        out_specs=[vm] * 4 + [any_],
        scratch_shapes=[pltpu.VMEM(a.shape, a.dtype) for a in (gs, tok, cot, mid, gates, gain, nf, disp, q, k, v, p, mixed, cos, sin)]
        + [V(n * 8, shard, wide), V(n, 4, 2 * shard, width_out), V(n, 4, 2 * shard, width_in),
                        W(2 * shard, width_out), W(2 * shard, width_in),
                        V(4, rows, D), V(2, rows, qkv_width), V(2, rows, 128), W(2, 8, D), V(rows, D), V(rows, D), W(rows, qkv_width)]
        + reduce_scratch(n, 2 * shard, width_out) + reduce_scratch(n, 2 * shard, width_in)
        + [D_((4,)), D_((7,)), D_((7,)), D_((n,)), D_((n,)), D_((2,)), D_((2,)), D_((15,))],
        compiler_params=pltpu.CompilerParams(collective_id=cid, has_side_effects=True, vmem_limit_bytes=62 << 20),
        name="backward_layer",
    )(gs, tok, cot, mid, gates, gain, nf, disp, q, k, v, p, mixed, cos, sin, w_all, gup)


def results_kernel(experts, arrived, layer_in, tok_in, down_in, out_in, qkv_in, tail_in,
                   up_ref, layer_ref, tok_ref, down_ref, proj_ref, qkv_ref, router_ref, gains_ref):
    n, width = arrived.shape[0], arrived.shape[2]
    f = FF // n
    for q in range(n):
        for j in range(width // f):
            lo = (j % 2) * FF + q * f
            up_ref[j // 2, :, lo : lo + f] = arrived[q, :, j * f : (j + 1) * f].astype(jnp.float32)

    layer_ref[...] = layer_in[...].astype(jnp.bfloat16)
    tok_ref[...] = tok_in[...]
    down_ref[...] = down_in[...]

    @pl.when(pl.program_id(0) == 0)
    def _():
        proj_ref[...] = out_in[...]
        qkv_ref[...] = qkv_in[...]
        turned = jnp.transpose(jnp.concatenate([tail_in[...], jnp.zeros((128 - tail_in.shape[0], 128), jnp.float32)], axis=0))
        router_ref[...] = turned[:experts, : tail_in.shape[0]]
        gains_ref[...] = turned[experts : experts + 8, : tail_in.shape[0]]


def results(arrived, layer, tok, down, proj, qkv, tail, held, experts):
    n, share, width = arrived.shape
    f32 = jnp.float32
    steps = 4
    rows = share // steps
    whole = lambda a: pl.BlockSpec(a.shape, lambda i: (0,) * len(a.shape))
    part = lambda a: pl.BlockSpec((a.shape[0] // steps, a.shape[1]), lambda i: (i, 0))
    shapes = [jax.ShapeDtypeStruct(a.shape, f32) for a in (tok, down, proj, qkv)]
    shapes += [jax.ShapeDtypeStruct((experts, tail.shape[0]), f32), jax.ShapeDtypeStruct((8, tail.shape[0]), f32)]
    return pl.pallas_call(
        functools.partial(results_kernel, experts),
        grid=(steps,),
        out_shape=[jax.ShapeDtypeStruct((held, share, 2 * FF), f32), jax.ShapeDtypeStruct(layer.shape, jnp.bfloat16)] + shapes,
        in_specs=[pl.BlockSpec((n, rows, width), lambda i: (0, i, 0))] + [part(a) for a in (layer, tok, down)] + [whole(a) for a in (proj, qkv, tail)],
        out_specs=[pl.BlockSpec((held, rows, 2 * FF), lambda i: (0, i, 0))] + [part(a) for a in (layer, tok, down)] + [whole(a) for a in shapes[2:]],
        compiler_params=pltpu.CompilerParams(vmem_limit_bytes=62 << 20),
        name="results",
    )(arrived, layer, tok, down, proj, qkv, tail)


def per_device_fast(n, tokens, segments, routes, cotangent, gain_attn, attn_in, attn_out, gain_ffn, router, expert_in, expert_out):
    micro, rows = tokens.shape[:2]
    total = micro * rows
    held = expert_in.shape[0]
    experts = held * 8
    f = FF // n
    x = tokens.reshape(total, D)
    cot = cotangent.reshape(total, D)
    w_all, cot_all, up, disp, middle, gates, gain, nf, q, k, v, p, mixed, cos, sin = forward_layer(
        x, cot, attn_in, attn_out, router, gain_attn, gain_ffn, expert_in, segments, routes, n, experts, 0)
    out, grad_sum, grad_up, grad_down = expert_layer(disp, cot_all, up, expert_out.reshape(held * f, D), middle, n, experts, 1)
    grad_tokens, grad_out, grad_in, grad_tail, grad_up = backward_layer(
        grad_sum, x, cot, middle, gates, gain, nf, disp, q, k, v, p, mixed, cos, sin, w_all, grad_up, n, experts, 2)
    grad_up, out, grad_tokens, grad_down, grad_out, grad_in, grad_router, grad_gains = results(
        grad_up, out, grad_tokens, grad_down, grad_out, grad_in, grad_tail, held, experts)
    return (
        out.reshape(micro, rows, D),
        grad_tokens.reshape(micro, rows, D),
        grad_gains[0],
        grad_in,
        grad_out,
        grad_gains[1],
        grad_router.T,
        grad_up,
        grad_down.reshape(held, f, D),
    )


def solution(mesh):
    placed = (
        P(None, ("dp", "expert"), None),
        P(None, ("dp", "expert"), None),
        P(None, ("dp", "expert"), None),
        P(None, ("dp", "expert"), None),
        P(("dp", "expert")),
        P(("dp", "expert"), None),
        P(("dp", "expert"), None),
        P(("dp", "expert")),
        P(("dp", "expert"), None),
        P("expert", "dp", None),
        P("expert", "dp", None),
    )
    fast = mesh.shape["expert"] == 8 and FF // mesh.shape["dp"] == 128
    body = functools.partial(per_device_fast, mesh.shape["dp"]) if fast else per_device
    return jax.shard_map(
        body,
        mesh=mesh,
        in_specs=placed,
        out_specs=(
            P(None, ("dp", "expert"), None),
            P(None, ("dp", "expert"), None),
            P(("dp", "expert")),
            P(("dp", "expert"), None),
            P(("dp", "expert"), None),
            P(("dp", "expert")),
            P(("dp", "expert"), None),
            P("expert", "dp", None),
            P("expert", "dp", None),
        ),
        check_vma=False,
    )
```
